32 devices in a mesh: wide: 16 (over z, y, core), narrow: 2 (over x).
Axes of the slice: x: 2, y: 2, z: 4, core: 2. Of those that a mesh axis runs over, the one named last changes fastest.
Arguments:
- tokens: bfloat16 [16384, 1152], P(('wide', 'narrow')), may hold values from -6 to 6
- condition: bfloat16 [256, 1152], replicated, may hold values from -6 to 6
- cotangent: bfloat16 [16384, 1152], P('wide'), may hold values from -6 to 6
- modulator: bfloat16 [1152, 6, 1152], P(None, None, 'narrow'), may hold values from -0.1875 to 0.1875
- modulator_bias: bfloat16 [6, 1152], P(None, 'narrow'), may hold values from -2 to 2
- qkv_weight: bfloat16 [1152, 3, 1152], P(None, None, 'narrow'), may hold values from -0.1875 to 0.1875
- qv_bias: bfloat16 [2, 1152], P(None, 'narrow'), may hold values from -2 to 2
- out_weight: bfloat16 [1152, 1152], P('narrow'), may hold values from -1.5 to 1.5
- out_bias: bfloat16 [1152], replicated, may hold values from -2 to 2
- up_weight: bfloat16 [1152, 4608], P(None, 'narrow'), may hold values from -0.1875 to 0.1875
- up_bias: bfloat16 [4608], P('narrow'), may hold values from -2 to 2
- down_weight: bfloat16 [4608, 1152], P('narrow'), may hold values from -0.09375 to 0.09375
- down_bias: bfloat16 [1152], replicated, may hold values from -2 to 2
- segment_ids: int32 [16384], replicated, may hold values from 0 to 255, as said below
- valid_counts: int32 [16], replicated, may hold values from 640 to 1024, as said below
Outputs:
- layer_out: bfloat16 [16384, 1152], P(('wide', 'narrow'))
- tokens_grad: float32 [16384, 1152], P(('wide', 'narrow'))
- condition_grad: float32 [256, 1152], replicated
- modulator_grad: float32 [1152, 6, 1152], P(None, None, 'narrow')
- modulator_bias_grad: float32 [6, 1152], P(None, 'narrow')
- qkv_weight_grad: float32 [1152, 3, 1152], P(None, None, 'narrow')
- qv_bias_grad: float32 [2, 1152], P(None, 'narrow')
- out_weight_grad: float32 [1152, 1152], P('narrow')
- out_bias_grad: float32 [1152], replicated
- up_weight_grad: float32 [1152, 4608], P(None, 'narrow')
- up_bias_grad: float32 [4608], P('narrow')
- down_weight_grad: float32 [4608, 1152], P('narrow')
- down_bias_grad: float32 [1152], replicated
The draws below stay inside these ranges and needn't reach their ends.
Inputs may be any that keep to these rules, and one draw needn't show every extreme that they name: `segment_ids`: over the valid slots of the packed stream, in order, ids never fall and each id covers at most 128 slots; some id covers exactly 128, and the last valid slot carries 256 - 1. A padding slot carries the id of its shard's last valid slot. `valid_counts`: the valid slots of a shard come first in it; one shard is full.
All inputs are finite; a program needn't handle non-finite values.
Results may differ from the reference program's by a relative error of at most 0.02.
Values may be sent and summed in bfloat16 or wider, within the bound.
A program may use at most 256 MiB of HBM per device.

```python
import jax
import jax.numpy as jnp
from jax import lax

D = 1152
HEADS = 16
HD = 72
FF = 4608
TOK_DEV = 1024
IMG_MAX = 128
IMG_MIN = 64
TOKENS = 16384
IMG_ROW = 256
IMAGES = 256
N_WIDE = 16


def packing_layout(key):
    base = jax.random.fold_in(key, 11)
    count_key, pick_key, length_key, longest_key = jax.random.split(base, 4)
    shards = TOKENS // TOK_DEV
    lowest = TOK_DEV - min(512, TOK_DEV) + IMG_MAX
    counts = jax.random.randint(count_key, (shards,), lowest, TOK_DEV + 1).astype(jnp.int32)
    chosen = jax.random.randint(pick_key, (), 0, shards).astype(jnp.int32)
    shard_index = jnp.arange(shards, dtype=jnp.int32)
    counts = jnp.where(shard_index == chosen, TOK_DEV, counts).astype(jnp.int32)
    lengths = jax.random.randint(length_key, (IMG_ROW,), IMG_MIN, IMG_MAX + 1).astype(jnp.int32)
    longest = jax.random.randint(longest_key, (), 0, 2).astype(jnp.int32)
    lengths = jnp.where(jnp.arange(IMG_ROW, dtype=jnp.int32) == longest, IMG_MAX, lengths).astype(jnp.int32)
    image_ends = jnp.cumsum(lengths).astype(jnp.int32)
    before = (jnp.cumsum(counts) - counts).astype(jnp.int32)
    slot_index = jnp.arange(TOK_DEV, dtype=jnp.int32)
    within = jnp.minimum(slot_index[None, :], counts[:, None] - 1)
    placed = before[:, None] + within
    image_local = jnp.sum((image_ends[None, None, :] <= placed[:, :, None]).astype(jnp.int32), axis=-1)
    total = jnp.sum(counts).astype(jnp.int32)
    last_image = jnp.sum((image_ends <= total - 1).astype(jnp.int32))
    image_local = jnp.where(image_local == last_image, IMG_ROW - 1, image_local).astype(jnp.int32)
    identity = image_local.reshape(TOKENS).astype(jnp.int32)
    return (identity, counts)


def draw_segment_ids(key, part):
    return packing_layout(key)[0]


def draw_valid_counts(key, part):
    return packing_layout(key)[1]


def levels(stream_key, shape, cuts, smallest, largest):
    factor_of, own = 1.0, jax.random.fold_in(stream_key, 6)
    for position, shards_of in cuts:
        heights = jnp.exp(jax.random.uniform(jax.random.fold_in(own, position), (shards_of,), jnp.float32, smallest / len(cuts), largest / len(cuts)))
        factor_of = factor_of * jnp.repeat(heights, shape[position] // shards_of).reshape([-1 if axis == position else 1 for axis in range(len(shape))])
    return factor_of


def gaussian(rng, extent, spread, reach, cuts=(), kind=jnp.bfloat16):
    drawn = spread * jax.random.normal(rng, extent, jnp.float32)
    if cuts:
        drawn = drawn * levels(rng, extent, cuts, -0.22, 0.18)
    return jnp.clip(drawn, -reach, reach).astype(kind)


def setup_inputs(seed: int = 0) -> dict:
    arg_keys = jax.random.split(jax.random.key(seed), 16)
    return {
        "tokens": gaussian(arg_keys[0], (TOKENS, D), 1.0, 6.0, ((0, 32),)),
        "condition": gaussian(arg_keys[1], (IMAGES, D), 1.0, 6.0),
        "cotangent": gaussian(arg_keys[2], (TOKENS, D), 1.0, 6.0, ((0, 16),)),
        "modulator": gaussian(arg_keys[3], (D, 6, D), D ** -0.5, 0.1875, ((2, 2),)),
        "modulator_bias": gaussian(arg_keys[4], (6, D), 0.3, 2.0, ((1, 2),)),
        "qkv_weight": gaussian(arg_keys[5], (D, 3, D), D ** -0.5, 0.1875, ((2, 2),)),
        "qv_bias": gaussian(arg_keys[6], (2, D), 0.3, 2.0, ((1, 2),)),
        "out_weight": gaussian(arg_keys[7], (D, D), HEADS ** -0.5, 1.5, ((0, 2),)),
        "out_bias": gaussian(arg_keys[8], (D,), 0.3, 2.0),
        "up_weight": gaussian(arg_keys[9], (D, FF), D ** -0.5, 0.1875, ((1, 2),)),
        "up_bias": gaussian(arg_keys[10], (FF,), 0.3, 2.0, ((0, 2),)),
        "down_weight": gaussian(arg_keys[11], (FF, D), FF ** -0.5, 0.09375, ((0, 2),)),
        "down_bias": gaussian(arg_keys[12], (D,), 0.3, 2.0),
        "segment_ids": draw_segment_ids(jax.random.fold_in(arg_keys[15], 71), 0),
        "valid_counts": draw_valid_counts(jax.random.fold_in(arg_keys[15], 71), 0),
    }


@jax.custom_vjp
def low(v):
    return lax.optimization_barrier(v.astype(jnp.bfloat16)).astype(jnp.float32)

@jax.custom_vjp
def low_back(v):
    return v

def low_keep(v):
    return (low(v), None)

def low_pass(kept, grad):
    return (grad,)

def back_keep(v):
    return (v, None)

def back_low(kept, grad):
    return (low(grad),)
low.defvjp(low_keep, low_pass)
low_back.defvjp(back_keep, back_low)

def high_dot(left_side, right_side):
    return jnp.dot(left_side, right_side, precision=lax.Precision.HIGHEST)

def norm_modulate(field, shift, scale):
    centred = field - lax.optimization_barrier(jnp.mean(field, axis=-1, keepdims=True))
    variance = lax.optimization_barrier(jnp.mean(centred * centred, axis=-1, keepdims=True))
    return centred * lax.rsqrt(variance + 1e-06) * (1.0 + scale) + shift

def shard_attention(queries, key_rows, values, query_ids, key_ids):
    scores = jnp.einsum('ihd,jhd->hij', queries, key_rows, precision=lax.Precision.HIGHEST) * HD ** (-0.5)
    scores = low_back(scores)
    same_seg = query_ids[:, None] == key_ids[None, :]
    scores = jnp.where(same_seg[None], scores, -1e+30)
    attend = jax.nn.softmax(scores, axis=-1)
    return jnp.einsum('hij,jhd->ihd', low(attend), values, precision=lax.Precision.HIGHEST)

def layer_forward(tokens, condition, modulator, modulator_bias, qkv_weight, qv_bias, out_weight, out_bias, up_weight, up_bias, down_weight, down_bias, segment_ids, live_mask):
    activated = low(jax.nn.silu(condition))
    modulation = jnp.einsum('md,djf->mjf', activated, modulator, precision=lax.Precision.HIGHEST) + modulator_bias[None]

    def per_token(index):
        return modulation[segment_ids, index]
    live_col = live_mask[:, None]
    norm_one = low(norm_modulate(tokens, per_token(0), per_token(1)))
    projected = high_dot(norm_one, qkv_weight.reshape(D, 3 * D))
    queries = low(low_back(projected[:, :D] + qv_bias[0]))
    key_rows = low(low_back(projected[:, D:2 * D]))
    values = low(low_back(projected[:, 2 * D:] + qv_bias[1]))
    key_ids = jnp.where(live_mask > 0, segment_ids, -1).astype(jnp.int32)
    pad_rows = jnp.zeros((TOK_DEV, HEADS, HD), jnp.float32)
    keys_all = jnp.concatenate([pad_rows, key_rows.reshape(TOKENS, HEADS, HD), pad_rows], axis=0)
    values_all = jnp.concatenate([pad_rows, values.reshape(TOKENS, HEADS, HD), pad_rows], axis=0)
    pad_ids = jnp.full((TOK_DEV,), -2, jnp.int32)
    ids_all = jnp.concatenate([pad_ids, key_ids, pad_ids]).astype(jnp.int32)

    def shard_step(carry, shard_parts):
        query_block, query_ids, start = shard_parts
        key_win = lax.dynamic_slice_in_dim(keys_all, start, 3 * TOK_DEV)
        value_win = lax.dynamic_slice_in_dim(values_all, start, 3 * TOK_DEV)
        id_win = lax.dynamic_slice_in_dim(ids_all, start, 3 * TOK_DEV)
        return (carry, shard_attention(query_block, key_win, value_win, query_ids, id_win))
    starts = (jnp.arange(N_WIDE) * TOK_DEV).astype(jnp.int32)
    shaped = (queries.reshape(N_WIDE, TOK_DEV, HEADS, HD), key_ids.reshape(N_WIDE, TOK_DEV), starts)
    unused, context = lax.scan(jax.checkpoint(shard_step), jnp.zeros((), jnp.float32), shaped)
    context = low(low_back(context.reshape(TOKENS, D)))
    attn = low_back(high_dot(context, out_weight) + out_bias)
    middle = tokens + live_col * per_token(2) * attn
    norm_two = low(norm_modulate(middle, per_token(3), per_token(4)))
    upper = low_back(high_dot(norm_two, up_weight) + up_bias)
    hidden = low(jax.nn.gelu(upper, approximate=True))
    branch = low_back(high_dot(hidden, down_weight) + down_bias)
    return middle + live_col * per_token(5) * branch

def reference(tokens, condition, cotangent, modulator, modulator_bias, qkv_weight, qv_bias, out_weight, out_bias, up_weight, up_bias, down_weight, down_bias, segment_ids, valid_counts):
    live_mask = (jnp.arange(TOK_DEV)[None, :] < valid_counts[:, None]).reshape(TOKENS).astype(jnp.float32)

    def forward(tokens_in, condition_in, modulator_in, modulator_bias_in, qkv_in, qv_bias_in, out_in, out_bias_in, up_in, up_bias_in, down_in, down_bias_in):
        return layer_forward(tokens_in, condition_in, modulator_in, modulator_bias_in, qkv_in, qv_bias_in, out_in, out_bias_in, up_in, up_bias_in, down_in, down_bias_in, segment_ids, live_mask)
    layer_out, pullback = jax.vjp(forward, tokens.astype(jnp.float32), condition.astype(jnp.float32), modulator.astype(jnp.float32), modulator_bias.astype(jnp.float32), qkv_weight.astype(jnp.float32), qv_bias.astype(jnp.float32), out_weight.astype(jnp.float32), out_bias.astype(jnp.float32), up_weight.astype(jnp.float32), up_bias.astype(jnp.float32), down_weight.astype(jnp.float32), down_bias.astype(jnp.float32))
    grads = pullback(cotangent.astype(jnp.float32))
    return (layer_out.astype(jnp.bfloat16), grads[0], grads[1], grads[2], grads[3], grads[4], grads[5], grads[6], grads[7], grads[8], grads[9], grads[10], grads[11])
```

```python
import jax
import jax.numpy as jnp
from jax import lax
from jax.sharding import PartitionSpec as P

HD = 72
IMG_MAX = 128
EPSILON = 1e-06
NEG_FILL = -1e30
F32 = jnp.float32
BF16 = jnp.bfloat16


def dot(left, right, dims, out=F32):
    return lax.dot_general(left, right, (dims, ((), ())), preferred_element_type=F32).astype(out)


def swap(part):
    return lax.ppermute(part, "narrow", [(0, 1), (1, 0)])


def narrow_gather(part):
    if lax.axis_size("narrow") != 2:
        return lax.all_gather(part, "narrow", axis=0, tiled=True)
    other = swap(part)
    first = lax.axis_index("narrow") == 0
    return jnp.where(
        first, jnp.concatenate([part, other], axis=0), jnp.concatenate([other, part], axis=0)
    )


def narrow_sum(part):
    if lax.axis_size("narrow") != 2:
        return lax.psum(part, "narrow").astype(F32)
    return part.astype(F32) + swap(part).astype(F32)


def narrow_scatter(part, dim=0):
    count = lax.axis_size("narrow")
    if count != 2:
        return lax.psum_scatter(part, "narrow", scatter_dimension=dim, tiled=True).astype(F32)
    size = part.shape[dim] // 2
    index = lax.axis_index("narrow")
    mine = lax.dynamic_slice_in_dim(part, index * size, size, axis=dim)
    theirs = lax.dynamic_slice_in_dim(part, (1 - index) * size, size, axis=dim)
    return mine.astype(F32) + swap(theirs).astype(F32)


def padded(cells, width):
    count = lax.axis_size("wide")
    ends = count - 1
    tail = cells[cells.shape[0] - width :]
    return (
        lax.ppermute(tail, "wide", [(i, (i + 1) % count) for i in range(ends)]),
        lax.ppermute(cells[:width], "wide", [((i + 1) % count, i) for i in range(ends)]),
    )


def norm(field):
    centred = field - jnp.mean(field, axis=-1, keepdims=True)
    rstd = lax.rsqrt(jnp.mean(centred * centred, axis=-1, keepdims=True) + EPSILON)
    return centred * rstd, rstd


def norm_back(grad, xhat, rstd):
    return rstd * (
        grad
        - jnp.mean(grad, axis=-1, keepdims=True)
        - xhat * jnp.mean(grad * xhat, axis=-1, keepdims=True)
    )


def gelu_pair(v):
    c = 0.7978845608028654
    sq = v * v
    t = jnp.tanh(c * v * (1.0 + 0.044715 * sq))
    half = 0.5 * (1.0 + t)
    slope = half + 0.5 * v * (1.0 - t * t) * c * (1.0 + 3 * 0.044715 * sq)
    return v * half, slope


def body(
    tokens,
    condition,
    cotangent,
    modulator,
    modulator_bias,
    qkv_weight,
    qv_bias,
    out_weight,
    out_bias,
    up_weight,
    up_bias,
    down_weight,
    down_bias,
    segment_ids,
    valid_counts,
):
    wide_count = lax.axis_size("wide")
    wide_index = lax.axis_index("wide")
    narrow_index = lax.axis_index("narrow")
    tok_dev = cotangent.shape[0]
    share = tokens.shape[0]
    width = tokens.shape[1]
    part_width = qkv_weight.shape[2]
    heads = part_width // HD
    img_row = condition.shape[0]
    span = IMG_MAX
    block = min(512, tok_dev)
    window = block + 2 * span
    scale_factor = HD ** (-0.5)
    own_count = valid_counts[wide_index]
    positions = jnp.arange(tok_dev, dtype=jnp.int32)
    own_ids = lax.dynamic_slice_in_dim(segment_ids, wide_index * tok_dev, tok_dev)
    live_full = (positions < own_count).astype(jnp.float32)
    share_start = narrow_index * share
    live = live_full[:, None]
    image_slots = jnp.arange(img_row, dtype=jnp.int32)
    onehot_full = (own_ids[:, None] == image_slots[None, :]).astype(BF16)
    onehot_share = lax.dynamic_slice_in_dim(onehot_full, share_start, share)
    cond_rows = condition.astype(F32)
    sigmoid_rows = jax.nn.sigmoid(cond_rows)
    activated = (cond_rows * sigmoid_rows).astype(BF16)
    tok_full = narrow_gather(tokens).astype(F32)
    mod_width = modulator.shape[2]
    mod_part = dot(activated, modulator.reshape(width, -1), ((1,), (0,)))
    mod_part = (mod_part.reshape(img_row, 6, -1) + modulator_bias.astype(F32)[None]).astype(BF16)
    mod_rows = jnp.moveaxis(mod_part, 2, 0)

    def per_token(parts):
        rows = narrow_gather(mod_rows[:, :, parts[0] : parts[1]])
        return [
            dot(onehot_full, rows[:, :, i], ((1,), (1,)), BF16).astype(F32)
            for i in range(parts[1] - parts[0])
        ]

    shift_one, scale_one = per_token((0, 2))
    gate_one, shift_two, scale_two, gate_two = per_token((2, 6))
    xhat_one, rstd_one = norm(tok_full)
    norm_one = (xhat_one * (1.0 + scale_one) + shift_one).astype(BF16)
    projected = dot(norm_one, qkv_weight.reshape(width, -1), ((1,), (0,)))
    bias_pair = qv_bias.astype(F32)
    queries = (projected[:, :part_width] + bias_pair[0]).astype(BF16)
    key_rows = projected[:, part_width : 2 * part_width].astype(BF16)
    value_rows = (projected[:, 2 * part_width :] + bias_pair[1]).astype(BF16)
    key_value = jnp.concatenate([key_rows, value_rows], axis=1)
    tail_start = own_count - span
    edge_rows = jnp.concatenate(
        [key_value[:span], lax.dynamic_slice_in_dim(key_value, tail_start, span)], axis=0
    )
    from_left, from_right = padded(edge_rows, span)
    extended = jnp.concatenate([from_left, key_value, from_right], axis=0)
    left_index = jnp.maximum(wide_index - 1, 0)
    right_index = jnp.minimum(wide_index + 1, wide_count - 1)
    left_count = valid_counts[left_index]
    left_ids = lax.dynamic_slice_in_dim(segment_ids, left_index * tok_dev + left_count - span, span)
    left_ids = jnp.where(wide_index > 0, left_ids, -2)
    right_ids = lax.dynamic_slice_in_dim(segment_ids, right_index * tok_dev, span)
    right_ids = jnp.where(wide_index < wide_count - 1, right_ids, -2)
    own_keys = jnp.where(positions < own_count, own_ids, -1)
    extended_ids = jnp.concatenate([left_ids, own_keys, right_ids])

    def block_parts(block_idx):
        row_start = block_idx * block
        query_block = queries[row_start : row_start + block].reshape(block, heads, HD)
        pair_block = extended[row_start : row_start + window]
        key_block = pair_block[:, :part_width].reshape(window, heads, HD)
        value_block = pair_block[:, part_width:].reshape(window, heads, HD)
        same_seg = (
            own_keys[row_start : row_start + block, None]
            == extended_ids[None, row_start : row_start + window]
        )
        return (query_block, key_block, value_block, same_seg)

    def masked_scores(query_block, key_block, same_seg):
        raw = (
            jnp.einsum("ihd,jhd->hij", query_block, key_block, preferred_element_type=jnp.float32)
            * scale_factor
        )
        return jnp.where(same_seg[None], raw, NEG_FILL)

    blocks = tok_dev // block
    outputs = []
    log_sums = []
    for block_idx in range(blocks):
        query_block, key_block, value_block, same_seg = block_parts(block_idx)
        masked = masked_scores(query_block, key_block, same_seg)
        top_score = jnp.max(masked, axis=-1, keepdims=True)
        expo = jnp.exp(masked - top_score)
        totals = jnp.sum(expo, axis=-1, keepdims=True)
        attend = expo / totals
        log_sums.append(top_score + jnp.log(totals))
        block_out = jnp.einsum(
            "hij,jhd->ihd",
            attend.astype(jnp.bfloat16),
            value_block,
            preferred_element_type=jnp.float32,
        )
        outputs.append(block_out.reshape(block, part_width))
    context = jnp.concatenate(outputs, axis=0).astype(jnp.bfloat16)
    attn = narrow_sum(dot(context, out_weight, ((1,), (0,)), BF16)) + out_bias.astype(F32)
    middle = tok_full + live * gate_one * attn
    xhat_two, rstd_two = norm(middle)
    norm_two = (xhat_two * (1.0 + scale_two) + shift_two).astype(BF16)
    upstream = cotangent.astype(F32)
    d_branch = (live * gate_two * upstream).astype(BF16)
    d_hidden = dot(d_branch, down_weight, ((1,), (1,)))
    upper = dot(norm_two, up_weight, ((1,), (0,))) + up_bias.astype(F32)
    gelu, slope = gelu_pair(upper)
    hidden = gelu.astype(BF16)
    d_upper = (d_hidden * slope).astype(BF16)
    d_norm_two = narrow_sum(dot(d_upper, up_weight, ((1,), (1,)), BF16))
    branch = narrow_scatter(dot(hidden, down_weight, ((1,), (0,)), BF16)) + down_bias.astype(F32)

    def own(rows):
        return lax.dynamic_slice_in_dim(rows, share_start, share)

    layer_out = (own(middle) + own(live * gate_two) * branch).astype(BF16)
    up_grad = dot(d_upper, norm_two, ((0,), (0,)), BF16)
    down_grad = dot(hidden, d_branch, ((0,), (0,)), BF16)
    bias_rows = jnp.concatenate(
        [
            jnp.sum(d_upper.astype(F32), axis=0),
            jnp.sum(d_branch.astype(F32), axis=0),
            jnp.zeros(((-d_upper.shape[1] - width) % (8 * width),), F32),
        ]
    ).reshape(-1, width)
    mlp_flat = jnp.concatenate([up_grad, down_grad, bias_rows.astype(BF16)], axis=0)
    mlp_flat = lax.psum(mlp_flat, "wide")
    ff = up_weight.shape[1]
    up_weight_grad = mlp_flat[:ff].T.astype(F32)
    down_weight_grad = mlp_flat[ff : 2 * ff].astype(F32)
    mlp_bias = mlp_flat[2 * ff :].reshape(-1).astype(F32)
    up_bias_grad = mlp_bias[:ff]
    down_bias_grad = mlp_bias[ff : ff + width]

    d_middle = upstream + norm_back(d_norm_two * (1.0 + scale_two), xhat_two, rstd_two)
    d_attn = (live * gate_one * d_middle).astype(BF16)
    out_weight_grad = dot(context, d_attn, ((0,), (0,)), BF16)
    d_context = dot(d_attn, out_weight, ((1,), (1,)), BF16)
    d_extended = jnp.zeros((tok_dev + 2 * span, 2 * part_width), jnp.float32)
    query_grads = []
    for block_idx in range(blocks):
        query_block, key_block, value_block, same_seg = block_parts(block_idx)
        attend = jnp.exp(masked_scores(query_block, key_block, same_seg) - log_sums[block_idx])
        row_start = block_idx * block
        grad_block = d_context[row_start : row_start + block].reshape(block, heads, HD)
        d_attend = jnp.einsum(
            "ihd,jhd->hij", grad_block, value_block, preferred_element_type=jnp.float32
        )
        centre = jnp.sum(attend * d_attend, axis=-1, keepdims=True)
        d_scores = (attend * (d_attend - centre)).astype(jnp.bfloat16)
        query_grad = (
            jnp.einsum("hij,jhd->ihd", d_scores, key_block, preferred_element_type=jnp.float32)
            * scale_factor
        )
        query_grads.append(query_grad.reshape(block, part_width))
        key_grad = (
            jnp.einsum("hij,ihd->jhd", d_scores, query_block, preferred_element_type=jnp.float32)
            * scale_factor
        )
        value_grad = jnp.einsum(
            "hij,ihd->jhd",
            attend.astype(jnp.bfloat16),
            grad_block,
            preferred_element_type=jnp.float32,
        )
        pair_grad = jnp.concatenate(
            [key_grad.reshape(window, part_width), value_grad.reshape(window, part_width)], axis=1
        )
        d_extended = d_extended.at[row_start : row_start + window].add(pair_grad)
    back_edges = jnp.concatenate([d_extended[:span], d_extended[span + tok_dev :]], axis=0)
    back_left, back_right = padded(back_edges.astype(jnp.bfloat16), span)
    d_local = d_extended[span : span + tok_dev]
    d_local = d_local.at[:span].add(back_left.astype(F32))
    tail_sum = lax.dynamic_slice_in_dim(d_local, tail_start, span) + back_right.astype(F32)
    d_local = lax.dynamic_update_slice_in_dim(d_local, tail_sum, tail_start, 0)
    d_queries = jnp.concatenate(query_grads, axis=0).astype(BF16)
    d_pairs = d_local.astype(BF16)
    d_projected = jnp.concatenate([d_queries, d_pairs], axis=1)
    d_norm_one = narrow_scatter(
        dot(d_projected, qkv_weight.reshape(width, -1), ((1,), (1,)), BF16)
    )
    qkv_grad = dot(d_projected, norm_one, ((0,), (0,)), BF16)
    bias_rows = jnp.concatenate(
        [
            jnp.sum(d_queries.astype(F32), axis=0),
            jnp.sum(d_pairs[:, part_width:].astype(F32), axis=0),
            jnp.sum(d_attn.astype(F32), axis=0),
            jnp.zeros(((-2 * part_width - width) % (8 * width),), F32),
        ]
    ).reshape(-1, width)
    xhat_own = own(xhat_one)
    tokens_grad = own(d_middle) + norm_back(
        d_norm_one * (1.0 + own(scale_one)), xhat_own, own(rstd_one)
    )

    def image_sum(hot, term):
        return dot(hot, term.astype(BF16), ((0,), (0,)))

    def feature_part(rows):
        return lax.dynamic_slice_in_dim(rows, narrow_index * mod_width, mod_width, axis=1)

    own_terms = jnp.stack(
        [
            image_sum(onehot_share, d_norm_one),
            image_sum(onehot_share, d_norm_one * xhat_own),
            image_sum(onehot_share, own(live * upstream) * branch),
        ]
    ).astype(BF16)
    own_terms = narrow_scatter(own_terms, 2).astype(BF16)
    full_terms = [
        image_sum(onehot_full, feature_part(live * d_middle * attn)),
        image_sum(onehot_full, feature_part(d_norm_two)),
        image_sum(onehot_full, feature_part(d_norm_two * xhat_two)),
    ]
    full_terms = jnp.stack(full_terms).astype(BF16)
    d_mod = jnp.concatenate([own_terms[:2], full_terms, own_terms[2:]], axis=0)
    attn_flat = jnp.concatenate(
        [qkv_grad, out_weight_grad, bias_rows.astype(BF16), d_mod.reshape(-1, width)], axis=0
    )
    attn_flat = lax.psum(attn_flat, "wide")
    rows_of = [3 * part_width, part_width, bias_rows.shape[0]]
    starts = [0, rows_of[0], rows_of[0] + rows_of[1], sum(rows_of)]
    qkv_weight_grad = (
        attn_flat[: starts[1]].T.reshape(width, 3, part_width).astype(F32)
    )
    out_weight_grad = attn_flat[starts[1] : starts[2]].astype(F32)
    attn_bias = attn_flat[starts[2] : starts[3]].reshape(-1).astype(F32)
    qv_bias_grad = attn_bias[: 2 * part_width].reshape(2, part_width)
    out_bias_grad = attn_bias[2 * part_width : 2 * part_width + width]
    d_mod = attn_flat[starts[3] :].reshape(6, img_row, mod_width)
    modulator_grad = jnp.stack(
        [dot(activated, d_mod[j], ((0,), (0,))) for j in range(6)], axis=1
    )
    modulator_bias_grad = jnp.sum(d_mod.astype(F32), axis=1)
    d_activated = sum(dot(d_mod[j], modulator[:, j], ((1,), (1,))) for j in range(6))
    cond_part = d_activated * sigmoid_rows * (1.0 + cond_rows * (1.0 - sigmoid_rows))
    condition_grad = narrow_sum(cond_part.astype(BF16))
    return (
        layer_out,
        tokens_grad,
        condition_grad,
        modulator_grad,
        modulator_bias_grad,
        qkv_weight_grad,
        qv_bias_grad,
        out_weight_grad,
        out_bias_grad,
        up_weight_grad,
        up_bias_grad,
        down_weight_grad,
        down_bias_grad,
    )


def solution(mesh):
    in_specs = (
        P(("wide", "narrow"), None),
        P(),
        P("wide", None),
        P(None, None, "narrow"),
        P(None, "narrow"),
        P(None, None, "narrow"),
        P(None, "narrow"),
        P("narrow", None),
        P(),
        P(None, "narrow"),
        P("narrow"),
        P("narrow", None),
        P(),
        P(),
        P(),
    )
    out_specs = (
        P(("wide", "narrow"), None),
        P(("wide", "narrow"), None),
        P(),
        P(None, None, "narrow"),
        P(None, "narrow"),
        P(None, None, "narrow"),
        P(None, "narrow"),
        P("narrow", None),
        P(),
        P(None, "narrow"),
        P("narrow"),
        P("narrow", None),
        P(),
    )
    return jax.shard_map(body, mesh=mesh, in_specs=in_specs, out_specs=out_specs, check_vma=False)
```

```python
import jax
import jax.numpy as jnp
from jax import lax
from jax.experimental import pallas as pl
from jax.experimental.pallas import tpu as pltpu
from jax.sharding import PartitionSpec as P

HD = 72
IMG_MAX = 128
EPSILON = 1e-06
NEG_FILL = -1e30
F32 = jnp.float32
BF16 = jnp.bfloat16


def dot(left, right, dims, out=F32):
    return lax.dot_general(left, right, (dims, ((), ())), preferred_element_type=F32).astype(out)


def swap(part):
    return lax.ppermute(part, "narrow", [(0, 1), (1, 0)])


def narrow_gather(part):
    if lax.axis_size("narrow") != 2:
        return lax.all_gather(part, "narrow", axis=0, tiled=True)
    other = swap(part)
    first = lax.axis_index("narrow") == 0
    return jnp.where(
        first, jnp.concatenate([part, other], axis=0), jnp.concatenate([other, part], axis=0)
    )


def narrow_sum(part):
    if lax.axis_size("narrow") != 2:
        return lax.psum(part, "narrow").astype(F32)
    return part.astype(F32) + swap(part).astype(F32)


def narrow_scatter(part, dim=0):
    count = lax.axis_size("narrow")
    if count != 2:
        return lax.psum_scatter(part, "narrow", scatter_dimension=dim, tiled=True).astype(F32)
    size = part.shape[dim] // 2
    index = lax.axis_index("narrow")
    mine = lax.dynamic_slice_in_dim(part, index * size, size, axis=dim)
    theirs = lax.dynamic_slice_in_dim(part, (1 - index) * size, size, axis=dim)
    return mine.astype(F32) + swap(theirs).astype(F32)


def padded(cells, width):
    count = lax.axis_size("wide")
    ends = count - 1
    tail = cells[cells.shape[0] - width :]
    return (
        lax.ppermute(tail, "wide", [(i, (i + 1) % count) for i in range(ends)]),
        lax.ppermute(cells[:width], "wide", [((i + 1) % count, i) for i in range(ends)]),
    )


MESH = pl.DeviceIdType.MESH
UNIT = 48


def ring_kernel(chips, subs, data, out, mine, theirs, slots, copy_sems, core_sems, ring_sems):
    wide = lax.axis_index("wide")
    chip, core = wide // 2, wide % 2
    half = chips // 2

    def place(position):
        position = lax.rem(position + 2 * chips, chips)
        side = position // half
        return (1 - side) * 2 * position + side * (2 * (chips - 1 - position) + 1)

    position = chip // 2 + (chip % 2) * (chips - 1 - 2 * (chip // 2))
    ahead = 2 * place(position + 1) + core
    behind = 2 * place(position - 1) + core
    sibling = 2 * chip + 1 - core
    barrier = pltpu.get_barrier_semaphore()
    for device in (ahead, behind, sibling):
        pl.semaphore_signal(barrier, inc=1, device_id={"wide": device}, device_id_type=MESH)
    pl.semaphore_wait(barrier, 3)

    def local(lane):
        return pltpu.make_async_copy(data.at[lane, :, core], mine.at[lane], copy_sems.at[lane])

    def across(lane):
        return pltpu.make_async_remote_copy(
            src_ref=data.at[lane, :, 1 - core],
            dst_ref=theirs.at[lane],
            send_sem=core_sems.at[0, lane],
            recv_sem=core_sems.at[1, lane],
            device_id={"wide": sibling},
            device_id_type=MESH,
        )

    for lane in range(2):
        across(lane).start()
        local(lane).start()

    def hop(lane, step, sub):
        rows = pl.ds(sub * UNIT, UNIT)
        if step == 0:
            first = place(position - 1 if lane == 0 else position + 1)
            source = mine.at[lane, first, rows]
        else:
            source = slots.at[lane, step - 1, rows]
        return pltpu.make_async_remote_copy(
            src_ref=source,
            dst_ref=slots.at[lane, step, rows],
            send_sem=ring_sems.at[0, lane, step, sub],
            recv_sem=ring_sems.at[1, lane, step, sub],
            device_id={"wide": ahead if lane == 0 else behind},
            device_id_type=MESH,
        )

    for lane in range(2):
        local(lane).wait()
        across(lane).wait()

        def merge(index, carry, lane=lane):
            mine[lane, index] = mine[lane, index] + theirs[lane, index]
            return carry

        lax.fori_loop(0, chips, merge, 0)
        for sub in range(subs):
            hop(lane, 0, sub).start()
    for step in range(chips - 1):
        for sub in range(subs):
            for lane in range(2):
                hop(lane, step, sub).wait_recv()
                offset = 2 + step
                index = place(position - offset if lane == 0 else position + offset)
                rows = pl.ds(sub * UNIT, UNIT)
                total = slots[lane, step, rows] + mine[lane, index, rows]
                if step == chips - 2:
                    out[lane, rows] = total
                else:
                    slots[lane, step, rows] = total
                    hop(lane, step + 1, sub).start()
    for step in range(chips - 1):
        for sub in range(subs):
            for lane in range(2):
                hop(lane, step, sub).wait_send()


def ring_scatter(flat, collective_id):
    chips = lax.axis_size("wide") // 2
    shard = flat.shape[0] // (4 * chips)
    width = flat.shape[1]
    subs = shard // UNIT
    data = flat.reshape(2, chips, 2, shard, width)
    return pl.pallas_call(
        lambda *refs: ring_kernel(chips, subs, *refs),
        out_shape=jax.ShapeDtypeStruct((2, shard, width), BF16),
        in_specs=[pl.BlockSpec(memory_space=pl.ANY)],
        out_specs=pl.BlockSpec(memory_space=pltpu.VMEM),
        scratch_shapes=[
            pltpu.VMEM((2, chips, shard, width), BF16),
            pltpu.VMEM((2, chips, shard, width), BF16),
            pltpu.VMEM((2, chips - 1, shard, width), BF16),
            pltpu.SemaphoreType.DMA((2,)),
            pltpu.SemaphoreType.DMA((2, 2)),
            pltpu.SemaphoreType.DMA((2, 2, chips - 1, subs)),
        ],
        compiler_params=pltpu.CompilerParams(
            collective_id=collective_id, has_side_effects=True, vmem_limit_bytes=40 << 20
        ),
        name="ring_scatter",
    )(data)


def wide_sum(flat, loose, collective_id):
    count = lax.axis_size("wide")
    rows, width = flat.shape
    if lax.axis_size("narrow") != 2 or rows % (2 * count * UNIT):
        return lax.psum(flat, "wide"), jnp.sum(
            lax.all_gather(loose, "wide", axis=0).astype(F32), axis=0
        )
    mine = ring_scatter(flat, collective_id)
    shard = rows // (2 * count)
    parts = jnp.concatenate([mine.reshape(2 * shard, width), loose], axis=0)
    parts = lax.all_gather(parts, "wide", axis=0)
    lanes = [parts[:, lane * shard : (lane + 1) * shard].reshape(-1, width) for lane in range(2)]
    return jnp.concatenate(lanes, axis=0), jnp.sum(parts[:, 2 * shard :].astype(F32), axis=0)


def norm(field):
    centred = field - jnp.mean(field, axis=-1, keepdims=True)
    rstd = lax.rsqrt(jnp.mean(centred * centred, axis=-1, keepdims=True) + EPSILON)
    return centred * rstd, rstd


def norm_back(grad, xhat, rstd):
    return rstd * (
        grad
        - jnp.mean(grad, axis=-1, keepdims=True)
        - xhat * jnp.mean(grad * xhat, axis=-1, keepdims=True)
    )


def gelu_pair(v):
    c = 0.7978845608028654
    sq = v * v
    t = jnp.tanh(c * v * (1.0 + 0.044715 * sq))
    half = 0.5 * (1.0 + t)
    slope = half + 0.5 * v * (1.0 - t * t) * c * (1.0 + 3 * 0.044715 * sq)
    return v * half, slope


def body(
    tokens,
    condition,
    cotangent,
    modulator,
    modulator_bias,
    qkv_weight,
    qv_bias,
    out_weight,
    out_bias,
    up_weight,
    up_bias,
    down_weight,
    down_bias,
    segment_ids,
    valid_counts,
):
    wide_count = lax.axis_size("wide")
    wide_index = lax.axis_index("wide")
    narrow_index = lax.axis_index("narrow")
    tok_dev = cotangent.shape[0]
    share = tokens.shape[0]
    width = tokens.shape[1]
    part_width = qkv_weight.shape[2]
    heads = part_width // HD
    img_row = condition.shape[0]
    span = IMG_MAX
    block = min(512, tok_dev)
    window = block + 2 * span
    scale_factor = HD ** (-0.5)
    own_count = valid_counts[wide_index]
    positions = jnp.arange(tok_dev, dtype=jnp.int32)
    own_ids = lax.dynamic_slice_in_dim(segment_ids, wide_index * tok_dev, tok_dev)
    live_full = (positions < own_count).astype(jnp.float32)
    share_start = narrow_index * share
    live = live_full[:, None]
    image_slots = jnp.arange(img_row, dtype=jnp.int32)
    onehot_full = (own_ids[:, None] == image_slots[None, :]).astype(BF16)
    onehot_share = lax.dynamic_slice_in_dim(onehot_full, share_start, share)
    cond_rows = condition.astype(F32)
    sigmoid_rows = jax.nn.sigmoid(cond_rows)
    activated = (cond_rows * sigmoid_rows).astype(BF16)
    tok_full = narrow_gather(tokens).astype(F32)
    mod_width = modulator.shape[2]
    mod_part = dot(activated, modulator.reshape(width, -1), ((1,), (0,)))
    mod_part = (mod_part.reshape(img_row, 6, -1) + modulator_bias.astype(F32)[None]).astype(BF16)
    mod_rows = jnp.moveaxis(mod_part, 2, 0)

    def per_token(parts):
        rows = narrow_gather(mod_rows[:, :, parts[0] : parts[1]])
        return [
            dot(onehot_full, rows[:, :, i], ((1,), (1,)), BF16).astype(F32)
            for i in range(parts[1] - parts[0])
        ]

    shift_one, scale_one = per_token((0, 2))
    gate_one, shift_two, scale_two, gate_two = per_token((2, 6))
    xhat_one, rstd_one = norm(tok_full)
    norm_one = (xhat_one * (1.0 + scale_one) + shift_one).astype(BF16)
    projected = dot(norm_one, qkv_weight.reshape(width, -1), ((1,), (0,)))
    bias_pair = qv_bias.astype(F32)
    queries = (projected[:, :part_width] + bias_pair[0]).astype(BF16)
    key_rows = projected[:, part_width : 2 * part_width].astype(BF16)
    value_rows = (projected[:, 2 * part_width :] + bias_pair[1]).astype(BF16)
    key_value = jnp.concatenate([key_rows, value_rows], axis=1)
    tail_start = own_count - span
    edge_rows = jnp.concatenate(
        [key_value[:span], lax.dynamic_slice_in_dim(key_value, tail_start, span)], axis=0
    )
    from_left, from_right = padded(edge_rows, span)
    extended = jnp.concatenate([from_left, key_value, from_right], axis=0)
    left_index = jnp.maximum(wide_index - 1, 0)
    right_index = jnp.minimum(wide_index + 1, wide_count - 1)
    left_count = valid_counts[left_index]
    left_ids = lax.dynamic_slice_in_dim(segment_ids, left_index * tok_dev + left_count - span, span)
    left_ids = jnp.where(wide_index > 0, left_ids, -2)
    right_ids = lax.dynamic_slice_in_dim(segment_ids, right_index * tok_dev, span)
    right_ids = jnp.where(wide_index < wide_count - 1, right_ids, -2)
    own_keys = jnp.where(positions < own_count, own_ids, -1)
    extended_ids = jnp.concatenate([left_ids, own_keys, right_ids])

    def block_parts(block_idx):
        row_start = block_idx * block
        query_block = queries[row_start : row_start + block].reshape(block, heads, HD)
        pair_block = extended[row_start : row_start + window]
        key_block = pair_block[:, :part_width].reshape(window, heads, HD)
        value_block = pair_block[:, part_width:].reshape(window, heads, HD)
        same_seg = (
            own_keys[row_start : row_start + block, None]
            == extended_ids[None, row_start : row_start + window]
        )
        return (query_block, key_block, value_block, same_seg)

    def masked_scores(query_block, key_block, same_seg):
        raw = (
            jnp.einsum("ihd,jhd->hij", query_block, key_block, preferred_element_type=jnp.float32)
            * scale_factor
        )
        return jnp.where(same_seg[None], raw, NEG_FILL)

    blocks = tok_dev // block

    def rows_of(rows, block_idx):
        return rows[block_idx * block : (block_idx + 1) * block]

    def own(parts):
        rows = jnp.concatenate(parts, axis=0)
        return lax.dynamic_slice_in_dim(rows, share_start, share)

    upstream = cotangent.astype(F32)
    contexts, log_sums, attns, middles, xhats, rstds = [], [], [], [], [], []
    norms, hiddens, d_uppers, d_branches, d_norms, branches = [], [], [], [], [], []
    for block_idx in range(blocks):
        query_block, key_block, value_block, same_seg = block_parts(block_idx)
        masked = masked_scores(query_block, key_block, same_seg)
        top_score = jnp.max(masked, axis=-1, keepdims=True)
        expo = jnp.exp(masked - top_score)
        totals = jnp.sum(expo, axis=-1, keepdims=True)
        attend = expo / totals
        log_sums.append(top_score + jnp.log(totals))
        block_out = jnp.einsum(
            "hij,jhd->ihd", attend.astype(BF16), value_block, preferred_element_type=F32
        )
        contexts.append(block_out.reshape(block, part_width).astype(BF16))
        attn_part = dot(contexts[-1], out_weight, ((1,), (0,)), BF16)
        attns.append(narrow_sum(attn_part) + out_bias.astype(F32))
    for block_idx in range(blocks):
        gate_b = rows_of(live * gate_two, block_idx)
        d_branches.append((gate_b * rows_of(upstream, block_idx)).astype(BF16))
        d_hidden = dot(d_branches[-1], down_weight, ((1,), (1,)), BF16).astype(F32)
        middle = rows_of(tok_full, block_idx) + rows_of(live * gate_one, block_idx) * attns[block_idx]
        xhat, rstd = norm(middle)
        middles.append(middle)
        xhats.append(xhat)
        rstds.append(rstd)
        scale_b, shift_b = rows_of(scale_two, block_idx), rows_of(shift_two, block_idx)
        norms.append((xhat * (1.0 + scale_b) + shift_b).astype(BF16))
        upper = dot(norms[-1], up_weight, ((1,), (0,))) + up_bias.astype(F32)
        gelu, slope = gelu_pair(upper)
        hiddens.append(gelu.astype(BF16))
        d_uppers.append((d_hidden * slope).astype(BF16))
        d_norms.append(narrow_sum(dot(d_uppers[-1], up_weight, ((1,), (1,)), BF16)))
    hidden = jnp.concatenate(hiddens, axis=0)
    d_upper = jnp.concatenate(d_uppers, axis=0)
    d_branch = jnp.concatenate(d_branches, axis=0)
    norm_two = jnp.concatenate(norms, axis=0)
    context = jnp.concatenate(contexts, axis=0)
    down_grad = dot(hidden, d_branch, ((0,), (0,)), BF16)
    up_grad = dot(d_upper, norm_two, ((0,), (0,)), BF16)
    up_grad, down_grad = lax.psum((up_grad, down_grad), "wide")
    up_weight_grad = up_grad.T.astype(F32)
    down_weight_grad = down_grad.astype(F32)
    branch_part = dot(hidden, down_weight, ((1,), (0,)), BF16)
    branch = narrow_scatter(branch_part) + down_bias.astype(F32)
    layer_out = (
        own(middles) + own([live * gate_two]) * branch
    ).astype(BF16)

    def image_sum(hot, term):
        return dot(hot, term.astype(BF16), ((0,), (0,)))

    def feature_part(rows):
        return lax.dynamic_slice_in_dim(rows, narrow_index * mod_width, mod_width, axis=1)

    first_bias = jnp.where(narrow_index == 0, down_bias.astype(F32), 0.0)
    d_gate_two = image_sum(onehot_full, live * upstream * (branch_part.astype(F32) + first_bias))
    d_gate_two = narrow_scatter(d_gate_two.astype(BF16), 1)
    d_middles, d_attns, d_contexts = [], [], []
    d_gate_one = d_shift_two = d_scale_two = 0.0
    for block_idx in range(blocks):
        scale_b = rows_of(scale_two, block_idx)
        d_norm = d_norms[block_idx]
        d_middle = rows_of(upstream, block_idx) + norm_back(
            d_norm * (1.0 + scale_b), xhats[block_idx], rstds[block_idx]
        )
        d_middles.append(d_middle)
        hot = rows_of(onehot_full, block_idx)
        live_b = rows_of(live, block_idx)
        d_attns.append((rows_of(live * gate_one, block_idx) * d_middle).astype(BF16))
        d_contexts.append(dot(d_attns[-1], out_weight, ((1,), (1,)), BF16))
        d_gate_one += image_sum(hot, feature_part(live_b * d_middle * attns[block_idx]))
        d_shift_two += image_sum(hot, feature_part(d_norm))
        d_scale_two += image_sum(hot, feature_part(d_norm * xhats[block_idx]))
    d_attn = jnp.concatenate(d_attns, axis=0)
    d_context = jnp.concatenate(d_contexts, axis=0)
    out_weight_grad = dot(context, d_attn, ((0,), (0,)), BF16)
    d_extended = jnp.zeros((tok_dev + 2 * span, 2 * part_width), jnp.float32)
    query_grads = []
    for block_idx in range(blocks):
        query_block, key_block, value_block, same_seg = block_parts(block_idx)
        attend = jnp.exp(masked_scores(query_block, key_block, same_seg) - log_sums[block_idx])
        row_start = block_idx * block
        grad_block = d_context[row_start : row_start + block].reshape(block, heads, HD)
        d_attend = jnp.einsum(
            "ihd,jhd->hij", grad_block, value_block, preferred_element_type=jnp.float32
        )
        centre = jnp.sum(attend * d_attend, axis=-1, keepdims=True)
        d_scores = (attend * (d_attend - centre)).astype(jnp.bfloat16)
        query_grad = (
            jnp.einsum("hij,jhd->ihd", d_scores, key_block, preferred_element_type=jnp.float32)
            * scale_factor
        )
        query_grads.append(query_grad.reshape(block, part_width))
        key_grad = (
            jnp.einsum("hij,ihd->jhd", d_scores, query_block, preferred_element_type=jnp.float32)
            * scale_factor
        )
        value_grad = jnp.einsum(
            "hij,ihd->jhd",
            attend.astype(jnp.bfloat16),
            grad_block,
            preferred_element_type=jnp.float32,
        )
        pair_grad = jnp.concatenate(
            [key_grad.reshape(window, part_width), value_grad.reshape(window, part_width)], axis=1
        )
        d_extended = d_extended.at[row_start : row_start + window].add(pair_grad)
    back_edges = jnp.concatenate([d_extended[:span], d_extended[span + tok_dev :]], axis=0)
    back_left, back_right = padded(back_edges.astype(jnp.bfloat16), span)
    d_local = d_extended[span : span + tok_dev]
    d_local = d_local.at[:span].add(back_left.astype(F32))
    tail_sum = lax.dynamic_slice_in_dim(d_local, tail_start, span) + back_right.astype(F32)
    d_local = lax.dynamic_update_slice_in_dim(d_local, tail_sum, tail_start, 0)
    d_queries = jnp.concatenate(query_grads, axis=0).astype(BF16)
    d_pairs = d_local.astype(BF16)
    d_projected = jnp.concatenate([d_queries, d_pairs], axis=1)
    d_norm_part = dot(d_projected, qkv_weight.reshape(width, -1), ((1,), (1,)), BF16)
    early = jnp.stack(
        [
            image_sum(onehot_full, d_norm_part),
            image_sum(onehot_full, d_norm_part.astype(F32) * xhat_one),
        ]
    ).astype(BF16)
    early = narrow_scatter(early, 2)
    d_norm_one = narrow_scatter(d_norm_part)
    qkv_grad = dot(d_projected, norm_one, ((0,), (0,)), BF16)
    loose_parts = [
        jnp.sum(d_upper.astype(F32), axis=0),
        jnp.sum(d_branch.astype(F32), axis=0),
        jnp.sum(d_queries.astype(F32), axis=0),
        jnp.sum(d_pairs[:, part_width:].astype(F32), axis=0),
        jnp.sum(d_attn.astype(F32), axis=0),
    ]
    loose = jnp.concatenate(loose_parts)
    loose = jnp.pad(loose, (0, (-loose.shape[0]) % (8 * width))).reshape(-1, width).astype(BF16)
    tokens_grad = own(d_middles) + norm_back(
        d_norm_one * (1.0 + own([scale_one])), own([xhat_one]), own([rstd_one])
    )
    late = jnp.stack([d_gate_one, d_shift_two, d_scale_two, d_gate_two])
    d_mod = jnp.concatenate([early.astype(BF16), late.astype(BF16)], axis=0)
    flat = jnp.concatenate([qkv_grad, out_weight_grad, d_mod.reshape(-1, width)], axis=0)
    flat, loose = wide_sum(flat, loose, 0)
    starts = [0, 3 * part_width, 4 * part_width]
    qkv_weight_grad = (
        flat[: starts[1]].T.reshape(width, 3, part_width).astype(F32)
    )
    out_weight_grad = flat[starts[1] : starts[2]].astype(F32)
    loose = loose.reshape(-1)
    bounds = [0]
    for part in loose_parts:
        bounds.append(bounds[-1] + part.shape[0])
    up_bias_grad, down_bias_grad, query_bias, value_bias, out_bias_grad = [
        loose[bounds[i] : bounds[i + 1]] for i in range(5)
    ]
    qv_bias_grad = jnp.stack([query_bias, value_bias])
    d_mod = flat[starts[2] :].reshape(6, img_row, mod_width)
    modulator_grad = jnp.stack(
        [dot(activated, d_mod[j], ((0,), (0,))) for j in range(6)], axis=1
    )
    modulator_bias_grad = jnp.sum(d_mod.astype(F32), axis=1)
    d_activated = sum(dot(d_mod[j], modulator[:, j], ((1,), (1,))) for j in range(6))
    cond_part = d_activated * sigmoid_rows * (1.0 + cond_rows * (1.0 - sigmoid_rows))
    condition_grad = narrow_sum(cond_part.astype(BF16))
    return (
        layer_out,
        tokens_grad,
        condition_grad,
        modulator_grad,
        modulator_bias_grad,
        qkv_weight_grad,
        qv_bias_grad,
        out_weight_grad,
        out_bias_grad,
        up_weight_grad,
        up_bias_grad,
        down_weight_grad,
        down_bias_grad,
    )


def solution(mesh):
    in_specs = (
        P(("wide", "narrow"), None),
        P(),
        P("wide", None),
        P(None, None, "narrow"),
        P(None, "narrow"),
        P(None, None, "narrow"),
        P(None, "narrow"),
        P("narrow", None),
        P(),
        P(None, "narrow"),
        P("narrow"),
        P("narrow", None),
        P(),
        P(),
        P(),
    )
    out_specs = (
        P(("wide", "narrow"), None),
        P(("wide", "narrow"), None),
        P(),
        P(None, None, "narrow"),
        P(None, "narrow"),
        P(None, None, "narrow"),
        P(None, "narrow"),
        P("narrow", None),
        P(),
        P(None, "narrow"),
        P("narrow"),
        P("narrow", None),
        P(),
    )
    return jax.shard_map(body, mesh=mesh, in_specs=in_specs, out_specs=out_specs, check_vma=False)
```

```python
import jax
import jax.numpy as jnp
from jax import lax
from jax.experimental import pallas as pl
from jax.experimental.pallas import tpu as pltpu
from jax.sharding import PartitionSpec as P

HD = 72
IMG_MAX = 128
EPSILON = 1e-06
NEG_FILL = -1e30
F32 = jnp.float32
BF16 = jnp.bfloat16


def dot(left, right, dims, out=F32):
    return lax.dot_general(left, right, (dims, ((), ())), preferred_element_type=F32).astype(out)


def swap(part):
    return lax.ppermute(part, "narrow", [(0, 1), (1, 0)])


def narrow_gather(part):
    if lax.axis_size("narrow") != 2:
        return lax.all_gather(part, "narrow", axis=0, tiled=True)
    other = swap(part)
    first = lax.axis_index("narrow") == 0
    return jnp.where(
        first, jnp.concatenate([part, other], axis=0), jnp.concatenate([other, part], axis=0)
    )


def narrow_sum(part):
    if lax.axis_size("narrow") != 2:
        return lax.psum(part, "narrow").astype(F32)
    return part.astype(F32) + swap(part).astype(F32)


def narrow_scatter(part, dim=0):
    count = lax.axis_size("narrow")
    if count != 2:
        return lax.psum_scatter(part, "narrow", scatter_dimension=dim, tiled=True).astype(F32)
    size = part.shape[dim] // 2
    index = lax.axis_index("narrow")
    mine = lax.dynamic_slice_in_dim(part, index * size, size, axis=dim)
    theirs = lax.dynamic_slice_in_dim(part, (1 - index) * size, size, axis=dim)
    return mine.astype(F32) + swap(theirs).astype(F32)


MESH = pl.DeviceIdType.MESH
UNIT = 48


def ring_kernel(chips, subs, swapped, *refs):
    data = refs[:2]
    out, mine, theirs, slots, copy_sems, core_sems, ring_sems = refs[2 + swapped :][:7]
    if swapped:
        part, (out, landing, *rest) = refs[2], refs[3:]
        mine, theirs, slots, copy_sems, core_sems, ring_sems, swap_sems = rest
    wide = lax.axis_index("wide")
    chip, core = wide // 2, wide % 2
    half = chips // 2

    def place(position):
        position = lax.rem(position + 2 * chips, chips)
        side = position // half
        return (1 - side) * 2 * position + side * (2 * (chips - 1 - position) + 1)

    position = chip // 2 + (chip % 2) * (chips - 1 - 2 * (chip // 2))
    ahead = 2 * place(position + 1) + core
    behind = 2 * place(position - 1) + core
    sibling = 2 * chip + 1 - core
    barrier = pltpu.get_barrier_semaphore()
    for device in (ahead, behind, sibling):
        pl.semaphore_signal(barrier, inc=1, device_id={"wide": device}, device_id_type=MESH)
    if swapped:
        facing = 1 - lax.axis_index("narrow")
        pl.semaphore_signal(barrier, inc=1, device_id={"narrow": facing}, device_id_type=MESH)
    pl.semaphore_wait(barrier, 3 + swapped)
    if swapped:
        share = landing.shape[0]
        turn = pltpu.make_async_remote_copy(
            src_ref=part.at[pl.ds(facing * share, share)],
            dst_ref=landing,
            send_sem=swap_sems.at[0],
            recv_sem=swap_sems.at[1],
            device_id={"narrow": facing},
            device_id_type=MESH,
        )
        turn.start()

    def local(lane):
        return pltpu.make_async_copy(data[lane].at[:, core], mine.at[lane], copy_sems.at[lane])

    def across(lane):
        return pltpu.make_async_remote_copy(
            src_ref=data[lane].at[:, 1 - core],
            dst_ref=theirs.at[lane],
            send_sem=core_sems.at[0, lane],
            recv_sem=core_sems.at[1, lane],
            device_id={"wide": sibling},
            device_id_type=MESH,
        )

    for lane in range(2):
        across(lane).start()
        local(lane).start()

    def hop(lane, step, sub):
        rows = pl.ds(sub * UNIT, UNIT)
        if step == 0:
            first = place(position - 1 if lane == 0 else position + 1)
            source = mine.at[lane, first, rows]
        else:
            source = slots.at[lane, step - 1, rows]
        return pltpu.make_async_remote_copy(
            src_ref=source,
            dst_ref=slots.at[lane, step, rows],
            send_sem=ring_sems.at[0, lane, step, sub],
            recv_sem=ring_sems.at[1, lane, step, sub],
            device_id={"wide": ahead if lane == 0 else behind},
            device_id_type=MESH,
        )

    for lane in range(2):
        local(lane).wait()
        across(lane).wait()

        def merge(index, carry, lane=lane):
            mine[lane, index] = mine[lane, index] + theirs[lane, index]
            return carry

        lax.fori_loop(0, chips, merge, 0)
        for sub in range(subs):
            hop(lane, 0, sub).start()
    for step in range(chips - 1):
        for sub in range(subs):
            for lane in range(2):
                hop(lane, step, sub).wait_recv()
                offset = 2 + step
                index = place(position - offset if lane == 0 else position + offset)
                rows = pl.ds(sub * UNIT, UNIT)
                total = slots[lane, step, rows] + mine[lane, index, rows]
                if step == chips - 2:
                    out[lane, rows] = total
                else:
                    slots[lane, step, rows] = total
                    hop(lane, step + 1, sub).start()
    for step in range(chips - 1):
        for sub in range(subs):
            for lane in range(2):
                hop(lane, step, sub).wait_send()
    if swapped:
        turn.wait()


def ring_scatter(lanes, part, collective_id):
    chips = lax.axis_size("wide") // 2
    rows, width = lanes[0].shape
    shard = rows // (2 * chips)
    subs = shard // UNIT
    operands = [lane.reshape(chips, 2, shard, width) for lane in lanes]
    shapes = [jax.ShapeDtypeStruct((2, shard, width), BF16)]
    specs = [pl.BlockSpec(memory_space=pltpu.VMEM)]
    scratch = [
        pltpu.VMEM((2, chips, shard, width), BF16),
        pltpu.VMEM((2, chips, shard, width), BF16),
        pltpu.VMEM((2, chips - 1, shard, width), BF16),
        pltpu.SemaphoreType.DMA((2,)),
        pltpu.SemaphoreType.DMA((2, 2)),
        pltpu.SemaphoreType.DMA((2, 2, chips - 1, subs)),
    ]
    if part is not None:
        operands.append(part)
        shapes.append(jax.ShapeDtypeStruct((part.shape[0] // 2, part.shape[1]), BF16))
        specs.append(pl.BlockSpec(memory_space=pl.ANY))
        scratch.append(pltpu.SemaphoreType.DMA((2,)))
    return pl.pallas_call(
        lambda *refs: ring_kernel(chips, subs, int(part is not None), *refs),
        out_shape=shapes,
        in_specs=[pl.BlockSpec(memory_space=pl.ANY)] * len(operands),
        out_specs=specs,
        scratch_shapes=scratch,
        compiler_params=pltpu.CompilerParams(
            collective_id=collective_id, has_side_effects=True, vmem_limit_bytes=40 << 20
        ),
        name="ring_scatter",
    )(*operands)


def ring_fits(lanes):
    count = lax.axis_size("wide")
    return lax.axis_size("narrow") == 2 and lanes[0].shape[0] % (count * UNIT) == 0


def wide_gather(mine, loose):
    shard, width = mine.shape[1:]
    parts = mine.reshape(2 * shard, width)
    if loose is not None:
        parts = jnp.concatenate([parts, loose], axis=0)
    parts = lax.all_gather(parts, "wide", axis=0)
    lanes = [parts[:, lane * shard : (lane + 1) * shard].reshape(-1, width) for lane in range(2)]
    return lanes, parts[:, 2 * shard :].astype(F32)


TILE = 256
LOG2E = 1.4426950408889634


def head_lanes(part_width):
    for head in range(part_width // HD):
        lo = head * HD // 128 * 128
        hi = min(-(-(head + 1) * HD // 128) * 128, part_width)
        lanes = lax.broadcasted_iota(jnp.int32, (1, hi - lo), 1) + lo
        yield head, lo, hi, (lanes >= head * HD) & (lanes < (head + 1) * HD)


def extend(first, left, own, right, ext):
    span = left.shape[1]
    ends = ext.shape[1] - span

    @pl.when(first)
    def _():
        for which in range(2):
            ext[which, :span] = left[which]
            ext[which, span:ends] = own[which][...]
            ext[which, ends:] = right[which]


def forward_kernel(tiles, q, k, v, left, right, q_ids, k_ids, out, lse, ext, total):
    tile = pl.program_id(0)
    part_width = q.shape[1]
    span = left.shape[1]
    ends = ext.shape[1] - span
    extend(tile == 0, left, (k, v), right, ext)
    scale = LOG2E * HD ** (-0.5)

    def run(extra):
        rows = pl.ds(pl.multiple_of(tile * TILE, TILE), TILE + 2 * span)
        keys, values = ext[0, rows], ext[1, rows]
        ids = k_ids[:, rows]
        if extra:
            keys = jnp.concatenate([keys, ext[0, ends:]], axis=0)
            values = jnp.concatenate([values, ext[1, ends:]], axis=0)
            ids = jnp.concatenate([ids, k_ids[:, ends:]], axis=1)
        same = q_ids[...] == ids
        queries = q[...]
        total[...] = jnp.zeros_like(total)
        packed = jnp.zeros((TILE, 128), F32)
        column = lax.broadcasted_iota(jnp.int32, (TILE, 128), 1)
        for head, lo, hi, mask in head_lanes(part_width):
            chosen = jnp.where(mask, queries[:, lo:hi], 0)
            scores = lax.dot_general(
                chosen, keys[:, lo:hi], (((1,), (1,)), ((), ())), preferred_element_type=F32
            )
            scores = jnp.where(same, scores * scale, NEG_FILL)
            top = jnp.max(scores, axis=1, keepdims=True)
            expo = jnp.exp2(scores - top)
            count = jnp.sum(expo, axis=1, keepdims=True)
            part = jnp.dot(expo.astype(BF16), values[:, lo:hi], preferred_element_type=F32)
            total[:, lo:hi] += jnp.where(mask, part / count, 0.0)
            packed = jnp.where(column == head, top + jnp.log2(count), packed)
        out[...] = total[...].astype(BF16)
        lse[...] = packed.T[: lse.shape[0]]

    split_tiles(tile, tiles, run)


def split_tiles(tile, tiles, run):
    first_extra = tiles - 512 // TILE
    extra = (tile >= first_extra) & (tile < tiles - 1)
    pl.when(extra)(lambda: run(True))
    pl.when(jnp.logical_not(extra))(lambda: run(False))


def rim_specs(part_width, span, tok_dev):
    whole = lambda shape: pl.BlockSpec(shape, lambda i: (0,) * len(shape))
    return whole((tok_dev, part_width)), whole((2, span, part_width))


def attention_forward(q, k, v, left, right, q_ids, k_ids):
    tok_dev, part_width = q.shape
    span = left.shape[1]
    tiles = tok_dev // TILE
    head_rows = -(-(part_width // HD) // 8) * 8
    own_spec, rim_spec = rim_specs(part_width, span, tok_dev)
    return pl.pallas_call(
        lambda *refs: forward_kernel(tiles, *refs),
        grid=(tiles,),
        out_shape=[
            jax.ShapeDtypeStruct((tok_dev, part_width), BF16),
            jax.ShapeDtypeStruct((head_rows, tok_dev), F32),
        ],
        in_specs=[
            pl.BlockSpec((TILE, part_width), lambda i: (i, 0)),
            own_spec,
            own_spec,
            rim_spec,
            rim_spec,
            pl.BlockSpec((TILE, 1), lambda i: (i, 0)),
            pl.BlockSpec((1, tok_dev + 2 * span), lambda i: (0, 0)),
        ],
        out_specs=[
            pl.BlockSpec((TILE, part_width), lambda i: (i, 0)),
            pl.BlockSpec((head_rows, TILE), lambda i: (0, i)),
        ],
        scratch_shapes=[
            pltpu.VMEM((2, tok_dev + 2 * span, part_width), BF16),
            pltpu.VMEM((TILE, part_width), F32),
        ],
        compiler_params=pltpu.CompilerParams(vmem_limit_bytes=40 << 20),
        cost_estimate=pl.CostEstimate(
            flops=4 * tok_dev * 512 * part_width,
            transcendentals=tok_dev * 512 * 8,
            bytes_accessed=8 * tok_dev * part_width,
        ),
        name="attention_forward",
    )(q, k, v, left, right, q_ids, k_ids)


def backward_kernel(tiles, q, k, v, left, right, grad, lse, q_ids, k_ids, *refs):
    d_q, d_own, d_rim, ext, d_ext, total = refs
    tile = pl.program_id(0)
    part_width = q.shape[1]
    span = left.shape[1]
    ends = ext.shape[1] - span
    extend(tile == 0, left, (k, v), right, ext)
    scale = HD ** (-0.5)

    @pl.when(tile == 0)
    def _():
        d_ext[...] = jnp.zeros_like(d_ext)

    def run(extra):
        rows = pl.ds(pl.multiple_of(tile * TILE, TILE), TILE + 2 * span)
        keys, values = ext[0, rows], ext[1, rows]
        ids = k_ids[rows]
        if extra:
            keys = jnp.concatenate([keys, ext[0, ends:]], axis=0)
            values = jnp.concatenate([values, ext[1, ends:]], axis=0)
            ids = jnp.concatenate([ids, k_ids[ends:]], axis=0)
        same = ids == q_ids[...]
        queries, grads = q[...], grad[...]
        total[...] = jnp.zeros_like(total)

        def across(left_side, right_side, dims):
            return lax.dot_general(
                left_side, right_side, (dims, ((), ())), preferred_element_type=F32
            )

        for head, lo, hi, mask in head_lanes(part_width):
            chosen = jnp.where(mask, queries[:, lo:hi], 0)
            pulled = jnp.where(mask, grads[:, lo:hi], 0)
            scores = across(keys[:, lo:hi], chosen, ((1,), (1,)))
            scores = jnp.where(same, scores * (scale * LOG2E), NEG_FILL)
            attend = jnp.exp2(scores - lse[head : head + 1])
            d_attend = across(values[:, lo:hi], pulled, ((1,), (1,)))
            centre = jnp.sum(attend * d_attend, axis=0, keepdims=True)
            d_scores = (attend * (d_attend - centre)).astype(BF16)
            d_key = across(d_scores, chosen, ((1,), (0,)))
            d_value = across(attend.astype(BF16), pulled, ((1,), (0,)))
            length = TILE + 2 * span
            d_ext[0, rows, lo:hi] += d_key[:length]
            d_ext[1, rows, lo:hi] += d_value[:length]
            if extra:
                d_ext[0, ends:, lo:hi] += d_key[length:]
                d_ext[1, ends:, lo:hi] += d_value[length:]
            d_query = across(d_scores, keys[:, lo:hi], ((0,), (0,)))
            total[:, lo:hi] += jnp.where(mask, d_query, 0.0)
        d_q[...] = (total[...] * scale).astype(BF16)

    split_tiles(tile, tiles, run)

    @pl.when(tile == tiles - 1)
    def _():
        for which, factor in ((0, scale), (1, 1.0)):
            d_rim[0, which] = (d_ext[which, :span] * factor).astype(BF16)
            d_own[which] = (d_ext[which, span:ends] * factor).astype(BF16)
            d_rim[1, which] = (d_ext[which, ends:] * factor).astype(BF16)


def attention_backward(q, k, v, left, right, grad, lse, q_ids, k_ids):
    tok_dev, part_width = q.shape
    span = left.shape[1]
    tiles = tok_dev // TILE
    own_spec, rim_spec = rim_specs(part_width, span, tok_dev)
    tile_spec = pl.BlockSpec((TILE, part_width), lambda i: (i, 0))
    return pl.pallas_call(
        lambda *refs: backward_kernel(tiles, *refs),
        grid=(tiles,),
        out_shape=[
            jax.ShapeDtypeStruct((tok_dev, part_width), BF16),
            jax.ShapeDtypeStruct((2, tok_dev, part_width), BF16),
            jax.ShapeDtypeStruct((2, 2, span, part_width), BF16),
        ],
        in_specs=[
            tile_spec,
            own_spec,
            own_spec,
            rim_spec,
            rim_spec,
            tile_spec,
            pl.BlockSpec((lse.shape[0], TILE), lambda i: (0, i)),
            pl.BlockSpec((1, TILE), lambda i: (0, i)),
            pl.BlockSpec((tok_dev + 2 * span, 1), lambda i: (0, 0)),
        ],
        out_specs=[
            tile_spec,
            pl.BlockSpec((2, tok_dev, part_width), lambda i: (0, 0, 0)),
            pl.BlockSpec((2, 2, span, part_width), lambda i: (0, 0, 0, 0)),
        ],
        scratch_shapes=[
            pltpu.VMEM((2, tok_dev + 2 * span, part_width), BF16),
            pltpu.VMEM((2, tok_dev + 2 * span, part_width), F32),
            pltpu.VMEM((TILE, part_width), F32),
        ],
        compiler_params=pltpu.CompilerParams(vmem_limit_bytes=48 << 20),
        cost_estimate=pl.CostEstimate(
            flops=10 * tok_dev * 512 * part_width,
            transcendentals=tok_dev * 512 * 8,
            bytes_accessed=16 * tok_dev * part_width,
        ),
        name="attention_backward",
    )(q, k, v, left, right, grad, lse, q_ids, k_ids)


def norm(field):
    centred = field - jnp.mean(field, axis=-1, keepdims=True)
    rstd = lax.rsqrt(jnp.mean(centred * centred, axis=-1, keepdims=True) + EPSILON)
    return centred * rstd, rstd


def norm_back(grad, xhat, rstd):
    return rstd * (
        grad
        - jnp.mean(grad, axis=-1, keepdims=True)
        - xhat * jnp.mean(grad * xhat, axis=-1, keepdims=True)
    )


def gelu_pair(v):
    c = 0.7978845608028654
    sq = v * v
    t = jnp.tanh(c * v * (1.0 + 0.044715 * sq))
    half = 0.5 * (1.0 + t)
    slope = half + 0.5 * v * (1.0 - t * t) * c * (1.0 + 3 * 0.044715 * sq)
    return v * half, slope


def body(
    tokens,
    condition,
    cotangent,
    modulator,
    modulator_bias,
    qkv_weight,
    qv_bias,
    out_weight,
    out_bias,
    up_weight,
    up_bias,
    down_weight,
    down_bias,
    segment_ids,
    valid_counts,
):
    wide_count = lax.axis_size("wide")
    wide_index = lax.axis_index("wide")
    narrow_index = lax.axis_index("narrow")
    tok_dev = cotangent.shape[0]
    share = tokens.shape[0]
    width = tokens.shape[1]
    part_width = qkv_weight.shape[2]
    img_row = condition.shape[0]
    span = IMG_MAX
    block = min(512, tok_dev)
    own_count = valid_counts[wide_index]
    positions = jnp.arange(tok_dev, dtype=jnp.int32)
    own_ids = lax.dynamic_slice_in_dim(segment_ids, wide_index * tok_dev, tok_dev)
    live_full = (positions < own_count).astype(jnp.float32)
    share_start = narrow_index * share
    live = live_full[:, None]
    image_slots = jnp.arange(img_row, dtype=jnp.int32)
    onehot_full = (own_ids[:, None] == image_slots[None, :]).astype(BF16)
    onehot_share = lax.dynamic_slice_in_dim(onehot_full, share_start, share)
    cond_rows = condition.astype(F32)
    sigmoid_rows = jax.nn.sigmoid(cond_rows)
    activated = (cond_rows * sigmoid_rows).astype(BF16)
    tok_full = narrow_gather(tokens)
    mod_width = modulator.shape[2]
    mod_rows = jnp.transpose(modulator, (1, 2, 0)).reshape(6 * mod_width, width)

    def per_token(lo, hi, after=None):
        part = dot(activated, mod_rows[lo * mod_width : hi * mod_width], ((1,), (1,)))
        part = part + modulator_bias[lo:hi].astype(F32).reshape(1, -1)
        rows = jnp.moveaxis(part.astype(BF16).reshape(img_row, hi - lo, -1), 2, 0)
        if after is not None:
            rows, after = lax.optimization_barrier((rows, after))
        rows = narrow_gather(rows)
        vectors = [
            dot(onehot_full, rows[:, :, i], ((1,), (1,)), BF16).astype(F32) for i in range(hi - lo)
        ]
        return vectors, after

    (shift_one, scale_one), _ = per_token(0, 2)
    (gate_one, shift_two, scale_two, gate_two), tok_full = per_token(2, 6, tok_full)
    tok_full = tok_full.astype(F32)
    xhat_one, rstd_one = norm(tok_full)
    norm_one = (xhat_one * (1.0 + scale_one) + shift_one).astype(BF16)
    flat_qkv = jnp.transpose(qkv_weight, (1, 2, 0)).reshape(3 * part_width, width)
    bias_pair = qv_bias.astype(F32)
    parts_qkv = [flat_qkv[i * part_width : (i + 1) * part_width] for i in range(3)]
    queries, key_rows, value_rows = [dot(norm_one, part, ((1,), (1,))) for part in parts_qkv]
    queries = (queries + bias_pair[0]).astype(BF16)
    key_rows = key_rows.astype(BF16)
    value_rows = (value_rows + bias_pair[1]).astype(BF16)
    tail_start = own_count - span

    def tail_of(rows):
        return lax.dynamic_slice_in_dim(rows, tail_start, span)

    def to_right(rows):
        return lax.ppermute(rows, "wide", [(i, i + 1) for i in range(wide_count - 1)])

    def to_left(rows):
        return lax.ppermute(rows, "wide", [(i + 1, i) for i in range(wide_count - 1)])

    from_left = to_right(jnp.stack([tail_of(key_rows), tail_of(value_rows)]))
    from_right = to_left(jnp.stack([key_rows[:span], value_rows[:span]]))
    left_index = jnp.maximum(wide_index - 1, 0)
    right_index = jnp.minimum(wide_index + 1, wide_count - 1)
    left_count = valid_counts[left_index]
    left_ids = lax.dynamic_slice_in_dim(segment_ids, left_index * tok_dev + left_count - span, span)
    left_ids = jnp.where(wide_index > 0, left_ids, -2)
    right_ids = lax.dynamic_slice_in_dim(segment_ids, right_index * tok_dev, span)
    right_ids = jnp.where(wide_index < wide_count - 1, right_ids, -2)
    own_keys = jnp.where(positions < own_count, own_ids, -1)
    extended_ids = jnp.concatenate([left_ids, own_keys, right_ids])
    context, log_sums = attention_forward(
        queries, key_rows, value_rows, from_left, from_right, own_keys[:, None], extended_ids[None]
    )
    blocks = tok_dev // block

    def rows_of(rows, block_idx):
        return rows[block_idx * block : (block_idx + 1) * block]

    def own(parts):
        rows = jnp.concatenate(parts, axis=0)
        return lax.dynamic_slice_in_dim(rows, share_start, share)

    upstream = cotangent.astype(F32)
    attns, middles, xhats, rstds = [], [], [], []
    norms, hiddens, d_uppers, d_branches, d_norms = [], [], [], [], []
    for block_idx in range(blocks):
        attn_part = dot(rows_of(context, block_idx), out_weight, ((1,), (0,)), BF16)
        attns.append(narrow_sum(attn_part) + out_bias.astype(F32))
    for block_idx in range(blocks):
        gate_b = rows_of(live * gate_two, block_idx)
        d_branches.append((gate_b * rows_of(upstream, block_idx)).astype(BF16))
        d_hidden = dot(d_branches[-1], down_weight, ((1,), (1,)), BF16).astype(F32)
        middle = rows_of(tok_full, block_idx) + rows_of(live * gate_one, block_idx) * attns[block_idx]
        xhat, rstd = norm(middle)
        middles.append(middle)
        xhats.append(xhat)
        rstds.append(rstd)
        scale_b, shift_b = rows_of(scale_two, block_idx), rows_of(shift_two, block_idx)
        norms.append((xhat * (1.0 + scale_b) + shift_b).astype(BF16))
        upper = dot(norms[-1], up_weight, ((1,), (0,))) + up_bias.astype(F32)
        gelu, slope = gelu_pair(upper)
        hiddens.append(gelu.astype(BF16))
        d_uppers.append((d_hidden * slope).astype(BF16))
        d_norms.append(narrow_sum(dot(d_uppers[-1], up_weight, ((1,), (1,)), BF16)))
    hidden = jnp.concatenate(hiddens, axis=0)
    d_upper = jnp.concatenate(d_uppers, axis=0)
    d_branch = jnp.concatenate(d_branches, axis=0)
    norm_two = jnp.concatenate(norms, axis=0)
    down_grad = dot(hidden, d_branch, ((0,), (0,)), BF16)
    up_grad = dot(d_upper, norm_two, ((0,), (0,)), BF16)
    if ring_fits([up_grad]):
        mine = ring_scatter([up_grad, down_grad], None, 1)[0]
        mine, d_norms = lax.optimization_barrier((mine, d_norms))
        (up_grad, down_grad), _ = wide_gather(mine, None)
    else:
        up_grad, down_grad = lax.psum((up_grad, down_grad), "wide")
    up_weight_grad = up_grad.T.astype(F32)
    down_weight_grad = down_grad.astype(F32)
    branch_part = dot(hidden, down_weight, ((1,), (0,)), BF16)
    branch = narrow_scatter(branch_part) + down_bias.astype(F32)
    layer_out = (
        own(middles) + own([live * gate_two]) * branch
    ).astype(BF16)

    def image_sum(hot, term):
        return dot(hot, term.astype(BF16), ((0,), (0,)))

    def feature_part(rows):
        return lax.dynamic_slice_in_dim(rows, narrow_index * mod_width, mod_width, axis=1)

    first_bias = jnp.where(narrow_index == 0, down_bias.astype(F32), 0.0)
    d_gate_two = image_sum(onehot_full, live * upstream * (branch_part.astype(F32) + first_bias))
    d_gate_two = narrow_scatter(d_gate_two.astype(BF16), 1)
    d_middles, d_attns, d_contexts = [], [], []
    d_gate_one = d_shift_two = d_scale_two = 0.0
    for block_idx in range(blocks):
        scale_b = rows_of(scale_two, block_idx)
        d_norm = d_norms[block_idx]
        d_middle = rows_of(upstream, block_idx) + norm_back(
            d_norm * (1.0 + scale_b), xhats[block_idx], rstds[block_idx]
        )
        d_middles.append(d_middle)
        hot = rows_of(onehot_full, block_idx)
        live_b = rows_of(live, block_idx)
        d_attns.append((rows_of(live * gate_one, block_idx) * d_middle).astype(BF16))
        d_contexts.append(dot(d_attns[-1], out_weight, ((1,), (1,)), BF16))
        d_gate_one += image_sum(hot, feature_part(live_b * d_middle * attns[block_idx]))
        d_shift_two += image_sum(hot, feature_part(d_norm))
        d_scale_two += image_sum(hot, feature_part(d_norm * xhats[block_idx]))
    d_attn = jnp.concatenate(d_attns, axis=0)
    d_context = jnp.concatenate(d_contexts, axis=0)
    out_weight_grad = dot(context, d_attn, ((0,), (0,)), BF16)
    d_queries, d_own, d_rim = attention_backward(
        queries,
        key_rows,
        value_rows,
        from_left,
        from_right,
        d_context,
        log_sums,
        own_keys[None],
        extended_ids[:, None],
    )
    back_left, back_right = to_right(d_rim[1]), to_left(d_rim[0])
    placed = lax.dynamic_update_slice(jnp.zeros_like(d_own), back_right, (0, tail_start, 0))
    back_left = jnp.pad(back_left, ((0, 0), (0, tok_dev - span), (0, 0)))
    d_own = (d_own.astype(F32) + placed.astype(F32) + back_left.astype(F32)).astype(BF16)
    d_parts = [d_queries, d_own[0], d_own[1]]
    d_norm_part = sum(dot(d_parts[i], parts_qkv[i], ((1,), (0,))) for i in range(3)).astype(BF16)
    early = jnp.stack(
        [
            image_sum(onehot_full, d_norm_part),
            image_sum(onehot_full, d_norm_part.astype(F32) * xhat_one),
        ]
    ).astype(BF16)
    early = narrow_scatter(early, 2)
    qkv_grads = [dot(part, norm_one, ((0,), (0,)), BF16) for part in d_parts]
    loose_parts = [
        jnp.sum(d_upper.astype(F32), axis=0),
        jnp.sum(d_branch.astype(F32), axis=0),
        jnp.sum(d_queries.astype(F32), axis=0),
        jnp.sum(d_own[1].astype(F32), axis=0),
        jnp.sum(d_attn.astype(F32), axis=0),
    ]
    loose = jnp.concatenate(loose_parts)
    loose = jnp.pad(loose, (0, (-loose.shape[0]) % (8 * width))).reshape(-1, width).astype(BF16)
    late = [d_gate_one, d_shift_two, d_scale_two, d_gate_two]
    terms = [term.astype(BF16) for term in [early[0], early[1]] + late]
    d_mod = [jnp.concatenate(terms[2 * i : 2 * i + 2], axis=1) for i in range(3)]
    if 2 * mod_width == width:
        d_mod_flat = jnp.concatenate(d_mod, axis=0)
    else:
        d_mod_flat = jnp.concatenate(d_mod, axis=1).reshape(-1, width)
    flat = jnp.concatenate(qkv_grads + [out_weight_grad, d_mod_flat], axis=0)
    lanes = [flat[: flat.shape[0] // 2], flat[flat.shape[0] // 2 :]]
    if ring_fits(lanes):
        mine, d_norm_other = ring_scatter(lanes, d_norm_part, 0)
        d_norm_one = own([d_norm_part.astype(F32)]) + d_norm_other.astype(F32)
        lanes, loose = wide_gather(mine, loose)
        flat = jnp.concatenate(lanes, axis=0)
    else:
        d_norm_one = narrow_scatter(d_norm_part)
        flat = lax.psum(flat, "wide")
        loose = lax.all_gather(loose, "wide", axis=0).astype(F32)
    loose = jnp.sum(loose, axis=0)
    tokens_grad = own(d_middles) + norm_back(
        d_norm_one * (1.0 + own([scale_one])), own([xhat_one]), own([rstd_one])
    )
    starts = [0, 3 * part_width, 4 * part_width]
    qkv_weight_grad = jnp.transpose(
        flat[: starts[1]].astype(F32).reshape(3, part_width, width), (2, 0, 1)
    )
    out_weight_grad = flat[starts[1] : starts[2]].astype(F32)
    loose = loose.reshape(-1)
    bounds = [0]
    for part in loose_parts:
        bounds.append(bounds[-1] + part.shape[0])
    up_bias_grad, down_bias_grad, query_bias, value_bias, out_bias_grad = [
        loose[bounds[i] : bounds[i + 1]] for i in range(5)
    ]
    qv_bias_grad = jnp.stack([query_bias, value_bias])
    d_mod_flat = flat[starts[2] :]
    if 2 * mod_width == width:
        d_mod = d_mod_flat.reshape(3, img_row, width)
    else:
        d_mod = jnp.moveaxis(d_mod_flat.reshape(img_row, 3, -1), 1, 0)
    modulator_grad = lax.dot_general(
        d_mod, activated, (((1,), (0,)), ((), ())), preferred_element_type=F32
    )
    modulator_grad = jnp.transpose(modulator_grad.reshape(6, mod_width, width), (2, 0, 1))
    modulator_bias_grad = jnp.sum(d_mod.astype(F32), axis=1).reshape(6, mod_width)
    mod_blocks = mod_rows.reshape(3, 2 * mod_width, width)
    d_activated = sum(dot(d_mod[i], mod_blocks[i], ((1,), (0,))) for i in range(3))
    cond_part = d_activated * sigmoid_rows * (1.0 + cond_rows * (1.0 - sigmoid_rows))
    condition_grad = narrow_sum(cond_part.astype(BF16))
    return (
        layer_out,
        tokens_grad,
        condition_grad,
        modulator_grad,
        modulator_bias_grad,
        qkv_weight_grad,
        qv_bias_grad,
        out_weight_grad,
        out_bias_grad,
        up_weight_grad,
        up_bias_grad,
        down_weight_grad,
        down_bias_grad,
    )


def solution(mesh):
    in_specs = (
        P(("wide", "narrow"), None),
        P(),
        P("wide", None),
        P(None, None, "narrow"),
        P(None, "narrow"),
        P(None, None, "narrow"),
        P(None, "narrow"),
        P("narrow", None),
        P(),
        P(None, "narrow"),
        P("narrow"),
        P("narrow", None),
        P(),
        P(),
        P(),
    )
    out_specs = (
        P(("wide", "narrow"), None),
        P(("wide", "narrow"), None),
        P(),
        P(None, None, "narrow"),
        P(None, "narrow"),
        P(None, None, "narrow"),
        P(None, "narrow"),
        P("narrow", None),
        P(),
        P(None, "narrow"),
        P("narrow"),
        P("narrow", None),
        P(),
    )
    return jax.shard_map(body, mesh=mesh, in_specs=in_specs, out_specs=out_specs, check_vma=False)
```

```python
import jax
import jax.numpy as jnp
from jax import lax
from jax.experimental import pallas as pl
from jax.experimental.pallas import tpu as pltpu
from jax.sharding import PartitionSpec as P

HD = 72
IMG_MAX = 128
EPSILON = 1e-06
NEG_FILL = -1e30
F32 = jnp.float32
BF16 = jnp.bfloat16


def dot(left, right, dims, out=F32):
    return lax.dot_general(left, right, (dims, ((), ())), preferred_element_type=F32).astype(out)


def swap(part):
    return lax.ppermute(part, "narrow", [(0, 1), (1, 0)])


def narrow_gather(part):
    if lax.axis_size("narrow") != 2:
        return lax.all_gather(part, "narrow", axis=0, tiled=True)
    other = swap(part)
    first = lax.axis_index("narrow") == 0
    return jnp.where(
        first, jnp.concatenate([part, other], axis=0), jnp.concatenate([other, part], axis=0)
    )


def narrow_other(part):
    if lax.axis_size("narrow") != 2:
        return (lax.psum(part.astype(F32), "narrow") - part.astype(F32)).astype(BF16)
    return swap(part)


def narrow_scatter(part, dim=0):
    count = lax.axis_size("narrow")
    if count != 2:
        return lax.psum_scatter(part, "narrow", scatter_dimension=dim, tiled=True).astype(F32)
    size = part.shape[dim] // 2
    index = lax.axis_index("narrow")
    mine = lax.dynamic_slice_in_dim(part, index * size, size, axis=dim)
    theirs = lax.dynamic_slice_in_dim(part, (1 - index) * size, size, axis=dim)
    return mine.astype(F32) + swap(theirs).astype(F32)


MESH = pl.DeviceIdType.MESH
UNIT = 48


def ring_kernel(chips, subs, swapped, *refs):
    data = refs[:2]
    out, mine, theirs, slots, copy_sems, core_sems, ring_sems = refs[2 + swapped :][:7]
    if swapped:
        part, (out, landing, *rest) = refs[2], refs[3:]
        mine, theirs, slots, copy_sems, core_sems, ring_sems, swap_sems = rest
    wide = lax.axis_index("wide")
    chip, core = wide // 2, wide % 2
    half = chips // 2

    def place(position):
        position = lax.rem(position + 2 * chips, chips)
        side = position // half
        return (1 - side) * 2 * position + side * (2 * (chips - 1 - position) + 1)

    position = chip // 2 + (chip % 2) * (chips - 1 - 2 * (chip // 2))
    ahead = 2 * place(position + 1) + core
    behind = 2 * place(position - 1) + core
    sibling = 2 * chip + 1 - core
    barrier = pltpu.get_barrier_semaphore()
    for device in (ahead, behind, sibling):
        pl.semaphore_signal(barrier, inc=1, device_id={"wide": device}, device_id_type=MESH)
    if swapped:
        facing = 1 - lax.axis_index("narrow")
        pl.semaphore_signal(barrier, inc=1, device_id={"narrow": facing}, device_id_type=MESH)
    pl.semaphore_wait(barrier, 3 + swapped)
    if swapped:
        share = landing.shape[0]
        turn = pltpu.make_async_remote_copy(
            src_ref=part.at[pl.ds(facing * share, share)],
            dst_ref=landing,
            send_sem=swap_sems.at[0],
            recv_sem=swap_sems.at[1],
            device_id={"narrow": facing},
            device_id_type=MESH,
        )
        turn.start()

    def local(lane):
        return pltpu.make_async_copy(data[lane].at[:, core], mine.at[lane], copy_sems.at[lane])

    def across(lane):
        return pltpu.make_async_remote_copy(
            src_ref=data[lane].at[:, 1 - core],
            dst_ref=theirs.at[lane],
            send_sem=core_sems.at[0, lane],
            recv_sem=core_sems.at[1, lane],
            device_id={"wide": sibling},
            device_id_type=MESH,
        )

    for lane in range(2):
        across(lane).start()
        local(lane).start()

    def hop(lane, step, sub):
        rows = pl.ds(sub * UNIT, UNIT)
        if step == 0:
            first = place(position - 1 if lane == 0 else position + 1)
            source = mine.at[lane, first, rows]
        else:
            source = slots.at[lane, step - 1, rows]
        return pltpu.make_async_remote_copy(
            src_ref=source,
            dst_ref=slots.at[lane, step, rows],
            send_sem=ring_sems.at[0, lane, step, sub],
            recv_sem=ring_sems.at[1, lane, step, sub],
            device_id={"wide": ahead if lane == 0 else behind},
            device_id_type=MESH,
        )

    for lane in range(2):
        local(lane).wait()
        across(lane).wait()

        def merge(index, carry, lane=lane):
            mine[lane, index] = mine[lane, index] + theirs[lane, index]
            return carry

        lax.fori_loop(0, chips, merge, 0)
        for sub in range(subs):
            hop(lane, 0, sub).start()
    for step in range(chips - 1):
        for sub in range(subs):
            for lane in range(2):
                hop(lane, step, sub).wait_recv()
                offset = 2 + step
                index = place(position - offset if lane == 0 else position + offset)
                rows = pl.ds(sub * UNIT, UNIT)
                total = slots[lane, step, rows] + mine[lane, index, rows]
                if step == chips - 2:
                    out[lane, rows] = total
                else:
                    slots[lane, step, rows] = total
                    hop(lane, step + 1, sub).start()
    for step in range(chips - 1):
        for sub in range(subs):
            for lane in range(2):
                hop(lane, step, sub).wait_send()
    if swapped:
        turn.wait()


def ring_scatter(lanes, part, collective_id):
    chips = lax.axis_size("wide") // 2
    rows, width = lanes[0].shape
    shard = rows // (2 * chips)
    subs = shard // UNIT
    operands = [lane.reshape(chips, 2, shard, width) for lane in lanes]
    shapes = [jax.ShapeDtypeStruct((2, shard, width), BF16)]
    specs = [pl.BlockSpec(memory_space=pltpu.VMEM)]
    scratch = [
        pltpu.VMEM((2, chips, shard, width), BF16),
        pltpu.VMEM((2, chips, shard, width), BF16),
        pltpu.VMEM((2, chips - 1, shard, width), BF16),
        pltpu.SemaphoreType.DMA((2,)),
        pltpu.SemaphoreType.DMA((2, 2)),
        pltpu.SemaphoreType.DMA((2, 2, chips - 1, subs)),
    ]
    if part is not None:
        operands.append(part)
        shapes.append(jax.ShapeDtypeStruct((part.shape[0] // 2, part.shape[1]), BF16))
        specs.append(pl.BlockSpec(memory_space=pl.ANY))
        scratch.append(pltpu.SemaphoreType.DMA((2,)))
    return pl.pallas_call(
        lambda *refs: ring_kernel(chips, subs, int(part is not None), *refs),
        out_shape=shapes,
        in_specs=[pl.BlockSpec(memory_space=pl.ANY)] * len(operands),
        out_specs=specs,
        scratch_shapes=scratch,
        compiler_params=pltpu.CompilerParams(
            collective_id=collective_id, has_side_effects=True, vmem_limit_bytes=40 << 20
        ),
        name="ring_scatter",
    )(*operands)


def ring_fits(lanes):
    count = lax.axis_size("wide")
    return lax.axis_size("narrow") == 2 and lanes[0].shape[0] % (count * UNIT) == 0


def wide_gather(mine, loose=None):
    shard, width = mine.shape[1:]
    parts = mine.reshape(2 * shard, width)
    if loose is not None:
        parts = jnp.concatenate([parts, loose], axis=0)
    return lax.all_gather(parts, "wide", axis=0)


def lanes_of(parts, shard):
    width = parts.shape[2]
    lanes = [parts[:, lane * shard : (lane + 1) * shard].reshape(-1, width) for lane in range(2)]
    return lanes, parts[:, 2 * shard :].astype(F32)


TILE = 256
LOG2E = 1.4426950408889634


def head_lanes(part_width):
    for head in range(part_width // HD):
        lo = head * HD // 128 * 128
        hi = min(-(-(head + 1) * HD // 128) * 128, part_width)
        lanes = lax.broadcasted_iota(jnp.int32, (1, hi - lo), 1) + lo
        yield head, lo, hi, (lanes >= head * HD) & (lanes < (head + 1) * HD)


def extend(first, left, own, right, ext):
    span = left.shape[1]
    ends = ext.shape[1] - span

    @pl.when(first)
    def _():
        for which in range(2):
            ext[which, :span] = left[which]
            ext[which, span:ends] = own[which][...]
            ext[which, ends:] = right[which]


def forward_kernel(tiles, q, k, v, left, right, q_ids, k_ids, out, lse, ext, total):
    tile = pl.program_id(0)
    part_width = q.shape[1]
    span = left.shape[1]
    ends = ext.shape[1] - span
    extend(tile == 0, left, (k, v), right, ext)
    scale = LOG2E * HD ** (-0.5)

    def run(extra):
        rows = pl.ds(pl.multiple_of(tile * TILE, TILE), TILE + 2 * span)
        keys, values = ext[0, rows], ext[1, rows]
        ids = k_ids[:, rows]
        if extra:
            keys = jnp.concatenate([keys, ext[0, ends:]], axis=0)
            values = jnp.concatenate([values, ext[1, ends:]], axis=0)
            ids = jnp.concatenate([ids, k_ids[:, ends:]], axis=1)
        same = q_ids[...] == ids
        queries = q[...]
        total[...] = jnp.zeros_like(total)
        packed = jnp.zeros((TILE, 128), F32)
        column = lax.broadcasted_iota(jnp.int32, (TILE, 128), 1)
        for head, lo, hi, mask in head_lanes(part_width):
            chosen = jnp.where(mask, queries[:, lo:hi], 0)
            scores = lax.dot_general(
                chosen, keys[:, lo:hi], (((1,), (1,)), ((), ())), preferred_element_type=F32
            )
            scores = jnp.where(same, scores * scale, NEG_FILL)
            top = jnp.max(scores, axis=1, keepdims=True)
            expo = jnp.exp2(scores - top)
            count = jnp.sum(expo, axis=1, keepdims=True)
            part = jnp.dot(expo.astype(BF16), values[:, lo:hi], preferred_element_type=F32)
            total[:, lo:hi] += jnp.where(mask, part / count, 0.0)
            packed = jnp.where(column == head, top + jnp.log2(count), packed)
        out[...] = total[...].astype(BF16)
        lse[...] = packed.T[: lse.shape[0]]

    split_tiles(tile, tiles, run)


def split_tiles(tile, tiles, run):
    first_extra = tiles - 512 // TILE
    extra = (tile >= first_extra) & (tile < tiles - 1)
    pl.when(extra)(lambda: run(True))
    pl.when(jnp.logical_not(extra))(lambda: run(False))


def rim_specs(part_width, span, tok_dev):
    whole = lambda shape: pl.BlockSpec(shape, lambda i: (0,) * len(shape))
    return whole((tok_dev, part_width)), whole((2, span, part_width))


def attention_forward(q, k, v, left, right, q_ids, k_ids):
    tok_dev, part_width = q.shape
    span = left.shape[1]
    tiles = tok_dev // TILE
    head_rows = -(-(part_width // HD) // 8) * 8
    own_spec, rim_spec = rim_specs(part_width, span, tok_dev)
    return pl.pallas_call(
        lambda *refs: forward_kernel(tiles, *refs),
        grid=(tiles,),
        out_shape=[
            jax.ShapeDtypeStruct((tok_dev, part_width), BF16),
            jax.ShapeDtypeStruct((head_rows, tok_dev), F32),
        ],
        in_specs=[
            pl.BlockSpec((TILE, part_width), lambda i: (i, 0)),
            own_spec,
            own_spec,
            rim_spec,
            rim_spec,
            pl.BlockSpec((TILE, 1), lambda i: (i, 0)),
            pl.BlockSpec((1, tok_dev + 2 * span), lambda i: (0, 0)),
        ],
        out_specs=[
            pl.BlockSpec((TILE, part_width), lambda i: (i, 0)),
            pl.BlockSpec((head_rows, TILE), lambda i: (0, i)),
        ],
        scratch_shapes=[
            pltpu.VMEM((2, tok_dev + 2 * span, part_width), BF16),
            pltpu.VMEM((TILE, part_width), F32),
        ],
        compiler_params=pltpu.CompilerParams(vmem_limit_bytes=40 << 20),
        cost_estimate=pl.CostEstimate(
            flops=4 * tok_dev * 512 * part_width,
            transcendentals=tok_dev * 512 * 8,
            bytes_accessed=8 * tok_dev * part_width,
        ),
        name="attention_forward",
    )(q, k, v, left, right, q_ids, k_ids)


def backward_kernel(tiles, q, k, v, left, right, grad, lse, q_ids, k_ids, *refs):
    d_q, d_own, d_rim, ext, d_ext, total = refs
    tile = pl.program_id(0)
    part_width = q.shape[1]
    span = left.shape[1]
    ends = ext.shape[1] - span
    extend(tile == 0, left, (k, v), right, ext)
    scale = HD ** (-0.5)

    @pl.when(tile == 0)
    def _():
        d_ext[...] = jnp.zeros_like(d_ext)

    def run(extra):
        rows = pl.ds(pl.multiple_of(tile * TILE, TILE), TILE + 2 * span)
        keys, values = ext[0, rows], ext[1, rows]
        ids = k_ids[rows]
        if extra:
            keys = jnp.concatenate([keys, ext[0, ends:]], axis=0)
            values = jnp.concatenate([values, ext[1, ends:]], axis=0)
            ids = jnp.concatenate([ids, k_ids[ends:]], axis=0)
        same = ids == q_ids[...]
        queries, grads = q[...], grad[...]
        total[...] = jnp.zeros_like(total)

        def across(left_side, right_side, dims):
            return lax.dot_general(
                left_side, right_side, (dims, ((), ())), preferred_element_type=F32
            )

        for head, lo, hi, mask in head_lanes(part_width):
            chosen = jnp.where(mask, queries[:, lo:hi], 0)
            pulled = jnp.where(mask, grads[:, lo:hi], 0)
            scores = across(keys[:, lo:hi], chosen, ((1,), (1,)))
            scores = jnp.where(same, scores * (scale * LOG2E), NEG_FILL)
            attend = jnp.exp2(scores - lse[head : head + 1])
            d_attend = across(values[:, lo:hi], pulled, ((1,), (1,)))
            centre = jnp.sum(attend * d_attend, axis=0, keepdims=True)
            d_scores = (attend * (d_attend - centre)).astype(BF16)
            d_key = across(d_scores, chosen, ((1,), (0,)))
            d_value = across(attend.astype(BF16), pulled, ((1,), (0,)))
            length = TILE + 2 * span
            d_ext[0, rows, lo:hi] += d_key[:length]
            d_ext[1, rows, lo:hi] += d_value[:length]
            if extra:
                d_ext[0, ends:, lo:hi] += d_key[length:]
                d_ext[1, ends:, lo:hi] += d_value[length:]
            d_query = across(d_scores, keys[:, lo:hi], ((0,), (0,)))
            total[:, lo:hi] += jnp.where(mask, d_query, 0.0)
        d_q[...] = (total[...] * scale).astype(BF16)

    split_tiles(tile, tiles, run)

    @pl.when(tile == tiles - 1)
    def _():
        for which, factor in ((0, scale), (1, 1.0)):
            d_rim[0, which] = (d_ext[which, :span] * factor).astype(BF16)
            d_own[which] = (d_ext[which, span:ends] * factor).astype(BF16)
            d_rim[1, which] = (d_ext[which, ends:] * factor).astype(BF16)


def attention_backward(q, k, v, left, right, grad, lse, q_ids, k_ids):
    tok_dev, part_width = q.shape
    span = left.shape[1]
    tiles = tok_dev // TILE
    own_spec, rim_spec = rim_specs(part_width, span, tok_dev)
    tile_spec = pl.BlockSpec((TILE, part_width), lambda i: (i, 0))
    return pl.pallas_call(
        lambda *refs: backward_kernel(tiles, *refs),
        grid=(tiles,),
        out_shape=[
            jax.ShapeDtypeStruct((tok_dev, part_width), BF16),
            jax.ShapeDtypeStruct((2, tok_dev, part_width), BF16),
            jax.ShapeDtypeStruct((2, 2, span, part_width), BF16),
        ],
        in_specs=[
            tile_spec,
            own_spec,
            own_spec,
            rim_spec,
            rim_spec,
            tile_spec,
            pl.BlockSpec((lse.shape[0], TILE), lambda i: (0, i)),
            pl.BlockSpec((1, TILE), lambda i: (0, i)),
            pl.BlockSpec((tok_dev + 2 * span, 1), lambda i: (0, 0)),
        ],
        out_specs=[
            tile_spec,
            pl.BlockSpec((2, tok_dev, part_width), lambda i: (0, 0, 0)),
            pl.BlockSpec((2, 2, span, part_width), lambda i: (0, 0, 0, 0)),
        ],
        scratch_shapes=[
            pltpu.VMEM((2, tok_dev + 2 * span, part_width), BF16),
            pltpu.VMEM((2, tok_dev + 2 * span, part_width), F32),
            pltpu.VMEM((TILE, part_width), F32),
        ],
        compiler_params=pltpu.CompilerParams(vmem_limit_bytes=48 << 20),
        cost_estimate=pl.CostEstimate(
            flops=10 * tok_dev * 512 * part_width,
            transcendentals=tok_dev * 512 * 8,
            bytes_accessed=16 * tok_dev * part_width,
        ),
        name="attention_backward",
    )(q, k, v, left, right, grad, lse, q_ids, k_ids)


def norm(field):
    centred = field - jnp.mean(field, axis=-1, keepdims=True)
    rstd = lax.rsqrt(jnp.mean(centred * centred, axis=-1, keepdims=True) + EPSILON)
    return centred * rstd, rstd


def norm_back(grad, xhat, rstd):
    return rstd * (
        grad
        - jnp.mean(grad, axis=-1, keepdims=True)
        - xhat * jnp.mean(grad * xhat, axis=-1, keepdims=True)
    )


def gelu_pair(v):
    c = 0.7978845608028654
    sq = v * v
    t = jnp.tanh(c * v * (1.0 + 0.044715 * sq))
    half = 0.5 * (1.0 + t)
    slope = half + 0.5 * v * (1.0 - t * t) * c * (1.0 + 3 * 0.044715 * sq)
    return v * half, slope


def matmul(left, right, dims=((1,), (0,))):
    return lax.dot_general(left, right, (dims, ((), ())), preferred_element_type=F32)


def pick(ids, table):
    slots = lax.broadcasted_iota(jnp.int32, (ids.shape[0], table.shape[0]), 1)
    return matmul((ids == slots).astype(BF16), table)


def gather_images(ids, terms, sums, fresh):
    slots = lax.broadcasted_iota(jnp.int32, (sums.shape[1], ids.shape[1]), 0)
    hot = (ids == slots).astype(BF16)
    for i, term in enumerate(terms):
        part = matmul(hot, term.astype(BF16))
        sums[i] = jnp.where(fresh, 0.0, sums[i]) + part


def halves_out(sums, out, halves):
    size = sums.shape[2] // halves
    for half in range(halves):
        for i in range(sums.shape[0]):
            out[half, i] = sums[i, :, half * size : (half + 1) * size].astype(BF16)


def whole(shape):
    return pl.BlockSpec(shape, lambda i: (0,) * len(shape))


def tiled(rows, width):
    return pl.BlockSpec((rows, width), lambda i: (i, 0))


def token_call(kernel, tokens, name, out_shape, in_specs, out_specs, scratch, flops, operands):
    size = sum(x.size * x.dtype.itemsize for x in operands)
    return pl.pallas_call(
        kernel,
        grid=(tokens // TILE,),
        out_shape=out_shape,
        in_specs=in_specs,
        out_specs=out_specs,
        scratch_shapes=scratch,
        compiler_params=pltpu.CompilerParams(vmem_limit_bytes=60 << 20),
        cost_estimate=pl.CostEstimate(
            flops=flops, transcendentals=0, bytes_accessed=size + size // 2
        ),
        name=name,
    )(*operands)


def shaped(shape, dtype=BF16):
    return jax.ShapeDtypeStruct(shape, dtype)


def project_kernel(tokens, ids, table, weight, bias, q, k, v, norm_one):
    xhat, _ = norm(tokens[...].astype(F32))
    normed = (xhat * (1.0 + pick(ids[...], table[1])) + pick(ids[...], table[0])).astype(BF16)
    norm_one[...] = normed
    size = q.shape[1]
    for i, out in enumerate((q, k, v)):
        rows = matmul(normed, weight[i * size : (i + 1) * size], ((1,), (1,)))
        if i != 1:
            rows = rows + bias[i // 2 : i // 2 + 1].astype(F32)
        out[...] = rows.astype(BF16)


def project(tokens, ids, table, weight, bias):
    count, width = tokens.shape
    size = weight.shape[0] // 3
    return token_call(
        project_kernel,
        count,
        "project",
        [shaped((count, size))] * 3 + [shaped((count, width))],
        [tiled(TILE, width), tiled(TILE, 1), whole(table.shape), whole(weight.shape), whole(bias.shape)],
        [tiled(TILE, size)] * 3 + [tiled(TILE, width)],
        [],
        6 * count * width * size,
        (tokens, ids, table, weight, bias),
    )


def mlp_kernel(
    tokens, mine, theirs, cotangent, ids, live, table, out_bias, up, up_bias, down, *outs
):
    norm_two, hidden, d_upper, d_branch, d_norm, branch = outs
    ids, live = ids[...], live[...]
    attn = mine[...].astype(F32) + theirs[...].astype(F32) + out_bias[...].astype(F32)
    middle = tokens[...].astype(F32) + live * pick(ids, table[0]) * attn
    xhat, _ = norm(middle)
    normed = (xhat * (1.0 + pick(ids, table[2])) + pick(ids, table[1])).astype(BF16)
    norm_two[...] = normed
    pulled = (live * pick(ids, table[3]) * cotangent[...].astype(F32)).astype(BF16)
    d_branch[...] = pulled
    width = up.shape[1]
    step = 384 if width % 384 == 0 else width
    back = ahead = 0.0
    for lo in range(0, width, step):
        cols = slice(lo, lo + step)
        upper = matmul(normed, up[:, cols]) + up_bias[:, cols].astype(F32)
        d_hidden = matmul(pulled, down[cols], ((1,), (1,)))
        value, slope = gelu_pair(upper)
        value = value.astype(BF16)
        d_up = (d_hidden * slope).astype(BF16)
        hidden[:, cols] = value
        d_upper[:, cols] = d_up
        back += matmul(d_up, up[:, cols], ((1,), (1,)))
        ahead += matmul(value, down[cols])
    d_norm[...] = back.astype(BF16)
    branch[...] = ahead.astype(BF16)


def mlp(tokens, mine, theirs, cotangent, ids, live, table, out_bias, up, up_bias, down):
    count, width = tokens.shape
    size = up.shape[1]
    row, col = tiled(TILE, width), tiled(TILE, 1)
    consts = (table, out_bias, up, up_bias, down)
    return token_call(
        mlp_kernel,
        count,
        "mlp",
        [shaped((count, n)) for n in (width, size, size, width, width, width)],
        [row, row, row, row, col, col] + [whole(x.shape) for x in consts],
        [tiled(TILE, n) for n in (width, size, size, width, width, width)],
        [],
        8 * count * width * size,
        (tokens, mine, theirs, cotangent, ids, live) + consts,
    )


def middle_kernel(
    halves, tokens, mine, theirs, cotangent, d_own, d_other, context, ids, live, ids_row, *refs
):
    table, out_bias, weight, d_middle, d_context, d_weight, d_images, d_bias, sums, total = refs
    first = pl.program_id(0) == 0
    last = pl.program_id(0) == pl.num_programs(0) - 1
    ids, live = ids[...], live[...]
    gate = live * pick(ids, table[0])
    attn = mine[...].astype(F32) + theirs[...].astype(F32) + out_bias[...].astype(F32)
    xhat, rstd = norm(tokens[...].astype(F32) + gate * attn)
    d_norm = d_own[...].astype(F32) + d_other[...].astype(F32)
    grad = cotangent[...].astype(F32) + norm_back(d_norm * (1.0 + pick(ids, table[2])), xhat, rstd)
    d_middle[...] = grad
    d_attn = (gate * grad).astype(BF16)
    d_context[...] = matmul(d_attn, weight[...], ((1,), (1,))).astype(BF16)
    part = matmul(context[...], d_attn, ((0,), (0,)))
    total[...] = jnp.where(first, 0.0, total[...]) + part
    column = jnp.sum(d_attn.astype(F32), axis=0, keepdims=True)
    d_bias[...] = jnp.where(first, 0.0, d_bias[...]) + column
    gather_images(ids_row[...], (live * grad * attn, d_norm, d_norm * xhat), sums, first)

    @pl.when(last)
    def _():
        d_weight[...] = total[...].astype(BF16)
        halves_out(sums, d_images, halves)


def middle_back(
    halves, tokens, mine, theirs, cotangent, d_own, d_other, context, ids, live, ids_row, table, out_bias, weight
):
    count, width = tokens.shape
    size = context.shape[1]
    images = table.shape[1]
    row, col = tiled(TILE, width), tiled(TILE, 1)
    consts = (table, out_bias, weight)
    return token_call(
        lambda *refs: middle_kernel(halves, *refs),
        count,
        "middle_back",
        [
            shaped((count, width), F32),
            shaped((count, size)),
            shaped((size, width)),
            shaped((halves, 3, images, width // halves)),
            shaped((1, width), F32),
        ],
        [row] * 6
        + [tiled(TILE, size), col, col, pl.BlockSpec((1, TILE), lambda i: (0, i))]
        + [whole(x.shape) for x in consts],
        [
            row,
            tiled(TILE, size),
            whole((size, width)),
            whole((halves, 3, images, width // halves)),
            whole((1, width)),
        ],
        [pltpu.VMEM((3, images, width), F32), pltpu.VMEM((size, width), F32)],
        4 * count * width * size,
        (tokens, mine, theirs, cotangent, d_own, d_other, context, ids, live, ids_row) + consts,
    )


def project_back_kernel(
    halves, split, tokens, norm_one, d_q, d_own, rims, tail_start, ids_row, weight, *refs
):
    d_norm, top, bottom, d_images, d_bias, sums, total = refs
    tile = pl.program_id(0)
    first = tile == 0
    last = tile == pl.num_programs(0) - 1
    span, size = rims.shape[2], d_q.shape[1]
    rows = lax.broadcasted_iota(jnp.int32, (TILE, span), 0) + tile * TILE
    cols = lax.broadcasted_iota(jnp.int32, (TILE, span), 1)
    head_rim = (rows == cols).astype(BF16)
    tail_rim = (rows == cols + tail_start[0]).astype(BF16)
    parts = [d_q[...]]
    for which in range(2):
        rim = matmul(head_rim, rims[0, which]) + matmul(tail_rim, rims[1, which])
        parts.append((d_own[which].astype(F32) + rim).astype(BF16))
    normed = norm_one[...]
    back = 0.0
    for i, part in enumerate(parts):
        span_rows = slice(i * size, (i + 1) * size)
        back += matmul(part, weight[span_rows])
        grown = matmul(part, normed, ((0,), (0,)))
        total[span_rows] = jnp.where(first, 0.0, total[span_rows]) + grown
    back = back.astype(BF16)
    d_norm[...] = back
    for i, part in ((0, parts[0]), (1, parts[2])):
        column = jnp.sum(part.astype(F32), axis=0, keepdims=True)
        d_bias[i : i + 1] = jnp.where(first, 0.0, d_bias[i : i + 1]) + column
    xhat, _ = norm(tokens[...].astype(F32))
    back = back.astype(F32)
    gather_images(ids_row[...], (back, back * xhat), sums, first)

    @pl.when(last)
    def _():
        top[...] = total[:split].astype(BF16)
        bottom[...] = total[split:].astype(BF16)
        halves_out(sums, d_images, halves)


def project_back(
    halves, split, images, tokens, norm_one, d_q, d_own, rims, tail_start, ids_row, weight
):
    count, width = tokens.shape
    size = d_q.shape[1]
    row = tiled(TILE, width)
    rest = 3 * size - split
    return token_call(
        lambda *refs: project_back_kernel(halves, split, *refs),
        count,
        "project_back",
        [
            shaped((count, width)),
            shaped((split, width)),
            shaped((rest, width)),
            shaped((halves, 2, images, width // halves)),
            shaped((2, size), F32),
        ],
        [
            row,
            row,
            tiled(TILE, size),
            pl.BlockSpec((2, TILE, size), lambda i: (0, i, 0)),
            whole(rims.shape),
            pl.BlockSpec(memory_space=pltpu.SMEM),
            pl.BlockSpec((1, TILE), lambda i: (0, i)),
            whole(weight.shape),
        ],
        [
            row,
            whole((split, width)),
            whole((rest, width)),
            whole((halves, 2, images, width // halves)),
            whole((2, size)),
        ],
        [pltpu.VMEM((2, images, width), F32), pltpu.VMEM((3 * size, width), F32)],
        12 * count * width * size,
        (tokens, norm_one, d_q, d_own, rims, tail_start, ids_row, weight),
    )


def body(
    tokens,
    condition,
    cotangent,
    modulator,
    modulator_bias,
    qkv_weight,
    qv_bias,
    out_weight,
    out_bias,
    up_weight,
    up_bias,
    down_weight,
    down_bias,
    segment_ids,
    valid_counts,
):
    wide_count = lax.axis_size("wide")
    narrow_count = lax.axis_size("narrow")
    wide_index = lax.axis_index("wide")
    narrow_index = lax.axis_index("narrow")
    tok_dev, width = cotangent.shape
    share = tokens.shape[0]
    part_width = qkv_weight.shape[2]
    mod_width = modulator.shape[2]
    img_row = condition.shape[0]
    span = IMG_MAX
    own_count = valid_counts[wide_index]
    positions = jnp.arange(tok_dev, dtype=jnp.int32)
    own_ids = lax.dynamic_slice_in_dim(segment_ids, wide_index * tok_dev, tok_dev)
    live = (positions < own_count).astype(F32)[:, None]
    share_start = narrow_index * share
    ids_col, ids_row = own_ids[:, None], own_ids[None]
    onehot_full = (ids_col == jnp.arange(img_row, dtype=jnp.int32)[None]).astype(BF16)

    def own(rows):
        return lax.dynamic_slice_in_dim(rows, share_start, share)

    cond_rows = condition.astype(F32)
    sigmoid_rows = jax.nn.sigmoid(cond_rows)
    activated = (cond_rows * sigmoid_rows).astype(BF16)
    tok_full = narrow_gather(tokens)
    mod_rows = jnp.transpose(modulator, (1, 2, 0)).reshape(6 * mod_width, width)

    def vectors(lo, hi, after=None):
        part = dot(activated, mod_rows[lo * mod_width : hi * mod_width], ((1,), (1,)))
        part = part + modulator_bias[lo:hi].astype(F32).reshape(1, -1)
        rows = jnp.moveaxis(part.astype(BF16).reshape(img_row, hi - lo, -1), 2, 0)
        if after is not None:
            rows, after = lax.optimization_barrier((rows, after))
        return jnp.transpose(narrow_gather(rows), (2, 1, 0)), after

    table_one, _ = vectors(0, 2)
    table_two, tok_full = vectors(2, 6, tok_full)
    flat_qkv = jnp.transpose(qkv_weight, (1, 2, 0)).reshape(3 * part_width, width)
    queries, key_rows, value_rows, norm_one = project(
        tok_full, ids_col, table_one, flat_qkv, qv_bias
    )
    tail_start = own_count - span

    def tail_of(rows):
        return lax.dynamic_slice_in_dim(rows, tail_start, span)

    def to_right(rows):
        return lax.ppermute(rows, "wide", [(i, i + 1) for i in range(wide_count - 1)])

    def to_left(rows):
        return lax.ppermute(rows, "wide", [(i + 1, i) for i in range(wide_count - 1)])

    from_left = to_right(jnp.stack([tail_of(key_rows), tail_of(value_rows)]))
    from_right = to_left(jnp.stack([key_rows[:span], value_rows[:span]]))
    left_index = jnp.maximum(wide_index - 1, 0)
    right_index = jnp.minimum(wide_index + 1, wide_count - 1)
    left_count = valid_counts[left_index]
    left_ids = lax.dynamic_slice_in_dim(segment_ids, left_index * tok_dev + left_count - span, span)
    left_ids = jnp.where(wide_index > 0, left_ids, -2)
    right_ids = lax.dynamic_slice_in_dim(segment_ids, right_index * tok_dev, span)
    right_ids = jnp.where(wide_index < wide_count - 1, right_ids, -2)
    own_keys = jnp.where(positions < own_count, own_ids, -1)
    extended_ids = jnp.concatenate([left_ids, own_keys, right_ids])
    context, log_sums = attention_forward(
        queries, key_rows, value_rows, from_left, from_right, own_keys[:, None], extended_ids[None]
    )
    block = min(512, tok_dev)
    blocks = tok_dev // block

    def rows_of(rows, block_idx):
        return rows[block_idx * block : (block_idx + 1) * block]

    out_row = out_bias[None]
    attn_parts, attn_others, mlp_outs, d_others = [], [], [], []
    for i in range(blocks):
        attn_parts.append(dot(rows_of(context, i), out_weight, ((1,), (0,)), BF16))
        attn_others.append(narrow_other(attn_parts[i]))
    for i in range(blocks):
        operands = [rows_of(rows, i) for rows in (tok_full, cotangent, ids_col, live)]
        mlp_outs.append(
            mlp(
                operands[0],
                attn_parts[i],
                attn_others[i],
                *operands[1:],
                table_two,
                out_row,
                up_weight,
                up_bias[None],
                down_weight,
            )
        )
        d_others.append(narrow_other(mlp_outs[i][4]))
    norm_two, hidden, d_upper, d_branch, d_norm, branch_part = [
        jnp.concatenate(parts, axis=0) for parts in zip(*mlp_outs)
    ]
    up_grad = dot(d_upper, norm_two, ((0,), (0,)), BF16)
    down_grad = dot(hidden, d_branch, ((0,), (0,)), BF16)
    if ring_fits([up_grad]):
        mine = ring_scatter([up_grad, down_grad], None, 1)[0]
        mine, d_others = lax.optimization_barrier((mine, d_others))
        gathered = wide_gather(mine)
    else:
        gathered = lax.psum((up_grad, down_grad), "wide")
    attn_part, attn_other, d_other = [
        jnp.concatenate(parts, axis=0) for parts in (attn_parts, attn_others, d_others)
    ]
    branch = narrow_scatter(branch_part) + down_bias.astype(F32)

    def image_sum(hot, term):
        return dot(hot, term.astype(BF16), ((0,), (0,)))

    first_bias = jnp.where(narrow_index == 0, down_bias.astype(F32), 0.0)
    d_gate_two = image_sum(
        onehot_full, live * cotangent.astype(F32) * (branch_part.astype(F32) + first_bias)
    )
    d_gate_two = narrow_scatter(d_gate_two.astype(BF16), 1)
    d_middle, d_context, out_weight_grad, images_two, out_bias_sum = middle_back(
        narrow_count,
        tok_full,
        attn_part,
        attn_other,
        cotangent,
        d_norm,
        d_other,
        context,
        ids_col,
        live,
        ids_row,
        table_two,
        out_row,
        out_weight,
    )
    d_queries, d_own, d_rim = attention_backward(
        queries,
        key_rows,
        value_rows,
        from_left,
        from_right,
        d_context,
        log_sums,
        own_keys[None],
        extended_ids[:, None],
    )
    rims = jnp.stack([to_right(d_rim[1]), to_left(d_rim[0])])
    lane_rows = (4 * part_width * width + 6 * img_row * mod_width) // (2 * width)
    split = min(lane_rows, 3 * part_width - 16)
    d_norm_part, top, bottom, images_one, qv_sums = project_back(
        narrow_count,
        split,
        img_row,
        tok_full,
        norm_one,
        d_queries,
        d_own,
        rims,
        tail_start[None],
        ids_row,
        flat_qkv,
    )

    def mine_of(images):
        return lax.dynamic_index_in_dim(images, narrow_index, 0, keepdims=False)

    if narrow_count == 2:
        theirs = lax.dynamic_index_in_dim(images_one, 1 - narrow_index, 0, keepdims=False)
        early = mine_of(images_one).astype(F32) + swap(theirs).astype(F32)
    else:
        early = mine_of(lax.psum(images_one, "narrow"))
    images_two = mine_of(images_two)
    loose_parts = [
        jnp.sum(d_upper.astype(F32), axis=0),
        jnp.sum(d_branch.astype(F32), axis=0),
        qv_sums[0],
        qv_sums[1],
        out_bias_sum[0],
    ]
    loose = jnp.concatenate(loose_parts)
    loose = jnp.pad(loose, (0, (-loose.shape[0]) % (8 * width))).reshape(-1, width).astype(BF16)
    terms = [early[0], early[1], images_two[0], images_two[1], images_two[2], d_gate_two]
    terms = [term.astype(BF16) for term in terms]
    d_mod = [jnp.concatenate(terms[2 * i : 2 * i + 2], axis=1) for i in range(3)]
    if 2 * mod_width == width:
        d_mod_flat = jnp.concatenate(d_mod, axis=0)
    else:
        d_mod_flat = jnp.concatenate(d_mod, axis=1).reshape(-1, width)
    rest = jnp.concatenate([bottom, out_weight_grad, d_mod_flat], axis=0)
    if ring_fits([top]) and top.shape == rest.shape:
        gathered, rest = lax.optimization_barrier((gathered, rest))
        mine, d_norm_other = ring_scatter([top, rest], d_norm_part, 0)
        (up_grad, down_grad), _ = lanes_of(gathered, gathered.shape[1] // 2)
        d_norm_one = own(d_norm_part).astype(F32) + d_norm_other.astype(F32)
        (top, rest), loose = lanes_of(wide_gather(mine, loose), mine.shape[1])
    else:
        up_grad, down_grad = gathered
        d_norm_one = narrow_scatter(d_norm_part)
        top, rest = lax.psum((top, rest), "wide")
        loose = lax.all_gather(loose, "wide", axis=0).astype(F32)
    tok_own = tokens.astype(F32)
    xhat_one, rstd_one = norm(tok_own)
    hot_own = own(onehot_full)
    scale_one = dot(hot_own, table_one[1], ((1,), (0,)))
    tokens_grad = own(d_middle) + norm_back(d_norm_one * (1.0 + scale_one), xhat_one, rstd_one)
    attn_own = own(attn_part).astype(F32) + own(attn_other).astype(F32) + out_bias.astype(F32)
    live_own = own(live)
    gates = [dot(hot_own, table_two[j], ((1,), (0,))) for j in (0, 3)]
    layer_out = (tok_own + live_own * (gates[0] * attn_own + gates[1] * branch)).astype(BF16)
    up_weight_grad = up_grad.T.astype(F32)
    down_weight_grad = down_grad.astype(F32)
    loose = jnp.sum(loose, axis=0)
    keep = 3 * part_width - split
    qkv_flat = jnp.concatenate([top.astype(F32), rest[:keep].astype(F32)], axis=0)
    qkv_weight_grad = jnp.transpose(qkv_flat.reshape(3, part_width, width), (2, 0, 1))
    out_weight_grad = rest[keep : keep + part_width].astype(F32)
    loose = loose.reshape(-1)
    bounds = [0]
    for part in loose_parts:
        bounds.append(bounds[-1] + part.shape[0])
    up_bias_grad, down_bias_grad, query_bias, value_bias, out_bias_grad = [
        loose[bounds[i] : bounds[i + 1]] for i in range(5)
    ]
    qv_bias_grad = jnp.stack([query_bias, value_bias])
    d_mod_flat = rest[keep + part_width :]
    if 2 * mod_width == width:
        d_mod = d_mod_flat.reshape(3, img_row, width)
    else:
        d_mod = jnp.moveaxis(d_mod_flat.reshape(img_row, 3, -1), 1, 0)
    modulator_grad = lax.dot_general(
        d_mod, activated, (((1,), (0,)), ((), ())), preferred_element_type=F32
    )
    modulator_grad = jnp.transpose(modulator_grad.reshape(6, mod_width, width), (2, 0, 1))
    modulator_bias_grad = jnp.sum(d_mod.astype(F32), axis=1).reshape(6, mod_width)
    mod_blocks = mod_rows.reshape(3, 2 * mod_width, width)
    d_activated = sum(dot(d_mod[i], mod_blocks[i], ((1,), (0,))) for i in range(3))
    cond_part = d_activated * sigmoid_rows * (1.0 + cond_rows * (1.0 - sigmoid_rows))
    cond_part = cond_part.astype(BF16)
    condition_grad = cond_part.astype(F32) + narrow_other(cond_part).astype(F32)
    return (
        layer_out,
        tokens_grad,
        condition_grad,
        modulator_grad,
        modulator_bias_grad,
        qkv_weight_grad,
        qv_bias_grad,
        out_weight_grad,
        out_bias_grad,
        up_weight_grad,
        up_bias_grad,
        down_weight_grad,
        down_bias_grad,
    )


def solution(mesh):
    in_specs = (
        P(("wide", "narrow"), None),
        P(),
        P("wide", None),
        P(None, None, "narrow"),
        P(None, "narrow"),
        P(None, None, "narrow"),
        P(None, "narrow"),
        P("narrow", None),
        P(),
        P(None, "narrow"),
        P("narrow"),
        P("narrow", None),
        P(),
        P(),
        P(),
    )
    out_specs = (
        P(("wide", "narrow"), None),
        P(("wide", "narrow"), None),
        P(),
        P(None, None, "narrow"),
        P(None, "narrow"),
        P(None, None, "narrow"),
        P(None, "narrow"),
        P("narrow", None),
        P(),
        P(None, "narrow"),
        P("narrow"),
        P("narrow", None),
        P(),
    )
    return jax.shard_map(body, mesh=mesh, in_specs=in_specs, out_specs=out_specs, check_vma=False)
```

```python
import jax
import jax.numpy as jnp
from jax import lax
from jax.experimental import pallas as pl
from jax.experimental.pallas import tpu as pltpu
from jax.sharding import PartitionSpec as P

HD = 72
IMG_MAX = 128
EPSILON = 1e-06
NEG_FILL = -1e30
F32 = jnp.float32
BF16 = jnp.bfloat16


def dot(left, right, dims, out=F32):
    return lax.dot_general(left, right, (dims, ((), ())), preferred_element_type=F32).astype(out)


def swap(part):
    return lax.ppermute(part, "narrow", [(0, 1), (1, 0)])


def narrow_gather(part):
    if lax.axis_size("narrow") != 2:
        return lax.all_gather(part, "narrow", axis=0, tiled=True)
    other = swap(part)
    first = lax.axis_index("narrow") == 0
    return jnp.where(
        first, jnp.concatenate([part, other], axis=0), jnp.concatenate([other, part], axis=0)
    )


def narrow_other(part):
    if lax.axis_size("narrow") != 2:
        return (lax.psum(part.astype(F32), "narrow") - part.astype(F32)).astype(BF16)
    return swap(part)


def narrow_scatter(part, dim=0):
    count = lax.axis_size("narrow")
    if count != 2:
        return lax.psum_scatter(part, "narrow", scatter_dimension=dim, tiled=True).astype(F32)
    size = part.shape[dim] // 2
    index = lax.axis_index("narrow")
    mine = lax.dynamic_slice_in_dim(part, index * size, size, axis=dim)
    theirs = lax.dynamic_slice_in_dim(part, (1 - index) * size, size, axis=dim)
    return mine.astype(F32) + swap(theirs).astype(F32)


MESH = pl.DeviceIdType.MESH
UNIT = 48


def ring_kernel(chips, subs, *refs):
    data, part, loose, out, landing, loose_out = refs[:2], *refs[2:7]
    mine, theirs, slots, last, loose_pair, loose_rows = refs[7:13]
    copy_sems, core_sems, ring_sems, swap_sems, gather_sems, pair_sems, own_sems = refs[13:20]
    loose_pair_sems, loose_sems = refs[20:]
    wide = lax.axis_index("wide")
    chip, core = wide // 2, wide % 2
    half = chips // 2

    def place(position):
        position = lax.rem(position + 2 * chips, chips)
        side = position // half
        return (1 - side) * 2 * position + side * (2 * (chips - 1 - position) + 1)

    position = chip // 2 + (chip % 2) * (chips - 1 - 2 * (chip // 2))
    ahead = 2 * place(position + 1) + core
    behind = 2 * place(position - 1) + core
    sibling = 2 * chip + 1 - core
    facing = 1 - lax.axis_index("narrow")
    barrier = pltpu.get_barrier_semaphore()
    for device in (ahead, behind, sibling):
        pl.semaphore_signal(barrier, inc=1, device_id={"wide": device}, device_id_type=MESH)
    pl.semaphore_signal(barrier, inc=1, device_id={"narrow": facing}, device_id_type=MESH)
    pl.semaphore_wait(barrier, 4)
    share = landing.shape[0]
    turn = pltpu.make_async_remote_copy(
        src_ref=part.at[pl.ds(facing * share, share)],
        dst_ref=landing,
        send_sem=swap_sems.at[0],
        recv_sem=swap_sems.at[1],
        device_id={"narrow": facing},
        device_id_type=MESH,
    )
    turn.start()
    loose_swap = pltpu.make_async_remote_copy(
        src_ref=loose,
        dst_ref=loose_pair,
        send_sem=loose_pair_sems.at[0],
        recv_sem=loose_pair_sems.at[1],
        device_id={"wide": sibling},
        device_id_type=MESH,
    )
    loose_swap.start()

    def loose_hop(step, index):
        return pltpu.make_async_remote_copy(
            src_ref=loose_rows.at[index],
            dst_ref=loose_rows.at[index],
            send_sem=loose_sems.at[0, step],
            recv_sem=loose_sems.at[1, step],
            device_id={"wide": ahead},
            device_id_type=MESH,
        )

    def local(lane):
        return pltpu.make_async_copy(data[lane].at[:, core], mine.at[lane], copy_sems.at[lane])

    def across(lane):
        return pltpu.make_async_remote_copy(
            src_ref=data[lane].at[:, 1 - core],
            dst_ref=theirs.at[lane],
            send_sem=core_sems.at[0, lane],
            recv_sem=core_sems.at[1, lane],
            device_id={"wide": sibling},
            device_id_type=MESH,
        )

    for lane in range(2):
        across(lane).start()
        local(lane).start()

    def rows_of(sub):
        return pl.ds(sub * UNIT, UNIT)

    def hop(lane, step, sub):
        rows = rows_of(sub)
        if step == 0:
            first = place(position - 1 if lane == 0 else position + 1)
            source = mine.at[lane, first, rows]
        else:
            source = slots.at[lane, step - 1, rows]
        return pltpu.make_async_remote_copy(
            src_ref=source,
            dst_ref=slots.at[lane, step, rows],
            send_sem=ring_sems.at[0, lane, step, sub],
            recv_sem=ring_sems.at[1, lane, step, sub],
            device_id={"wide": ahead if lane == 0 else behind},
            device_id_type=MESH,
        )

    def held(lane, step, sub, side):
        index = place(position - step if lane == 0 else position + step)
        return out.at[lane, index, side, rows_of(sub)]

    def send_on(lane, step, sub):
        source = last.at[lane, rows_of(sub)] if step == 0 else held(lane, step, sub, core)
        return pltpu.make_async_remote_copy(
            src_ref=source,
            dst_ref=held(lane, step, sub, core),
            send_sem=gather_sems.at[0, lane, step, sub],
            recv_sem=gather_sems.at[1, lane, step, sub],
            device_id={"wide": ahead if lane == 0 else behind},
            device_id_type=MESH,
        )

    def landed(lane, step, sub):
        return pltpu.make_async_remote_copy(
            src_ref=last.at[lane, rows_of(sub)],
            dst_ref=held(lane, step + 1, sub, core),
            send_sem=gather_sems.at[0, lane, step, sub],
            recv_sem=gather_sems.at[1, lane, step, sub],
            device_id={"wide": ahead if lane == 0 else behind},
            device_id_type=MESH,
        )

    def pair(lane, step, sub, side):
        source = last.at[lane, rows_of(sub)] if step == 0 else held(lane, step, sub, core)
        return pltpu.make_async_remote_copy(
            src_ref=source,
            dst_ref=held(lane, step, sub, side),
            send_sem=pair_sems.at[0, lane, step, sub],
            recv_sem=pair_sems.at[1, lane, step, sub],
            device_id={"wide": sibling},
            device_id_type=MESH,
        )

    def keep(lane, sub):
        return pltpu.make_async_copy(
            last.at[lane, rows_of(sub)], held(lane, 0, sub, core), own_sems.at[lane, sub]
        )

    loose_swap.wait()
    loose_rows[chip] = loose[...] + loose_pair[...]
    loose_hop(0, chip).start()
    for lane in range(2):
        local(lane).wait()
        across(lane).wait()

        def merge(index, carry, lane=lane):
            mine[lane, index] = mine[lane, index] + theirs[lane, index]
            return carry

        lax.fori_loop(0, chips, merge, 0)
        for sub in range(subs):
            hop(lane, 0, sub).start()
    for step in range(chips - 1):
        passed = place(position - 1 - step)
        loose_hop(step, passed).wait_recv()
        if step < chips - 2:
            loose_hop(step + 1, passed).start()
        for sub in range(subs):
            for lane in range(2):
                hop(lane, step, sub).wait_recv()
                offset = 2 + step
                index = place(position - offset if lane == 0 else position + offset)
                rows = rows_of(sub)
                total = slots[lane, step, rows] + mine[lane, index, rows]
                if step == chips - 2:
                    last[lane, rows] = total
                    send_on(lane, 0, sub).start()
                    pair(lane, 0, sub, core).start()
                    keep(lane, sub).start()
                else:
                    slots[lane, step, rows] = total
                    hop(lane, step + 1, sub).start()
    for step in range(chips - 1):
        for sub in range(subs):
            for lane in range(2):
                landed(lane, step, sub).wait_recv()
                if step < chips - 2:
                    send_on(lane, step + 1, sub).start()
                pair(lane, step + 1, sub, core).start()
    loose_out[...] = jnp.sum(loose_rows[...], axis=0)
    for step in range(chips):
        if step < chips - 1:
            loose_hop(step, place(position - step)).wait_send()
        for sub in range(subs):
            for lane in range(2):
                pair(lane, step, sub, 1 - core).wait_recv()
                pair(lane, step, sub, core).wait_send()
                if step == 0:
                    keep(lane, sub).wait()
                if step < chips - 1:
                    hop(lane, step, sub).wait_send()
                    send_on(lane, step, sub).wait_send()
    turn.wait()


def ring_sum(lanes, part, loose, collective_id):
    chips = lax.axis_size("wide") // 2
    rows, width = lanes[0].shape
    shard = rows // (2 * chips)
    subs = shard // UNIT
    anywhere = pl.BlockSpec(memory_space=pl.ANY)
    inside = pl.BlockSpec(memory_space=pltpu.VMEM)
    sums, landed, loose_sum = pl.pallas_call(
        lambda *refs: ring_kernel(chips, subs, *refs),
        out_shape=[
            jax.ShapeDtypeStruct((2, chips, 2, shard, width), BF16),
            jax.ShapeDtypeStruct((part.shape[0] // 2, part.shape[1]), BF16),
            jax.ShapeDtypeStruct(loose.shape, F32),
        ],
        in_specs=[anywhere] * 3 + [inside],
        out_specs=[anywhere] * 2 + [inside],
        scratch_shapes=[
            pltpu.VMEM((2, chips, shard, width), BF16),
            pltpu.VMEM((2, chips, shard, width), BF16),
            pltpu.VMEM((2, chips - 1, shard, width), BF16),
            pltpu.VMEM((2, shard, width), BF16),
            pltpu.VMEM(loose.shape, F32),
            pltpu.VMEM((chips,) + loose.shape, F32),
            pltpu.SemaphoreType.DMA((2,)),
            pltpu.SemaphoreType.DMA((2, 2)),
            pltpu.SemaphoreType.DMA((2, 2, chips - 1, subs)),
            pltpu.SemaphoreType.DMA((2,)),
            pltpu.SemaphoreType.DMA((2, 2, chips - 1, subs)),
            pltpu.SemaphoreType.DMA((2, 2, chips, subs)),
            pltpu.SemaphoreType.DMA((2, subs)),
            pltpu.SemaphoreType.DMA((2,)),
            pltpu.SemaphoreType.DMA((2, chips - 1)),
        ],
        compiler_params=pltpu.CompilerParams(
            collective_id=collective_id, has_side_effects=True, vmem_limit_bytes=40 << 20
        ),
        name="ring_sum",
    )(*[lane.reshape(chips, 2, shard, width) for lane in lanes], part, loose)
    return sums.reshape(2 * rows, width), landed, loose_sum


def ring_fits(lanes):
    count = lax.axis_size("wide")
    return lax.axis_size("narrow") == 2 and lanes[0].shape[0] % (count * UNIT) == 0


TILE = 256
LOG2E = 1.4426950408889634


def head_lanes(part_width):
    for head in range(part_width // HD):
        lo = head * HD // 128 * 128
        hi = min(-(-(head + 1) * HD // 128) * 128, part_width)
        lanes = lax.broadcasted_iota(jnp.int32, (1, hi - lo), 1) + lo
        yield head, lo, hi, (lanes >= head * HD) & (lanes < (head + 1) * HD)


def extend(first, left, own, right, ext):
    span = left.shape[1]
    ends = ext.shape[1] - span

    @pl.when(first)
    def _():
        for which in range(2):
            ext[which, :span] = left[which]
            ext[which, span:ends] = own[which][...]
            ext[which, ends:] = right[which]


def forward_kernel(tiles, q, k, v, left, right, q_ids, k_ids, out, lse, ext, total):
    tile = pl.program_id(0)
    part_width = q.shape[1]
    span = left.shape[1]
    ends = ext.shape[1] - span
    extend(tile == 0, left, (k, v), right, ext)
    scale = LOG2E * HD ** (-0.5)

    def run(extra):
        rows = pl.ds(pl.multiple_of(tile * TILE, TILE), TILE + 2 * span)
        keys, values = ext[0, rows], ext[1, rows]
        ids = k_ids[:, rows]
        if extra:
            keys = jnp.concatenate([keys, ext[0, ends:]], axis=0)
            values = jnp.concatenate([values, ext[1, ends:]], axis=0)
            ids = jnp.concatenate([ids, k_ids[:, ends:]], axis=1)
        same = q_ids[...] == ids
        queries = q[...]
        total[...] = jnp.zeros_like(total)
        packed = jnp.zeros((TILE, 128), F32)
        column = lax.broadcasted_iota(jnp.int32, (TILE, 128), 1)
        for head, lo, hi, mask in head_lanes(part_width):
            chosen = jnp.where(mask, queries[:, lo:hi], 0)
            scores = lax.dot_general(
                chosen, keys[:, lo:hi], (((1,), (1,)), ((), ())), preferred_element_type=F32
            )
            scores = jnp.where(same, scores * scale, NEG_FILL)
            top = jnp.max(scores, axis=1, keepdims=True)
            expo = jnp.exp2(scores - top)
            count = jnp.sum(expo, axis=1, keepdims=True)
            part = jnp.dot(expo.astype(BF16), values[:, lo:hi], preferred_element_type=F32)
            total[:, lo:hi] += jnp.where(mask, part / count, 0.0)
            packed = jnp.where(column == head, top + jnp.log2(count), packed)
        out[...] = total[...].astype(BF16)
        lse[...] = packed.T[: lse.shape[0]]

    split_tiles(tile, tiles, run)


def split_tiles(tile, tiles, run):
    first_extra = tiles - 512 // TILE
    extra = (tile >= first_extra) & (tile < tiles - 1)
    pl.when(extra)(lambda: run(True))
    pl.when(jnp.logical_not(extra))(lambda: run(False))


def rim_specs(part_width, span, tok_dev):
    whole = lambda shape: pl.BlockSpec(shape, lambda i: (0,) * len(shape))
    return whole((tok_dev, part_width)), whole((2, span, part_width))


def attention_forward(q, k, v, left, right, q_ids, k_ids):
    tok_dev, part_width = q.shape
    span = left.shape[1]
    tiles = tok_dev // TILE
    head_rows = -(-(part_width // HD) // 8) * 8
    own_spec, rim_spec = rim_specs(part_width, span, tok_dev)
    return pl.pallas_call(
        lambda *refs: forward_kernel(tiles, *refs),
        grid=(tiles,),
        out_shape=[
            jax.ShapeDtypeStruct((tok_dev, part_width), BF16),
            jax.ShapeDtypeStruct((head_rows, tok_dev), F32),
        ],
        in_specs=[
            pl.BlockSpec((TILE, part_width), lambda i: (i, 0)),
            own_spec,
            own_spec,
            rim_spec,
            rim_spec,
            pl.BlockSpec((TILE, 1), lambda i: (i, 0)),
            pl.BlockSpec((1, tok_dev + 2 * span), lambda i: (0, 0)),
        ],
        out_specs=[
            pl.BlockSpec((TILE, part_width), lambda i: (i, 0)),
            pl.BlockSpec((head_rows, TILE), lambda i: (0, i)),
        ],
        scratch_shapes=[
            pltpu.VMEM((2, tok_dev + 2 * span, part_width), BF16),
            pltpu.VMEM((TILE, part_width), F32),
        ],
        compiler_params=pltpu.CompilerParams(vmem_limit_bytes=40 << 20),
        cost_estimate=pl.CostEstimate(
            flops=4 * tok_dev * 512 * part_width,
            transcendentals=tok_dev * 512 * 8,
            bytes_accessed=8 * tok_dev * part_width,
        ),
        name="attention_forward",
    )(q, k, v, left, right, q_ids, k_ids)


def backward_kernel(tiles, q, k, v, left, right, grad, lse, q_ids, k_ids, *refs):
    d_q, d_own, d_rim, ext, d_ext, total = refs
    tile = pl.program_id(0)
    part_width = q.shape[1]
    span = left.shape[1]
    ends = ext.shape[1] - span
    extend(tile == 0, left, (k, v), right, ext)
    scale = HD ** (-0.5)

    @pl.when(tile == 0)
    def _():
        d_ext[...] = jnp.zeros_like(d_ext)

    def run(extra):
        rows = pl.ds(pl.multiple_of(tile * TILE, TILE), TILE + 2 * span)
        keys, values = ext[0, rows], ext[1, rows]
        ids = k_ids[rows]
        if extra:
            keys = jnp.concatenate([keys, ext[0, ends:]], axis=0)
            values = jnp.concatenate([values, ext[1, ends:]], axis=0)
            ids = jnp.concatenate([ids, k_ids[ends:]], axis=0)
        same = ids == q_ids[...]
        queries, grads = q[...], grad[...]
        total[...] = jnp.zeros_like(total)

        def across(left_side, right_side, dims):
            return lax.dot_general(
                left_side, right_side, (dims, ((), ())), preferred_element_type=F32
            )

        for head, lo, hi, mask in head_lanes(part_width):
            chosen = jnp.where(mask, queries[:, lo:hi], 0)
            pulled = jnp.where(mask, grads[:, lo:hi], 0)
            scores = across(keys[:, lo:hi], chosen, ((1,), (1,)))
            scores = jnp.where(same, scores * (scale * LOG2E), NEG_FILL)
            attend = jnp.exp2(scores - lse[head : head + 1])
            d_attend = across(values[:, lo:hi], pulled, ((1,), (1,)))
            centre = jnp.sum(attend * d_attend, axis=0, keepdims=True)
            d_scores = (attend * (d_attend - centre)).astype(BF16)
            d_key = across(d_scores, chosen, ((1,), (0,)))
            d_value = across(attend.astype(BF16), pulled, ((1,), (0,)))
            length = TILE + 2 * span
            d_ext[0, rows, lo:hi] += d_key[:length]
            d_ext[1, rows, lo:hi] += d_value[:length]
            if extra:
                d_ext[0, ends:, lo:hi] += d_key[length:]
                d_ext[1, ends:, lo:hi] += d_value[length:]
            d_query = across(d_scores, keys[:, lo:hi], ((0,), (0,)))
            total[:, lo:hi] += jnp.where(mask, d_query, 0.0)
        d_q[...] = (total[...] * scale).astype(BF16)

    split_tiles(tile, tiles, run)

    @pl.when(tile == tiles - 1)
    def _():
        for which, factor in ((0, scale), (1, 1.0)):
            d_rim[0, which] = (d_ext[which, :span] * factor).astype(BF16)
            d_own[which] = (d_ext[which, span:ends] * factor).astype(BF16)
            d_rim[1, which] = (d_ext[which, ends:] * factor).astype(BF16)


def attention_backward(q, k, v, left, right, grad, lse, q_ids, k_ids):
    tok_dev, part_width = q.shape
    span = left.shape[1]
    tiles = tok_dev // TILE
    own_spec, rim_spec = rim_specs(part_width, span, tok_dev)
    tile_spec = pl.BlockSpec((TILE, part_width), lambda i: (i, 0))
    return pl.pallas_call(
        lambda *refs: backward_kernel(tiles, *refs),
        grid=(tiles,),
        out_shape=[
            jax.ShapeDtypeStruct((tok_dev, part_width), BF16),
            jax.ShapeDtypeStruct((2, tok_dev, part_width), BF16),
            jax.ShapeDtypeStruct((2, 2, span, part_width), BF16),
        ],
        in_specs=[
            tile_spec,
            own_spec,
            own_spec,
            rim_spec,
            rim_spec,
            tile_spec,
            pl.BlockSpec((lse.shape[0], TILE), lambda i: (0, i)),
            pl.BlockSpec((1, TILE), lambda i: (0, i)),
            pl.BlockSpec((tok_dev + 2 * span, 1), lambda i: (0, 0)),
        ],
        out_specs=[
            tile_spec,
            pl.BlockSpec((2, tok_dev, part_width), lambda i: (0, 0, 0)),
            pl.BlockSpec((2, 2, span, part_width), lambda i: (0, 0, 0, 0)),
        ],
        scratch_shapes=[
            pltpu.VMEM((2, tok_dev + 2 * span, part_width), BF16),
            pltpu.VMEM((2, tok_dev + 2 * span, part_width), F32),
            pltpu.VMEM((TILE, part_width), F32),
        ],
        compiler_params=pltpu.CompilerParams(vmem_limit_bytes=48 << 20),
        cost_estimate=pl.CostEstimate(
            flops=10 * tok_dev * 512 * part_width,
            transcendentals=tok_dev * 512 * 8,
            bytes_accessed=16 * tok_dev * part_width,
        ),
        name="attention_backward",
    )(q, k, v, left, right, grad, lse, q_ids, k_ids)


def norm(field):
    centred = field - jnp.mean(field, axis=-1, keepdims=True)
    rstd = lax.rsqrt(jnp.mean(centred * centred, axis=-1, keepdims=True) + EPSILON)
    return centred * rstd, rstd


def norm_back(grad, xhat, rstd):
    return rstd * (
        grad
        - jnp.mean(grad, axis=-1, keepdims=True)
        - xhat * jnp.mean(grad * xhat, axis=-1, keepdims=True)
    )


def gelu_pair(v):
    c = 0.7978845608028654
    sq = v * v
    t = jnp.tanh(c * v * (1.0 + 0.044715 * sq))
    half = 0.5 * (1.0 + t)
    slope = half + 0.5 * v * (1.0 - t * t) * c * (1.0 + 3 * 0.044715 * sq)
    return v * half, slope


def matmul(left, right, dims=((1,), (0,))):
    return lax.dot_general(left, right, (dims, ((), ())), preferred_element_type=F32)


def pick(ids, table):
    slots = lax.broadcasted_iota(jnp.int32, (ids.shape[0], table.shape[0]), 1)
    return matmul((ids == slots).astype(BF16), table)


def gather_images(ids, terms, sums, fresh):
    slots = lax.broadcasted_iota(jnp.int32, (sums.shape[1], ids.shape[1]), 0)
    hot = (ids == slots).astype(BF16)
    for i, term in enumerate(terms):
        part = matmul(hot, term.astype(BF16))
        sums[i] = jnp.where(fresh, 0.0, sums[i]) + part


def halves_out(sums, out, halves):
    size = sums.shape[2] // halves
    for half in range(halves):
        for i in range(sums.shape[0]):
            out[half, i] = sums[i, :, half * size : (half + 1) * size].astype(BF16)


def whole(shape):
    return pl.BlockSpec(shape, lambda i: (0,) * len(shape))


def tiled(rows, width):
    return pl.BlockSpec((rows, width), lambda i: (i, 0))


def token_call(kernel, tokens, name, out_shape, in_specs, out_specs, scratch, flops, operands):
    size = sum(x.size * x.dtype.itemsize for x in operands)
    return pl.pallas_call(
        kernel,
        grid=(tokens // TILE,),
        out_shape=out_shape,
        in_specs=in_specs,
        out_specs=out_specs,
        scratch_shapes=scratch,
        compiler_params=pltpu.CompilerParams(vmem_limit_bytes=60 << 20),
        cost_estimate=pl.CostEstimate(
            flops=flops, transcendentals=0, bytes_accessed=size + size // 2
        ),
        name=name,
    )(*operands)


def shaped(shape, dtype=BF16):
    return jax.ShapeDtypeStruct(shape, dtype)


def project_kernel(tokens, ids, table, weight, bias, q, k, v, norm_one):
    xhat, _ = norm(tokens[...].astype(F32))
    normed = (xhat * (1.0 + pick(ids[...], table[1])) + pick(ids[...], table[0])).astype(BF16)
    norm_one[...] = normed
    size = q.shape[1]
    for i, out in enumerate((q, k, v)):
        rows = matmul(normed, weight[i * size : (i + 1) * size], ((1,), (1,)))
        if i != 1:
            rows = rows + bias[i // 2 : i // 2 + 1].astype(F32)
        out[...] = rows.astype(BF16)


def project(tokens, ids, table, weight, bias):
    count, width = tokens.shape
    size = weight.shape[0] // 3
    return token_call(
        project_kernel,
        count,
        "project",
        [shaped((count, size))] * 3 + [shaped((count, width))],
        [tiled(TILE, width), tiled(TILE, 1), whole(table.shape), whole(weight.shape), whole(bias.shape)],
        [tiled(TILE, size)] * 3 + [tiled(TILE, width)],
        [],
        6 * count * width * size,
        (tokens, ids, table, weight, bias),
    )


def mlp_kernel(
    tokens, mine, theirs, cotangent, ids, live, table, out_bias, up, up_bias, down, *outs
):
    norm_two, hidden, d_upper, d_branch, d_norm, branch = outs
    ids, live = ids[...], live[...]
    attn = mine[...].astype(F32) + theirs[...].astype(F32) + out_bias[...].astype(F32)
    middle = tokens[...].astype(F32) + live * pick(ids, table[0]) * attn
    xhat, _ = norm(middle)
    normed = (xhat * (1.0 + pick(ids, table[2])) + pick(ids, table[1])).astype(BF16)
    norm_two[...] = normed
    pulled = (live * pick(ids, table[3]) * cotangent[...].astype(F32)).astype(BF16)
    d_branch[...] = pulled
    width = up.shape[1]
    step = 384 if width % 384 == 0 else width
    back = ahead = 0.0
    for lo in range(0, width, step):
        cols = slice(lo, lo + step)
        upper = matmul(normed, up[:, cols]) + up_bias[:, cols].astype(F32)
        d_hidden = matmul(pulled, down[cols], ((1,), (1,)))
        value, slope = gelu_pair(upper)
        value = value.astype(BF16)
        d_up = (d_hidden * slope).astype(BF16)
        hidden[:, cols] = value
        d_upper[:, cols] = d_up
        back += matmul(d_up, up[:, cols], ((1,), (1,)))
        ahead += matmul(value, down[cols])
    d_norm[...] = back.astype(BF16)
    branch[...] = ahead.astype(BF16)


def mlp(tokens, mine, theirs, cotangent, ids, live, table, out_bias, up, up_bias, down):
    count, width = tokens.shape
    size = up.shape[1]
    row, col = tiled(TILE, width), tiled(TILE, 1)
    consts = (table, out_bias, up, up_bias, down)
    return token_call(
        mlp_kernel,
        count,
        "mlp",
        [shaped((count, n)) for n in (width, size, size, width, width, width)],
        [row, row, row, row, col, col] + [whole(x.shape) for x in consts],
        [tiled(TILE, n) for n in (width, size, size, width, width, width)],
        [],
        8 * count * width * size,
        (tokens, mine, theirs, cotangent, ids, live) + consts,
    )


def middle_kernel(
    halves, tokens, mine, theirs, cotangent, d_own, d_other, context, ids, live, ids_row, *refs
):
    table, out_bias, weight, d_middle, d_context, d_weight, d_images, d_bias, sums, total = refs
    first = pl.program_id(0) == 0
    last = pl.program_id(0) == pl.num_programs(0) - 1
    ids, live = ids[...], live[...]
    gate = live * pick(ids, table[0])
    attn = mine[...].astype(F32) + theirs[...].astype(F32) + out_bias[...].astype(F32)
    xhat, rstd = norm(tokens[...].astype(F32) + gate * attn)
    d_norm = d_own[...].astype(F32) + d_other[...].astype(F32)
    grad = cotangent[...].astype(F32) + norm_back(d_norm * (1.0 + pick(ids, table[2])), xhat, rstd)
    d_middle[...] = grad
    d_attn = (gate * grad).astype(BF16)
    d_context[...] = matmul(d_attn, weight[...], ((1,), (1,))).astype(BF16)
    part = matmul(context[...], d_attn, ((0,), (0,)))
    total[...] = jnp.where(first, 0.0, total[...]) + part
    column = jnp.sum(d_attn.astype(F32), axis=0, keepdims=True)
    d_bias[...] = jnp.where(first, 0.0, d_bias[...]) + column
    gather_images(ids_row[...], (live * grad * attn, d_norm, d_norm * xhat), sums, first)

    @pl.when(last)
    def _():
        d_weight[...] = total[...].astype(BF16)
        halves_out(sums, d_images, halves)


def middle_back(
    halves, tokens, mine, theirs, cotangent, d_own, d_other, context, ids, live, ids_row, table, out_bias, weight
):
    count, width = tokens.shape
    size = context.shape[1]
    images = table.shape[1]
    row, col = tiled(TILE, width), tiled(TILE, 1)
    consts = (table, out_bias, weight)
    return token_call(
        lambda *refs: middle_kernel(halves, *refs),
        count,
        "middle_back",
        [
            shaped((count, width), F32),
            shaped((count, size)),
            shaped((size, width)),
            shaped((halves, 3, images, width // halves)),
            shaped((1, width), F32),
        ],
        [row] * 6
        + [tiled(TILE, size), col, col, pl.BlockSpec((1, TILE), lambda i: (0, i))]
        + [whole(x.shape) for x in consts],
        [
            row,
            tiled(TILE, size),
            whole((size, width)),
            whole((halves, 3, images, width // halves)),
            whole((1, width)),
        ],
        [pltpu.VMEM((3, images, width), F32), pltpu.VMEM((size, width), F32)],
        4 * count * width * size,
        (tokens, mine, theirs, cotangent, d_own, d_other, context, ids, live, ids_row) + consts,
    )


def project_back_kernel(
    halves, split, tokens, norm_one, d_q, d_own, rims, tail_start, ids_row, weight, *refs
):
    d_norm, top, bottom, d_images, d_bias, sums, total = refs
    tile = pl.program_id(0)
    first = tile == 0
    last = tile == pl.num_programs(0) - 1
    span, size = rims.shape[2], d_q.shape[1]
    rows = lax.broadcasted_iota(jnp.int32, (TILE, span), 0) + tile * TILE
    cols = lax.broadcasted_iota(jnp.int32, (TILE, span), 1)
    head_rim = (rows == cols).astype(BF16)
    tail_rim = (rows == cols + tail_start[0]).astype(BF16)
    parts = [d_q[...]]
    for which in range(2):
        rim = matmul(head_rim, rims[0, which]) + matmul(tail_rim, rims[1, which])
        parts.append((d_own[which].astype(F32) + rim).astype(BF16))
    normed = norm_one[...]
    back = 0.0
    for i, part in enumerate(parts):
        span_rows = slice(i * size, (i + 1) * size)
        back += matmul(part, weight[span_rows])
        grown = matmul(part, normed, ((0,), (0,)))
        total[span_rows] = jnp.where(first, 0.0, total[span_rows]) + grown
    back = back.astype(BF16)
    d_norm[...] = back
    for i, part in ((0, parts[0]), (1, parts[2])):
        column = jnp.sum(part.astype(F32), axis=0, keepdims=True)
        d_bias[i : i + 1] = jnp.where(first, 0.0, d_bias[i : i + 1]) + column
    xhat, _ = norm(tokens[...].astype(F32))
    back = back.astype(F32)
    gather_images(ids_row[...], (back, back * xhat), sums, first)

    @pl.when(last)
    def _():
        top[...] = total[:split].astype(BF16)
        bottom[...] = total[split:].astype(BF16)
        halves_out(sums, d_images, halves)


def project_back(
    halves, split, images, tokens, norm_one, d_q, d_own, rims, tail_start, ids_row, weight
):
    count, width = tokens.shape
    size = d_q.shape[1]
    row = tiled(TILE, width)
    rest = 3 * size - split
    return token_call(
        lambda *refs: project_back_kernel(halves, split, *refs),
        count,
        "project_back",
        [
            shaped((count, width)),
            shaped((split, width)),
            shaped((rest, width)),
            shaped((halves, 2, images, width // halves)),
            shaped((2, size), F32),
        ],
        [
            row,
            row,
            tiled(TILE, size),
            pl.BlockSpec((2, TILE, size), lambda i: (0, i, 0)),
            whole(rims.shape),
            pl.BlockSpec(memory_space=pltpu.SMEM),
            pl.BlockSpec((1, TILE), lambda i: (0, i)),
            whole(weight.shape),
        ],
        [
            row,
            whole((split, width)),
            whole((rest, width)),
            whole((halves, 2, images, width // halves)),
            whole((2, size)),
        ],
        [pltpu.VMEM((2, images, width), F32), pltpu.VMEM((3 * size, width), F32)],
        12 * count * width * size,
        (tokens, norm_one, d_q, d_own, rims, tail_start, ids_row, weight),
    )


def body(
    tokens,
    condition,
    cotangent,
    modulator,
    modulator_bias,
    qkv_weight,
    qv_bias,
    out_weight,
    out_bias,
    up_weight,
    up_bias,
    down_weight,
    down_bias,
    segment_ids,
    valid_counts,
):
    wide_count = lax.axis_size("wide")
    narrow_count = lax.axis_size("narrow")
    wide_index = lax.axis_index("wide")
    narrow_index = lax.axis_index("narrow")
    tok_dev, width = cotangent.shape
    share = tokens.shape[0]
    part_width = qkv_weight.shape[2]
    mod_width = modulator.shape[2]
    img_row = condition.shape[0]
    span = IMG_MAX
    own_count = valid_counts[wide_index]
    positions = jnp.arange(tok_dev, dtype=jnp.int32)
    own_ids = lax.dynamic_slice_in_dim(segment_ids, wide_index * tok_dev, tok_dev)
    live = (positions < own_count).astype(F32)[:, None]
    share_start = narrow_index * share
    ids_col, ids_row = own_ids[:, None], own_ids[None]
    onehot_full = (ids_col == jnp.arange(img_row, dtype=jnp.int32)[None]).astype(BF16)

    def own(rows):
        return lax.dynamic_slice_in_dim(rows, share_start, share)

    cond_rows = condition.astype(F32)
    sigmoid_rows = jax.nn.sigmoid(cond_rows)
    activated = (cond_rows * sigmoid_rows).astype(BF16)
    tok_full = narrow_gather(tokens)
    mod_rows = jnp.transpose(modulator, (1, 2, 0)).reshape(6 * mod_width, width)

    def vectors(lo, hi, after=None):
        part = dot(activated, mod_rows[lo * mod_width : hi * mod_width], ((1,), (1,)))
        part = part + modulator_bias[lo:hi].astype(F32).reshape(1, -1)
        rows = jnp.moveaxis(part.astype(BF16).reshape(img_row, hi - lo, -1), 2, 0)
        if after is not None:
            rows, after = lax.optimization_barrier((rows, after))
        return jnp.transpose(narrow_gather(rows), (2, 1, 0)), after

    table_one, _ = vectors(0, 2)
    table_two, tok_full = vectors(2, 6, tok_full)
    flat_qkv = jnp.transpose(qkv_weight, (1, 2, 0)).reshape(3 * part_width, width)
    queries, key_rows, value_rows, norm_one = project(
        tok_full, ids_col, table_one, flat_qkv, qv_bias
    )
    tail_start = own_count - span

    def tail_of(rows):
        return lax.dynamic_slice_in_dim(rows, tail_start, span)

    def to_right(rows):
        return lax.ppermute(rows, "wide", [(i, i + 1) for i in range(wide_count - 1)])

    def to_left(rows):
        return lax.ppermute(rows, "wide", [(i + 1, i) for i in range(wide_count - 1)])

    from_left = to_right(jnp.stack([tail_of(key_rows), tail_of(value_rows)]))
    from_right = to_left(jnp.stack([key_rows[:span], value_rows[:span]]))
    left_index = jnp.maximum(wide_index - 1, 0)
    right_index = jnp.minimum(wide_index + 1, wide_count - 1)
    left_count = valid_counts[left_index]
    left_ids = lax.dynamic_slice_in_dim(segment_ids, left_index * tok_dev + left_count - span, span)
    left_ids = jnp.where(wide_index > 0, left_ids, -2)
    right_ids = lax.dynamic_slice_in_dim(segment_ids, right_index * tok_dev, span)
    right_ids = jnp.where(wide_index < wide_count - 1, right_ids, -2)
    own_keys = jnp.where(positions < own_count, own_ids, -1)
    extended_ids = jnp.concatenate([left_ids, own_keys, right_ids])
    context, log_sums = attention_forward(
        queries, key_rows, value_rows, from_left, from_right, own_keys[:, None], extended_ids[None]
    )
    block = min(512, tok_dev)
    blocks = tok_dev // block

    def rows_of(rows, block_idx):
        return rows[block_idx * block : (block_idx + 1) * block]

    out_row = out_bias[None]
    attn_parts, attn_others, mlp_outs, d_others = [], [], [], []
    for i in range(blocks):
        attn_parts.append(dot(rows_of(context, i), out_weight, ((1,), (0,)), BF16))
        attn_others.append(narrow_other(attn_parts[i]))
    for i in range(blocks):
        operands = [rows_of(rows, i) for rows in (tok_full, cotangent, ids_col, live)]
        mlp_outs.append(
            mlp(
                operands[0],
                attn_parts[i],
                attn_others[i],
                *operands[1:],
                table_two,
                out_row,
                up_weight,
                up_bias[None],
                down_weight,
            )
        )
        d_others.append(narrow_other(mlp_outs[i][4]))
    norm_two, hidden, d_upper, d_branch, d_norm, branch_part = [
        jnp.concatenate(parts, axis=0) for parts in zip(*mlp_outs)
    ]
    up_grad = dot(d_upper, norm_two, ((0,), (0,)), BF16)
    down_grad = dot(hidden, d_branch, ((0,), (0,)), BF16)
    up_grad, down_grad = lax.psum((up_grad, down_grad), "wide")
    attn_part, attn_other, d_other = [
        jnp.concatenate(parts, axis=0) for parts in (attn_parts, attn_others, d_others)
    ]
    branch = narrow_scatter(branch_part) + down_bias.astype(F32)

    def image_sum(hot, term):
        return dot(hot, term.astype(BF16), ((0,), (0,)))

    first_bias = jnp.where(narrow_index == 0, down_bias.astype(F32), 0.0)
    d_gate_two = image_sum(
        onehot_full, live * cotangent.astype(F32) * (branch_part.astype(F32) + first_bias)
    )
    d_gate_two = narrow_scatter(d_gate_two.astype(BF16), 1)
    d_middle, d_context, out_weight_grad, images_two, out_bias_sum = middle_back(
        narrow_count,
        tok_full,
        attn_part,
        attn_other,
        cotangent,
        d_norm,
        d_other,
        context,
        ids_col,
        live,
        ids_row,
        table_two,
        out_row,
        out_weight,
    )
    d_queries, d_own, d_rim = attention_backward(
        queries,
        key_rows,
        value_rows,
        from_left,
        from_right,
        d_context,
        log_sums,
        own_keys[None],
        extended_ids[:, None],
    )
    rims = jnp.stack([to_right(d_rim[1]), to_left(d_rim[0])])
    lane_rows = (4 * part_width * width + 6 * img_row * mod_width) // (2 * width)
    split = min(lane_rows, 3 * part_width - 16)
    d_norm_part, top, bottom, images_one, qv_sums = project_back(
        narrow_count,
        split,
        img_row,
        tok_full,
        norm_one,
        d_queries,
        d_own,
        rims,
        tail_start[None],
        ids_row,
        flat_qkv,
    )

    def mine_of(images):
        return lax.dynamic_index_in_dim(images, narrow_index, 0, keepdims=False)

    if narrow_count == 2:
        theirs = lax.dynamic_index_in_dim(images_one, 1 - narrow_index, 0, keepdims=False)
        early = mine_of(images_one).astype(F32) + swap(theirs).astype(F32)
    else:
        early = mine_of(lax.psum(images_one, "narrow"))
    images_two = mine_of(images_two)
    loose_parts = [
        jnp.sum(d_upper.astype(F32), axis=0),
        jnp.sum(d_branch.astype(F32), axis=0),
        qv_sums[0],
        qv_sums[1],
        out_bias_sum[0],
    ]
    loose = jnp.concatenate(loose_parts)
    loose = jnp.pad(loose, (0, (-loose.shape[0]) % (8 * width))).reshape(-1, width)
    terms = [early[0], early[1], images_two[0], images_two[1], images_two[2], d_gate_two]
    terms = [term.astype(BF16) for term in terms]
    d_mod = [jnp.concatenate(terms[2 * i : 2 * i + 2], axis=1) for i in range(3)]
    if 2 * mod_width == width:
        d_mod_flat = jnp.concatenate(d_mod, axis=0)
    else:
        d_mod_flat = jnp.concatenate(d_mod, axis=1).reshape(-1, width)
    rest = jnp.concatenate([bottom, out_weight_grad, d_mod_flat], axis=0)
    if ring_fits([top]) and top.shape == rest.shape:
        flat, d_norm_other, loose = ring_sum([top, rest], d_norm_part, loose, 0)
        d_norm_one = own(d_norm_part).astype(F32) + d_norm_other.astype(F32)
    else:
        d_norm_one = narrow_scatter(d_norm_part)
        flat = jnp.concatenate(lax.psum((top, rest), "wide"), axis=0)
        loose = lax.psum(loose, "wide")
    tok_own = tokens.astype(F32)
    xhat_one, rstd_one = norm(tok_own)
    hot_own = own(onehot_full)
    scale_one = dot(hot_own, table_one[1], ((1,), (0,)))
    tokens_grad = own(d_middle) + norm_back(d_norm_one * (1.0 + scale_one), xhat_one, rstd_one)
    attn_own = own(attn_part).astype(F32) + own(attn_other).astype(F32) + out_bias.astype(F32)
    live_own = own(live)
    gates = [dot(hot_own, table_two[j], ((1,), (0,))) for j in (0, 3)]
    layer_out = (tok_own + live_own * (gates[0] * attn_own + gates[1] * branch)).astype(BF16)
    up_weight_grad = up_grad.T.astype(F32)
    down_weight_grad = down_grad.astype(F32)
    keep = 3 * part_width
    qkv_flat = flat[:keep].astype(F32)
    qkv_weight_grad = jnp.transpose(qkv_flat.reshape(3, part_width, width), (2, 0, 1))
    out_weight_grad = flat[keep : keep + part_width].astype(F32)
    loose = loose.reshape(-1)
    bounds = [0]
    for part in loose_parts:
        bounds.append(bounds[-1] + part.shape[0])
    up_bias_grad, down_bias_grad, query_bias, value_bias, out_bias_grad = [
        loose[bounds[i] : bounds[i + 1]] for i in range(5)
    ]
    qv_bias_grad = jnp.stack([query_bias, value_bias])
    d_mod_flat = flat[keep + part_width :]
    if 2 * mod_width == width:
        d_mod = d_mod_flat.reshape(3, img_row, width)
    else:
        d_mod = jnp.moveaxis(d_mod_flat.reshape(img_row, 3, -1), 1, 0)
    modulator_grad = lax.dot_general(
        d_mod, activated, (((1,), (0,)), ((), ())), preferred_element_type=F32
    )
    modulator_grad = jnp.transpose(modulator_grad.reshape(6, mod_width, width), (2, 0, 1))
    modulator_bias_grad = jnp.sum(d_mod.astype(F32), axis=1).reshape(6, mod_width)
    mod_blocks = mod_rows.reshape(3, 2 * mod_width, width)
    d_activated = sum(dot(d_mod[i], mod_blocks[i], ((1,), (0,))) for i in range(3))
    cond_part = d_activated * sigmoid_rows * (1.0 + cond_rows * (1.0 - sigmoid_rows))
    cond_part = cond_part.astype(BF16)
    condition_grad = cond_part.astype(F32) + narrow_other(cond_part).astype(F32)
    return (
        layer_out,
        tokens_grad,
        condition_grad,
        modulator_grad,
        modulator_bias_grad,
        qkv_weight_grad,
        qv_bias_grad,
        out_weight_grad,
        out_bias_grad,
        up_weight_grad,
        up_bias_grad,
        down_weight_grad,
        down_bias_grad,
    )


def solution(mesh):
    in_specs = (
        P(("wide", "narrow"), None),
        P(),
        P("wide", None),
        P(None, None, "narrow"),
        P(None, "narrow"),
        P(None, None, "narrow"),
        P(None, "narrow"),
        P("narrow", None),
        P(),
        P(None, "narrow"),
        P("narrow"),
        P("narrow", None),
        P(),
        P(),
        P(),
    )
    out_specs = (
        P(("wide", "narrow"), None),
        P(("wide", "narrow"), None),
        P(),
        P(None, None, "narrow"),
        P(None, "narrow"),
        P(None, None, "narrow"),
        P(None, "narrow"),
        P("narrow", None),
        P(),
        P(None, "narrow"),
        P("narrow"),
        P("narrow", None),
        P(),
    )
    return jax.shard_map(body, mesh=mesh, in_specs=in_specs, out_specs=out_specs, check_vma=False)
```

```python
import jax
import jax.numpy as jnp
from jax import lax
from jax.experimental import pallas as pl
from jax.experimental.pallas import tpu as pltpu
from jax.sharding import PartitionSpec as P

HD = 72
IMG_MAX = 128
EPSILON = 1e-06
NEG_FILL = -1e30
F32 = jnp.float32
BF16 = jnp.bfloat16


def dot(left, right, dims, out=F32):
    return lax.dot_general(left, right, (dims, ((), ())), preferred_element_type=F32).astype(out)


def swap(part):
    return lax.ppermute(part, "narrow", [(0, 1), (1, 0)])


def narrow_gather(part):
    if lax.axis_size("narrow") != 2:
        return lax.all_gather(part, "narrow", axis=0, tiled=True)
    other = swap(part)
    first = lax.axis_index("narrow") == 0
    return jnp.where(
        first, jnp.concatenate([part, other], axis=0), jnp.concatenate([other, part], axis=0)
    )


def narrow_other(part):
    if lax.axis_size("narrow") != 2:
        return (lax.psum(part.astype(F32), "narrow") - part.astype(F32)).astype(BF16)
    return swap(part)


def narrow_scatter(part, dim=0):
    count = lax.axis_size("narrow")
    if count != 2:
        return lax.psum_scatter(part, "narrow", scatter_dimension=dim, tiled=True).astype(F32)
    size = part.shape[dim] // 2
    index = lax.axis_index("narrow")
    mine = lax.dynamic_slice_in_dim(part, index * size, size, axis=dim)
    theirs = lax.dynamic_slice_in_dim(part, (1 - index) * size, size, axis=dim)
    return mine.astype(F32) + swap(theirs).astype(F32)


MESH = pl.DeviceIdType.MESH
UNIT = 48


def ring_kernel(chips, subs, *refs):
    data, part, loose, out, landing, loose_out = refs[:2], *refs[2:7]
    mine, theirs, slots, last, loose_pair, loose_rows = refs[7:13]
    copy_sems, core_sems, ring_sems, swap_sems, gather_sems, pair_sems, own_sems = refs[13:20]
    loose_pair_sems, loose_sems = refs[20:]
    wide = lax.axis_index("wide")
    chip, core = wide // 2, wide % 2
    half = chips // 2

    def place(position):
        position = lax.rem(position + 2 * chips, chips)
        side = position // half
        return (1 - side) * 2 * position + side * (2 * (chips - 1 - position) + 1)

    position = chip // 2 + (chip % 2) * (chips - 1 - 2 * (chip // 2))
    ahead = 2 * place(position + 1) + core
    behind = 2 * place(position - 1) + core
    sibling = 2 * chip + 1 - core
    facing = 1 - lax.axis_index("narrow")
    barrier = pltpu.get_barrier_semaphore()
    for device in (ahead, behind, sibling):
        pl.semaphore_signal(barrier, inc=1, device_id={"wide": device}, device_id_type=MESH)
    pl.semaphore_signal(barrier, inc=1, device_id={"narrow": facing}, device_id_type=MESH)
    pl.semaphore_wait(barrier, 4)
    share = landing.shape[0]
    turn = pltpu.make_async_remote_copy(
        src_ref=part.at[pl.ds(facing * share, share)],
        dst_ref=landing,
        send_sem=swap_sems.at[0],
        recv_sem=swap_sems.at[1],
        device_id={"narrow": facing},
        device_id_type=MESH,
    )
    turn.start()
    loose_swap = pltpu.make_async_remote_copy(
        src_ref=loose,
        dst_ref=loose_pair,
        send_sem=loose_pair_sems.at[0],
        recv_sem=loose_pair_sems.at[1],
        device_id={"wide": sibling},
        device_id_type=MESH,
    )
    loose_swap.start()

    def loose_hop(step, index):
        return pltpu.make_async_remote_copy(
            src_ref=loose_rows.at[index],
            dst_ref=loose_rows.at[index],
            send_sem=loose_sems.at[0, step],
            recv_sem=loose_sems.at[1, step],
            device_id={"wide": ahead},
            device_id_type=MESH,
        )

    def local(lane):
        return pltpu.make_async_copy(data[lane].at[:, core], mine.at[lane], copy_sems.at[lane])

    def across(lane):
        return pltpu.make_async_remote_copy(
            src_ref=data[lane].at[:, 1 - core],
            dst_ref=theirs.at[lane],
            send_sem=core_sems.at[0, lane],
            recv_sem=core_sems.at[1, lane],
            device_id={"wide": sibling},
            device_id_type=MESH,
        )

    for lane in range(2):
        across(lane).start()
        local(lane).start()

    def rows_of(sub):
        return pl.ds(sub * UNIT, UNIT)

    def hop(lane, step, sub):
        rows = rows_of(sub)
        if step == 0:
            first = place(position - 1 if lane == 0 else position + 1)
            source = mine.at[lane, first, rows]
        else:
            source = slots.at[lane, step - 1, rows]
        return pltpu.make_async_remote_copy(
            src_ref=source,
            dst_ref=slots.at[lane, step, rows],
            send_sem=ring_sems.at[0, lane, step, sub],
            recv_sem=ring_sems.at[1, lane, step, sub],
            device_id={"wide": ahead if lane == 0 else behind},
            device_id_type=MESH,
        )

    def held(lane, step, sub, side):
        index = place(position - step if lane == 0 else position + step)
        return out.at[lane, index, side, rows_of(sub)]

    def send_on(lane, step, sub):
        source = last.at[lane, rows_of(sub)] if step == 0 else held(lane, step, sub, core)
        return pltpu.make_async_remote_copy(
            src_ref=source,
            dst_ref=held(lane, step, sub, core),
            send_sem=gather_sems.at[0, lane, step, sub],
            recv_sem=gather_sems.at[1, lane, step, sub],
            device_id={"wide": ahead if lane == 0 else behind},
            device_id_type=MESH,
        )

    def landed(lane, step, sub):
        return pltpu.make_async_remote_copy(
            src_ref=last.at[lane, rows_of(sub)],
            dst_ref=held(lane, step + 1, sub, core),
            send_sem=gather_sems.at[0, lane, step, sub],
            recv_sem=gather_sems.at[1, lane, step, sub],
            device_id={"wide": ahead if lane == 0 else behind},
            device_id_type=MESH,
        )

    def pair(lane, step, sub, side):
        source = last.at[lane, rows_of(sub)] if step == 0 else held(lane, step, sub, core)
        return pltpu.make_async_remote_copy(
            src_ref=source,
            dst_ref=held(lane, step, sub, side),
            send_sem=pair_sems.at[0, lane, step, sub],
            recv_sem=pair_sems.at[1, lane, step, sub],
            device_id={"wide": sibling},
            device_id_type=MESH,
        )

    def keep(lane, sub):
        return pltpu.make_async_copy(
            last.at[lane, rows_of(sub)], held(lane, 0, sub, core), own_sems.at[lane, sub]
        )

    loose_swap.wait()
    loose_rows[chip] = loose[...] + loose_pair[...]
    loose_hop(0, chip).start()
    for lane in range(2):
        local(lane).wait()
        across(lane).wait()

        def merge(index, carry, lane=lane):
            mine[lane, index] = mine[lane, index] + theirs[lane, index]
            return carry

        lax.fori_loop(0, chips, merge, 0)
        for sub in range(subs):
            hop(lane, 0, sub).start()
    for step in range(chips - 1):
        passed = place(position - 1 - step)
        loose_hop(step, passed).wait_recv()
        if step < chips - 2:
            loose_hop(step + 1, passed).start()
        for sub in range(subs):
            for lane in range(2):
                hop(lane, step, sub).wait_recv()
                offset = 2 + step
                index = place(position - offset if lane == 0 else position + offset)
                rows = rows_of(sub)
                total = slots[lane, step, rows] + mine[lane, index, rows]
                if step == chips - 2:
                    last[lane, rows] = total
                    send_on(lane, 0, sub).start()
                    pair(lane, 0, sub, core).start()
                    keep(lane, sub).start()
                else:
                    slots[lane, step, rows] = total
                    hop(lane, step + 1, sub).start()
    for step in range(chips - 1):
        for sub in range(subs):
            for lane in range(2):
                landed(lane, step, sub).wait_recv()
                if step < chips - 2:
                    send_on(lane, step + 1, sub).start()
                pair(lane, step + 1, sub, core).start()
    loose_out[...] = jnp.sum(loose_rows[...], axis=0)
    for step in range(chips):
        if step < chips - 1:
            loose_hop(step, place(position - step)).wait_send()
        for sub in range(subs):
            for lane in range(2):
                pair(lane, step, sub, 1 - core).wait_recv()
                pair(lane, step, sub, core).wait_send()
                if step == 0:
                    keep(lane, sub).wait()
                if step < chips - 1:
                    hop(lane, step, sub).wait_send()
                    send_on(lane, step, sub).wait_send()
    turn.wait()


def ring_sum(lanes, part, loose, collective_id):
    chips = lax.axis_size("wide") // 2
    rows, width = lanes[0].shape
    shard = rows // (2 * chips)
    subs = shard // UNIT
    anywhere = pl.BlockSpec(memory_space=pl.ANY)
    inside = pl.BlockSpec(memory_space=pltpu.VMEM)
    sums, landed, loose_sum = pl.pallas_call(
        lambda *refs: ring_kernel(chips, subs, *refs),
        out_shape=[
            jax.ShapeDtypeStruct((2, chips, 2, shard, width), BF16),
            jax.ShapeDtypeStruct((part.shape[0] // 2, part.shape[1]), BF16),
            jax.ShapeDtypeStruct(loose.shape, F32),
        ],
        in_specs=[anywhere] * 3 + [inside],
        out_specs=[anywhere] * 2 + [inside],
        scratch_shapes=[
            pltpu.VMEM((2, chips, shard, width), BF16),
            pltpu.VMEM((2, chips, shard, width), BF16),
            pltpu.VMEM((2, chips - 1, shard, width), BF16),
            pltpu.VMEM((2, shard, width), BF16),
            pltpu.VMEM(loose.shape, F32),
            pltpu.VMEM((chips,) + loose.shape, F32),
            pltpu.SemaphoreType.DMA((2,)),
            pltpu.SemaphoreType.DMA((2, 2)),
            pltpu.SemaphoreType.DMA((2, 2, chips - 1, subs)),
            pltpu.SemaphoreType.DMA((2,)),
            pltpu.SemaphoreType.DMA((2, 2, chips - 1, subs)),
            pltpu.SemaphoreType.DMA((2, 2, chips, subs)),
            pltpu.SemaphoreType.DMA((2, subs)),
            pltpu.SemaphoreType.DMA((2,)),
            pltpu.SemaphoreType.DMA((2, chips - 1)),
        ],
        compiler_params=pltpu.CompilerParams(
            collective_id=collective_id, has_side_effects=True, vmem_limit_bytes=40 << 20
        ),
        name="ring_sum",
    )(*[lane.reshape(chips, 2, shard, width) for lane in lanes], part, loose)
    return sums.reshape(2 * rows, width), landed, loose_sum


def ring_fits(lanes):
    count = lax.axis_size("wide")
    return lax.axis_size("narrow") == 2 and lanes[0].shape[0] % (count * UNIT) == 0


TILE = 256
LOG2E = 1.4426950408889634


def head_lanes(part_width):
    for head in range(part_width // HD):
        lo = head * HD // 128 * 128
        hi = min(-(-(head + 1) * HD // 128) * 128, part_width)
        lanes = lax.broadcasted_iota(jnp.int32, (1, hi - lo), 1) + lo
        yield head, lo, hi, (lanes >= head * HD) & (lanes < (head + 1) * HD)


def extend(first, left, own, right, ext):
    span = left.shape[1]
    ends = ext.shape[1] - span

    @pl.when(first)
    def _():
        for which in range(2):
            ext[which, :span] = left[which]
            ext[which, span:ends] = own[which][...]
            ext[which, ends:] = right[which]


def forward_kernel(tiles, q, k, v, left, right, q_ids, k_ids, out, lse, ext, total):
    tile = pl.program_id(0)
    part_width = q.shape[1]
    span = left.shape[1]
    ends = ext.shape[1] - span
    extend(tile == 0, left, (k, v), right, ext)
    scale = LOG2E * HD ** (-0.5)

    def run(extra):
        rows = pl.ds(pl.multiple_of(tile * TILE, TILE), TILE + 2 * span)
        keys, values = ext[0, rows], ext[1, rows]
        ids = k_ids[:, rows]
        if extra:
            keys = jnp.concatenate([keys, ext[0, ends:]], axis=0)
            values = jnp.concatenate([values, ext[1, ends:]], axis=0)
            ids = jnp.concatenate([ids, k_ids[:, ends:]], axis=1)
        same = q_ids[...] == ids
        queries = q[...]
        total[...] = jnp.zeros_like(total)
        packed = jnp.zeros((TILE, 128), F32)
        column = lax.broadcasted_iota(jnp.int32, (TILE, 128), 1)
        for head, lo, hi, mask in head_lanes(part_width):
            chosen = jnp.where(mask, queries[:, lo:hi], 0)
            scores = lax.dot_general(
                chosen, keys[:, lo:hi], (((1,), (1,)), ((), ())), preferred_element_type=F32
            )
            scores = jnp.where(same, scores * scale, NEG_FILL)
            top = jnp.max(scores, axis=1, keepdims=True)
            expo = jnp.exp2(scores - top)
            count = jnp.sum(expo, axis=1, keepdims=True)
            part = jnp.dot(expo.astype(BF16), values[:, lo:hi], preferred_element_type=F32)
            total[:, lo:hi] += jnp.where(mask, part / count, 0.0)
            packed = jnp.where(column == head, top + jnp.log2(count), packed)
        out[...] = total[...].astype(BF16)
        lse[...] = packed.T[: lse.shape[0]]

    split_tiles(tile, tiles, run)


def split_tiles(tile, tiles, run):
    first_extra = tiles - 512 // TILE
    extra = (tile >= first_extra) & (tile < tiles - 1)
    pl.when(extra)(lambda: run(True))
    pl.when(jnp.logical_not(extra))(lambda: run(False))


def rim_specs(part_width, span, tok_dev):
    whole = lambda shape: pl.BlockSpec(shape, lambda i: (0,) * len(shape))
    return whole((tok_dev, part_width)), whole((2, span, part_width))


def attention_forward(q, k, v, left, right, q_ids, k_ids):
    tok_dev, part_width = q.shape
    span = left.shape[1]
    tiles = tok_dev // TILE
    head_rows = -(-(part_width // HD) // 8) * 8
    own_spec, rim_spec = rim_specs(part_width, span, tok_dev)
    return pl.pallas_call(
        lambda *refs: forward_kernel(tiles, *refs),
        grid=(tiles,),
        out_shape=[
            jax.ShapeDtypeStruct((tok_dev, part_width), BF16),
            jax.ShapeDtypeStruct((head_rows, tok_dev), F32),
        ],
        in_specs=[
            pl.BlockSpec((TILE, part_width), lambda i: (i, 0)),
            own_spec,
            own_spec,
            rim_spec,
            rim_spec,
            pl.BlockSpec((TILE, 1), lambda i: (i, 0)),
            pl.BlockSpec((1, tok_dev + 2 * span), lambda i: (0, 0)),
        ],
        out_specs=[
            pl.BlockSpec((TILE, part_width), lambda i: (i, 0)),
            pl.BlockSpec((head_rows, TILE), lambda i: (0, i)),
        ],
        scratch_shapes=[
            pltpu.VMEM((2, tok_dev + 2 * span, part_width), BF16),
            pltpu.VMEM((TILE, part_width), F32),
        ],
        compiler_params=pltpu.CompilerParams(vmem_limit_bytes=40 << 20),
        cost_estimate=pl.CostEstimate(
            flops=4 * tok_dev * 512 * part_width,
            transcendentals=tok_dev * 512 * 8,
            bytes_accessed=8 * tok_dev * part_width,
        ),
        name="attention_forward",
    )(q, k, v, left, right, q_ids, k_ids)


def backward_kernel(tiles, q, k, v, left, right, grad, lse, q_ids, k_ids, *refs):
    d_q, d_own, d_rim, ext, d_ext, total = refs
    tile = pl.program_id(0)
    part_width = q.shape[1]
    span = left.shape[1]
    ends = ext.shape[1] - span
    extend(tile == 0, left, (k, v), right, ext)
    scale = HD ** (-0.5)

    @pl.when(tile == 0)
    def _():
        d_ext[...] = jnp.zeros_like(d_ext)

    def run(extra):
        rows = pl.ds(pl.multiple_of(tile * TILE, TILE), TILE + 2 * span)
        keys, values = ext[0, rows], ext[1, rows]
        ids = k_ids[rows]
        if extra:
            keys = jnp.concatenate([keys, ext[0, ends:]], axis=0)
            values = jnp.concatenate([values, ext[1, ends:]], axis=0)
            ids = jnp.concatenate([ids, k_ids[ends:]], axis=0)
        same = ids == q_ids[...]
        queries, grads = q[...], grad[...]
        total[...] = jnp.zeros_like(total)

        def across(left_side, right_side, dims):
            return lax.dot_general(
                left_side, right_side, (dims, ((), ())), preferred_element_type=F32
            )

        for head, lo, hi, mask in head_lanes(part_width):
            chosen = jnp.where(mask, queries[:, lo:hi], 0)
            pulled = jnp.where(mask, grads[:, lo:hi], 0)
            scores = across(keys[:, lo:hi], chosen, ((1,), (1,)))
            scores = jnp.where(same, scores * (scale * LOG2E), NEG_FILL)
            attend = jnp.exp2(scores - lse[head : head + 1])
            d_attend = across(values[:, lo:hi], pulled, ((1,), (1,)))
            centre = jnp.sum(attend * d_attend, axis=0, keepdims=True)
            d_scores = (attend * (d_attend - centre)).astype(BF16)
            d_key = across(d_scores, chosen, ((1,), (0,)))
            d_value = across(attend.astype(BF16), pulled, ((1,), (0,)))
            length = TILE + 2 * span
            d_ext[0, rows, lo:hi] += d_key[:length]
            d_ext[1, rows, lo:hi] += d_value[:length]
            if extra:
                d_ext[0, ends:, lo:hi] += d_key[length:]
                d_ext[1, ends:, lo:hi] += d_value[length:]
            d_query = across(d_scores, keys[:, lo:hi], ((0,), (0,)))
            total[:, lo:hi] += jnp.where(mask, d_query, 0.0)
        d_q[...] = (total[...] * scale).astype(BF16)

    split_tiles(tile, tiles, run)

    @pl.when(tile == tiles - 1)
    def _():
        for which, factor in ((0, scale), (1, 1.0)):
            d_rim[0, which] = (d_ext[which, :span] * factor).astype(BF16)
            d_own[which] = (d_ext[which, span:ends] * factor).astype(BF16)
            d_rim[1, which] = (d_ext[which, ends:] * factor).astype(BF16)


def attention_backward(q, k, v, left, right, grad, lse, q_ids, k_ids):
    tok_dev, part_width = q.shape
    span = left.shape[1]
    tiles = tok_dev // TILE
    own_spec, rim_spec = rim_specs(part_width, span, tok_dev)
    tile_spec = pl.BlockSpec((TILE, part_width), lambda i: (i, 0))
    return pl.pallas_call(
        lambda *refs: backward_kernel(tiles, *refs),
        grid=(tiles,),
        out_shape=[
            jax.ShapeDtypeStruct((tok_dev, part_width), BF16),
            jax.ShapeDtypeStruct((2, tok_dev, part_width), BF16),
            jax.ShapeDtypeStruct((2, 2, span, part_width), BF16),
        ],
        in_specs=[
            tile_spec,
            own_spec,
            own_spec,
            rim_spec,
            rim_spec,
            tile_spec,
            pl.BlockSpec((lse.shape[0], TILE), lambda i: (0, i)),
            pl.BlockSpec((1, TILE), lambda i: (0, i)),
            pl.BlockSpec((tok_dev + 2 * span, 1), lambda i: (0, 0)),
        ],
        out_specs=[
            tile_spec,
            pl.BlockSpec((2, tok_dev, part_width), lambda i: (0, 0, 0)),
            pl.BlockSpec((2, 2, span, part_width), lambda i: (0, 0, 0, 0)),
        ],
        scratch_shapes=[
            pltpu.VMEM((2, tok_dev + 2 * span, part_width), BF16),
            pltpu.VMEM((2, tok_dev + 2 * span, part_width), F32),
            pltpu.VMEM((TILE, part_width), F32),
        ],
        compiler_params=pltpu.CompilerParams(vmem_limit_bytes=48 << 20),
        cost_estimate=pl.CostEstimate(
            flops=tok_dev * part_width, transcendentals=0, bytes_accessed=tok_dev * part_width
        ),
        name="attention_backward",
    )(q, k, v, left, right, grad, lse, q_ids, k_ids)


def norm(field):
    centred = field - jnp.mean(field, axis=-1, keepdims=True)
    rstd = lax.rsqrt(jnp.mean(centred * centred, axis=-1, keepdims=True) + EPSILON)
    return centred * rstd, rstd


def norm_back(grad, xhat, rstd):
    return rstd * (
        grad
        - jnp.mean(grad, axis=-1, keepdims=True)
        - xhat * jnp.mean(grad * xhat, axis=-1, keepdims=True)
    )


def gelu_pair(v):
    c = 0.7978845608028654
    sq = v * v
    t = jnp.tanh(c * v * (1.0 + 0.044715 * sq))
    half = 0.5 * (1.0 + t)
    slope = half + 0.5 * v * (1.0 - t * t) * c * (1.0 + 3 * 0.044715 * sq)
    return v * half, slope


def matmul(left, right, dims=((1,), (0,))):
    return lax.dot_general(left, right, (dims, ((), ())), preferred_element_type=F32)


def pick(ids, table):
    slots = lax.broadcasted_iota(jnp.int32, (ids.shape[0], table.shape[0]), 1)
    return matmul((ids == slots).astype(BF16), table)


def gather_images(ids, terms, sums, fresh):
    slots = lax.broadcasted_iota(jnp.int32, (sums.shape[1], ids.shape[1]), 0)
    hot = (ids == slots).astype(BF16)
    for i, term in enumerate(terms):
        part = matmul(hot, term.astype(BF16))
        sums[i] = jnp.where(fresh, 0.0, sums[i]) + part


def halves_out(sums, out, halves):
    size = sums.shape[2] // halves
    for half in range(halves):
        for i in range(sums.shape[0]):
            out[half, i] = sums[i, :, half * size : (half + 1) * size].astype(BF16)


def whole(shape):
    return pl.BlockSpec(shape, lambda i: (0,) * len(shape))


def tiled(rows, width):
    return pl.BlockSpec((rows, width), lambda i: (i, 0))


def token_call(kernel, tokens, name, out_shape, in_specs, out_specs, scratch, flops, operands):
    size = sum(x.size * x.dtype.itemsize for x in operands)
    return pl.pallas_call(
        kernel,
        grid=(tokens // TILE,),
        out_shape=out_shape,
        in_specs=in_specs,
        out_specs=out_specs,
        scratch_shapes=scratch,
        compiler_params=pltpu.CompilerParams(vmem_limit_bytes=60 << 20),
        cost_estimate=pl.CostEstimate(
            flops=flops, transcendentals=0, bytes_accessed=size if flops else tokens
        ),
        name=name,
    )(*operands)


def shaped(shape, dtype=BF16):
    return jax.ShapeDtypeStruct(shape, dtype)


def project_kernel(tokens, ids, table, weight, bias, q, k, v, norm_one):
    xhat, _ = norm(tokens[...].astype(F32))
    normed = (xhat * (1.0 + pick(ids[...], table[1])) + pick(ids[...], table[0])).astype(BF16)
    norm_one[...] = normed
    size = q.shape[1]
    for i, out in enumerate((q, k, v)):
        rows = matmul(normed, weight[i * size : (i + 1) * size], ((1,), (1,)))
        if i != 1:
            rows = rows + bias[i // 2 : i // 2 + 1].astype(F32)
        out[...] = rows.astype(BF16)


def project(tokens, ids, table, weight, bias):
    count, width = tokens.shape
    size = weight.shape[0] // 3
    return token_call(
        project_kernel,
        count,
        "project",
        [shaped((count, size))] * 3 + [shaped((count, width))],
        [tiled(TILE, width), tiled(TILE, 1), whole(table.shape), whole(weight.shape), whole(bias.shape)],
        [tiled(TILE, size)] * 3 + [tiled(TILE, width)],
        [],
        6 * count * width * size,
        (tokens, ids, table, weight, bias),
    )


def mlp_kernel(
    tokens, mine, theirs, cotangent, ids, live, table, out_bias, up, up_bias, down, *outs
):
    norm_two, hidden, d_upper, d_branch, d_norm, branch = outs
    ids, live = ids[...], live[...]
    attn = mine[...].astype(F32) + theirs[...].astype(F32) + out_bias[...].astype(F32)
    middle = tokens[...].astype(F32) + live * pick(ids, table[0]) * attn
    xhat, _ = norm(middle)
    normed = (xhat * (1.0 + pick(ids, table[2])) + pick(ids, table[1])).astype(BF16)
    norm_two[...] = normed
    pulled = (live * pick(ids, table[3]) * cotangent[...].astype(F32)).astype(BF16)
    d_branch[...] = pulled
    width = up.shape[1]
    step = 384 if width % 384 == 0 else width
    back = ahead = 0.0
    for lo in range(0, width, step):
        cols = slice(lo, lo + step)
        upper = matmul(normed, up[:, cols]) + up_bias[:, cols].astype(F32)
        d_hidden = matmul(pulled, down[cols], ((1,), (1,)))
        value, slope = gelu_pair(upper)
        value = value.astype(BF16)
        d_up = (d_hidden * slope).astype(BF16)
        hidden[:, cols] = value
        d_upper[:, cols] = d_up
        back += matmul(d_up, up[:, cols], ((1,), (1,)))
        ahead += matmul(value, down[cols])
    d_norm[...] = back.astype(BF16)
    branch[...] = ahead.astype(BF16)


def mlp(tokens, mine, theirs, cotangent, ids, live, table, out_bias, up, up_bias, down):
    count, width = tokens.shape
    size = up.shape[1]
    row, col = tiled(TILE, width), tiled(TILE, 1)
    consts = (table, out_bias, up, up_bias, down)
    return token_call(
        mlp_kernel,
        count,
        "mlp",
        [shaped((count, n)) for n in (width, size, size, width, width, width)],
        [row, row, row, row, col, col] + [whole(x.shape) for x in consts],
        [tiled(TILE, n) for n in (width, size, size, width, width, width)],
        [],
        8 * count * width * size,
        (tokens, mine, theirs, cotangent, ids, live) + consts,
    )


def middle_kernel(
    halves, tokens, mine, theirs, cotangent, d_own, d_other, context, ids, live, ids_row, *refs
):
    table, out_bias, weight, d_middle, d_context, d_weight, d_images, d_bias, sums, total = refs
    first = pl.program_id(0) == 0
    last = pl.program_id(0) == pl.num_programs(0) - 1
    ids, live = ids[...], live[...]
    gate = live * pick(ids, table[0])
    attn = mine[...].astype(F32) + theirs[...].astype(F32) + out_bias[...].astype(F32)
    xhat, rstd = norm(tokens[...].astype(F32) + gate * attn)
    d_norm = d_own[...].astype(F32) + d_other[...].astype(F32)
    grad = cotangent[...].astype(F32) + norm_back(d_norm * (1.0 + pick(ids, table[2])), xhat, rstd)
    d_middle[...] = grad
    d_attn = (gate * grad).astype(BF16)
    d_context[...] = matmul(d_attn, weight[...], ((1,), (1,))).astype(BF16)
    part = matmul(context[...], d_attn, ((0,), (0,)))
    total[...] = jnp.where(first, 0.0, total[...]) + part
    column = jnp.sum(d_attn.astype(F32), axis=0, keepdims=True)
    d_bias[...] = jnp.where(first, 0.0, d_bias[...]) + column
    gather_images(ids_row[...], (live * grad * attn, d_norm, d_norm * xhat), sums, first)

    @pl.when(last)
    def _():
        d_weight[...] = total[...].astype(BF16)
        halves_out(sums, d_images, halves)


def middle_back(
    halves, tokens, mine, theirs, cotangent, d_own, d_other, context, ids, live, ids_row, table, out_bias, weight
):
    count, width = tokens.shape
    size = context.shape[1]
    images = table.shape[1]
    row, col = tiled(TILE, width), tiled(TILE, 1)
    consts = (table, out_bias, weight)
    return token_call(
        lambda *refs: middle_kernel(halves, *refs),
        count,
        "middle_back",
        [
            shaped((count, width), F32),
            shaped((count, size)),
            shaped((size, width)),
            shaped((halves, 3, images, width // halves)),
            shaped((1, width), F32),
        ],
        [row] * 6
        + [tiled(TILE, size), col, col, pl.BlockSpec((1, TILE), lambda i: (0, i))]
        + [whole(x.shape) for x in consts],
        [
            row,
            tiled(TILE, size),
            whole((size, width)),
            whole((halves, 3, images, width // halves)),
            whole((1, width)),
        ],
        [pltpu.VMEM((3, images, width), F32), pltpu.VMEM((size, width), F32)],
        0,
        (tokens, mine, theirs, cotangent, d_own, d_other, context, ids, live, ids_row) + consts,
    )


def project_back_kernel(
    halves, split, tokens, norm_one, d_q, d_own, rims, tail_start, ids_row, weight, *refs
):
    d_norm, top, bottom, d_images, d_bias, sums, total = refs
    tile = pl.program_id(0)
    first = tile == 0
    last = tile == pl.num_programs(0) - 1
    span, size = rims.shape[2], d_q.shape[1]
    rows = lax.broadcasted_iota(jnp.int32, (TILE, span), 0) + tile * TILE
    cols = lax.broadcasted_iota(jnp.int32, (TILE, span), 1)
    head_rim = (rows == cols).astype(BF16)
    tail_rim = (rows == cols + tail_start[0]).astype(BF16)
    parts = [d_q[...]]
    for which in range(2):
        rim = matmul(head_rim, rims[0, which]) + matmul(tail_rim, rims[1, which])
        parts.append((d_own[which].astype(F32) + rim).astype(BF16))
    normed = norm_one[...]
    back = 0.0
    for i, part in enumerate(parts):
        span_rows = slice(i * size, (i + 1) * size)
        back += matmul(part, weight[span_rows])
        grown = matmul(part, normed, ((0,), (0,)))
        total[span_rows] = jnp.where(first, 0.0, total[span_rows]) + grown
    back = back.astype(BF16)
    d_norm[...] = back
    for i, part in ((0, parts[0]), (1, parts[2])):
        column = jnp.sum(part.astype(F32), axis=0, keepdims=True)
        d_bias[i : i + 1] = jnp.where(first, 0.0, d_bias[i : i + 1]) + column
    xhat, _ = norm(tokens[...].astype(F32))
    back = back.astype(F32)
    gather_images(ids_row[...], (back, back * xhat), sums, first)

    @pl.when(last)
    def _():
        top[...] = total[:split].astype(BF16)
        bottom[...] = total[split:].astype(BF16)
        halves_out(sums, d_images, halves)


def project_back(
    halves, split, images, tokens, norm_one, d_q, d_own, rims, tail_start, ids_row, weight
):
    count, width = tokens.shape
    size = d_q.shape[1]
    row = tiled(TILE, width)
    rest = 3 * size - split
    return token_call(
        lambda *refs: project_back_kernel(halves, split, *refs),
        count,
        "project_back",
        [
            shaped((count, width)),
            shaped((split, width)),
            shaped((rest, width)),
            shaped((halves, 2, images, width // halves)),
            shaped((2, size), F32),
        ],
        [
            row,
            row,
            tiled(TILE, size),
            pl.BlockSpec((2, TILE, size), lambda i: (0, i, 0)),
            whole(rims.shape),
            pl.BlockSpec(memory_space=pltpu.SMEM),
            pl.BlockSpec((1, TILE), lambda i: (0, i)),
            whole(weight.shape),
        ],
        [
            row,
            whole((split, width)),
            whole((rest, width)),
            whole((halves, 2, images, width // halves)),
            whole((2, size)),
        ],
        [pltpu.VMEM((2, images, width), F32), pltpu.VMEM((3 * size, width), F32)],
        0,
        (tokens, norm_one, d_q, d_own, rims, tail_start, ids_row, weight),
    )


def body(
    tokens,
    condition,
    cotangent,
    modulator,
    modulator_bias,
    qkv_weight,
    qv_bias,
    out_weight,
    out_bias,
    up_weight,
    up_bias,
    down_weight,
    down_bias,
    segment_ids,
    valid_counts,
):
    wide_count = lax.axis_size("wide")
    narrow_count = lax.axis_size("narrow")
    wide_index = lax.axis_index("wide")
    narrow_index = lax.axis_index("narrow")
    tok_dev, width = cotangent.shape
    share = tokens.shape[0]
    part_width = qkv_weight.shape[2]
    mod_width = modulator.shape[2]
    img_row = condition.shape[0]
    span = IMG_MAX
    own_count = valid_counts[wide_index]
    positions = jnp.arange(tok_dev, dtype=jnp.int32)
    own_ids = lax.dynamic_slice_in_dim(segment_ids, wide_index * tok_dev, tok_dev)
    live = (positions < own_count).astype(F32)[:, None]
    share_start = narrow_index * share
    ids_col, ids_row = own_ids[:, None], own_ids[None]
    onehot_full = (ids_col == jnp.arange(img_row, dtype=jnp.int32)[None]).astype(BF16)

    def own(rows):
        return lax.dynamic_slice_in_dim(rows, share_start, share)

    cond_rows = condition.astype(F32)
    sigmoid_rows = jax.nn.sigmoid(cond_rows)
    activated = (cond_rows * sigmoid_rows).astype(BF16)
    tok_full = narrow_gather(tokens)
    mod_rows = jnp.transpose(modulator, (1, 2, 0)).reshape(6 * mod_width, width)

    def vectors(lo, hi, after=None):
        part = dot(activated, mod_rows[lo * mod_width : hi * mod_width], ((1,), (1,)))
        part = part + modulator_bias[lo:hi].astype(F32).reshape(1, -1)
        rows = jnp.moveaxis(part.astype(BF16).reshape(img_row, hi - lo, -1), 2, 0)
        if after is not None:
            rows, after = lax.optimization_barrier((rows, after))
        return jnp.transpose(narrow_gather(rows), (2, 1, 0)), after

    table_one, _ = vectors(0, 2)
    table_two, tok_full = vectors(2, 6, tok_full)
    flat_qkv = jnp.transpose(qkv_weight, (1, 2, 0)).reshape(3 * part_width, width)
    queries, key_rows, value_rows, norm_one = project(
        tok_full, ids_col, table_one, flat_qkv, qv_bias
    )
    tail_start = own_count - span

    def tail_of(rows):
        return lax.dynamic_slice_in_dim(rows, tail_start, span)

    def to_right(rows):
        return lax.ppermute(rows, "wide", [(i, i + 1) for i in range(wide_count - 1)])

    def to_left(rows):
        return lax.ppermute(rows, "wide", [(i + 1, i) for i in range(wide_count - 1)])

    from_left = to_right(jnp.stack([tail_of(key_rows), tail_of(value_rows)]))
    from_right = to_left(jnp.stack([key_rows[:span], value_rows[:span]]))
    left_index = jnp.maximum(wide_index - 1, 0)
    right_index = jnp.minimum(wide_index + 1, wide_count - 1)
    left_count = valid_counts[left_index]
    left_ids = lax.dynamic_slice_in_dim(segment_ids, left_index * tok_dev + left_count - span, span)
    left_ids = jnp.where(wide_index > 0, left_ids, -2)
    right_ids = lax.dynamic_slice_in_dim(segment_ids, right_index * tok_dev, span)
    right_ids = jnp.where(wide_index < wide_count - 1, right_ids, -2)
    own_keys = jnp.where(positions < own_count, own_ids, -1)
    extended_ids = jnp.concatenate([left_ids, own_keys, right_ids])
    context, log_sums = attention_forward(
        queries, key_rows, value_rows, from_left, from_right, own_keys[:, None], extended_ids[None]
    )
    block = min(512, tok_dev)
    blocks = tok_dev // block

    def rows_of(rows, block_idx):
        return rows[block_idx * block : (block_idx + 1) * block]

    out_row = out_bias[None]
    attn_parts, attn_others, mlp_outs, d_others = [], [], [], []
    for i in range(blocks):
        attn_parts.append(dot(rows_of(context, i), out_weight, ((1,), (0,)), BF16))
        attn_others.append(narrow_other(attn_parts[i]))
    for i in range(blocks):
        operands = [rows_of(rows, i) for rows in (tok_full, cotangent, ids_col, live)]
        mlp_outs.append(
            mlp(
                operands[0],
                attn_parts[i],
                attn_others[i],
                *operands[1:],
                table_two,
                out_row,
                up_weight,
                up_bias[None],
                down_weight,
            )
        )
        d_others.append(narrow_other(mlp_outs[i][4]))
    norm_two, hidden, d_upper, d_branch, d_norm, branch_part = [
        jnp.concatenate(parts, axis=0) for parts in zip(*mlp_outs)
    ]
    core = wide_index % 2
    paired = wide_count % 2 == 0 and d_upper.shape[1] % 256 == 0
    if paired:
        half = d_upper.shape[1] // 2
        pairs = [(i, i ^ 1) for i in range(wide_count)]
        cores = [list(range(i, wide_count, 2)) for i in range(2)]

        def grads_of(which):
            cols = [lax.dynamic_slice_in_dim(x, which * half, half, axis=1) for x in (d_upper, hidden)]
            return dot(norm_two, cols[0], ((0,), (0,)), BF16), dot(cols[1], d_branch, ((0,), (0,)), BF16)

        got = [lax.ppermute(part, "wide", pairs) for part in grads_of(1 - core)]
        sums = [
            (part.astype(F32) + other.astype(F32)).astype(BF16)
            for part, other in zip(grads_of(core), got)
        ]
        sums, d_others = lax.optimization_barrier((sums, d_others))
        mlp_grads = lax.psum(sums, "wide", axis_index_groups=cores)
    else:
        mlp_grads = lax.psum(
            (
                dot(norm_two, d_upper, ((0,), (0,)), BF16),
                dot(hidden, d_branch, ((0,), (0,)), BF16),
            ),
            "wide",
        )
    attn_part, attn_other, d_other = [
        jnp.concatenate(parts, axis=0) for parts in (attn_parts, attn_others, d_others)
    ]
    branch = narrow_scatter(branch_part) + down_bias.astype(F32)

    def image_sum(hot, term):
        return dot(hot, term.astype(BF16), ((0,), (0,)))

    first_bias = jnp.where(narrow_index == 0, down_bias.astype(F32), 0.0)
    d_gate_two = image_sum(
        onehot_full, live * cotangent.astype(F32) * (branch_part.astype(F32) + first_bias)
    )
    d_gate_two = narrow_scatter(d_gate_two.astype(BF16), 1)
    d_middle, d_context, out_weight_grad, images_two, out_bias_sum = middle_back(
        narrow_count,
        tok_full,
        attn_part,
        attn_other,
        cotangent,
        d_norm,
        d_other,
        context,
        ids_col,
        live,
        ids_row,
        table_two,
        out_row,
        out_weight,
    )
    d_queries, d_own, d_rim = attention_backward(
        queries,
        key_rows,
        value_rows,
        from_left,
        from_right,
        d_context,
        log_sums,
        own_keys[None],
        extended_ids[:, None],
    )
    rims = jnp.stack([to_right(d_rim[1]), to_left(d_rim[0])])
    lane_rows = (4 * part_width * width + 6 * img_row * mod_width) // (2 * width)
    split = min(lane_rows, 3 * part_width - 16)
    d_norm_part, top, bottom, images_one, qv_sums = project_back(
        narrow_count,
        split,
        img_row,
        tok_full,
        norm_one,
        d_queries,
        d_own,
        rims,
        tail_start[None],
        ids_row,
        flat_qkv,
    )

    def mine_of(images):
        return lax.dynamic_index_in_dim(images, narrow_index, 0, keepdims=False)

    if narrow_count == 2:
        theirs = lax.dynamic_index_in_dim(images_one, 1 - narrow_index, 0, keepdims=False)
        early = mine_of(images_one).astype(F32) + swap(theirs).astype(F32)
    else:
        early = mine_of(lax.psum(images_one, "narrow"))
    images_two = mine_of(images_two)
    loose_parts = [
        jnp.sum(d_upper.astype(F32), axis=0),
        jnp.sum(d_branch.astype(F32), axis=0),
        qv_sums[0],
        qv_sums[1],
        out_bias_sum[0],
    ]
    loose = jnp.concatenate(loose_parts)
    loose = jnp.pad(loose, (0, (-loose.shape[0]) % (8 * width))).reshape(-1, width)
    terms = [early[0], early[1], images_two[0], images_two[1], images_two[2], d_gate_two]
    terms = [term.astype(BF16) for term in terms]
    d_mod = [jnp.concatenate(terms[2 * i : 2 * i + 2], axis=1) for i in range(3)]
    if 2 * mod_width == width:
        d_mod_flat = jnp.concatenate(d_mod, axis=0)
    else:
        d_mod_flat = jnp.concatenate(d_mod, axis=1).reshape(-1, width)
    rest = jnp.concatenate([bottom, out_weight_grad, d_mod_flat], axis=0)
    if ring_fits([top]) and top.shape == rest.shape:
        mlp_grads, rest = lax.optimization_barrier((mlp_grads, rest))
        flat, d_norm_other, loose = ring_sum([top, rest], d_norm_part, loose, 0)
        d_norm_one = own(d_norm_part).astype(F32) + d_norm_other.astype(F32)
    else:
        d_norm_one = narrow_scatter(d_norm_part)
        flat = jnp.concatenate(lax.psum((top, rest), "wide"), axis=0)
        loose = lax.psum(loose, "wide")
    tok_own = tokens.astype(F32)
    xhat_one, rstd_one = norm(tok_own)
    hot_own = own(onehot_full)
    scale_one = dot(hot_own, table_one[1], ((1,), (0,)))
    tokens_grad = own(d_middle) + norm_back(d_norm_one * (1.0 + scale_one), xhat_one, rstd_one)
    attn_own = own(attn_part).astype(F32) + own(attn_other).astype(F32) + out_bias.astype(F32)
    live_own = own(live)
    gates = [dot(hot_own, table_two[j], ((1,), (0,))) for j in (0, 3)]
    layer_out = (tok_own + live_own * (gates[0] * attn_own + gates[1] * branch)).astype(BF16)
    if paired:
        others = [lax.ppermute(part, "wide", pairs) for part in mlp_grads]
        mlp_grads = [
            jnp.where(
                core == 0,
                jnp.concatenate([part, other], axis=axis),
                jnp.concatenate([other, part], axis=axis),
            )
            for axis, part, other in zip((1, 0), mlp_grads, others)
        ]
    up_weight_grad, down_weight_grad = [part.astype(F32) for part in mlp_grads]
    keep = 3 * part_width
    qkv_flat = flat[:keep].astype(F32)
    qkv_weight_grad = jnp.transpose(qkv_flat.reshape(3, part_width, width), (2, 0, 1))
    out_weight_grad = flat[keep : keep + part_width].astype(F32)
    loose = loose.reshape(-1)
    bounds = [0]
    for part in loose_parts:
        bounds.append(bounds[-1] + part.shape[0])
    up_bias_grad, down_bias_grad, query_bias, value_bias, out_bias_grad = [
        loose[bounds[i] : bounds[i + 1]] for i in range(5)
    ]
    qv_bias_grad = jnp.stack([query_bias, value_bias])
    d_mod_flat = flat[keep + part_width :]
    if 2 * mod_width == width:
        d_mod = d_mod_flat.reshape(3, img_row, width)
    else:
        d_mod = jnp.moveaxis(d_mod_flat.reshape(img_row, 3, -1), 1, 0)
    modulator_grad = lax.dot_general(
        d_mod, activated, (((1,), (0,)), ((), ())), preferred_element_type=F32
    )
    modulator_grad = jnp.transpose(modulator_grad.reshape(6, mod_width, width), (2, 0, 1))
    modulator_bias_grad = jnp.sum(d_mod.astype(F32), axis=1).reshape(6, mod_width)
    mod_blocks = mod_rows.reshape(3, 2 * mod_width, width)
    d_activated = sum(dot(d_mod[i], mod_blocks[i], ((1,), (0,))) for i in range(3))
    cond_part = d_activated * sigmoid_rows * (1.0 + cond_rows * (1.0 - sigmoid_rows))
    cond_part = cond_part.astype(BF16)
    condition_grad = cond_part.astype(F32) + narrow_other(cond_part).astype(F32)
    return (
        layer_out,
        tokens_grad,
        condition_grad,
        modulator_grad,
        modulator_bias_grad,
        qkv_weight_grad,
        qv_bias_grad,
        out_weight_grad,
        out_bias_grad,
        up_weight_grad,
        up_bias_grad,
        down_weight_grad,
        down_bias_grad,
    )


def solution(mesh):
    in_specs = (
        P(("wide", "narrow"), None),
        P(),
        P("wide", None),
        P(None, None, "narrow"),
        P(None, "narrow"),
        P(None, None, "narrow"),
        P(None, "narrow"),
        P("narrow", None),
        P(),
        P(None, "narrow"),
        P("narrow"),
        P("narrow", None),
        P(),
        P(),
        P(),
    )
    out_specs = (
        P(("wide", "narrow"), None),
        P(("wide", "narrow"), None),
        P(),
        P(None, None, "narrow"),
        P(None, "narrow"),
        P(None, None, "narrow"),
        P(None, "narrow"),
        P("narrow", None),
        P(),
        P(None, "narrow"),
        P("narrow"),
        P("narrow", None),
        P(),
    )
    return jax.shard_map(body, mesh=mesh, in_specs=in_specs, out_specs=out_specs, check_vma=False)
```

```python
import jax
import jax.numpy as jnp
from jax import lax
from jax.experimental import pallas as pl
from jax.experimental.pallas import tpu as pltpu
from jax.sharding import PartitionSpec as P

HD = 72
IMG_MAX = 128
EPSILON = 1e-06
NEG_FILL = -1e30
F32 = jnp.float32
BF16 = jnp.bfloat16


def dot(left, right, dims, out=F32):
    return lax.dot_general(left, right, (dims, ((), ())), preferred_element_type=F32).astype(out)


def swap(part):
    return lax.ppermute(part, "narrow", [(0, 1), (1, 0)])


def narrow_gather(part):
    if lax.axis_size("narrow") != 2:
        return lax.all_gather(part, "narrow", axis=0, tiled=True)
    other = swap(part)
    first = lax.axis_index("narrow") == 0
    return jnp.where(
        first, jnp.concatenate([part, other], axis=0), jnp.concatenate([other, part], axis=0)
    )


def narrow_other(part):
    if lax.axis_size("narrow") != 2:
        return (lax.psum(part.astype(F32), "narrow") - part.astype(F32)).astype(BF16)
    return swap(part)


def narrow_scatter(part, dim=0):
    count = lax.axis_size("narrow")
    if count != 2:
        return lax.psum_scatter(part, "narrow", scatter_dimension=dim, tiled=True).astype(F32)
    size = part.shape[dim] // 2
    index = lax.axis_index("narrow")
    mine = lax.dynamic_slice_in_dim(part, index * size, size, axis=dim)
    theirs = lax.dynamic_slice_in_dim(part, (1 - index) * size, size, axis=dim)
    return mine.astype(F32) + swap(theirs).astype(F32)


MESH = pl.DeviceIdType.MESH
UNIT = 48


def ring_kernel(chips, subs, full, *refs):
    data = refs[:2]
    if full:
        part, loose, out, landing, loose_out, *refs = refs[2:]
        last, loose_pair, loose_rows, *sems = refs[6:]
        swap_sems, gather_sems, pair_sems, own_sems, loose_pair_sems, loose_sems = sems
    else:
        last, *refs = refs[2:]
    mine, theirs, slots, copy_sems, core_sems, ring_sems = refs[:6]
    wide = lax.axis_index("wide")
    chip, core = wide // 2, wide % 2
    half = chips // 2

    def place(position):
        position = lax.rem(position + 2 * chips, chips)
        side = position // half
        return (1 - side) * 2 * position + side * (2 * (chips - 1 - position) + 1)

    position = chip // 2 + (chip % 2) * (chips - 1 - 2 * (chip // 2))
    ahead = 2 * place(position + 1) + core
    behind = 2 * place(position - 1) + core
    sibling = 2 * chip + 1 - core
    barrier = pltpu.get_barrier_semaphore()
    for device in (ahead, behind, sibling):
        pl.semaphore_signal(barrier, inc=1, device_id={"wide": device}, device_id_type=MESH)
    if full:
        facing = 1 - lax.axis_index("narrow")
        pl.semaphore_signal(barrier, inc=1, device_id={"narrow": facing}, device_id_type=MESH)
    pl.semaphore_wait(barrier, 3 + int(full))

    def local(lane):
        return pltpu.make_async_copy(data[lane].at[:, core], mine.at[lane], copy_sems.at[lane])

    def needed(lane, order):
        return place(position - 1 - order if lane == 0 else position + 1 + order)

    def across(lane, order):
        index = needed(lane, order)
        return pltpu.make_async_remote_copy(
            src_ref=data[lane].at[index, 1 - core],
            dst_ref=theirs.at[lane, index],
            send_sem=core_sems.at[0, lane, order],
            recv_sem=core_sems.at[1, lane, order],
            device_id={"wide": sibling},
            device_id_type=MESH,
        )

    for order in range(chips):
        for lane in range(2):
            across(lane, order).start()
            if order == 0:
                local(lane).start()
    if full:
        share = landing.shape[0]
        turn = pltpu.make_async_remote_copy(
            src_ref=part.at[pl.ds(facing * share, share)],
            dst_ref=landing,
            send_sem=swap_sems.at[0],
            recv_sem=swap_sems.at[1],
            device_id={"narrow": facing},
            device_id_type=MESH,
        )
        turn.start()
        loose_swap = pltpu.make_async_remote_copy(
            src_ref=loose,
            dst_ref=loose_pair,
            send_sem=loose_pair_sems.at[0],
            recv_sem=loose_pair_sems.at[1],
            device_id={"wide": sibling},
            device_id_type=MESH,
        )
        loose_swap.start()

    def loose_hop(step, index):
        return pltpu.make_async_remote_copy(
            src_ref=loose_rows.at[index],
            dst_ref=loose_rows.at[index],
            send_sem=loose_sems.at[0, step],
            recv_sem=loose_sems.at[1, step],
            device_id={"wide": ahead},
            device_id_type=MESH,
        )

    def rows_of(sub):
        return pl.ds(sub * UNIT, UNIT)

    def hop(lane, step, sub):
        rows = rows_of(sub)
        if step == 0:
            first = place(position - 1 if lane == 0 else position + 1)
            source = mine.at[lane, first, rows]
        else:
            source = slots.at[lane, step - 1, rows]
        return pltpu.make_async_remote_copy(
            src_ref=source,
            dst_ref=slots.at[lane, step, rows],
            send_sem=ring_sems.at[0, lane, step, sub],
            recv_sem=ring_sems.at[1, lane, step, sub],
            device_id={"wide": ahead if lane == 0 else behind},
            device_id_type=MESH,
        )

    def held(lane, step, sub, side):
        index = place(position - step if lane == 0 else position + step)
        return out.at[lane, index, side, rows_of(sub)]

    def send_on(lane, step, sub):
        source = last.at[lane, rows_of(sub)] if step == 0 else held(lane, step, sub, core)
        return pltpu.make_async_remote_copy(
            src_ref=source,
            dst_ref=held(lane, step, sub, core),
            send_sem=gather_sems.at[0, lane, step, sub],
            recv_sem=gather_sems.at[1, lane, step, sub],
            device_id={"wide": ahead if lane == 0 else behind},
            device_id_type=MESH,
        )

    def landed(lane, step, sub):
        return pltpu.make_async_remote_copy(
            src_ref=last.at[lane, rows_of(sub)],
            dst_ref=held(lane, step + 1, sub, core),
            send_sem=gather_sems.at[0, lane, step, sub],
            recv_sem=gather_sems.at[1, lane, step, sub],
            device_id={"wide": ahead if lane == 0 else behind},
            device_id_type=MESH,
        )

    def pair(lane, step, sub, side):
        source = last.at[lane, rows_of(sub)] if step == 0 else held(lane, step, sub, core)
        return pltpu.make_async_remote_copy(
            src_ref=source,
            dst_ref=held(lane, step, sub, side),
            send_sem=pair_sems.at[0, lane, step, sub],
            recv_sem=pair_sems.at[1, lane, step, sub],
            device_id={"wide": sibling},
            device_id_type=MESH,
        )

    def keep(lane, sub):
        return pltpu.make_async_copy(
            last.at[lane, rows_of(sub)], held(lane, 0, sub, core), own_sems.at[lane, sub]
        )

    def pair_sum(lane, order, rows):
        index = needed(lane, order)
        return mine[lane, index, rows].astype(F32) + theirs[lane, index, rows].astype(F32)

    for lane in range(2):
        local(lane).wait()
        across(lane, 0).wait_recv()
        for sub in range(subs):
            mine[lane, needed(lane, 0), rows_of(sub)] = pair_sum(lane, 0, rows_of(sub)).astype(BF16)
            hop(lane, 0, sub).start()
    if full:
        loose_swap.wait()
        loose_rows[chip] = loose[...] + loose_pair[...]
        loose_hop(0, chip).start()
    for step in range(chips - 1):
        for sub in range(subs):
            for lane in range(2):
                if sub == 0:
                    across(lane, step + 1).wait_recv()
                rows = rows_of(sub)
                extra = pair_sum(lane, step + 1, rows)
                hop(lane, step, sub).wait_recv()
                total = (slots[lane, step, rows].astype(F32) + extra).astype(BF16)
                if step < chips - 2:
                    slots[lane, step, rows] = total
                    hop(lane, step + 1, sub).start()
                else:
                    last[lane, rows] = total
                    if full:
                        send_on(lane, 0, sub).start()
                        pair(lane, 0, sub, core).start()
                        keep(lane, sub).start()
        if full:
            passed = place(position - 1 - step)
            loose_hop(step, passed).wait_recv()
            if step < chips - 2:
                loose_hop(step + 1, passed).start()
    if full:
        for step in range(chips - 1):
            for sub in range(subs):
                for lane in range(2):
                    landed(lane, step, sub).wait_recv()
                    if step < chips - 2:
                        send_on(lane, step + 1, sub).start()
                    pair(lane, step + 1, sub, core).start()
        loose_out[...] = jnp.sum(loose_rows[...], axis=0)
    for step in range(chips):
        if full and step < chips - 1:
            loose_hop(step, place(position - step)).wait_send()
        for lane in range(2):
            across(lane, step).wait_send()
            for sub in range(subs):
                if step < chips - 1:
                    hop(lane, step, sub).wait_send()
                if full:
                    pair(lane, step, sub, 1 - core).wait_recv()
                    pair(lane, step, sub, core).wait_send()
                    if step == 0:
                        keep(lane, sub).wait()
                    if step < chips - 1:
                        send_on(lane, step, sub).wait_send()
    if full:
        turn.wait()


def ring_scratch(chips, shard, width):
    return [
        pltpu.VMEM((2, chips, shard, width), BF16),
        pltpu.VMEM((2, chips, shard, width), BF16),
        pltpu.VMEM((2, chips - 1, shard, width), BF16),
        pltpu.SemaphoreType.DMA((2,)),
        pltpu.SemaphoreType.DMA((2, 2, chips)),
        pltpu.SemaphoreType.DMA((2, 2, chips - 1, shard // UNIT)),
    ]


def ring_scatter(lanes, collective_id):
    chips = lax.axis_size("wide") // 2
    rows, width = lanes[0].shape
    shard = rows // (2 * chips)
    return pl.pallas_call(
        lambda *refs: ring_kernel(chips, shard // UNIT, False, *refs),
        out_shape=jax.ShapeDtypeStruct((2, shard, width), BF16),
        in_specs=[pl.BlockSpec(memory_space=pl.ANY)] * 2,
        out_specs=pl.BlockSpec(memory_space=pltpu.VMEM),
        scratch_shapes=ring_scratch(chips, shard, width),
        compiler_params=pltpu.CompilerParams(
            collective_id=collective_id, has_side_effects=True, vmem_limit_bytes=40 << 20
        ),
        name="ring_scatter",
    )(*[lane.reshape(chips, 2, shard, width) for lane in lanes])


def ring_sum(lanes, part, loose, collective_id):
    chips = lax.axis_size("wide") // 2
    rows, width = lanes[0].shape
    shard = rows // (2 * chips)
    subs = shard // UNIT
    anywhere = pl.BlockSpec(memory_space=pl.ANY)
    inside = pl.BlockSpec(memory_space=pltpu.VMEM)
    sums, landed, loose_sum = pl.pallas_call(
        lambda *refs: ring_kernel(chips, subs, True, *refs),
        out_shape=[
            jax.ShapeDtypeStruct((2, chips, 2, shard, width), BF16),
            jax.ShapeDtypeStruct((part.shape[0] // 2, part.shape[1]), BF16),
            jax.ShapeDtypeStruct(loose.shape, F32),
        ],
        in_specs=[anywhere] * 3 + [inside],
        out_specs=[anywhere] * 2 + [inside],
        scratch_shapes=ring_scratch(chips, shard, width)
        + [
            pltpu.VMEM((2, shard, width), BF16),
            pltpu.VMEM(loose.shape, F32),
            pltpu.VMEM((chips,) + loose.shape, F32),
            pltpu.SemaphoreType.DMA((2,)),
            pltpu.SemaphoreType.DMA((2, 2, chips - 1, subs)),
            pltpu.SemaphoreType.DMA((2, 2, chips, subs)),
            pltpu.SemaphoreType.DMA((2, subs)),
            pltpu.SemaphoreType.DMA((2,)),
            pltpu.SemaphoreType.DMA((2, chips - 1)),
        ],
        compiler_params=pltpu.CompilerParams(
            collective_id=collective_id, has_side_effects=True, vmem_limit_bytes=40 << 20
        ),
        name="ring_sum",
    )(*[lane.reshape(chips, 2, shard, width) for lane in lanes], part, loose)
    return sums.reshape(2 * rows, width), landed, loose_sum


def ring_fits(lanes):
    count = lax.axis_size("wide")
    return lax.axis_size("narrow") == 2 and lanes[0].shape[0] % (count * UNIT) == 0


TILE = 256
LOG2E = 1.4426950408889634


def head_lanes(part_width):
    for head in range(part_width // HD):
        lo = head * HD // 128 * 128
        hi = min(-(-(head + 1) * HD // 128) * 128, part_width)
        lanes = lax.broadcasted_iota(jnp.int32, (1, hi - lo), 1) + lo
        yield head, lo, hi, (lanes >= head * HD) & (lanes < (head + 1) * HD)


def extend(first, left, own, right, ext):
    span = left.shape[1]
    ends = ext.shape[1] - span

    @pl.when(first)
    def _():
        for which in range(2):
            ext[which, :span] = left[which]
            ext[which, span:ends] = own[which][...]
            ext[which, ends:] = right[which]


def forward_kernel(tiles, q, k, v, left, right, q_ids, k_ids, out, lse, ext, total):
    tile = pl.program_id(0)
    part_width = q.shape[1]
    span = left.shape[1]
    ends = ext.shape[1] - span
    extend(tile == 0, left, (k, v), right, ext)
    scale = LOG2E * HD ** (-0.5)

    def run(extra):
        rows = pl.ds(pl.multiple_of(tile * TILE, TILE), TILE + 2 * span)
        keys, values = ext[0, rows], ext[1, rows]
        ids = k_ids[:, rows]
        if extra:
            keys = jnp.concatenate([keys, ext[0, ends:]], axis=0)
            values = jnp.concatenate([values, ext[1, ends:]], axis=0)
            ids = jnp.concatenate([ids, k_ids[:, ends:]], axis=1)
        same = q_ids[...] == ids
        queries = q[...]
        total[...] = jnp.zeros_like(total)
        packed = jnp.zeros((TILE, 128), F32)
        column = lax.broadcasted_iota(jnp.int32, (TILE, 128), 1)
        for head, lo, hi, mask in head_lanes(part_width):
            chosen = jnp.where(mask, queries[:, lo:hi], 0)
            scores = lax.dot_general(
                chosen, keys[:, lo:hi], (((1,), (1,)), ((), ())), preferred_element_type=F32
            )
            scores = jnp.where(same, scores * scale, NEG_FILL)
            top = jnp.max(scores, axis=1, keepdims=True)
            expo = jnp.exp2(scores - top)
            count = jnp.sum(expo, axis=1, keepdims=True)
            part = jnp.dot(expo.astype(BF16), values[:, lo:hi], preferred_element_type=F32)
            total[:, lo:hi] += jnp.where(mask, part / count, 0.0)
            packed = jnp.where(column == head, top + jnp.log2(count), packed)
        out[...] = total[...].astype(BF16)
        lse[...] = packed.T[: lse.shape[0]]

    split_tiles(tile, tiles, run)


def split_tiles(tile, tiles, run):
    first_extra = tiles - 512 // TILE
    extra = (tile >= first_extra) & (tile < tiles - 1)
    pl.when(extra)(lambda: run(True))
    pl.when(jnp.logical_not(extra))(lambda: run(False))


def rim_specs(part_width, span, tok_dev):
    whole = lambda shape: pl.BlockSpec(shape, lambda i: (0,) * len(shape))
    return whole((tok_dev, part_width)), whole((2, span, part_width))


def attention_forward(q, k, v, left, right, q_ids, k_ids):
    tok_dev, part_width = q.shape
    span = left.shape[1]
    tiles = tok_dev // TILE
    head_rows = -(-(part_width // HD) // 8) * 8
    own_spec, rim_spec = rim_specs(part_width, span, tok_dev)
    return pl.pallas_call(
        lambda *refs: forward_kernel(tiles, *refs),
        grid=(tiles,),
        out_shape=[
            jax.ShapeDtypeStruct((tok_dev, part_width), BF16),
            jax.ShapeDtypeStruct((head_rows, tok_dev), F32),
        ],
        in_specs=[
            pl.BlockSpec((TILE, part_width), lambda i: (i, 0)),
            own_spec,
            own_spec,
            rim_spec,
            rim_spec,
            pl.BlockSpec((TILE, 1), lambda i: (i, 0)),
            pl.BlockSpec((1, tok_dev + 2 * span), lambda i: (0, 0)),
        ],
        out_specs=[
            pl.BlockSpec((TILE, part_width), lambda i: (i, 0)),
            pl.BlockSpec((head_rows, TILE), lambda i: (0, i)),
        ],
        scratch_shapes=[
            pltpu.VMEM((2, tok_dev + 2 * span, part_width), BF16),
            pltpu.VMEM((TILE, part_width), F32),
        ],
        compiler_params=pltpu.CompilerParams(vmem_limit_bytes=40 << 20),
        cost_estimate=pl.CostEstimate(
            flops=4 * tok_dev * 512 * part_width,
            transcendentals=tok_dev * 512 * 8,
            bytes_accessed=8 * tok_dev * part_width,
        ),
        name="attention_forward",
    )(q, k, v, left, right, q_ids, k_ids)


def backward_kernel(tiles, q, k, v, left, right, grad, lse, q_ids, k_ids, *refs):
    d_q, d_own, d_rim, ext, d_ext, total = refs
    tile = pl.program_id(0)
    part_width = q.shape[1]
    span = left.shape[1]
    ends = ext.shape[1] - span
    extend(tile == 0, left, (k, v), right, ext)
    scale = HD ** (-0.5)

    @pl.when(tile == 0)
    def _():
        d_ext[...] = jnp.zeros_like(d_ext)

    def run(extra):
        rows = pl.ds(pl.multiple_of(tile * TILE, TILE), TILE + 2 * span)
        keys, values = ext[0, rows], ext[1, rows]
        ids = k_ids[rows]
        if extra:
            keys = jnp.concatenate([keys, ext[0, ends:]], axis=0)
            values = jnp.concatenate([values, ext[1, ends:]], axis=0)
            ids = jnp.concatenate([ids, k_ids[ends:]], axis=0)
        same = ids == q_ids[...]
        queries, grads = q[...], grad[...]
        total[...] = jnp.zeros_like(total)

        def across(left_side, right_side, dims):
            return lax.dot_general(
                left_side, right_side, (dims, ((), ())), preferred_element_type=F32
            )

        for head, lo, hi, mask in head_lanes(part_width):
            chosen = jnp.where(mask, queries[:, lo:hi], 0)
            pulled = jnp.where(mask, grads[:, lo:hi], 0)
            scores = across(keys[:, lo:hi], chosen, ((1,), (1,)))
            scores = jnp.where(same, scores * (scale * LOG2E), NEG_FILL)
            attend = jnp.exp2(scores - lse[head : head + 1])
            d_attend = across(values[:, lo:hi], pulled, ((1,), (1,)))
            centre = jnp.sum(attend * d_attend, axis=0, keepdims=True)
            d_scores = (attend * (d_attend - centre)).astype(BF16)
            d_key = across(d_scores, chosen, ((1,), (0,)))
            d_value = across(attend.astype(BF16), pulled, ((1,), (0,)))
            length = TILE + 2 * span
            d_ext[0, rows, lo:hi] += d_key[:length]
            d_ext[1, rows, lo:hi] += d_value[:length]
            if extra:
                d_ext[0, ends:, lo:hi] += d_key[length:]
                d_ext[1, ends:, lo:hi] += d_value[length:]
            d_query = across(d_scores, keys[:, lo:hi], ((0,), (0,)))
            total[:, lo:hi] += jnp.where(mask, d_query, 0.0)
        d_q[...] = (total[...] * scale).astype(BF16)

    split_tiles(tile, tiles, run)

    @pl.when(tile == tiles - 1)
    def _():
        for which, factor in ((0, scale), (1, 1.0)):
            d_rim[0, which] = (d_ext[which, :span] * factor).astype(BF16)
            d_own[which] = (d_ext[which, span:ends] * factor).astype(BF16)
            d_rim[1, which] = (d_ext[which, ends:] * factor).astype(BF16)


def attention_backward(q, k, v, left, right, grad, lse, q_ids, k_ids):
    tok_dev, part_width = q.shape
    span = left.shape[1]
    tiles = tok_dev // TILE
    own_spec, rim_spec = rim_specs(part_width, span, tok_dev)
    tile_spec = pl.BlockSpec((TILE, part_width), lambda i: (i, 0))
    return pl.pallas_call(
        lambda *refs: backward_kernel(tiles, *refs),
        grid=(tiles,),
        out_shape=[
            jax.ShapeDtypeStruct((tok_dev, part_width), BF16),
            jax.ShapeDtypeStruct((2, tok_dev, part_width), BF16),
            jax.ShapeDtypeStruct((2, 2, span, part_width), BF16),
        ],
        in_specs=[
            tile_spec,
            own_spec,
            own_spec,
            rim_spec,
            rim_spec,
            tile_spec,
            pl.BlockSpec((lse.shape[0], TILE), lambda i: (0, i)),
            pl.BlockSpec((1, TILE), lambda i: (0, i)),
            pl.BlockSpec((tok_dev + 2 * span, 1), lambda i: (0, 0)),
        ],
        out_specs=[
            tile_spec,
            pl.BlockSpec((2, tok_dev, part_width), lambda i: (0, 0, 0)),
            pl.BlockSpec((2, 2, span, part_width), lambda i: (0, 0, 0, 0)),
        ],
        scratch_shapes=[
            pltpu.VMEM((2, tok_dev + 2 * span, part_width), BF16),
            pltpu.VMEM((2, tok_dev + 2 * span, part_width), F32),
            pltpu.VMEM((TILE, part_width), F32),
        ],
        compiler_params=pltpu.CompilerParams(vmem_limit_bytes=48 << 20),
        cost_estimate=pl.CostEstimate(
            flops=10 * tok_dev * 512 * part_width,
            transcendentals=tok_dev * 512 * 8,
            bytes_accessed=16 * tok_dev * part_width,
        ),
        name="attention_backward",
    )(q, k, v, left, right, grad, lse, q_ids, k_ids)


def norm(field):
    centred = field - jnp.mean(field, axis=-1, keepdims=True)
    rstd = lax.rsqrt(jnp.mean(centred * centred, axis=-1, keepdims=True) + EPSILON)
    return centred * rstd, rstd


def norm_back(grad, xhat, rstd):
    return rstd * (
        grad
        - jnp.mean(grad, axis=-1, keepdims=True)
        - xhat * jnp.mean(grad * xhat, axis=-1, keepdims=True)
    )


def gelu_pair(v):
    c = 0.7978845608028654
    sq = v * v
    t = jnp.tanh(c * v * (1.0 + 0.044715 * sq))
    half = 0.5 * (1.0 + t)
    slope = half + 0.5 * v * (1.0 - t * t) * c * (1.0 + 3 * 0.044715 * sq)
    return v * half, slope


def matmul(left, right, dims=((1,), (0,))):
    return lax.dot_general(left, right, (dims, ((), ())), preferred_element_type=F32)


def pick(ids, table):
    slots = lax.broadcasted_iota(jnp.int32, (ids.shape[0], table.shape[0]), 1)
    return matmul((ids == slots).astype(BF16), table)


def gather_images(ids, terms, sums, fresh):
    slots = lax.broadcasted_iota(jnp.int32, (sums.shape[1], ids.shape[1]), 0)
    hot = (ids == slots).astype(BF16)
    for i, term in enumerate(terms):
        part = matmul(hot, term.astype(BF16))
        sums[i] = jnp.where(fresh, 0.0, sums[i]) + part


def halves_out(sums, out, halves):
    size = sums.shape[2] // halves
    for half in range(halves):
        for i in range(sums.shape[0]):
            out[half, i] = sums[i, :, half * size : (half + 1) * size].astype(BF16)


def whole(shape):
    return pl.BlockSpec(shape, lambda i: (0,) * len(shape))


def tiled(rows, width):
    return pl.BlockSpec((rows, width), lambda i: (i, 0))


def token_call(kernel, tokens, name, out_shape, in_specs, out_specs, scratch, flops, operands):
    size = sum(x.size * x.dtype.itemsize for x in operands)
    return pl.pallas_call(
        kernel,
        grid=(tokens // TILE,),
        out_shape=out_shape,
        in_specs=in_specs,
        out_specs=out_specs,
        scratch_shapes=scratch,
        compiler_params=pltpu.CompilerParams(vmem_limit_bytes=60 << 20),
        cost_estimate=pl.CostEstimate(
            flops=flops, transcendentals=0, bytes_accessed=size + size // 2
        ),
        name=name,
    )(*operands)


def shaped(shape, dtype=BF16):
    return jax.ShapeDtypeStruct(shape, dtype)


def project_kernel(tokens, ids, table, weight, bias, q, k, v, norm_one):
    xhat, _ = norm(tokens[...].astype(F32))
    normed = (xhat * (1.0 + pick(ids[...], table[1])) + pick(ids[...], table[0])).astype(BF16)
    norm_one[...] = normed
    size = q.shape[1]
    for i, out in enumerate((q, k, v)):
        rows = matmul(normed, weight[i * size : (i + 1) * size], ((1,), (1,)))
        if i != 1:
            rows = rows + bias[i // 2 : i // 2 + 1].astype(F32)
        out[...] = rows.astype(BF16)


def project(tokens, ids, table, weight, bias):
    count, width = tokens.shape
    size = weight.shape[0] // 3
    return token_call(
        project_kernel,
        count,
        "project",
        [shaped((count, size))] * 3 + [shaped((count, width))],
        [tiled(TILE, width), tiled(TILE, 1), whole(table.shape), whole(weight.shape), whole(bias.shape)],
        [tiled(TILE, size)] * 3 + [tiled(TILE, width)],
        [],
        6 * count * width * size,
        (tokens, ids, table, weight, bias),
    )


def mlp_kernel(
    tokens, mine, theirs, cotangent, ids, live, table, out_bias, up, up_bias, down, *outs
):
    norm_two, hidden, d_upper, d_branch, d_norm, branch, up_sum, down_sum = outs
    first = pl.program_id(0) == 0
    ids, live = ids[...], live[...]
    attn = mine[...].astype(F32) + theirs[...].astype(F32) + out_bias[...].astype(F32)
    middle = tokens[...].astype(F32) + live * pick(ids, table[0]) * attn
    xhat, _ = norm(middle)
    normed = (xhat * (1.0 + pick(ids, table[2])) + pick(ids, table[1])).astype(BF16)
    norm_two[...] = normed
    pulled = (live * pick(ids, table[3]) * cotangent[...].astype(F32)).astype(BF16)
    d_branch[...] = pulled
    column = jnp.sum(pulled.astype(F32), axis=0, keepdims=True)
    down_sum[...] = jnp.where(first, 0.0, down_sum[...]) + column
    width = up.shape[1]
    step = 384 if width % 384 == 0 else width
    back = ahead = 0.0
    for lo in range(0, width, step):
        cols = slice(lo, lo + step)
        upper = matmul(normed, up[:, cols]) + up_bias[:, cols].astype(F32)
        d_hidden = matmul(pulled, down[cols], ((1,), (1,)))
        value, slope = gelu_pair(upper)
        value = value.astype(BF16)
        d_up = (d_hidden * slope).astype(BF16)
        hidden[:, cols] = value
        d_upper[:, cols] = d_up
        column = jnp.sum(d_up.astype(F32), axis=0, keepdims=True)
        up_sum[:, cols] = jnp.where(first, 0.0, up_sum[:, cols]) + column
        back += matmul(d_up, up[:, cols], ((1,), (1,)))
        ahead += matmul(value, down[cols])
    d_norm[...] = back.astype(BF16)
    branch[...] = ahead.astype(BF16)


def mlp(tokens, mine, theirs, cotangent, ids, live, table, out_bias, up, up_bias, down):
    count, width = tokens.shape
    size = up.shape[1]
    row, col = tiled(TILE, width), tiled(TILE, 1)
    consts = (table, out_bias, up, up_bias, down)
    return token_call(
        mlp_kernel,
        count,
        "mlp",
        [shaped((count, n)) for n in (width, size, size, width, width, width)]
        + [shaped((1, n), F32) for n in (size, width)],
        [row, row, row, row, col, col] + [whole(x.shape) for x in consts],
        [tiled(TILE, n) for n in (width, size, size, width, width, width)]
        + [whole((1, n)) for n in (size, width)],
        [],
        8 * count * width * size,
        (tokens, mine, theirs, cotangent, ids, live) + consts,
    )


def middle_kernel(halves, blocks, *refs):
    tokens, cotangent, context, ids, live, ids_row, *refs = refs
    parts = [refs[i * blocks : (i + 1) * blocks] for i in range(4)]
    table, out_bias, weight, d_middle, d_context, d_weight, d_images, d_bias, sums, total = refs[
        4 * blocks :
    ]
    tile = pl.program_id(0)
    first = tile == 0
    last = tile == pl.num_programs(0) - 1

    def rows_at(refs):
        rows = refs[0][...]
        for i in range(1, blocks):
            rows = jnp.where(tile >= i * (pl.num_programs(0) // blocks), refs[i][...], rows)
        return rows.astype(F32)

    mine, theirs, d_own, d_other = [rows_at(part) for part in parts]
    ids, live = ids[...], live[...]
    gate = live * pick(ids, table[0])
    attn = mine + theirs + out_bias[...].astype(F32)
    xhat, rstd = norm(tokens[...].astype(F32) + gate * attn)
    d_norm = d_own + d_other
    grad = cotangent[...].astype(F32) + norm_back(d_norm * (1.0 + pick(ids, table[2])), xhat, rstd)
    d_middle[...] = grad
    d_attn = (gate * grad).astype(BF16)
    d_context[...] = matmul(d_attn, weight[...], ((1,), (1,))).astype(BF16)
    part = matmul(context[...], d_attn, ((0,), (0,)))
    total[...] = jnp.where(first, 0.0, total[...]) + part
    column = jnp.sum(d_attn.astype(F32), axis=0, keepdims=True)
    d_bias[...] = jnp.where(first, 0.0, d_bias[...]) + column
    gather_images(ids_row[...], (live * grad * attn, d_norm, d_norm * xhat), sums, first)

    @pl.when(last)
    def _():
        d_weight[...] = total[...].astype(BF16)
        halves_out(sums, d_images, halves)


def middle_back(halves, parts, tokens, cotangent, context, ids, live, ids_row, table, out_bias, weight):
    count, width = tokens.shape
    size = context.shape[1]
    images = table.shape[1]
    blocks = len(parts[0])
    tiles = count // TILE // blocks
    row, col = tiled(TILE, width), tiled(TILE, 1)
    consts = (table, out_bias, weight)

    def block_spec(i):
        return pl.BlockSpec((TILE, width), lambda t: (jnp.clip(t - i * tiles, 0, tiles - 1), 0))

    return token_call(
        lambda *refs: middle_kernel(halves, blocks, *refs),
        count,
        "middle_back",
        [
            shaped((count, width), F32),
            shaped((count, size)),
            shaped((size, width)),
            shaped((halves, 3, images, width // halves)),
            shaped((1, width), F32),
        ],
        [row, row, tiled(TILE, size), col, col, pl.BlockSpec((1, TILE), lambda i: (0, i))]
        + [block_spec(i) for _ in parts for i in range(blocks)]
        + [whole(x.shape) for x in consts],
        [
            row,
            tiled(TILE, size),
            whole((size, width)),
            whole((halves, 3, images, width // halves)),
            whole((1, width)),
        ],
        [pltpu.VMEM((3, images, width), F32), pltpu.VMEM((size, width), F32)],
        4 * count * width * size,
        (tokens, cotangent, context, ids, live, ids_row) + tuple(sum(parts, [])) + consts,
    )


def project_back_kernel(halves, tokens, d_q, d_own, rims, tail_start, ids_row, weight, *refs):
    d_norm, d_kv, d_images, sums = refs
    tile = pl.program_id(0)
    span, size = rims.shape[2], d_q.shape[1]
    rows = lax.broadcasted_iota(jnp.int32, (TILE, span), 0) + tile * TILE
    cols = lax.broadcasted_iota(jnp.int32, (TILE, span), 1)
    head_rim = (rows == cols).astype(BF16)
    tail_rim = (rows == cols + tail_start[0]).astype(BF16)
    back = matmul(d_q[...], weight[:size])
    for which in range(2):
        rim = matmul(head_rim, rims[0, which]) + matmul(tail_rim, rims[1, which])
        part = (d_own[which].astype(F32) + rim).astype(BF16)
        d_kv[which] = part
        back += matmul(part, weight[(which + 1) * size : (which + 2) * size])
    back = back.astype(BF16)
    d_norm[...] = back
    xhat, _ = norm(tokens[...].astype(F32))
    back = back.astype(F32)
    gather_images(ids_row[...], (back, back * xhat), sums, tile == 0)

    @pl.when(tile == pl.num_programs(0) - 1)
    def _():
        part = sums.shape[2] // halves
        for half in range(halves):
            cut = slice(half * part, (half + 1) * part)
            both = jnp.concatenate([sums[0, :, cut], sums[1, :, cut]], axis=1)
            d_images[half] = both.astype(BF16)


def project_back(halves, images, tokens, d_q, d_own, rims, tail_start, ids_row, weight):
    count, width = tokens.shape
    size = d_q.shape[1]
    row = tiled(TILE, width)
    pair = pl.BlockSpec((2, TILE, size), lambda i: (0, i, 0))
    sums = (halves, images, 2 * width // halves)
    return token_call(
        lambda *refs: project_back_kernel(halves, *refs),
        count,
        "project_back",
        [shaped((count, width)), shaped((2, count, size)), shaped(sums)],
        [
            row,
            tiled(TILE, size),
            pair,
            whole(rims.shape),
            pl.BlockSpec(memory_space=pltpu.SMEM),
            pl.BlockSpec((1, TILE), lambda i: (0, i)),
            whole(weight.shape),
        ],
        [row, pair, whole(sums)],
        [pltpu.VMEM((2, images, width), F32)],
        6 * count * width * size,
        (tokens, d_q, d_own, rims, tail_start, ids_row, weight),
    )


def qkv_grads_kernel(split, norm_one, d_q, d_kv, top, bottom, d_bias, total):
    tile = pl.program_id(0)
    first = tile == 0
    size = d_q.shape[1]
    parts = [d_q[...], d_kv[0], d_kv[1]]
    normed = norm_one[...]
    for i, part in enumerate(parts):
        rows = slice(i * size, (i + 1) * size)
        total[rows] = jnp.where(first, 0.0, total[rows]) + matmul(part, normed, ((0,), (0,)))
    for i, part in ((0, parts[0]), (1, parts[2])):
        column = jnp.sum(part.astype(F32), axis=0, keepdims=True)
        d_bias[i : i + 1] = jnp.where(first, 0.0, d_bias[i : i + 1]) + column

    @pl.when(tile == pl.num_programs(0) - 1)
    def _():
        top[...] = total[:split].astype(BF16)
        bottom[...] = total[split:].astype(BF16)


def qkv_grads(split, norm_one, d_q, d_kv):
    count, width = norm_one.shape
    size = d_q.shape[1]
    shapes = [(split, width), (3 * size - split, width), (2, size)]
    return token_call(
        lambda *refs: qkv_grads_kernel(split, *refs),
        count,
        "qkv_grads",
        [shaped(shapes[0]), shaped(shapes[1]), shaped(shapes[2], F32)],
        [tiled(TILE, width), tiled(TILE, size), pl.BlockSpec((2, TILE, size), lambda i: (0, i, 0))],
        [whole(shape) for shape in shapes],
        [pltpu.VMEM((3 * size, width), F32)],
        6 * count * width * size,
        (norm_one, d_q, d_kv),
    )


def body(
    tokens,
    condition,
    cotangent,
    modulator,
    modulator_bias,
    qkv_weight,
    qv_bias,
    out_weight,
    out_bias,
    up_weight,
    up_bias,
    down_weight,
    down_bias,
    segment_ids,
    valid_counts,
):
    wide_count = lax.axis_size("wide")
    narrow_count = lax.axis_size("narrow")
    wide_index = lax.axis_index("wide")
    narrow_index = lax.axis_index("narrow")
    tok_dev, width = cotangent.shape
    share = tokens.shape[0]
    part_width = qkv_weight.shape[2]
    mod_width = modulator.shape[2]
    img_row = condition.shape[0]
    span = IMG_MAX
    own_count = valid_counts[wide_index]
    positions = jnp.arange(tok_dev, dtype=jnp.int32)
    own_ids = lax.dynamic_slice_in_dim(segment_ids, wide_index * tok_dev, tok_dev)
    live = (positions < own_count).astype(F32)[:, None]
    share_start = narrow_index * share
    ids_col, ids_row = own_ids[:, None], own_ids[None]
    onehot_full = (ids_col == jnp.arange(img_row, dtype=jnp.int32)[None]).astype(BF16)

    def own(rows):
        return lax.dynamic_slice_in_dim(rows, share_start, share)

    cond_rows = condition.astype(F32)
    sigmoid_rows = jax.nn.sigmoid(cond_rows)
    activated = (cond_rows * sigmoid_rows).astype(BF16)
    tok_full = narrow_gather(tokens)
    mod_rows = jnp.transpose(modulator, (1, 2, 0)).reshape(6 * mod_width, width)

    def vectors(lo, hi, after=None):
        part = dot(activated, mod_rows[lo * mod_width : hi * mod_width], ((1,), (1,)))
        part = part + modulator_bias[lo:hi].astype(F32).reshape(1, -1)
        rows = jnp.moveaxis(part.astype(BF16).reshape(img_row, hi - lo, -1), 2, 0)
        if after is not None:
            rows, after = lax.optimization_barrier((rows, after))
        return jnp.transpose(narrow_gather(rows), (2, 1, 0)), after

    table_one, _ = vectors(0, 2)
    table_two, tok_full = vectors(2, 6, tok_full)
    flat_qkv = jnp.transpose(qkv_weight, (1, 2, 0)).reshape(3 * part_width, width)
    queries, key_rows, value_rows, norm_one = project(
        tok_full, ids_col, table_one, flat_qkv, qv_bias
    )
    tail_start = own_count - span

    def tail_of(rows):
        return lax.dynamic_slice_in_dim(rows, tail_start, span)

    def to_right(rows):
        return lax.ppermute(rows, "wide", [(i, i + 1) for i in range(wide_count - 1)])

    def to_left(rows):
        return lax.ppermute(rows, "wide", [(i + 1, i) for i in range(wide_count - 1)])

    from_left = to_right(jnp.stack([tail_of(key_rows), tail_of(value_rows)]))
    from_right = to_left(jnp.stack([key_rows[:span], value_rows[:span]]))
    left_index = jnp.maximum(wide_index - 1, 0)
    right_index = jnp.minimum(wide_index + 1, wide_count - 1)
    left_count = valid_counts[left_index]
    left_ids = lax.dynamic_slice_in_dim(segment_ids, left_index * tok_dev + left_count - span, span)
    left_ids = jnp.where(wide_index > 0, left_ids, -2)
    right_ids = lax.dynamic_slice_in_dim(segment_ids, right_index * tok_dev, span)
    right_ids = jnp.where(wide_index < wide_count - 1, right_ids, -2)
    own_keys = jnp.where(positions < own_count, own_ids, -1)
    extended_ids = jnp.concatenate([left_ids, own_keys, right_ids])
    context, log_sums = attention_forward(
        queries, key_rows, value_rows, from_left, from_right, own_keys[:, None], extended_ids[None]
    )
    block = min(512, tok_dev)
    blocks = tok_dev // block

    def rows_of(rows, block_idx):
        return rows[block_idx * block : (block_idx + 1) * block]

    out_row = out_bias[None]
    attn_parts, attn_others, mlp_outs, d_others = [], [], [], []
    for i in range(blocks):
        attn_parts.append(dot(rows_of(context, i), out_weight, ((1,), (0,)), BF16))
        attn_others.append(narrow_other(attn_parts[i]))
    for i in range(blocks):
        operands = [rows_of(rows, i) for rows in (tok_full, cotangent, ids_col, live)]
        mlp_outs.append(
            mlp(
                operands[0],
                attn_parts[i],
                attn_others[i],
                *operands[1:],
                table_two,
                out_row,
                up_weight,
                up_bias[None],
                down_weight,
            )
        )
        d_others.append(narrow_other(mlp_outs[i][4]))
    norm_two, hidden, d_upper, d_branch = [
        jnp.concatenate(parts, axis=0) for parts in list(zip(*mlp_outs))[:4]
    ]
    d_norms = [outs[4] for outs in mlp_outs]
    branch_parts = [outs[5] for outs in mlp_outs]
    up_sum, down_sum = [sum(outs[i] for outs in mlp_outs)[0] for i in (6, 7)]
    up_grad = dot(d_upper, norm_two, ((0,), (0,)), BF16)
    down_grad = dot(hidden, d_branch, ((0,), (0,)), BF16)
    halved = narrow_count == 2 and blocks == 2 and share == block

    def own_of(parts, index):
        if halved:
            return jnp.where(index == 0, parts[0], parts[1])
        return lax.dynamic_slice_in_dim(jnp.concatenate(parts, axis=0), index * share, share)

    if halved:
        branch_other = swap(own_of(branch_parts, 1 - narrow_index))
    if ring_fits([up_grad]):
        mine = ring_scatter([up_grad, down_grad], 1)
        mine, d_others = lax.optimization_barrier((mine, d_others))
        up_grad, down_grad = [
            lax.all_gather(mine[lane], "wide", axis=0, tiled=True) for lane in range(2)
        ]
    else:
        up_grad, down_grad = lax.psum((up_grad, down_grad), "wide")
    if halved:
        branch = own_of(branch_parts, narrow_index).astype(F32) + branch_other.astype(F32)
    else:
        branch = narrow_scatter(jnp.concatenate(branch_parts, axis=0))
    branch = branch + down_bias.astype(F32)
    first_bias = jnp.where(narrow_index == 0, down_bias.astype(F32), 0.0)
    d_gate_two = 0.0
    for i in range(blocks):
        term = rows_of(live, i) * rows_of(cotangent, i).astype(F32)
        term = term * (branch_parts[i].astype(F32) + first_bias)
        d_gate_two += dot(rows_of(onehot_full, i), term.astype(BF16), ((0,), (0,)))
    d_gate_two = narrow_scatter(d_gate_two.astype(BF16), 1)
    d_middle, d_context, out_weight_grad, images_two, out_bias_sum = middle_back(
        narrow_count,
        [attn_parts, attn_others, d_norms, d_others],
        tok_full,
        cotangent,
        context,
        ids_col,
        live,
        ids_row,
        table_two,
        out_row,
        out_weight,
    )
    d_queries, d_own, d_rim = attention_backward(
        queries,
        key_rows,
        value_rows,
        from_left,
        from_right,
        d_context,
        log_sums,
        own_keys[None],
        extended_ids[:, None],
    )
    rims = jnp.stack([to_right(d_rim[1]), to_left(d_rim[0])])
    lane_rows = (4 * part_width * width + 6 * img_row * mod_width) // (2 * width)
    split = min(lane_rows, 3 * part_width - 16)
    d_norm_part, d_kv, images_one = project_back(
        narrow_count, img_row, tok_full, d_queries, d_own, rims, tail_start[None], ids_row, flat_qkv
    )
    top, bottom, qv_sums = qkv_grads(split, norm_one, d_queries, d_kv)

    def mine_of(images):
        return lax.dynamic_index_in_dim(images, narrow_index, 0, keepdims=False)

    if narrow_count == 2:
        theirs = lax.dynamic_index_in_dim(images_one, 1 - narrow_index, 0, keepdims=False)
        early = mine_of(images_one).astype(F32) + swap(theirs).astype(F32)
    else:
        early = mine_of(lax.psum(images_one, "narrow"))
    images_two = mine_of(images_two)
    loose_parts = [
        up_sum,
        down_sum,
        qv_sums[0],
        qv_sums[1],
        out_bias_sum[0],
    ]
    loose = jnp.concatenate(loose_parts)
    loose = jnp.pad(loose, (0, (-loose.shape[0]) % (8 * width))).reshape(-1, width)
    terms = [images_two[0], images_two[1], images_two[2], d_gate_two.astype(BF16)]
    d_mod = [early.astype(BF16)]
    d_mod += [jnp.concatenate(terms[2 * i : 2 * i + 2], axis=1) for i in range(2)]
    if 2 * mod_width == width:
        d_mod_flat = jnp.concatenate(d_mod, axis=0)
    else:
        d_mod_flat = jnp.concatenate(d_mod, axis=1).reshape(-1, width)
    rest = jnp.concatenate([bottom, out_weight_grad, d_mod_flat], axis=0)
    if ring_fits([top]) and top.shape == rest.shape:
        flat, d_norm_other, loose = ring_sum([top, rest], d_norm_part, loose, 0)
        d_norm_one = own(d_norm_part).astype(F32) + d_norm_other.astype(F32)
    else:
        d_norm_one = narrow_scatter(d_norm_part)
        flat = jnp.concatenate(lax.psum((top, rest), "wide"), axis=0)
        loose = lax.psum(loose, "wide")
    tok_own = tokens.astype(F32)
    xhat_one, rstd_one = norm(tok_own)
    hot_own = own(onehot_full)
    scale_one = dot(hot_own, table_one[1], ((1,), (0,)))
    tokens_grad = own(d_middle) + norm_back(d_norm_one * (1.0 + scale_one), xhat_one, rstd_one)
    attn_own = sum(own_of(parts, narrow_index).astype(F32) for parts in (attn_parts, attn_others))
    attn_own = attn_own + out_bias.astype(F32)
    live_own = own(live)
    gates = [dot(hot_own, table_two[j], ((1,), (0,))) for j in (0, 3)]
    layer_out = (tok_own + live_own * (gates[0] * attn_own + gates[1] * branch)).astype(BF16)
    up_weight_grad = up_grad.T.astype(F32)
    down_weight_grad = down_grad.astype(F32)
    keep = 3 * part_width
    qkv_flat = flat[:keep].astype(F32)
    qkv_weight_grad = jnp.transpose(qkv_flat.reshape(3, part_width, width), (2, 0, 1))
    out_weight_grad = flat[keep : keep + part_width].astype(F32)
    loose = loose.reshape(-1)
    bounds = [0]
    for part in loose_parts:
        bounds.append(bounds[-1] + part.shape[0])
    up_bias_grad, down_bias_grad, query_bias, value_bias, out_bias_grad = [
        loose[bounds[i] : bounds[i + 1]] for i in range(5)
    ]
    qv_bias_grad = jnp.stack([query_bias, value_bias])
    d_mod_flat = flat[keep + part_width :]
    if 2 * mod_width == width:
        d_mod = d_mod_flat.reshape(3, img_row, width)
    else:
        d_mod = jnp.moveaxis(d_mod_flat.reshape(img_row, 3, -1), 1, 0)
    modulator_grad = lax.dot_general(
        d_mod, activated, (((1,), (0,)), ((), ())), preferred_element_type=F32
    )
    modulator_grad = jnp.transpose(modulator_grad.reshape(6, mod_width, width), (2, 0, 1))
    modulator_bias_grad = jnp.sum(d_mod.astype(F32), axis=1).reshape(6, mod_width)
    mod_blocks = mod_rows.reshape(3, 2 * mod_width, width)
    d_activated = sum(dot(d_mod[i], mod_blocks[i], ((1,), (0,))) for i in range(3))
    cond_part = d_activated * sigmoid_rows * (1.0 + cond_rows * (1.0 - sigmoid_rows))
    cond_part = cond_part.astype(BF16)
    condition_grad = cond_part.astype(F32) + narrow_other(cond_part).astype(F32)
    return (
        layer_out,
        tokens_grad,
        condition_grad,
        modulator_grad,
        modulator_bias_grad,
        qkv_weight_grad,
        qv_bias_grad,
        out_weight_grad,
        out_bias_grad,
        up_weight_grad,
        up_bias_grad,
        down_weight_grad,
        down_bias_grad,
    )


def solution(mesh):
    in_specs = (
        P(("wide", "narrow"), None),
        P(),
        P("wide", None),
        P(None, None, "narrow"),
        P(None, "narrow"),
        P(None, None, "narrow"),
        P(None, "narrow"),
        P("narrow", None),
        P(),
        P(None, "narrow"),
        P("narrow"),
        P("narrow", None),
        P(),
        P(),
        P(),
    )
    out_specs = (
        P(("wide", "narrow"), None),
        P(("wide", "narrow"), None),
        P(),
        P(None, None, "narrow"),
        P(None, "narrow"),
        P(None, None, "narrow"),
        P(None, "narrow"),
        P("narrow", None),
        P(),
        P(None, "narrow"),
        P("narrow"),
        P("narrow", None),
        P(),
    )
    return jax.shard_map(body, mesh=mesh, in_specs=in_specs, out_specs=out_specs, check_vma=False)
```

```python
import jax
import jax.numpy as jnp
from jax import lax
from jax.experimental import pallas as pl
from jax.experimental.pallas import tpu as pltpu
from jax.sharding import PartitionSpec as P

HD = 72
IMG_MAX = 128
EPSILON = 1e-06
NEG_FILL = -1e30
F32 = jnp.float32
BF16 = jnp.bfloat16


def dot(left, right, dims, out=F32):
    return lax.dot_general(left, right, (dims, ((), ())), preferred_element_type=F32).astype(out)


def swap(part):
    return lax.ppermute(part, "narrow", [(0, 1), (1, 0)])


def narrow_gather(part):
    if lax.axis_size("narrow") != 2:
        return lax.all_gather(part, "narrow", axis=0, tiled=True)
    other = swap(part)
    first = lax.axis_index("narrow") == 0
    return jnp.where(
        first, jnp.concatenate([part, other], axis=0), jnp.concatenate([other, part], axis=0)
    )


def narrow_other(part):
    if lax.axis_size("narrow") != 2:
        return (lax.psum(part.astype(F32), "narrow") - part.astype(F32)).astype(BF16)
    return swap(part)


def narrow_scatter(part, dim=0):
    count = lax.axis_size("narrow")
    if count != 2:
        return lax.psum_scatter(part, "narrow", scatter_dimension=dim, tiled=True).astype(F32)
    size = part.shape[dim] // 2
    index = lax.axis_index("narrow")
    mine = lax.dynamic_slice_in_dim(part, index * size, size, axis=dim)
    theirs = lax.dynamic_slice_in_dim(part, (1 - index) * size, size, axis=dim)
    return mine.astype(F32) + swap(theirs).astype(F32)


MESH = pl.DeviceIdType.MESH
UNIT = 48


def ring_kernel(chips, subs, full, *refs):
    data = refs[:2]
    if full:
        part, loose, out, landing, loose_out, *refs = refs[2:]
        last, loose_pair, loose_rows, *sems = refs[6:]
        swap_sems, gather_sems, pair_sems, own_sems, loose_pair_sems, loose_sems = sems
    else:
        last, *refs = refs[2:]
    mine, theirs, slots, copy_sems, core_sems, ring_sems = refs[:6]
    wide = lax.axis_index("wide")
    chip, core = wide // 2, wide % 2
    half = chips // 2

    def place(position):
        position = lax.rem(position + 2 * chips, chips)
        side = position // half
        return (1 - side) * 2 * position + side * (2 * (chips - 1 - position) + 1)

    position = chip // 2 + (chip % 2) * (chips - 1 - 2 * (chip // 2))
    ahead = 2 * place(position + 1) + core
    behind = 2 * place(position - 1) + core
    sibling = 2 * chip + 1 - core
    barrier = pltpu.get_barrier_semaphore()
    for device in (ahead, behind, sibling):
        pl.semaphore_signal(barrier, inc=1, device_id={"wide": device}, device_id_type=MESH)
    if full:
        facing = 1 - lax.axis_index("narrow")
        pl.semaphore_signal(barrier, inc=1, device_id={"narrow": facing}, device_id_type=MESH)
    pl.semaphore_wait(barrier, 3 + int(full))

    def local(lane):
        return pltpu.make_async_copy(data[lane].at[:, core], mine.at[lane], copy_sems.at[lane])

    def needed(lane, order):
        return place(position - 1 - order if lane == 0 else position + 1 + order)

    def across(lane, order):
        index = needed(lane, order)
        return pltpu.make_async_remote_copy(
            src_ref=data[lane].at[index, 1 - core],
            dst_ref=theirs.at[lane, index],
            send_sem=core_sems.at[0, lane, order],
            recv_sem=core_sems.at[1, lane, order],
            device_id={"wide": sibling},
            device_id_type=MESH,
        )

    for order in range(chips):
        for lane in range(2):
            across(lane, order).start()
            if order == 0:
                local(lane).start()
    if full:
        share = landing.shape[0]
        turn = pltpu.make_async_remote_copy(
            src_ref=part.at[pl.ds(facing * share, share)],
            dst_ref=landing,
            send_sem=swap_sems.at[0],
            recv_sem=swap_sems.at[1],
            device_id={"narrow": facing},
            device_id_type=MESH,
        )
        turn.start()
        loose_swap = pltpu.make_async_remote_copy(
            src_ref=loose,
            dst_ref=loose_pair,
            send_sem=loose_pair_sems.at[0],
            recv_sem=loose_pair_sems.at[1],
            device_id={"wide": sibling},
            device_id_type=MESH,
        )
        loose_swap.start()

    def loose_hop(step, index):
        return pltpu.make_async_remote_copy(
            src_ref=loose_rows.at[index],
            dst_ref=loose_rows.at[index],
            send_sem=loose_sems.at[0, step],
            recv_sem=loose_sems.at[1, step],
            device_id={"wide": ahead},
            device_id_type=MESH,
        )

    def rows_of(sub):
        return pl.ds(sub * UNIT, UNIT)

    def hop(lane, step, sub):
        rows = rows_of(sub)
        if step == 0:
            first = place(position - 1 if lane == 0 else position + 1)
            source = mine.at[lane, first, rows]
        else:
            source = slots.at[lane, step - 1, rows]
        return pltpu.make_async_remote_copy(
            src_ref=source,
            dst_ref=slots.at[lane, step, rows],
            send_sem=ring_sems.at[0, lane, step, sub],
            recv_sem=ring_sems.at[1, lane, step, sub],
            device_id={"wide": ahead if lane == 0 else behind},
            device_id_type=MESH,
        )

    def held(lane, step, sub, side):
        index = place(position - step if lane == 0 else position + step)
        return out.at[lane, index, side, rows_of(sub)]

    def send_on(lane, step, sub):
        source = last.at[lane, rows_of(sub)] if step == 0 else held(lane, step, sub, core)
        return pltpu.make_async_remote_copy(
            src_ref=source,
            dst_ref=held(lane, step, sub, core),
            send_sem=gather_sems.at[0, lane, step, sub],
            recv_sem=gather_sems.at[1, lane, step, sub],
            device_id={"wide": ahead if lane == 0 else behind},
            device_id_type=MESH,
        )

    def landed(lane, step, sub):
        return pltpu.make_async_remote_copy(
            src_ref=last.at[lane, rows_of(sub)],
            dst_ref=held(lane, step + 1, sub, core),
            send_sem=gather_sems.at[0, lane, step, sub],
            recv_sem=gather_sems.at[1, lane, step, sub],
            device_id={"wide": ahead if lane == 0 else behind},
            device_id_type=MESH,
        )

    def pair(lane, step, sub, side):
        source = last.at[lane, rows_of(sub)] if step == 0 else held(lane, step, sub, core)
        return pltpu.make_async_remote_copy(
            src_ref=source,
            dst_ref=held(lane, step, sub, side),
            send_sem=pair_sems.at[0, lane, step, sub],
            recv_sem=pair_sems.at[1, lane, step, sub],
            device_id={"wide": sibling},
            device_id_type=MESH,
        )

    def keep(lane, sub):
        return pltpu.make_async_copy(
            last.at[lane, rows_of(sub)], held(lane, 0, sub, core), own_sems.at[lane, sub]
        )

    def pair_sum(lane, order, rows):
        index = needed(lane, order)
        return mine[lane, index, rows].astype(F32) + theirs[lane, index, rows].astype(F32)

    for lane in range(2):
        local(lane).wait()
        across(lane, 0).wait_recv()
        for sub in range(subs):
            mine[lane, needed(lane, 0), rows_of(sub)] = pair_sum(lane, 0, rows_of(sub)).astype(BF16)
            hop(lane, 0, sub).start()
    if full:
        loose_swap.wait()
        loose_rows[chip] = loose[...] + loose_pair[...]
        loose_hop(0, chip).start()
    for step in range(chips - 1):
        for sub in range(subs):
            for lane in range(2):
                if sub == 0:
                    across(lane, step + 1).wait_recv()
                rows = rows_of(sub)
                extra = pair_sum(lane, step + 1, rows)
                hop(lane, step, sub).wait_recv()
                total = (slots[lane, step, rows].astype(F32) + extra).astype(BF16)
                if step < chips - 2:
                    slots[lane, step, rows] = total
                    hop(lane, step + 1, sub).start()
                else:
                    last[lane, rows] = total
                    if full:
                        send_on(lane, 0, sub).start()
                        pair(lane, 0, sub, core).start()
                        keep(lane, sub).start()
        if full:
            passed = place(position - 1 - step)
            loose_hop(step, passed).wait_recv()
            if step < chips - 2:
                loose_hop(step + 1, passed).start()
    if full:
        for step in range(chips - 1):
            for sub in range(subs):
                for lane in range(2):
                    landed(lane, step, sub).wait_recv()
                    if step < chips - 2:
                        send_on(lane, step + 1, sub).start()
                    pair(lane, step + 1, sub, core).start()
        loose_out[...] = jnp.sum(loose_rows[...], axis=0)
    for step in range(chips):
        if full and step < chips - 1:
            loose_hop(step, place(position - step)).wait_send()
        for lane in range(2):
            across(lane, step).wait_send()
            for sub in range(subs):
                if step < chips - 1:
                    hop(lane, step, sub).wait_send()
                if full:
                    pair(lane, step, sub, 1 - core).wait_recv()
                    pair(lane, step, sub, core).wait_send()
                    if step == 0:
                        keep(lane, sub).wait()
                    if step < chips - 1:
                        send_on(lane, step, sub).wait_send()
    if full:
        turn.wait()


def ring_scratch(chips, shard, width):
    return [
        pltpu.VMEM((2, chips, shard, width), BF16),
        pltpu.VMEM((2, chips, shard, width), BF16),
        pltpu.VMEM((2, chips - 1, shard, width), BF16),
        pltpu.SemaphoreType.DMA((2,)),
        pltpu.SemaphoreType.DMA((2, 2, chips)),
        pltpu.SemaphoreType.DMA((2, 2, chips - 1, shard // UNIT)),
    ]


def ring_scatter(lanes, collective_id):
    chips = lax.axis_size("wide") // 2
    rows, width = lanes[0].shape
    shard = rows // (2 * chips)
    return pl.pallas_call(
        lambda *refs: ring_kernel(chips, shard // UNIT, False, *refs),
        out_shape=jax.ShapeDtypeStruct((2, shard, width), BF16),
        in_specs=[pl.BlockSpec(memory_space=pl.ANY)] * 2,
        out_specs=pl.BlockSpec(memory_space=pltpu.VMEM),
        scratch_shapes=ring_scratch(chips, shard, width),
        compiler_params=pltpu.CompilerParams(
            collective_id=collective_id, has_side_effects=True, vmem_limit_bytes=40 << 20
        ),
        name="ring_scatter",
    )(*[lane.reshape(chips, 2, shard, width) for lane in lanes])


def ring_sum(lanes, part, loose, collective_id):
    chips = lax.axis_size("wide") // 2
    rows, width = lanes[0].shape
    shard = rows // (2 * chips)
    subs = shard // UNIT
    anywhere = pl.BlockSpec(memory_space=pl.ANY)
    inside = pl.BlockSpec(memory_space=pltpu.VMEM)
    sums, landed, loose_sum = pl.pallas_call(
        lambda *refs: ring_kernel(chips, subs, True, *refs),
        out_shape=[
            jax.ShapeDtypeStruct((2, chips, 2, shard, width), BF16),
            jax.ShapeDtypeStruct((part.shape[0] // 2, part.shape[1]), BF16),
            jax.ShapeDtypeStruct(loose.shape, F32),
        ],
        in_specs=[anywhere] * 3 + [inside],
        out_specs=[anywhere] * 2 + [inside],
        scratch_shapes=ring_scratch(chips, shard, width)
        + [
            pltpu.VMEM((2, shard, width), BF16),
            pltpu.VMEM(loose.shape, F32),
            pltpu.VMEM((chips,) + loose.shape, F32),
            pltpu.SemaphoreType.DMA((2,)),
            pltpu.SemaphoreType.DMA((2, 2, chips - 1, subs)),
            pltpu.SemaphoreType.DMA((2, 2, chips, subs)),
            pltpu.SemaphoreType.DMA((2, subs)),
            pltpu.SemaphoreType.DMA((2,)),
            pltpu.SemaphoreType.DMA((2, chips - 1)),
        ],
        compiler_params=pltpu.CompilerParams(
            collective_id=collective_id, has_side_effects=True, vmem_limit_bytes=40 << 20
        ),
        name="ring_sum",
    )(*[lane.reshape(chips, 2, shard, width) for lane in lanes], part, loose)
    return sums.reshape(2 * rows, width), landed, loose_sum


def ring_fits(lanes):
    count = lax.axis_size("wide")
    return lax.axis_size("narrow") == 2 and lanes[0].shape[0] % (count * UNIT) == 0


TILE = 256
LOG2E = 1.4426950408889634


def head_lanes(part_width):
    for head in range(part_width // HD):
        lo = head * HD // 128 * 128
        hi = min(-(-(head + 1) * HD // 128) * 128, part_width)
        lanes = lax.broadcasted_iota(jnp.int32, (1, hi - lo), 1) + lo
        yield head, lo, hi, (lanes >= head * HD) & (lanes < (head + 1) * HD)


def extend(first, left, own, right, ext):
    span = left.shape[1]
    ends = ext.shape[1] - span

    @pl.when(first)
    def _():
        for which in range(2):
            ext[which, :span] = left[which]
            ext[which, span:ends] = own[which][...]
            ext[which, ends:] = right[which]


def forward_kernel(tiles, q, k, v, left, right, q_ids, k_ids, out, lse, ext, total):
    tile = pl.program_id(0)
    part_width = q.shape[1]
    span = left.shape[1]
    ends = ext.shape[1] - span
    extend(tile == 0, left, (k, v), right, ext)
    scale = LOG2E * HD ** (-0.5)

    def run(extra):
        rows = pl.ds(pl.multiple_of(tile * TILE, TILE), TILE + 2 * span)
        keys, values = ext[0, rows], ext[1, rows]
        ids = k_ids[:, rows]
        if extra:
            keys = jnp.concatenate([keys, ext[0, ends:]], axis=0)
            values = jnp.concatenate([values, ext[1, ends:]], axis=0)
            ids = jnp.concatenate([ids, k_ids[:, ends:]], axis=1)
        same = q_ids[...] == ids
        queries = q[...]
        total[...] = jnp.zeros_like(total)
        packed = jnp.zeros((TILE, 128), F32)
        column = lax.broadcasted_iota(jnp.int32, (TILE, 128), 1)
        for head, lo, hi, mask in head_lanes(part_width):
            chosen = jnp.where(mask, queries[:, lo:hi], 0)
            scores = lax.dot_general(
                chosen, keys[:, lo:hi], (((1,), (1,)), ((), ())), preferred_element_type=F32
            )
            scores = jnp.where(same, scores * scale, NEG_FILL)
            top = jnp.max(scores, axis=1, keepdims=True)
            expo = jnp.exp2(scores - top)
            count = jnp.sum(expo, axis=1, keepdims=True)
            part = jnp.dot(expo.astype(BF16), values[:, lo:hi], preferred_element_type=F32)
            total[:, lo:hi] += jnp.where(mask, part / count, 0.0)
            packed = jnp.where(column == head, top + jnp.log2(count), packed)
        out[...] = total[...].astype(BF16)
        lse[...] = packed.T[: lse.shape[0]]

    split_tiles(tile, tiles, run)


def split_tiles(tile, tiles, run):
    first_extra = tiles - 512 // TILE
    extra = (tile >= first_extra) & (tile < tiles - 1)
    pl.when(extra)(lambda: run(True))
    pl.when(jnp.logical_not(extra))(lambda: run(False))


def rim_specs(part_width, span, tok_dev):
    whole = lambda shape: pl.BlockSpec(shape, lambda i: (0,) * len(shape))
    return whole((tok_dev, part_width)), whole((2, span, part_width))


def attention_forward(q, k, v, left, right, q_ids, k_ids):
    tok_dev, part_width = q.shape
    span = left.shape[1]
    tiles = tok_dev // TILE
    head_rows = -(-(part_width // HD) // 8) * 8
    own_spec, rim_spec = rim_specs(part_width, span, tok_dev)
    return pl.pallas_call(
        lambda *refs: forward_kernel(tiles, *refs),
        grid=(tiles,),
        out_shape=[
            jax.ShapeDtypeStruct((tok_dev, part_width), BF16),
            jax.ShapeDtypeStruct((head_rows, tok_dev), F32),
        ],
        in_specs=[
            pl.BlockSpec((TILE, part_width), lambda i: (i, 0)),
            own_spec,
            own_spec,
            rim_spec,
            rim_spec,
            pl.BlockSpec((TILE, 1), lambda i: (i, 0)),
            pl.BlockSpec((1, tok_dev + 2 * span), lambda i: (0, 0)),
        ],
        out_specs=[
            pl.BlockSpec((TILE, part_width), lambda i: (i, 0)),
            pl.BlockSpec((head_rows, TILE), lambda i: (0, i)),
        ],
        scratch_shapes=[
            pltpu.VMEM((2, tok_dev + 2 * span, part_width), BF16),
            pltpu.VMEM((TILE, part_width), F32),
        ],
        compiler_params=pltpu.CompilerParams(vmem_limit_bytes=40 << 20),
        cost_estimate=pl.CostEstimate(
            flops=4 * tok_dev * 512 * part_width,
            transcendentals=tok_dev * 512 * 8,
            bytes_accessed=8 * tok_dev * part_width,
        ),
        name="attention_forward",
    )(q, k, v, left, right, q_ids, k_ids)


def backward_kernel(tiles, q, k, v, left, right, grad, lse, q_ids, k_ids, *refs):
    d_q, d_own, d_rim, ext, d_ext, total = refs
    tile = pl.program_id(0)
    part_width = q.shape[1]
    span = left.shape[1]
    ends = ext.shape[1] - span
    extend(tile == 0, left, (k, v), right, ext)
    scale = HD ** (-0.5)

    @pl.when(tile == 0)
    def _():
        d_ext[...] = jnp.zeros_like(d_ext)

    def run(extra):
        rows = pl.ds(pl.multiple_of(tile * TILE, TILE), TILE + 2 * span)
        keys, values = ext[0, rows], ext[1, rows]
        ids = k_ids[rows]
        if extra:
            keys = jnp.concatenate([keys, ext[0, ends:]], axis=0)
            values = jnp.concatenate([values, ext[1, ends:]], axis=0)
            ids = jnp.concatenate([ids, k_ids[ends:]], axis=0)
        same = ids == q_ids[...]
        queries, grads = q[...], grad[...]
        total[...] = jnp.zeros_like(total)

        def across(left_side, right_side, dims):
            return lax.dot_general(
                left_side, right_side, (dims, ((), ())), preferred_element_type=F32
            )

        for head, lo, hi, mask in head_lanes(part_width):
            chosen = jnp.where(mask, queries[:, lo:hi], 0)
            pulled = jnp.where(mask, grads[:, lo:hi], 0)
            scores = across(keys[:, lo:hi], chosen, ((1,), (1,)))
            scores = jnp.where(same, scores * (scale * LOG2E), NEG_FILL)
            attend = jnp.exp2(scores - lse[head : head + 1])
            d_attend = across(values[:, lo:hi], pulled, ((1,), (1,)))
            centre = jnp.sum(attend * d_attend, axis=0, keepdims=True)
            d_scores = (attend * (d_attend - centre)).astype(BF16)
            d_key = across(d_scores, chosen, ((1,), (0,)))
            d_value = across(attend.astype(BF16), pulled, ((1,), (0,)))
            length = TILE + 2 * span
            d_ext[0, rows, lo:hi] += d_key[:length]
            d_ext[1, rows, lo:hi] += d_value[:length]
            if extra:
                d_ext[0, ends:, lo:hi] += d_key[length:]
                d_ext[1, ends:, lo:hi] += d_value[length:]
            d_query = across(d_scores, keys[:, lo:hi], ((0,), (0,)))
            total[:, lo:hi] += jnp.where(mask, d_query, 0.0)
        d_q[...] = (total[...] * scale).astype(BF16)

    split_tiles(tile, tiles, run)

    @pl.when(tile == tiles - 1)
    def _():
        for which, factor in ((0, scale), (1, 1.0)):
            d_rim[0, which] = (d_ext[which, :span] * factor).astype(BF16)
            d_own[which] = (d_ext[which, span:ends] * factor).astype(BF16)
            d_rim[1, which] = (d_ext[which, ends:] * factor).astype(BF16)


def attention_backward(q, k, v, left, right, grad, lse, q_ids, k_ids):
    tok_dev, part_width = q.shape
    span = left.shape[1]
    tiles = tok_dev // TILE
    own_spec, rim_spec = rim_specs(part_width, span, tok_dev)
    tile_spec = pl.BlockSpec((TILE, part_width), lambda i: (i, 0))
    return pl.pallas_call(
        lambda *refs: backward_kernel(tiles, *refs),
        grid=(tiles,),
        out_shape=[
            jax.ShapeDtypeStruct((tok_dev, part_width), BF16),
            jax.ShapeDtypeStruct((2, tok_dev, part_width), BF16),
            jax.ShapeDtypeStruct((2, 2, span, part_width), BF16),
        ],
        in_specs=[
            tile_spec,
            own_spec,
            own_spec,
            rim_spec,
            rim_spec,
            tile_spec,
            pl.BlockSpec((lse.shape[0], TILE), lambda i: (0, i)),
            pl.BlockSpec((1, TILE), lambda i: (0, i)),
            pl.BlockSpec((tok_dev + 2 * span, 1), lambda i: (0, 0)),
        ],
        out_specs=[
            tile_spec,
            pl.BlockSpec((2, tok_dev, part_width), lambda i: (0, 0, 0)),
            pl.BlockSpec((2, 2, span, part_width), lambda i: (0, 0, 0, 0)),
        ],
        scratch_shapes=[
            pltpu.VMEM((2, tok_dev + 2 * span, part_width), BF16),
            pltpu.VMEM((2, tok_dev + 2 * span, part_width), F32),
            pltpu.VMEM((TILE, part_width), F32),
        ],
        compiler_params=pltpu.CompilerParams(vmem_limit_bytes=48 << 20),
        cost_estimate=pl.CostEstimate(
            flops=10 * tok_dev * 512 * part_width,
            transcendentals=tok_dev * 512 * 8,
            bytes_accessed=16 * tok_dev * part_width,
        ),
        name="attention_backward",
    )(q, k, v, left, right, grad, lse, q_ids, k_ids)


def norm(field):
    centred = field - jnp.mean(field, axis=-1, keepdims=True)
    rstd = lax.rsqrt(jnp.mean(centred * centred, axis=-1, keepdims=True) + EPSILON)
    return centred * rstd, rstd


def norm_back(grad, xhat, rstd):
    return rstd * (
        grad
        - jnp.mean(grad, axis=-1, keepdims=True)
        - xhat * jnp.mean(grad * xhat, axis=-1, keepdims=True)
    )


def gelu_pair(v):
    c = 0.7978845608028654
    sq = v * v
    t = jnp.tanh(c * v * (1.0 + 0.044715 * sq))
    half = 0.5 * (1.0 + t)
    slope = half + 0.5 * v * (1.0 - t * t) * c * (1.0 + 3 * 0.044715 * sq)
    return v * half, slope


def matmul(left, right, dims=((1,), (0,))):
    return lax.dot_general(left, right, (dims, ((), ())), preferred_element_type=F32)


def pick(ids, table):
    slots = lax.broadcasted_iota(jnp.int32, (ids.shape[0], table.shape[0]), 1)
    return matmul((ids == slots).astype(BF16), table)


def gather_images(ids, terms, sums, fresh):
    slots = lax.broadcasted_iota(jnp.int32, (sums.shape[1], ids.shape[1]), 0)
    hot = (ids == slots).astype(BF16)
    for i, term in enumerate(terms):
        part = matmul(hot, term.astype(BF16))
        sums[i] = jnp.where(fresh, 0.0, sums[i]) + part


def halves_out(sums, out, halves):
    size = sums.shape[2] // halves
    for half in range(halves):
        for i in range(sums.shape[0]):
            out[half, i] = sums[i, :, half * size : (half + 1) * size].astype(BF16)


def whole(shape):
    return pl.BlockSpec(shape, lambda i: (0,) * len(shape))


def tiled(rows, width):
    return pl.BlockSpec((rows, width), lambda i: (i, 0))


def token_call(kernel, tokens, name, out_shape, in_specs, out_specs, scratch, flops, operands):
    size = sum(x.size * x.dtype.itemsize for x in operands)
    return pl.pallas_call(
        kernel,
        grid=(tokens // TILE,),
        out_shape=out_shape,
        in_specs=in_specs,
        out_specs=out_specs,
        scratch_shapes=scratch,
        compiler_params=pltpu.CompilerParams(vmem_limit_bytes=60 << 20),
        cost_estimate=pl.CostEstimate(
            flops=flops, transcendentals=0, bytes_accessed=size + size // 2
        ),
        name=name,
    )(*operands)


def shaped(shape, dtype=BF16):
    return jax.ShapeDtypeStruct(shape, dtype)


def project_kernel(tokens, ids, table, weight, bias, q, k, v, norm_one):
    xhat, _ = norm(tokens[...].astype(F32))
    normed = (xhat * (1.0 + pick(ids[...], table[1])) + pick(ids[...], table[0])).astype(BF16)
    norm_one[...] = normed
    size = q.shape[1]
    for i, out in enumerate((q, k, v)):
        rows = matmul(normed, weight[i * size : (i + 1) * size], ((1,), (1,)))
        if i != 1:
            rows = rows + bias[i // 2 : i // 2 + 1].astype(F32)
        out[...] = rows.astype(BF16)


def project(tokens, ids, table, weight, bias):
    count, width = tokens.shape
    size = weight.shape[0] // 3
    return token_call(
        project_kernel,
        count,
        "project",
        [shaped((count, size))] * 3 + [shaped((count, width))],
        [tiled(TILE, width), tiled(TILE, 1), whole(table.shape), whole(weight.shape), whole(bias.shape)],
        [tiled(TILE, size)] * 3 + [tiled(TILE, width)],
        [],
        6 * count * width * size,
        (tokens, ids, table, weight, bias),
    )


def mlp_kernel(
    tokens, mine, theirs, cotangent, ids, live, table, out_bias, up, up_bias, down, *outs
):
    norm_two, hidden, d_upper, d_branch, d_norm, branch, up_sum, down_sum = outs
    first = pl.program_id(0) == 0
    ids, live = ids[...], live[...]
    attn = mine[...].astype(F32) + theirs[...].astype(F32) + out_bias[...].astype(F32)
    middle = tokens[...].astype(F32) + live * pick(ids, table[0]) * attn
    xhat, _ = norm(middle)
    normed = (xhat * (1.0 + pick(ids, table[2])) + pick(ids, table[1])).astype(BF16)
    norm_two[...] = normed
    pulled = (live * pick(ids, table[3]) * cotangent[...].astype(F32)).astype(BF16)
    d_branch[...] = pulled
    column = jnp.sum(pulled.astype(F32), axis=0, keepdims=True)
    down_sum[...] = jnp.where(first, 0.0, down_sum[...]) + column
    width = up.shape[1]
    step = 384 if width % 384 == 0 else width
    back = ahead = 0.0
    for lo in range(0, width, step):
        cols = slice(lo, lo + step)
        upper = matmul(normed, up[:, cols]) + up_bias[:, cols].astype(F32)
        d_hidden = matmul(pulled, down[cols], ((1,), (1,)))
        value, slope = gelu_pair(upper)
        value = value.astype(BF16)
        d_up = (d_hidden * slope).astype(BF16)
        hidden[:, cols] = value
        d_upper[:, cols] = d_up
        column = jnp.sum(d_up.astype(F32), axis=0, keepdims=True)
        up_sum[:, cols] = jnp.where(first, 0.0, up_sum[:, cols]) + column
        back += matmul(d_up, up[:, cols], ((1,), (1,)))
        ahead += matmul(value, down[cols])
    d_norm[...] = back.astype(BF16)
    branch[...] = ahead.astype(BF16)


def mlp(tokens, mine, theirs, cotangent, ids, live, table, out_bias, up, up_bias, down):
    count, width = tokens.shape
    size = up.shape[1]
    row, col = tiled(TILE, width), tiled(TILE, 1)
    consts = (table, out_bias, up, up_bias, down)
    return token_call(
        mlp_kernel,
        count,
        "mlp",
        [shaped((count, n)) for n in (width, size, size, width, width, width)]
        + [shaped((1, n), F32) for n in (size, width)],
        [row, row, row, row, col, col] + [whole(x.shape) for x in consts],
        [tiled(TILE, n) for n in (width, size, size, width, width, width)]
        + [whole((1, n)) for n in (size, width)],
        [],
        8 * count * width * size,
        (tokens, mine, theirs, cotangent, ids, live) + consts,
    )


def middle_kernel(halves, blocks, *refs):
    tokens, cotangent, context, ids, live, ids_row, *refs = refs
    parts = [refs[i * blocks : (i + 1) * blocks] for i in range(4)]
    table, out_bias, weight, d_middle, d_context, d_weight, d_images, d_bias, sums, total = refs[
        4 * blocks :
    ]
    tile = pl.program_id(0)
    first = tile == 0
    last = tile == pl.num_programs(0) - 1

    def rows_at(refs):
        rows = refs[0][...]
        for i in range(1, blocks):
            rows = jnp.where(tile >= i * (pl.num_programs(0) // blocks), refs[i][...], rows)
        return rows.astype(F32)

    mine, theirs, d_own, d_other = [rows_at(part) for part in parts]
    ids, live = ids[...], live[...]
    gate = live * pick(ids, table[0])
    attn = mine + theirs + out_bias[...].astype(F32)
    xhat, rstd = norm(tokens[...].astype(F32) + gate * attn)
    d_norm = d_own + d_other
    grad = cotangent[...].astype(F32) + norm_back(d_norm * (1.0 + pick(ids, table[2])), xhat, rstd)
    d_middle[...] = grad
    d_attn = (gate * grad).astype(BF16)
    d_context[...] = matmul(d_attn, weight[...], ((1,), (1,))).astype(BF16)
    part = matmul(context[...], d_attn, ((0,), (0,)))
    total[...] = jnp.where(first, 0.0, total[...]) + part
    column = jnp.sum(d_attn.astype(F32), axis=0, keepdims=True)
    d_bias[...] = jnp.where(first, 0.0, d_bias[...]) + column
    gather_images(ids_row[...], (live * grad * attn, d_norm, d_norm * xhat), sums, first)

    @pl.when(last)
    def _():
        d_weight[...] = total[...].astype(BF16)
        halves_out(sums, d_images, halves)


def middle_back(halves, parts, tokens, cotangent, context, ids, live, ids_row, table, out_bias, weight):
    count, width = tokens.shape
    size = context.shape[1]
    images = table.shape[1]
    blocks = len(parts[0])
    tiles = count // TILE // blocks
    row, col = tiled(TILE, width), tiled(TILE, 1)
    consts = (table, out_bias, weight)

    def block_spec(i):
        return pl.BlockSpec((TILE, width), lambda t: (jnp.clip(t - i * tiles, 0, tiles - 1), 0))

    return token_call(
        lambda *refs: middle_kernel(halves, blocks, *refs),
        count,
        "middle_back",
        [
            shaped((count, width), F32),
            shaped((count, size)),
            shaped((size, width)),
            shaped((halves, 3, images, width // halves)),
            shaped((1, width), F32),
        ],
        [row, row, tiled(TILE, size), col, col, pl.BlockSpec((1, TILE), lambda i: (0, i))]
        + [block_spec(i) for _ in parts for i in range(blocks)]
        + [whole(x.shape) for x in consts],
        [
            row,
            tiled(TILE, size),
            whole((size, width)),
            whole((halves, 3, images, width // halves)),
            whole((1, width)),
        ],
        [pltpu.VMEM((3, images, width), F32), pltpu.VMEM((size, width), F32)],
        4 * count * width * size,
        (tokens, cotangent, context, ids, live, ids_row) + tuple(sum(parts, [])) + consts,
    )


def project_back_kernel(halves, tokens, d_q, d_own, rims, tail_start, ids_row, weight, *refs):
    d_norm, d_kv, d_images, sums = refs
    tile = pl.program_id(0)
    span, size = rims.shape[2], d_q.shape[1]
    rows = lax.broadcasted_iota(jnp.int32, (TILE, span), 0) + tile * TILE
    cols = lax.broadcasted_iota(jnp.int32, (TILE, span), 1)
    head_rim = (rows == cols).astype(BF16)
    tail_rim = (rows == cols + tail_start[0]).astype(BF16)
    back = matmul(d_q[...], weight[:size])
    for which in range(2):
        rim = matmul(head_rim, rims[0, which]) + matmul(tail_rim, rims[1, which])
        part = (d_own[which].astype(F32) + rim).astype(BF16)
        d_kv[which] = part
        back += matmul(part, weight[(which + 1) * size : (which + 2) * size])
    back = back.astype(BF16)
    d_norm[...] = back
    xhat, _ = norm(tokens[...].astype(F32))
    back = back.astype(F32)
    gather_images(ids_row[...], (back, back * xhat), sums, tile == 0)

    @pl.when(tile == pl.num_programs(0) - 1)
    def _():
        part = sums.shape[2] // halves
        for half in range(halves):
            cut = slice(half * part, (half + 1) * part)
            both = jnp.concatenate([sums[0, :, cut], sums[1, :, cut]], axis=1)
            d_images[half] = both.astype(BF16)


def project_back(halves, images, tokens, d_q, d_own, rims, tail_start, ids_row, weight):
    count, width = tokens.shape
    size = d_q.shape[1]
    row = tiled(TILE, width)
    pair = pl.BlockSpec((2, TILE, size), lambda i: (0, i, 0))
    sums = (halves, images, 2 * width // halves)
    return token_call(
        lambda *refs: project_back_kernel(halves, *refs),
        count,
        "project_back",
        [shaped((count, width)), shaped((2, count, size)), shaped(sums)],
        [
            row,
            tiled(TILE, size),
            pair,
            whole(rims.shape),
            pl.BlockSpec(memory_space=pltpu.SMEM),
            pl.BlockSpec((1, TILE), lambda i: (0, i)),
            whole(weight.shape),
        ],
        [row, pair, whole(sums)],
        [pltpu.VMEM((2, images, width), F32)],
        6 * count * width * size,
        (tokens, d_q, d_own, rims, tail_start, ids_row, weight),
    )


def qkv_grads_kernel(split, norm_one, d_q, d_kv, top, bottom, d_bias, total):
    tile = pl.program_id(0)
    first = tile == 0
    size = d_q.shape[1]
    parts = [d_q[...], d_kv[0], d_kv[1]]
    normed = norm_one[...]
    for i, part in enumerate(parts):
        rows = slice(i * size, (i + 1) * size)
        total[rows] = jnp.where(first, 0.0, total[rows]) + matmul(part, normed, ((0,), (0,)))
    for i, part in ((0, parts[0]), (1, parts[2])):
        column = jnp.sum(part.astype(F32), axis=0, keepdims=True)
        d_bias[i : i + 1] = jnp.where(first, 0.0, d_bias[i : i + 1]) + column

    @pl.when(tile == pl.num_programs(0) - 1)
    def _():
        top[...] = total[:split].astype(BF16)
        bottom[...] = total[split:].astype(BF16)


def qkv_grads(split, norm_one, d_q, d_kv):
    count, width = norm_one.shape
    size = d_q.shape[1]
    shapes = [(split, width), (3 * size - split, width), (2, size)]
    return token_call(
        lambda *refs: qkv_grads_kernel(split, *refs),
        count,
        "qkv_grads",
        [shaped(shapes[0]), shaped(shapes[1]), shaped(shapes[2], F32)],
        [tiled(TILE, width), tiled(TILE, size), pl.BlockSpec((2, TILE, size), lambda i: (0, i, 0))],
        [whole(shape) for shape in shapes],
        [pltpu.VMEM((3 * size, width), F32)],
        6 * count * width * size,
        (norm_one, d_q, d_kv),
    )


def turned(part):
    rows, width = part.shape
    step = 384 if rows % 384 == 0 else rows

    def kernel(source, out):
        out[...] = source[...].astype(F32).T

    return pl.pallas_call(
        kernel,
        grid=(rows // step,),
        out_shape=shaped((width, rows), F32),
        in_specs=[tiled(step, width)],
        out_specs=pl.BlockSpec((width, step), lambda i: (0, i)),
        name="turned",
    )(part)


def widened(flat, counts):
    width = flat.shape[1]
    step = next(n for n in (192, 96, 48, 16) if all(count % n == 0 for count in counts))
    starts = [sum(counts[:i]) // step for i in range(len(counts))]
    tiles = [count // step for count in counts]

    def spec(start, size):
        return pl.BlockSpec((step, width), lambda i: (jnp.clip(i - start, 0, size - 1), 0))

    def kernel(source, *outs):
        tile = pl.program_id(0)
        for out, start, size in zip(outs, starts, tiles):

            @pl.when((tile >= start) & (tile < start + size))
            def _():
                out[...] = source[...].astype(F32)

    return pl.pallas_call(
        kernel,
        grid=(sum(tiles),),
        out_shape=[shaped((count, width), F32) for count in counts],
        in_specs=[tiled(step, width)],
        out_specs=[spec(*pair) for pair in zip(starts, tiles)],
        name="widened",
    )(flat)


def body(
    tokens,
    condition,
    cotangent,
    modulator,
    modulator_bias,
    qkv_weight,
    qv_bias,
    out_weight,
    out_bias,
    up_weight,
    up_bias,
    down_weight,
    down_bias,
    segment_ids,
    valid_counts,
):
    wide_count = lax.axis_size("wide")
    narrow_count = lax.axis_size("narrow")
    wide_index = lax.axis_index("wide")
    narrow_index = lax.axis_index("narrow")
    tok_dev, width = cotangent.shape
    share = tokens.shape[0]
    part_width = qkv_weight.shape[2]
    mod_width = modulator.shape[2]
    img_row = condition.shape[0]
    span = IMG_MAX
    own_count = valid_counts[wide_index]
    positions = jnp.arange(tok_dev, dtype=jnp.int32)
    own_ids = lax.dynamic_slice_in_dim(segment_ids, wide_index * tok_dev, tok_dev)
    live = (positions < own_count).astype(F32)[:, None]
    share_start = narrow_index * share
    ids_col, ids_row = own_ids[:, None], own_ids[None]
    onehot_full = (ids_col == jnp.arange(img_row, dtype=jnp.int32)[None]).astype(BF16)

    def own(rows):
        return lax.dynamic_slice_in_dim(rows, share_start, share)

    cond_rows = condition.astype(F32)
    sigmoid_rows = jax.nn.sigmoid(cond_rows)
    activated = (cond_rows * sigmoid_rows).astype(BF16)
    tok_full = narrow_gather(tokens)
    mod_rows = jnp.transpose(modulator, (1, 2, 0)).reshape(6 * mod_width, width)

    def vectors(lo, hi, after=None):
        part = dot(activated, mod_rows[lo * mod_width : hi * mod_width], ((1,), (1,)))
        part = part + modulator_bias[lo:hi].astype(F32).reshape(1, -1)
        rows = jnp.moveaxis(part.astype(BF16).reshape(img_row, hi - lo, -1), 2, 0)
        if after is not None:
            rows, after = lax.optimization_barrier((rows, after))
        return jnp.transpose(narrow_gather(rows), (2, 1, 0)), after

    table_one, _ = vectors(0, 2)
    table_two, tok_full = vectors(2, 6, tok_full)
    flat_qkv = jnp.transpose(qkv_weight, (1, 2, 0)).reshape(3 * part_width, width)
    queries, key_rows, value_rows, norm_one = project(
        tok_full, ids_col, table_one, flat_qkv, qv_bias
    )
    tail_start = own_count - span

    def tail_of(rows):
        return lax.dynamic_slice_in_dim(rows, tail_start, span)

    def to_right(rows):
        return lax.ppermute(rows, "wide", [(i, i + 1) for i in range(wide_count - 1)])

    def to_left(rows):
        return lax.ppermute(rows, "wide", [(i + 1, i) for i in range(wide_count - 1)])

    from_left = to_right(jnp.stack([tail_of(key_rows), tail_of(value_rows)]))
    from_right = to_left(jnp.stack([key_rows[:span], value_rows[:span]]))
    left_index = jnp.maximum(wide_index - 1, 0)
    right_index = jnp.minimum(wide_index + 1, wide_count - 1)
    left_count = valid_counts[left_index]
    left_ids = lax.dynamic_slice_in_dim(segment_ids, left_index * tok_dev + left_count - span, span)
    left_ids = jnp.where(wide_index > 0, left_ids, -2)
    right_ids = lax.dynamic_slice_in_dim(segment_ids, right_index * tok_dev, span)
    right_ids = jnp.where(wide_index < wide_count - 1, right_ids, -2)
    own_keys = jnp.where(positions < own_count, own_ids, -1)
    extended_ids = jnp.concatenate([left_ids, own_keys, right_ids])
    context, log_sums = attention_forward(
        queries, key_rows, value_rows, from_left, from_right, own_keys[:, None], extended_ids[None]
    )
    block = min(512, tok_dev)
    blocks = tok_dev // block

    def rows_of(rows, block_idx):
        return rows[block_idx * block : (block_idx + 1) * block]

    out_row = out_bias[None]
    attn_parts, attn_others, mlp_outs, d_others = [], [], [], []
    for i in range(blocks):
        attn_parts.append(dot(rows_of(context, i), out_weight, ((1,), (0,)), BF16))
        attn_others.append(narrow_other(attn_parts[i]))
    for i in range(blocks):
        operands = [rows_of(rows, i) for rows in (tok_full, cotangent, ids_col, live)]
        mlp_outs.append(
            mlp(
                operands[0],
                attn_parts[i],
                attn_others[i],
                *operands[1:],
                table_two,
                out_row,
                up_weight,
                up_bias[None],
                down_weight,
            )
        )
        d_others.append(narrow_other(mlp_outs[i][4]))
    norm_two, hidden, d_upper, d_branch = [
        jnp.concatenate(parts, axis=0) for parts in list(zip(*mlp_outs))[:4]
    ]
    d_norms = [outs[4] for outs in mlp_outs]
    branch_parts = [outs[5] for outs in mlp_outs]
    up_sum, down_sum = [sum(outs[i] for outs in mlp_outs)[0] for i in (6, 7)]
    up_grad = dot(d_upper, norm_two, ((0,), (0,)), BF16)
    down_grad = dot(hidden, d_branch, ((0,), (0,)), BF16)
    halved = narrow_count == 2 and blocks == 2 and share == block

    def own_of(parts, index):
        if halved:
            return jnp.where(index == 0, parts[0], parts[1])
        return lax.dynamic_slice_in_dim(jnp.concatenate(parts, axis=0), index * share, share)

    if halved:
        branch_other = swap(own_of(branch_parts, 1 - narrow_index))
    if ring_fits([up_grad]):
        mine = ring_scatter([up_grad, down_grad], 1)
        mine, d_others = lax.optimization_barrier((mine, d_others))
        up_grad, down_grad = [
            lax.all_gather(mine[lane], "wide", axis=0, tiled=True) for lane in range(2)
        ]
    else:
        up_grad, down_grad = lax.psum((up_grad, down_grad), "wide")
    if halved:
        branch = own_of(branch_parts, narrow_index).astype(F32) + branch_other.astype(F32)
    else:
        branch = narrow_scatter(jnp.concatenate(branch_parts, axis=0))
    branch = branch + down_bias.astype(F32)
    d_middle, d_context, out_weight_grad, images_two, out_bias_sum = middle_back(
        narrow_count,
        [attn_parts, attn_others, d_norms, d_others],
        tok_full,
        cotangent,
        context,
        ids_col,
        live,
        ids_row,
        table_two,
        out_row,
        out_weight,
    )
    d_context, branch_parts = lax.optimization_barrier((d_context, branch_parts))
    first_bias = jnp.where(narrow_index == 0, down_bias.astype(F32), 0.0)
    d_gate_two = 0.0
    for i in range(blocks):
        term = rows_of(live, i) * rows_of(cotangent, i).astype(F32)
        term = term * (branch_parts[i].astype(F32) + first_bias)
        d_gate_two += dot(rows_of(onehot_full, i), term.astype(BF16), ((0,), (0,)))
    d_gate_two = narrow_scatter(d_gate_two.astype(BF16), 1)
    d_queries, d_own, d_rim = attention_backward(
        queries,
        key_rows,
        value_rows,
        from_left,
        from_right,
        d_context,
        log_sums,
        own_keys[None],
        extended_ids[:, None],
    )
    rims = jnp.stack([to_right(d_rim[1]), to_left(d_rim[0])])
    lane_rows = (4 * part_width * width + 6 * img_row * mod_width) // (2 * width)
    split = min(lane_rows, 3 * part_width - 16)
    d_norm_part, d_kv, images_one = project_back(
        narrow_count, img_row, tok_full, d_queries, d_own, rims, tail_start[None], ids_row, flat_qkv
    )
    top, bottom, qv_sums = qkv_grads(split, norm_one, d_queries, d_kv)

    def mine_of(images):
        return lax.dynamic_index_in_dim(images, narrow_index, 0, keepdims=False)

    if narrow_count == 2:
        theirs = lax.dynamic_index_in_dim(images_one, 1 - narrow_index, 0, keepdims=False)
        early = mine_of(images_one).astype(F32) + swap(theirs).astype(F32)
    else:
        early = mine_of(lax.psum(images_one, "narrow"))
    images_two = mine_of(images_two)
    loose_parts = [up_sum, down_sum, qv_sums[0], qv_sums[1], out_bias_sum[0]]
    longest = max(part.shape[0] for part in loose_parts)
    loose = [jnp.pad(part[None], ((0, 0), (0, longest - part.shape[0]))) for part in loose_parts]
    loose = jnp.concatenate(loose + [jnp.zeros((3, longest), F32)], axis=0)
    terms = [images_two[0], images_two[1], images_two[2], d_gate_two.astype(BF16)]
    d_mod = [early.astype(BF16)]
    d_mod += [jnp.concatenate(terms[2 * i : 2 * i + 2], axis=1) for i in range(2)]
    if 2 * mod_width == width:
        d_mod_flat = jnp.concatenate(d_mod, axis=0)
    else:
        d_mod_flat = jnp.concatenate(d_mod, axis=1).reshape(-1, width)
    rest = jnp.concatenate([bottom, out_weight_grad, d_mod_flat], axis=0)
    if ring_fits([top]) and top.shape == rest.shape:
        flat, d_norm_other, loose = ring_sum([top, rest], d_norm_part, loose, 0)
        d_norm_one = own(d_norm_part).astype(F32) + d_norm_other.astype(F32)
    else:
        d_norm_one = narrow_scatter(d_norm_part)
        flat = jnp.concatenate(lax.psum((top, rest), "wide"), axis=0)
        loose = lax.psum(loose, "wide")
    tok_own = tokens.astype(F32)
    xhat_one, rstd_one = norm(tok_own)
    hot_own = own(onehot_full)
    scale_one = dot(hot_own, table_one[1], ((1,), (0,)))
    tokens_grad = own(d_middle) + norm_back(d_norm_one * (1.0 + scale_one), xhat_one, rstd_one)
    attn_own = sum(own_of(parts, narrow_index).astype(F32) for parts in (attn_parts, attn_others))
    attn_own = attn_own + out_bias.astype(F32)
    live_own = own(live)
    gates = [dot(hot_own, table_two[j], ((1,), (0,))) for j in (0, 3)]
    layer_out = (tok_own + live_own * (gates[0] * attn_own + gates[1] * branch)).astype(BF16)
    up_weight_grad = turned(up_grad)
    down_weight_grad = down_grad.astype(F32)
    keep = 3 * part_width
    qkv_flat, out_weight_grad = widened(flat, (keep, part_width))
    qkv_weight_grad = jnp.transpose(qkv_flat.reshape(3, part_width, width), (2, 0, 1))
    up_bias_grad, down_bias_grad, query_bias, value_bias, out_bias_grad = [
        loose[i, : part.shape[0]] for i, part in enumerate(loose_parts)
    ]
    qv_bias_grad = jnp.stack([query_bias, value_bias])
    d_mod_flat = flat[keep + part_width :]
    if 2 * mod_width == width:
        d_mod = d_mod_flat.reshape(3, img_row, width)
    else:
        d_mod = jnp.moveaxis(d_mod_flat.reshape(img_row, 3, -1), 1, 0)
    modulator_grad = lax.dot_general(
        d_mod, activated, (((1,), (0,)), ((), ())), preferred_element_type=F32
    )
    modulator_grad = jnp.transpose(modulator_grad.reshape(6, mod_width, width), (2, 0, 1))
    modulator_bias_grad = jnp.sum(d_mod.astype(F32), axis=1).reshape(6, mod_width)
    mod_blocks = mod_rows.reshape(3, 2 * mod_width, width)
    d_activated = sum(dot(d_mod[i], mod_blocks[i], ((1,), (0,))) for i in range(3))
    cond_part = d_activated * sigmoid_rows * (1.0 + cond_rows * (1.0 - sigmoid_rows))
    cond_part = cond_part.astype(BF16)
    condition_grad = cond_part.astype(F32) + narrow_other(cond_part).astype(F32)
    return (
        layer_out,
        tokens_grad,
        condition_grad,
        modulator_grad,
        modulator_bias_grad,
        qkv_weight_grad,
        qv_bias_grad,
        out_weight_grad,
        out_bias_grad,
        up_weight_grad,
        up_bias_grad,
        down_weight_grad,
        down_bias_grad,
    )


def solution(mesh):
    in_specs = (
        P(("wide", "narrow"), None),
        P(),
        P("wide", None),
        P(None, None, "narrow"),
        P(None, "narrow"),
        P(None, None, "narrow"),
        P(None, "narrow"),
        P("narrow", None),
        P(),
        P(None, "narrow"),
        P("narrow"),
        P("narrow", None),
        P(),
        P(),
        P(),
    )
    out_specs = (
        P(("wide", "narrow"), None),
        P(("wide", "narrow"), None),
        P(),
        P(None, None, "narrow"),
        P(None, "narrow"),
        P(None, None, "narrow"),
        P(None, "narrow"),
        P("narrow", None),
        P(),
        P(None, "narrow"),
        P("narrow"),
        P("narrow", None),
        P(),
    )
    return jax.shard_map(body, mesh=mesh, in_specs=in_specs, out_specs=out_specs, check_vma=False)
```

```python
import jax
import jax.numpy as jnp
from jax import lax
from jax.experimental import pallas as pl
from jax.experimental.pallas import tpu as pltpu
from jax.sharding import PartitionSpec as P

HD = 72
IMG_MAX = 128
EPSILON = 1e-06
NEG_FILL = -1e30
F32 = jnp.float32
BF16 = jnp.bfloat16


def dot(left, right, dims, out=F32):
    return lax.dot_general(left, right, (dims, ((), ())), preferred_element_type=F32).astype(out)


def swap(part):
    return lax.ppermute(part, "narrow", [(0, 1), (1, 0)])


def narrow_gather(part, other=None):
    if lax.axis_size("narrow") != 2:
        return lax.all_gather(part, "narrow", axis=0, tiled=True)
    other = swap(part) if other is None else other
    first = lax.axis_index("narrow") == 0
    return jnp.where(
        first, jnp.concatenate([part, other], axis=0), jnp.concatenate([other, part], axis=0)
    )


def narrow_other(part):
    if lax.axis_size("narrow") != 2:
        return (lax.psum(part.astype(F32), "narrow") - part.astype(F32)).astype(BF16)
    return swap(part)


def narrow_scatter(part, dim=0):
    count = lax.axis_size("narrow")
    if count != 2:
        return lax.psum_scatter(part, "narrow", scatter_dimension=dim, tiled=True).astype(F32)
    size = part.shape[dim] // 2
    index = lax.axis_index("narrow")
    mine = lax.dynamic_slice_in_dim(part, index * size, size, axis=dim)
    theirs = lax.dynamic_slice_in_dim(part, (1 - index) * size, size, axis=dim)
    return mine.astype(F32) + swap(theirs).astype(F32)


MESH = pl.DeviceIdType.MESH
UNIT = 48


def ring_kernel(chips, subs, full, *refs):
    data = refs[:2]
    if full:
        part, loose, out, landing, loose_out, *refs = refs[2:]
        last, loose_pair, loose_rows, *sems = refs[6:]
        swap_sems, gather_sems, pair_sems, own_sems, loose_pair_sems, loose_sems = sems
    else:
        last, *refs = refs[2:]
    mine, theirs, slots, copy_sems, core_sems, ring_sems = refs[:6]
    wide = lax.axis_index("wide")
    chip, core = wide // 2, wide % 2
    half = chips // 2

    def place(position):
        position = lax.rem(position + 2 * chips, chips)
        side = position // half
        return (1 - side) * 2 * position + side * (2 * (chips - 1 - position) + 1)

    position = chip // 2 + (chip % 2) * (chips - 1 - 2 * (chip // 2))
    ahead = 2 * place(position + 1) + core
    behind = 2 * place(position - 1) + core
    sibling = 2 * chip + 1 - core
    barrier = pltpu.get_barrier_semaphore()
    for device in (ahead, behind, sibling):
        pl.semaphore_signal(barrier, inc=1, device_id={"wide": device}, device_id_type=MESH)
    if full:
        facing = 1 - lax.axis_index("narrow")
        pl.semaphore_signal(barrier, inc=1, device_id={"narrow": facing}, device_id_type=MESH)
    pl.semaphore_wait(barrier, 3 + int(full))

    def local(lane):
        return pltpu.make_async_copy(data[lane].at[:, core], mine.at[lane], copy_sems.at[lane])

    def needed(lane, order):
        return place(position - 1 - order if lane == 0 else position + 1 + order)

    def across(lane, order):
        index = needed(lane, order)
        return pltpu.make_async_remote_copy(
            src_ref=data[lane].at[index, 1 - core],
            dst_ref=theirs.at[lane, index],
            send_sem=core_sems.at[0, lane, order],
            recv_sem=core_sems.at[1, lane, order],
            device_id={"wide": sibling},
            device_id_type=MESH,
        )

    for order in range(chips):
        for lane in range(2):
            across(lane, order).start()
            if order == 0:
                local(lane).start()
    if full:
        share = landing.shape[0]
        turn = pltpu.make_async_remote_copy(
            src_ref=part.at[pl.ds(facing * share, share)],
            dst_ref=landing,
            send_sem=swap_sems.at[0],
            recv_sem=swap_sems.at[1],
            device_id={"narrow": facing},
            device_id_type=MESH,
        )
        turn.start()
        loose_swap = pltpu.make_async_remote_copy(
            src_ref=loose,
            dst_ref=loose_pair,
            send_sem=loose_pair_sems.at[0],
            recv_sem=loose_pair_sems.at[1],
            device_id={"wide": sibling},
            device_id_type=MESH,
        )
        loose_swap.start()

    def loose_hop(step, index):
        return pltpu.make_async_remote_copy(
            src_ref=loose_rows.at[index],
            dst_ref=loose_rows.at[index],
            send_sem=loose_sems.at[0, step],
            recv_sem=loose_sems.at[1, step],
            device_id={"wide": ahead},
            device_id_type=MESH,
        )

    def rows_of(sub):
        return pl.ds(sub * UNIT, UNIT)

    def hop(lane, step, sub):
        rows = rows_of(sub)
        if step == 0:
            first = place(position - 1 if lane == 0 else position + 1)
            source = mine.at[lane, first, rows]
        else:
            source = slots.at[lane, step - 1, rows]
        return pltpu.make_async_remote_copy(
            src_ref=source,
            dst_ref=slots.at[lane, step, rows],
            send_sem=ring_sems.at[0, lane, step, sub],
            recv_sem=ring_sems.at[1, lane, step, sub],
            device_id={"wide": ahead if lane == 0 else behind},
            device_id_type=MESH,
        )

    def held(lane, step, sub, side):
        index = place(position - step if lane == 0 else position + step)
        return out.at[lane, index, side, rows_of(sub)]

    def send_on(lane, step, sub):
        source = last.at[lane, rows_of(sub)] if step == 0 else held(lane, step, sub, core)
        return pltpu.make_async_remote_copy(
            src_ref=source,
            dst_ref=held(lane, step, sub, core),
            send_sem=gather_sems.at[0, lane, step, sub],
            recv_sem=gather_sems.at[1, lane, step, sub],
            device_id={"wide": ahead if lane == 0 else behind},
            device_id_type=MESH,
        )

    def landed(lane, step, sub):
        return pltpu.make_async_remote_copy(
            src_ref=last.at[lane, rows_of(sub)],
            dst_ref=held(lane, step + 1, sub, core),
            send_sem=gather_sems.at[0, lane, step, sub],
            recv_sem=gather_sems.at[1, lane, step, sub],
            device_id={"wide": ahead if lane == 0 else behind},
            device_id_type=MESH,
        )

    def pair(lane, step, sub, side):
        source = last.at[lane, rows_of(sub)] if step == 0 else held(lane, step, sub, core)
        return pltpu.make_async_remote_copy(
            src_ref=source,
            dst_ref=held(lane, step, sub, side),
            send_sem=pair_sems.at[0, lane, step, sub],
            recv_sem=pair_sems.at[1, lane, step, sub],
            device_id={"wide": sibling},
            device_id_type=MESH,
        )

    def keep(lane, sub):
        return pltpu.make_async_copy(
            last.at[lane, rows_of(sub)], held(lane, 0, sub, core), own_sems.at[lane, sub]
        )

    def pair_sum(lane, order, rows):
        index = needed(lane, order)
        return mine[lane, index, rows].astype(F32) + theirs[lane, index, rows].astype(F32)

    for lane in range(2):
        local(lane).wait()
        across(lane, 0).wait_recv()
        for sub in range(subs):
            mine[lane, needed(lane, 0), rows_of(sub)] = pair_sum(lane, 0, rows_of(sub)).astype(BF16)
            hop(lane, 0, sub).start()
    if full:
        loose_swap.wait()
        loose_rows[chip] = loose[...] + loose_pair[...]
        loose_hop(0, chip).start()
    for step in range(chips - 1):
        for sub in range(subs):
            for lane in range(2):
                if sub == 0:
                    across(lane, step + 1).wait_recv()
                rows = rows_of(sub)
                extra = pair_sum(lane, step + 1, rows)
                hop(lane, step, sub).wait_recv()
                total = (slots[lane, step, rows].astype(F32) + extra).astype(BF16)
                if step < chips - 2:
                    slots[lane, step, rows] = total
                    hop(lane, step + 1, sub).start()
                else:
                    last[lane, rows] = total
                    if full:
                        send_on(lane, 0, sub).start()
                        pair(lane, 0, sub, core).start()
                        keep(lane, sub).start()
        if full:
            passed = place(position - 1 - step)
            loose_hop(step, passed).wait_recv()
            if step < chips - 2:
                loose_hop(step + 1, passed).start()
    if full:
        for step in range(chips - 1):
            for sub in range(subs):
                for lane in range(2):
                    landed(lane, step, sub).wait_recv()
                    if step < chips - 2:
                        send_on(lane, step + 1, sub).start()
                    pair(lane, step + 1, sub, core).start()
        loose_out[...] = jnp.sum(loose_rows[...], axis=0)
    for step in range(chips):
        if full and step < chips - 1:
            loose_hop(step, place(position - step)).wait_send()
        for lane in range(2):
            across(lane, step).wait_send()
            for sub in range(subs):
                if step < chips - 1:
                    hop(lane, step, sub).wait_send()
                if full:
                    pair(lane, step, sub, 1 - core).wait_recv()
                    pair(lane, step, sub, core).wait_send()
                    if step == 0:
                        keep(lane, sub).wait()
                    if step < chips - 1:
                        send_on(lane, step, sub).wait_send()
    if full:
        turn.wait()


def ring_scratch(chips, shard, width):
    return [
        pltpu.VMEM((2, chips, shard, width), BF16),
        pltpu.VMEM((2, chips, shard, width), BF16),
        pltpu.VMEM((2, chips - 1, shard, width), BF16),
        pltpu.SemaphoreType.DMA((2,)),
        pltpu.SemaphoreType.DMA((2, 2, chips)),
        pltpu.SemaphoreType.DMA((2, 2, chips - 1, shard // UNIT)),
    ]


def ring_scatter(lanes, collective_id):
    chips = lax.axis_size("wide") // 2
    rows, width = lanes[0].shape
    shard = rows // (2 * chips)
    return pl.pallas_call(
        lambda *refs: ring_kernel(chips, shard // UNIT, False, *refs),
        out_shape=jax.ShapeDtypeStruct((2, shard, width), BF16),
        in_specs=[pl.BlockSpec(memory_space=pl.ANY)] * 2,
        out_specs=pl.BlockSpec(memory_space=pltpu.VMEM),
        scratch_shapes=ring_scratch(chips, shard, width),
        compiler_params=pltpu.CompilerParams(
            collective_id=collective_id, has_side_effects=True, vmem_limit_bytes=40 << 20
        ),
        name="ring_scatter",
    )(*[lane.reshape(chips, 2, shard, width) for lane in lanes])


def ring_sum(lanes, part, loose, collective_id):
    chips = lax.axis_size("wide") // 2
    rows, width = lanes[0].shape
    shard = rows // (2 * chips)
    subs = shard // UNIT
    anywhere = pl.BlockSpec(memory_space=pl.ANY)
    inside = pl.BlockSpec(memory_space=pltpu.VMEM)
    sums, landed, loose_sum = pl.pallas_call(
        lambda *refs: ring_kernel(chips, subs, True, *refs),
        out_shape=[
            jax.ShapeDtypeStruct((2, chips, 2, shard, width), BF16),
            jax.ShapeDtypeStruct((part.shape[0] // 2, part.shape[1]), BF16),
            jax.ShapeDtypeStruct(loose.shape, F32),
        ],
        in_specs=[anywhere] * 3 + [inside],
        out_specs=[anywhere] * 2 + [inside],
        scratch_shapes=ring_scratch(chips, shard, width)
        + [
            pltpu.VMEM((2, shard, width), BF16),
            pltpu.VMEM(loose.shape, F32),
            pltpu.VMEM((chips,) + loose.shape, F32),
            pltpu.SemaphoreType.DMA((2,)),
            pltpu.SemaphoreType.DMA((2, 2, chips - 1, subs)),
            pltpu.SemaphoreType.DMA((2, 2, chips, subs)),
            pltpu.SemaphoreType.DMA((2, subs)),
            pltpu.SemaphoreType.DMA((2,)),
            pltpu.SemaphoreType.DMA((2, chips - 1)),
        ],
        compiler_params=pltpu.CompilerParams(
            collective_id=collective_id, has_side_effects=True, vmem_limit_bytes=40 << 20
        ),
        name="ring_sum",
    )(*[lane.reshape(chips, 2, shard, width) for lane in lanes], part, loose)
    return sums.reshape(2 * rows, width), landed, loose_sum


def ring_fits(lanes):
    count = lax.axis_size("wide")
    return lax.axis_size("narrow") == 2 and lanes[0].shape[0] % (count * UNIT) == 0


TILE = 256
LOG2E = 1.4426950408889634


def head_lanes(part_width):
    for head in range(part_width // HD):
        lo = head * HD // 128 * 128
        hi = min(-(-(head + 1) * HD // 128) * 128, part_width)
        lanes = lax.broadcasted_iota(jnp.int32, (1, hi - lo), 1) + lo
        yield head, lo, hi, (lanes >= head * HD) & (lanes < (head + 1) * HD)


def extend(first, left, own, right, ext):
    span = left.shape[1]
    ends = ext.shape[1] - span

    @pl.when(first)
    def _():
        for which in range(2):
            ext[which, :span] = left[which]
            ext[which, span:ends] = own[which][...]
            ext[which, ends:] = right[which]


def forward_kernel(tiles, q, k, v, left, right, q_ids, k_ids, out, lse, ext, total):
    tile = pl.program_id(0)
    part_width = q.shape[1]
    span = left.shape[1]
    ends = ext.shape[1] - span
    extend(tile == 0, left, (k, v), right, ext)
    scale = LOG2E * HD ** (-0.5)

    def run(extra):
        rows = pl.ds(pl.multiple_of(tile * TILE, TILE), TILE + 2 * span)
        keys, values = ext[0, rows], ext[1, rows]
        ids = k_ids[:, rows]
        if extra:
            keys = jnp.concatenate([keys, ext[0, ends:]], axis=0)
            values = jnp.concatenate([values, ext[1, ends:]], axis=0)
            ids = jnp.concatenate([ids, k_ids[:, ends:]], axis=1)
        same = q_ids[...] == ids
        queries = q[...]
        total[...] = jnp.zeros_like(total)
        packed = jnp.zeros((TILE, 128), F32)
        column = lax.broadcasted_iota(jnp.int32, (TILE, 128), 1)
        for head, lo, hi, mask in head_lanes(part_width):
            chosen = jnp.where(mask, queries[:, lo:hi], 0)
            scores = lax.dot_general(
                chosen, keys[:, lo:hi], (((1,), (1,)), ((), ())), preferred_element_type=F32
            )
            scores = jnp.where(same, scores * scale, NEG_FILL)
            top = jnp.max(scores, axis=1, keepdims=True)
            expo = jnp.exp2(scores - top)
            count = jnp.sum(expo, axis=1, keepdims=True)
            part = jnp.dot(expo.astype(BF16), values[:, lo:hi], preferred_element_type=F32)
            total[:, lo:hi] += jnp.where(mask, part / count, 0.0)
            packed = jnp.where(column == head, top + jnp.log2(count), packed)
        out[...] = total[...].astype(BF16)
        lse[...] = packed.T[: lse.shape[0]]

    split_tiles(tile, tiles, run)


def split_tiles(tile, tiles, run):
    first_extra = tiles - 512 // TILE
    extra = (tile >= first_extra) & (tile < tiles - 1)
    pl.when(extra)(lambda: run(True))
    pl.when(jnp.logical_not(extra))(lambda: run(False))


def rim_specs(part_width, span, tok_dev):
    whole = lambda shape: pl.BlockSpec(shape, lambda i: (0,) * len(shape))
    return whole((tok_dev, part_width)), whole((2, span, part_width))


def attention_forward(q, k, v, left, right, q_ids, k_ids):
    tok_dev, part_width = q.shape
    span = left.shape[1]
    tiles = tok_dev // TILE
    head_rows = -(-(part_width // HD) // 8) * 8
    own_spec, rim_spec = rim_specs(part_width, span, tok_dev)
    return pl.pallas_call(
        lambda *refs: forward_kernel(tiles, *refs),
        grid=(tiles,),
        out_shape=[
            jax.ShapeDtypeStruct((tok_dev, part_width), BF16),
            jax.ShapeDtypeStruct((head_rows, tok_dev), F32),
        ],
        in_specs=[
            pl.BlockSpec((TILE, part_width), lambda i: (i, 0)),
            own_spec,
            own_spec,
            rim_spec,
            rim_spec,
            pl.BlockSpec((TILE, 1), lambda i: (i, 0)),
            pl.BlockSpec((1, tok_dev + 2 * span), lambda i: (0, 0)),
        ],
        out_specs=[
            pl.BlockSpec((TILE, part_width), lambda i: (i, 0)),
            pl.BlockSpec((head_rows, TILE), lambda i: (0, i)),
        ],
        scratch_shapes=[
            pltpu.VMEM((2, tok_dev + 2 * span, part_width), BF16),
            pltpu.VMEM((TILE, part_width), F32),
        ],
        compiler_params=pltpu.CompilerParams(vmem_limit_bytes=40 << 20),
        cost_estimate=pl.CostEstimate(
            flops=4 * tok_dev * 512 * part_width,
            transcendentals=tok_dev * 512 * 8,
            bytes_accessed=8 * tok_dev * part_width,
        ),
        name="attention_forward",
    )(q, k, v, left, right, q_ids, k_ids)


def backward_kernel(tiles, q, k, v, left, right, grad, lse, q_ids, k_ids, *refs):
    d_q, d_own, d_rim, ext, d_ext, total = refs
    tile = pl.program_id(0)
    part_width = q.shape[1]
    span = left.shape[1]
    ends = ext.shape[1] - span
    extend(tile == 0, left, (k, v), right, ext)
    scale = HD ** (-0.5)

    @pl.when(tile == 0)
    def _():
        d_ext[...] = jnp.zeros_like(d_ext)

    def run(extra):
        rows = pl.ds(pl.multiple_of(tile * TILE, TILE), TILE + 2 * span)
        keys, values = ext[0, rows], ext[1, rows]
        ids = k_ids[rows]
        if extra:
            keys = jnp.concatenate([keys, ext[0, ends:]], axis=0)
            values = jnp.concatenate([values, ext[1, ends:]], axis=0)
            ids = jnp.concatenate([ids, k_ids[ends:]], axis=0)
        same = ids == q_ids[...]
        queries, grads = q[...], grad[...]
        total[...] = jnp.zeros_like(total)

        def across(left_side, right_side, dims):
            return lax.dot_general(
                left_side, right_side, (dims, ((), ())), preferred_element_type=F32
            )

        for head, lo, hi, mask in head_lanes(part_width):
            chosen = jnp.where(mask, queries[:, lo:hi], 0)
            pulled = jnp.where(mask, grads[:, lo:hi], 0)
            scores = across(keys[:, lo:hi], chosen, ((1,), (1,)))
            scores = jnp.where(same, scores * (scale * LOG2E), NEG_FILL)
            attend = jnp.exp2(scores - lse[head : head + 1])
            d_attend = across(values[:, lo:hi], pulled, ((1,), (1,)))
            centre = jnp.sum(attend * d_attend, axis=0, keepdims=True)
            d_scores = (attend * (d_attend - centre)).astype(BF16)
            d_key = across(d_scores, chosen, ((1,), (0,)))
            d_value = across(attend.astype(BF16), pulled, ((1,), (0,)))
            length = TILE + 2 * span
            d_ext[0, rows, lo:hi] += d_key[:length]
            d_ext[1, rows, lo:hi] += d_value[:length]
            if extra:
                d_ext[0, ends:, lo:hi] += d_key[length:]
                d_ext[1, ends:, lo:hi] += d_value[length:]
            d_query = across(d_scores, keys[:, lo:hi], ((0,), (0,)))
            total[:, lo:hi] += jnp.where(mask, d_query, 0.0)
        d_q[...] = (total[...] * scale).astype(BF16)

    split_tiles(tile, tiles, run)

    @pl.when(tile == tiles - 1)
    def _():
        for which, factor in ((0, scale), (1, 1.0)):
            d_rim[0, which] = (d_ext[which, :span] * factor).astype(BF16)
            d_own[which] = (d_ext[which, span:ends] * factor).astype(BF16)
            d_rim[1, which] = (d_ext[which, ends:] * factor).astype(BF16)


def attention_backward(q, k, v, left, right, grad, lse, q_ids, k_ids):
    tok_dev, part_width = q.shape
    span = left.shape[1]
    tiles = tok_dev // TILE
    own_spec, rim_spec = rim_specs(part_width, span, tok_dev)
    tile_spec = pl.BlockSpec((TILE, part_width), lambda i: (i, 0))
    return pl.pallas_call(
        lambda *refs: backward_kernel(tiles, *refs),
        grid=(tiles,),
        out_shape=[
            jax.ShapeDtypeStruct((tok_dev, part_width), BF16),
            jax.ShapeDtypeStruct((2, tok_dev, part_width), BF16),
            jax.ShapeDtypeStruct((2, 2, span, part_width), BF16),
        ],
        in_specs=[
            tile_spec,
            own_spec,
            own_spec,
            rim_spec,
            rim_spec,
            tile_spec,
            pl.BlockSpec((lse.shape[0], TILE), lambda i: (0, i)),
            pl.BlockSpec((1, TILE), lambda i: (0, i)),
            pl.BlockSpec((tok_dev + 2 * span, 1), lambda i: (0, 0)),
        ],
        out_specs=[
            tile_spec,
            pl.BlockSpec((2, tok_dev, part_width), lambda i: (0, 0, 0)),
            pl.BlockSpec((2, 2, span, part_width), lambda i: (0, 0, 0, 0)),
        ],
        scratch_shapes=[
            pltpu.VMEM((2, tok_dev + 2 * span, part_width), BF16),
            pltpu.VMEM((2, tok_dev + 2 * span, part_width), F32),
            pltpu.VMEM((TILE, part_width), F32),
        ],
        compiler_params=pltpu.CompilerParams(vmem_limit_bytes=48 << 20),
        cost_estimate=pl.CostEstimate(
            flops=10 * tok_dev * 512 * part_width,
            transcendentals=tok_dev * 512 * 8,
            bytes_accessed=16 * tok_dev * part_width,
        ),
        name="attention_backward",
    )(q, k, v, left, right, grad, lse, q_ids, k_ids)


def norm(field):
    centred = field - jnp.mean(field, axis=-1, keepdims=True)
    rstd = lax.rsqrt(jnp.mean(centred * centred, axis=-1, keepdims=True) + EPSILON)
    return centred * rstd, rstd


def norm_back(grad, xhat, rstd):
    return rstd * (
        grad
        - jnp.mean(grad, axis=-1, keepdims=True)
        - xhat * jnp.mean(grad * xhat, axis=-1, keepdims=True)
    )


def gelu_pair(v):
    c = 0.7978845608028654
    sq = v * v
    t = jnp.tanh(c * v * (1.0 + 0.044715 * sq))
    half = 0.5 * (1.0 + t)
    slope = half + 0.5 * v * (1.0 - t * t) * c * (1.0 + 3 * 0.044715 * sq)
    return v * half, slope


def matmul(left, right, dims=((1,), (0,))):
    return lax.dot_general(left, right, (dims, ((), ())), preferred_element_type=F32)


def pick(ids, table):
    slots = lax.broadcasted_iota(jnp.int32, (ids.shape[0], table.shape[0]), 1)
    return matmul((ids == slots).astype(BF16), table)


def gather_images(ids, terms, sums, fresh):
    slots = lax.broadcasted_iota(jnp.int32, (sums.shape[1], ids.shape[1]), 0)
    hot = (ids == slots).astype(BF16)
    for i, term in enumerate(terms):
        part = matmul(hot, term.astype(BF16))
        sums[i] = jnp.where(fresh, 0.0, sums[i]) + part


def halves_out(sums, out, halves):
    size = sums.shape[2] // halves
    for half in range(halves):
        for i in range(sums.shape[0]):
            out[half, i] = sums[i, :, half * size : (half + 1) * size].astype(BF16)


def whole(shape):
    return pl.BlockSpec(shape, lambda i: (0,) * len(shape))


def tiled(rows, width):
    return pl.BlockSpec((rows, width), lambda i: (i, 0))


def token_call(kernel, tokens, name, out_shape, in_specs, out_specs, scratch, flops, operands):
    size = sum(x.size * x.dtype.itemsize for x in operands)
    return pl.pallas_call(
        kernel,
        grid=(tokens // TILE,),
        out_shape=out_shape,
        in_specs=in_specs,
        out_specs=out_specs,
        scratch_shapes=scratch,
        compiler_params=pltpu.CompilerParams(vmem_limit_bytes=60 << 20),
        cost_estimate=pl.CostEstimate(
            flops=flops, transcendentals=0, bytes_accessed=size + size // 2
        ),
        name=name,
    )(*operands)


def shaped(shape, dtype=BF16):
    return jax.ShapeDtypeStruct(shape, dtype)


def project_kernel(split, *refs):
    if split:
        index, mine, theirs, *refs = refs
        held = pl.program_id(0) // (pl.num_programs(0) // 2) == index[0]
        rows = jnp.where(held, mine[...], theirs[...])
    else:
        tokens, *refs = refs
        rows = tokens[...]
    ids, table, weight, bias, q, k, v, norm_one = refs
    xhat, _ = norm(rows.astype(F32))
    normed = (xhat * (1.0 + pick(ids[...], table[1])) + pick(ids[...], table[0])).astype(BF16)
    norm_one[...] = normed
    size = q.shape[1]
    for i, out in enumerate((q, k, v)):
        rows = matmul(normed, weight[i * size : (i + 1) * size], ((1,), (1,)))
        if i != 1:
            rows = rows + bias[i // 2 : i // 2 + 1].astype(F32)
        out[...] = rows.astype(BF16)


def project(sources, ids, table, weight, bias):
    split = len(sources) == 3
    count, width = ids.shape[0], weight.shape[1]
    size = weight.shape[0] // 3
    specs = [tiled(TILE, width)]
    if split:
        half = pl.BlockSpec((TILE, width), lambda i: (i % (count // TILE // 2), 0))
        specs = [pl.BlockSpec(memory_space=pltpu.SMEM), half, half]
    return token_call(
        lambda *refs: project_kernel(split, *refs),
        count,
        "project",
        [shaped((count, size))] * 3 + [shaped((count, width))],
        specs + [tiled(TILE, 1), whole(table.shape), whole(weight.shape), whole(bias.shape)],
        [tiled(TILE, size)] * 3 + [tiled(TILE, width)],
        [],
        6 * count * width * size,
        tuple(sources) + (ids, table, weight, bias),
    )


def mlp_kernel(
    tokens, mine, theirs, cotangent, ids, live, table, out_bias, up, up_bias, down, *outs
):
    norm_two, hidden, d_upper, d_branch, d_norm, branch, up_sum, down_sum = outs
    first = pl.program_id(0) == 0
    ids, live = ids[...], live[...]
    attn = mine[...].astype(F32) + theirs[...].astype(F32) + out_bias[...].astype(F32)
    middle = tokens[...].astype(F32) + live * pick(ids, table[0]) * attn
    xhat, _ = norm(middle)
    normed = (xhat * (1.0 + pick(ids, table[2])) + pick(ids, table[1])).astype(BF16)
    norm_two[...] = normed
    pulled = (live * pick(ids, table[3]) * cotangent[...].astype(F32)).astype(BF16)
    d_branch[...] = pulled
    column = jnp.sum(pulled.astype(F32), axis=0, keepdims=True)
    down_sum[...] = jnp.where(first, 0.0, down_sum[...]) + column
    width = up.shape[1]
    step = 384 if width % 384 == 0 else width
    back = ahead = 0.0
    for lo in range(0, width, step):
        cols = slice(lo, lo + step)
        upper = matmul(normed, up[:, cols]) + up_bias[:, cols].astype(F32)
        d_hidden = matmul(pulled, down[cols], ((1,), (1,)))
        value, slope = gelu_pair(upper)
        value = value.astype(BF16)
        d_up = (d_hidden * slope).astype(BF16)
        hidden[:, cols] = value
        d_upper[:, cols] = d_up
        column = jnp.sum(d_up.astype(F32), axis=0, keepdims=True)
        up_sum[:, cols] = jnp.where(first, 0.0, up_sum[:, cols]) + column
        back += matmul(d_up, up[:, cols], ((1,), (1,)))
        ahead += matmul(value, down[cols])
    d_norm[...] = back.astype(BF16)
    branch[...] = ahead.astype(BF16)


def mlp(start, tokens, mine, theirs, cotangent, ids, live, table, out_bias, up, up_bias, down):
    count, width = mine.shape
    size = up.shape[1]
    first = start // TILE
    here = tiled(TILE, width)
    row = pl.BlockSpec((TILE, width), lambda i: (i + first, 0))
    col = pl.BlockSpec((TILE, 1), lambda i: (i + first, 0))
    consts = (table, out_bias, up, up_bias, down)
    return token_call(
        mlp_kernel,
        count,
        "mlp",
        [shaped((count, n)) for n in (width, size, size, width, width, width)]
        + [shaped((1, n), F32) for n in (size, width)],
        [row, here, here, row, col, col] + [whole(x.shape) for x in consts],
        [tiled(TILE, n) for n in (width, size, size, width, width, width)]
        + [whole((1, n)) for n in (size, width)],
        [],
        8 * count * width * size,
        (tokens, mine, theirs, cotangent, ids, live) + consts,
    )


def middle_kernel(halves, blocks, *refs):
    tokens, cotangent, context, ids, live, ids_row, *refs = refs
    parts = [refs[i * blocks : (i + 1) * blocks] for i in range(4)]
    table, out_bias, weight, d_middle, d_context, d_weight, d_images, d_bias, sums, total = refs[
        4 * blocks :
    ]
    tile = pl.program_id(0)
    first = tile == 0
    last = tile == pl.num_programs(0) - 1

    def rows_at(refs):
        rows = refs[0][...]
        for i in range(1, blocks):
            rows = jnp.where(tile >= i * (pl.num_programs(0) // blocks), refs[i][...], rows)
        return rows.astype(F32)

    mine, theirs, d_own, d_other = [rows_at(part) for part in parts]
    ids, live = ids[...], live[...]
    gate = live * pick(ids, table[0])
    attn = mine + theirs + out_bias[...].astype(F32)
    xhat, rstd = norm(tokens[...].astype(F32) + gate * attn)
    d_norm = d_own + d_other
    grad = cotangent[...].astype(F32) + norm_back(d_norm * (1.0 + pick(ids, table[2])), xhat, rstd)
    d_middle[...] = grad
    d_attn = (gate * grad).astype(BF16)
    d_context[...] = matmul(d_attn, weight[...], ((1,), (1,))).astype(BF16)
    part = matmul(context[...], d_attn, ((0,), (0,)))
    total[...] = jnp.where(first, 0.0, total[...]) + part
    column = jnp.sum(d_attn.astype(F32), axis=0, keepdims=True)
    d_bias[...] = jnp.where(first, 0.0, d_bias[...]) + column
    gather_images(ids_row[...], (live * grad * attn, d_norm, d_norm * xhat), sums, first)

    @pl.when(last)
    def _():
        d_weight[...] = total[...].astype(BF16)
        halves_out(sums, d_images, halves)


def middle_back(halves, parts, tokens, cotangent, context, ids, live, ids_row, table, out_bias, weight):
    count, width = tokens.shape
    size = context.shape[1]
    images = table.shape[1]
    blocks = len(parts[0])
    tiles = count // TILE // blocks
    row, col = tiled(TILE, width), tiled(TILE, 1)
    consts = (table, out_bias, weight)

    def block_spec(i):
        return pl.BlockSpec((TILE, width), lambda t: (jnp.clip(t - i * tiles, 0, tiles - 1), 0))

    return token_call(
        lambda *refs: middle_kernel(halves, blocks, *refs),
        count,
        "middle_back",
        [
            shaped((count, width), F32),
            shaped((count, size)),
            shaped((size, width)),
            shaped((halves, 3, images, width // halves)),
            shaped((1, width), F32),
        ],
        [row, row, tiled(TILE, size), col, col, pl.BlockSpec((1, TILE), lambda i: (0, i))]
        + [block_spec(i) for _ in parts for i in range(blocks)]
        + [whole(x.shape) for x in consts],
        [
            row,
            tiled(TILE, size),
            whole((size, width)),
            whole((halves, 3, images, width // halves)),
            whole((1, width)),
        ],
        [pltpu.VMEM((3, images, width), F32), pltpu.VMEM((size, width), F32)],
        4 * count * width * size,
        (tokens, cotangent, context, ids, live, ids_row) + tuple(sum(parts, [])) + consts,
    )


def project_back_kernel(halves, tokens, d_q, d_own, rims, tail_start, ids_row, weight, *refs):
    d_norm, d_kv, d_images, sums = refs
    tile = pl.program_id(0)
    span, size = rims.shape[2], d_q.shape[1]
    rows = lax.broadcasted_iota(jnp.int32, (TILE, span), 0) + tile * TILE
    cols = lax.broadcasted_iota(jnp.int32, (TILE, span), 1)
    head_rim = (rows == cols).astype(BF16)
    tail_rim = (rows == cols + tail_start[0]).astype(BF16)
    back = matmul(d_q[...], weight[:size])
    for which in range(2):
        rim = matmul(head_rim, rims[0, which]) + matmul(tail_rim, rims[1, which])
        part = (d_own[which].astype(F32) + rim).astype(BF16)
        d_kv[which] = part
        back += matmul(part, weight[(which + 1) * size : (which + 2) * size])
    back = back.astype(BF16)
    d_norm[...] = back
    xhat, _ = norm(tokens[...].astype(F32))
    back = back.astype(F32)
    gather_images(ids_row[...], (back, back * xhat), sums, tile == 0)

    @pl.when(tile == pl.num_programs(0) - 1)
    def _():
        part = sums.shape[2] // halves
        for half in range(halves):
            cut = slice(half * part, (half + 1) * part)
            both = jnp.concatenate([sums[0, :, cut], sums[1, :, cut]], axis=1)
            d_images[half] = both.astype(BF16)


def project_back(halves, images, tokens, d_q, d_own, rims, tail_start, ids_row, weight):
    count, width = tokens.shape
    size = d_q.shape[1]
    row = tiled(TILE, width)
    pair = pl.BlockSpec((2, TILE, size), lambda i: (0, i, 0))
    sums = (halves, images, 2 * width // halves)
    return token_call(
        lambda *refs: project_back_kernel(halves, *refs),
        count,
        "project_back",
        [shaped((count, width)), shaped((2, count, size)), shaped(sums)],
        [
            row,
            tiled(TILE, size),
            pair,
            whole(rims.shape),
            pl.BlockSpec(memory_space=pltpu.SMEM),
            pl.BlockSpec((1, TILE), lambda i: (0, i)),
            whole(weight.shape),
        ],
        [row, pair, whole(sums)],
        [pltpu.VMEM((2, images, width), F32)],
        6 * count * width * size,
        (tokens, d_q, d_own, rims, tail_start, ids_row, weight),
    )


def qkv_grads_kernel(split, norm_one, d_q, d_kv, top, bottom, d_bias, total):
    tile = pl.program_id(0)
    first = tile == 0
    size = d_q.shape[1]
    parts = [d_q[...], d_kv[0], d_kv[1]]
    normed = norm_one[...]
    for i, part in enumerate(parts):
        rows = slice(i * size, (i + 1) * size)
        total[rows] = jnp.where(first, 0.0, total[rows]) + matmul(part, normed, ((0,), (0,)))
    for i, part in ((0, parts[0]), (1, parts[2])):
        column = jnp.sum(part.astype(F32), axis=0, keepdims=True)
        d_bias[i : i + 1] = jnp.where(first, 0.0, d_bias[i : i + 1]) + column

    @pl.when(tile == pl.num_programs(0) - 1)
    def _():
        top[...] = total[:split].astype(BF16)
        bottom[...] = total[split:].astype(BF16)


def qkv_grads(split, norm_one, d_q, d_kv):
    count, width = norm_one.shape
    size = d_q.shape[1]
    shapes = [(split, width), (3 * size - split, width), (2, size)]
    return token_call(
        lambda *refs: qkv_grads_kernel(split, *refs),
        count,
        "qkv_grads",
        [shaped(shapes[0]), shaped(shapes[1]), shaped(shapes[2], F32)],
        [tiled(TILE, width), tiled(TILE, size), pl.BlockSpec((2, TILE, size), lambda i: (0, i, 0))],
        [whole(shape) for shape in shapes],
        [pltpu.VMEM((3 * size, width), F32)],
        6 * count * width * size,
        (norm_one, d_q, d_kv),
    )


def turned(part):
    rows, width = part.shape
    step = 384 if rows % 384 == 0 else rows

    def kernel(source, out):
        out[...] = source[...].astype(F32).T

    return pl.pallas_call(
        kernel,
        grid=(rows // step,),
        out_shape=shaped((width, rows), F32),
        in_specs=[tiled(step, width)],
        out_specs=pl.BlockSpec((width, step), lambda i: (0, i)),
        name="turned",
    )(part)


def widened(flat, counts):
    width = flat.shape[1]
    step = next(n for n in (192, 96, 48, 16) if all(count % n == 0 for count in counts))
    starts = [sum(counts[:i]) // step for i in range(len(counts))]
    tiles = [count // step for count in counts]

    def spec(start, size):
        return pl.BlockSpec((step, width), lambda i: (jnp.clip(i - start, 0, size - 1), 0))

    def kernel(source, *outs):
        tile = pl.program_id(0)
        for out, start, size in zip(outs, starts, tiles):

            @pl.when((tile >= start) & (tile < start + size))
            def _():
                out[...] = source[...].astype(F32)

    return pl.pallas_call(
        kernel,
        grid=(sum(tiles),),
        out_shape=[shaped((count, width), F32) for count in counts],
        in_specs=[tiled(step, width)],
        out_specs=[spec(*pair) for pair in zip(starts, tiles)],
        name="widened",
    )(flat)


def body(
    tokens,
    condition,
    cotangent,
    modulator,
    modulator_bias,
    qkv_weight,
    qv_bias,
    out_weight,
    out_bias,
    up_weight,
    up_bias,
    down_weight,
    down_bias,
    segment_ids,
    valid_counts,
):
    wide_count = lax.axis_size("wide")
    narrow_count = lax.axis_size("narrow")
    wide_index = lax.axis_index("wide")
    narrow_index = lax.axis_index("narrow")
    tok_dev, width = cotangent.shape
    share = tokens.shape[0]
    part_width = qkv_weight.shape[2]
    mod_width = modulator.shape[2]
    img_row = condition.shape[0]
    span = IMG_MAX
    own_count = valid_counts[wide_index]
    positions = jnp.arange(tok_dev, dtype=jnp.int32)
    own_ids = lax.dynamic_slice_in_dim(segment_ids, wide_index * tok_dev, tok_dev)
    live = (positions < own_count).astype(F32)[:, None]
    share_start = narrow_index * share
    ids_col, ids_row = own_ids[:, None], own_ids[None]
    onehot_full = (ids_col == jnp.arange(img_row, dtype=jnp.int32)[None]).astype(BF16)

    def own(rows):
        return lax.dynamic_slice_in_dim(rows, share_start, share)

    cond_rows = condition.astype(F32)
    sigmoid_rows = jax.nn.sigmoid(cond_rows)
    activated = (cond_rows * sigmoid_rows).astype(BF16)
    halves_held = narrow_count == 2 and share % TILE == 0
    tok_other = swap(tokens) if halves_held else None
    tok_full = narrow_gather(tokens, tok_other)
    mod_rows = jnp.transpose(modulator, (1, 2, 0)).reshape(6 * mod_width, width)

    def vectors(lo, hi):
        part = dot(activated, mod_rows[lo * mod_width : hi * mod_width], ((1,), (1,)))
        part = part + modulator_bias[lo:hi].astype(F32).reshape(1, -1)
        rows = jnp.moveaxis(part.astype(BF16).reshape(img_row, hi - lo, -1), 2, 0)
        return rows

    def table_of(rows, other=None):
        return jnp.transpose(narrow_gather(rows, other), (2, 1, 0))

    table_one = table_of(vectors(0, 2))
    rows_two = vectors(2, 6)
    sources = [narrow_index[None], tokens, tok_other] if halves_held else [tok_full]
    rows_two, sources[-1] = lax.optimization_barrier((rows_two, sources[-1]))
    other_two = swap(rows_two) if narrow_count == 2 else None
    flat_qkv = jnp.transpose(qkv_weight, (1, 2, 0)).reshape(3 * part_width, width)
    queries, key_rows, value_rows, norm_one = project(
        sources, ids_col, table_one, flat_qkv, qv_bias
    )
    other_two, queries = lax.optimization_barrier((other_two, queries))
    table_two = table_of(rows_two, other_two)
    tail_start = own_count - span

    def tail_of(rows):
        return lax.dynamic_slice_in_dim(rows, tail_start, span)

    def to_right(rows):
        return lax.ppermute(rows, "wide", [(i, i + 1) for i in range(wide_count - 1)])

    def to_left(rows):
        return lax.ppermute(rows, "wide", [(i + 1, i) for i in range(wide_count - 1)])

    from_left = to_right(jnp.stack([tail_of(key_rows), tail_of(value_rows)]))
    from_right = to_left(jnp.stack([key_rows[:span], value_rows[:span]]))
    left_index = jnp.maximum(wide_index - 1, 0)
    right_index = jnp.minimum(wide_index + 1, wide_count - 1)
    left_count = valid_counts[left_index]
    left_ids = lax.dynamic_slice_in_dim(segment_ids, left_index * tok_dev + left_count - span, span)
    left_ids = jnp.where(wide_index > 0, left_ids, -2)
    right_ids = lax.dynamic_slice_in_dim(segment_ids, right_index * tok_dev, span)
    right_ids = jnp.where(wide_index < wide_count - 1, right_ids, -2)
    own_keys = jnp.where(positions < own_count, own_ids, -1)
    extended_ids = jnp.concatenate([left_ids, own_keys, right_ids])
    context, log_sums = attention_forward(
        queries, key_rows, value_rows, from_left, from_right, own_keys[:, None], extended_ids[None]
    )
    block = min(512, tok_dev)
    blocks = tok_dev // block

    def rows_of(rows, block_idx):
        return rows[block_idx * block : (block_idx + 1) * block]

    out_row = out_bias[None]
    attn_parts, attn_others, mlp_outs, d_others = [], [], [], []
    for i in range(blocks):
        attn_parts.append(dot(rows_of(context, i), out_weight, ((1,), (0,)), BF16))
        attn_others.append(narrow_other(attn_parts[i]))
    for i in range(blocks):
        mlp_outs.append(
            mlp(
                i * block,
                tok_full,
                attn_parts[i],
                attn_others[i],
                cotangent,
                ids_col,
                live,
                table_two,
                out_row,
                up_weight,
                up_bias[None],
                down_weight,
            )
        )
        d_others.append(narrow_other(mlp_outs[i][4]))
    norm_two, hidden, d_upper, d_branch = [
        jnp.concatenate(parts, axis=0) for parts in list(zip(*mlp_outs))[:4]
    ]
    d_norms = [outs[4] for outs in mlp_outs]
    branch_parts = [outs[5] for outs in mlp_outs]
    up_sum, down_sum = [sum(outs[i] for outs in mlp_outs)[0] for i in (6, 7)]
    up_grad = dot(d_upper, norm_two, ((0,), (0,)), BF16)
    down_grad = dot(hidden, d_branch, ((0,), (0,)), BF16)
    halved = narrow_count == 2 and blocks == 2 and share == block

    def own_of(parts, index):
        if halved:
            return jnp.where(index == 0, parts[0], parts[1])
        return lax.dynamic_slice_in_dim(jnp.concatenate(parts, axis=0), index * share, share)

    if halved:
        branch_other = swap(own_of(branch_parts, 1 - narrow_index))
    if ring_fits([up_grad]):
        mine = ring_scatter([up_grad, down_grad], 1)
        mine, d_others = lax.optimization_barrier((mine, d_others))
        up_grad, down_grad = [
            lax.all_gather(mine[lane], "wide", axis=0, tiled=True) for lane in range(2)
        ]
    else:
        up_grad, down_grad = lax.psum((up_grad, down_grad), "wide")
    if halved:
        branch = own_of(branch_parts, narrow_index).astype(F32) + branch_other.astype(F32)
    else:
        branch = narrow_scatter(jnp.concatenate(branch_parts, axis=0))
    branch = branch + down_bias.astype(F32)
    d_middle, d_context, out_weight_grad, images_two, out_bias_sum = middle_back(
        narrow_count,
        [attn_parts, attn_others, d_norms, d_others],
        tok_full,
        cotangent,
        context,
        ids_col,
        live,
        ids_row,
        table_two,
        out_row,
        out_weight,
    )
    d_context, branch_parts = lax.optimization_barrier((d_context, branch_parts))
    first_bias = jnp.where(narrow_index == 0, down_bias.astype(F32), 0.0)
    d_gate_two = 0.0
    for i in range(blocks):
        term = rows_of(live, i) * rows_of(cotangent, i).astype(F32)
        term = term * (branch_parts[i].astype(F32) + first_bias)
        d_gate_two += dot(rows_of(onehot_full, i), term.astype(BF16), ((0,), (0,)))
    d_gate_two = narrow_scatter(d_gate_two.astype(BF16), 1)
    d_queries, d_own, d_rim = attention_backward(
        queries,
        key_rows,
        value_rows,
        from_left,
        from_right,
        d_context,
        log_sums,
        own_keys[None],
        extended_ids[:, None],
    )
    rims = jnp.stack([to_right(d_rim[1]), to_left(d_rim[0])])
    lane_rows = (4 * part_width * width + 6 * img_row * mod_width) // (2 * width)
    split = min(lane_rows, 3 * part_width - 16)
    d_norm_part, d_kv, images_one = project_back(
        narrow_count, img_row, tok_full, d_queries, d_own, rims, tail_start[None], ids_row, flat_qkv
    )
    top, bottom, qv_sums = qkv_grads(split, norm_one, d_queries, d_kv)

    def mine_of(images):
        return lax.dynamic_index_in_dim(images, narrow_index, 0, keepdims=False)

    if narrow_count == 2:
        theirs = lax.dynamic_index_in_dim(images_one, 1 - narrow_index, 0, keepdims=False)
        early = mine_of(images_one).astype(F32) + swap(theirs).astype(F32)
    else:
        early = mine_of(lax.psum(images_one, "narrow"))
    images_two = mine_of(images_two)
    loose_parts = [up_sum, down_sum, qv_sums[0], qv_sums[1], out_bias_sum[0]]
    longest = max(part.shape[0] for part in loose_parts)
    loose = [jnp.pad(part[None], ((0, 0), (0, longest - part.shape[0]))) for part in loose_parts]
    loose = jnp.concatenate(loose + [jnp.zeros((3, longest), F32)], axis=0)
    terms = [images_two[0], images_two[1], images_two[2], d_gate_two.astype(BF16)]
    d_mod = [early.astype(BF16)]
    d_mod += [jnp.concatenate(terms[2 * i : 2 * i + 2], axis=1) for i in range(2)]
    if 2 * mod_width == width:
        d_mod_flat = jnp.concatenate(d_mod, axis=0)
    else:
        d_mod_flat = jnp.concatenate(d_mod, axis=1).reshape(-1, width)
    rest = jnp.concatenate([bottom, out_weight_grad, d_mod_flat], axis=0)
    if ring_fits([top]) and top.shape == rest.shape:
        flat, d_norm_other, loose = ring_sum([top, rest], d_norm_part, loose, 0)
        d_norm_one = own(d_norm_part).astype(F32) + d_norm_other.astype(F32)
    else:
        d_norm_one = narrow_scatter(d_norm_part)
        flat = jnp.concatenate(lax.psum((top, rest), "wide"), axis=0)
        loose = lax.psum(loose, "wide")
    tok_own = tokens.astype(F32)
    xhat_one, rstd_one = norm(tok_own)
    hot_own = own(onehot_full)
    scale_one = dot(hot_own, table_one[1], ((1,), (0,)))
    tokens_grad = own(d_middle) + norm_back(d_norm_one * (1.0 + scale_one), xhat_one, rstd_one)
    attn_own = sum(own_of(parts, narrow_index).astype(F32) for parts in (attn_parts, attn_others))
    attn_own = attn_own + out_bias.astype(F32)
    live_own = own(live)
    gates = [dot(hot_own, table_two[j], ((1,), (0,))) for j in (0, 3)]
    layer_out = (tok_own + live_own * (gates[0] * attn_own + gates[1] * branch)).astype(BF16)
    up_weight_grad = turned(up_grad)
    down_weight_grad = down_grad.astype(F32)
    keep = 3 * part_width
    qkv_flat, out_weight_grad = widened(flat, (keep, part_width))
    qkv_weight_grad = jnp.transpose(qkv_flat.reshape(3, part_width, width), (2, 0, 1))
    up_bias_grad, down_bias_grad, query_bias, value_bias, out_bias_grad = [
        loose[i, : part.shape[0]] for i, part in enumerate(loose_parts)
    ]
    qv_bias_grad = jnp.stack([query_bias, value_bias])
    d_mod_flat = flat[keep + part_width :]
    if 2 * mod_width == width:
        d_mod = d_mod_flat.reshape(3, img_row, width)
    else:
        d_mod = jnp.moveaxis(d_mod_flat.reshape(img_row, 3, -1), 1, 0)
    modulator_grad = lax.dot_general(
        d_mod, activated, (((1,), (0,)), ((), ())), preferred_element_type=F32
    )
    modulator_grad = jnp.transpose(modulator_grad.reshape(6, mod_width, width), (2, 0, 1))
    modulator_bias_grad = jnp.sum(d_mod.astype(F32), axis=1).reshape(6, mod_width)
    mod_blocks = mod_rows.reshape(3, 2 * mod_width, width)
    d_activated = sum(dot(d_mod[i], mod_blocks[i], ((1,), (0,))) for i in range(3))
    cond_part = d_activated * sigmoid_rows * (1.0 + cond_rows * (1.0 - sigmoid_rows))
    cond_part = cond_part.astype(BF16)
    condition_grad = cond_part.astype(F32) + narrow_other(cond_part).astype(F32)
    return (
        layer_out,
        tokens_grad,
        condition_grad,
        modulator_grad,
        modulator_bias_grad,
        qkv_weight_grad,
        qv_bias_grad,
        out_weight_grad,
        out_bias_grad,
        up_weight_grad,
        up_bias_grad,
        down_weight_grad,
        down_bias_grad,
    )


def solution(mesh):
    in_specs = (
        P(("wide", "narrow"), None),
        P(),
        P("wide", None),
        P(None, None, "narrow"),
        P(None, "narrow"),
        P(None, None, "narrow"),
        P(None, "narrow"),
        P("narrow", None),
        P(),
        P(None, "narrow"),
        P("narrow"),
        P("narrow", None),
        P(),
        P(),
        P(),
    )
    out_specs = (
        P(("wide", "narrow"), None),
        P(("wide", "narrow"), None),
        P(),
        P(None, None, "narrow"),
        P(None, "narrow"),
        P(None, None, "narrow"),
        P(None, "narrow"),
        P("narrow", None),
        P(),
        P(None, "narrow"),
        P("narrow"),
        P("narrow", None),
        P(),
    )
    return jax.shard_map(body, mesh=mesh, in_specs=in_specs, out_specs=out_specs, check_vma=False)
```

```python
import jax
import jax.numpy as jnp
from jax import lax
from jax.experimental import pallas as pl
from jax.experimental.pallas import tpu as pltpu
from jax.sharding import PartitionSpec as P

HD = 72
IMG_MAX = 128
EPSILON = 1e-06
NEG_FILL = -1e30
F32 = jnp.float32
BF16 = jnp.bfloat16


def dot(left, right, dims, out=F32):
    return lax.dot_general(left, right, (dims, ((), ())), preferred_element_type=F32).astype(out)


def swap(part):
    return lax.ppermute(part, "narrow", [(0, 1), (1, 0)])


def narrow_gather(part, other=None):
    if lax.axis_size("narrow") != 2:
        return lax.all_gather(part, "narrow", axis=0, tiled=True)
    other = swap(part) if other is None else other
    first = lax.axis_index("narrow") == 0
    return jnp.where(
        first, jnp.concatenate([part, other], axis=0), jnp.concatenate([other, part], axis=0)
    )


def narrow_other(part):
    if lax.axis_size("narrow") != 2:
        return (lax.psum(part.astype(F32), "narrow") - part.astype(F32)).astype(BF16)
    return swap(part)


def narrow_scatter(part, dim=0):
    count = lax.axis_size("narrow")
    if count != 2:
        return lax.psum_scatter(part, "narrow", scatter_dimension=dim, tiled=True).astype(F32)
    size = part.shape[dim] // 2
    index = lax.axis_index("narrow")
    mine = lax.dynamic_slice_in_dim(part, index * size, size, axis=dim)
    theirs = lax.dynamic_slice_in_dim(part, (1 - index) * size, size, axis=dim)
    return mine.astype(F32) + swap(theirs).astype(F32)


MESH = pl.DeviceIdType.MESH
UNIT = 48


def ring_kernel(chips, subs, full, *refs):
    data = refs[:2]
    if full:
        part, loose, out, landing, loose_out, *refs = refs[2:]
        last, loose_pair, loose_rows, *sems = refs[6:]
        swap_sems, gather_sems, pair_sems, own_sems, loose_pair_sems, loose_sems = sems
    else:
        last, *refs = refs[2:]
    mine, theirs, slots, copy_sems, core_sems, ring_sems = refs[:6]
    wide = lax.axis_index("wide")
    chip, core = wide // 2, wide % 2
    half = chips // 2

    def place(position):
        position = lax.rem(position + 2 * chips, chips)
        side = position // half
        return (1 - side) * 2 * position + side * (2 * (chips - 1 - position) + 1)

    position = chip // 2 + (chip % 2) * (chips - 1 - 2 * (chip // 2))
    ahead = 2 * place(position + 1) + core
    behind = 2 * place(position - 1) + core
    sibling = 2 * chip + 1 - core
    barrier = pltpu.get_barrier_semaphore()
    for device in (ahead, behind, sibling):
        pl.semaphore_signal(barrier, inc=1, device_id={"wide": device}, device_id_type=MESH)
    if full:
        facing = 1 - lax.axis_index("narrow")
        pl.semaphore_signal(barrier, inc=1, device_id={"narrow": facing}, device_id_type=MESH)
    pl.semaphore_wait(barrier, 3 + int(full))

    def local(lane):
        return pltpu.make_async_copy(data[lane].at[:, core], mine.at[lane], copy_sems.at[lane])

    def needed(lane, order):
        return place(position - 1 - order if lane == 0 else position + 1 + order)

    def across(lane, order):
        index = needed(lane, order)
        return pltpu.make_async_remote_copy(
            src_ref=data[lane].at[index, 1 - core],
            dst_ref=theirs.at[lane, index],
            send_sem=core_sems.at[0, lane, order],
            recv_sem=core_sems.at[1, lane, order],
            device_id={"wide": sibling},
            device_id_type=MESH,
        )

    for order in range(chips):
        for lane in range(2):
            across(lane, order).start()
            if order == 0:
                local(lane).start()
    if full:
        share = landing.shape[0]
        turn = pltpu.make_async_remote_copy(
            src_ref=part.at[pl.ds(facing * share, share)],
            dst_ref=landing,
            send_sem=swap_sems.at[0],
            recv_sem=swap_sems.at[1],
            device_id={"narrow": facing},
            device_id_type=MESH,
        )
        turn.start()
        loose_swap = pltpu.make_async_remote_copy(
            src_ref=loose,
            dst_ref=loose_pair,
            send_sem=loose_pair_sems.at[0],
            recv_sem=loose_pair_sems.at[1],
            device_id={"wide": sibling},
            device_id_type=MESH,
        )
        loose_swap.start()

    def loose_hop(step, index):
        return pltpu.make_async_remote_copy(
            src_ref=loose_rows.at[index],
            dst_ref=loose_rows.at[index],
            send_sem=loose_sems.at[0, step],
            recv_sem=loose_sems.at[1, step],
            device_id={"wide": ahead},
            device_id_type=MESH,
        )

    def rows_of(sub):
        return pl.ds(sub * UNIT, UNIT)

    def hop(lane, step, sub):
        rows = rows_of(sub)
        if step == 0:
            first = place(position - 1 if lane == 0 else position + 1)
            source = mine.at[lane, first, rows]
        else:
            source = slots.at[lane, step - 1, rows]
        return pltpu.make_async_remote_copy(
            src_ref=source,
            dst_ref=slots.at[lane, step, rows],
            send_sem=ring_sems.at[0, lane, step, sub],
            recv_sem=ring_sems.at[1, lane, step, sub],
            device_id={"wide": ahead if lane == 0 else behind},
            device_id_type=MESH,
        )

    def held(lane, step, sub, side):
        index = place(position - step if lane == 0 else position + step)
        return out.at[lane, index, side, rows_of(sub)]

    def send_on(lane, step, sub):
        source = last.at[lane, rows_of(sub)] if step == 0 else held(lane, step, sub, core)
        return pltpu.make_async_remote_copy(
            src_ref=source,
            dst_ref=held(lane, step, sub, core),
            send_sem=gather_sems.at[0, lane, step, sub],
            recv_sem=gather_sems.at[1, lane, step, sub],
            device_id={"wide": ahead if lane == 0 else behind},
            device_id_type=MESH,
        )

    def landed(lane, step, sub):
        return pltpu.make_async_remote_copy(
            src_ref=last.at[lane, rows_of(sub)],
            dst_ref=held(lane, step + 1, sub, core),
            send_sem=gather_sems.at[0, lane, step, sub],
            recv_sem=gather_sems.at[1, lane, step, sub],
            device_id={"wide": ahead if lane == 0 else behind},
            device_id_type=MESH,
        )

    def pair(lane, step, sub, side):
        source = last.at[lane, rows_of(sub)] if step == 0 else held(lane, step, sub, core)
        return pltpu.make_async_remote_copy(
            src_ref=source,
            dst_ref=held(lane, step, sub, side),
            send_sem=pair_sems.at[0, lane, step, sub],
            recv_sem=pair_sems.at[1, lane, step, sub],
            device_id={"wide": sibling},
            device_id_type=MESH,
        )

    def keep(lane, sub):
        return pltpu.make_async_copy(
            last.at[lane, rows_of(sub)], held(lane, 0, sub, core), own_sems.at[lane, sub]
        )

    def pair_sum(lane, order, rows):
        index = needed(lane, order)
        return mine[lane, index, rows].astype(F32) + theirs[lane, index, rows].astype(F32)

    for lane in range(2):
        local(lane).wait()
        across(lane, 0).wait_recv()
        for sub in range(subs):
            mine[lane, needed(lane, 0), rows_of(sub)] = pair_sum(lane, 0, rows_of(sub)).astype(BF16)
            hop(lane, 0, sub).start()
    if full:
        loose_swap.wait()
        loose_rows[chip] = loose[...] + loose_pair[...]
        loose_hop(0, chip).start()
    for step in range(chips - 1):
        for sub in range(subs):
            for lane in range(2):
                if sub == 0:
                    across(lane, step + 1).wait_recv()
                rows = rows_of(sub)
                extra = pair_sum(lane, step + 1, rows)
                hop(lane, step, sub).wait_recv()
                total = (slots[lane, step, rows].astype(F32) + extra).astype(BF16)
                if step < chips - 2:
                    slots[lane, step, rows] = total
                    hop(lane, step + 1, sub).start()
                else:
                    last[lane, rows] = total
                    if full:
                        send_on(lane, 0, sub).start()
                        pair(lane, 0, sub, core).start()
                        keep(lane, sub).start()
        if full:
            passed = place(position - 1 - step)
            loose_hop(step, passed).wait_recv()
            if step < chips - 2:
                loose_hop(step + 1, passed).start()
    if full:
        for step in range(chips - 1):
            for sub in range(subs):
                for lane in range(2):
                    landed(lane, step, sub).wait_recv()
                    if step < chips - 2:
                        send_on(lane, step + 1, sub).start()
                    pair(lane, step + 1, sub, core).start()
        loose_out[...] = jnp.sum(loose_rows[...], axis=0)
    for step in range(chips):
        if full and step < chips - 1:
            loose_hop(step, place(position - step)).wait_send()
        for lane in range(2):
            across(lane, step).wait_send()
            for sub in range(subs):
                if step < chips - 1:
                    hop(lane, step, sub).wait_send()
                if full:
                    pair(lane, step, sub, 1 - core).wait_recv()
                    pair(lane, step, sub, core).wait_send()
                    if step == 0:
                        keep(lane, sub).wait()
                    if step < chips - 1:
                        send_on(lane, step, sub).wait_send()
    if full:
        turn.wait()


def ring_scratch(chips, shard, width):
    return [
        pltpu.VMEM((2, chips, shard, width), BF16),
        pltpu.VMEM((2, chips, shard, width), BF16),
        pltpu.VMEM((2, chips - 1, shard, width), BF16),
        pltpu.SemaphoreType.DMA((2,)),
        pltpu.SemaphoreType.DMA((2, 2, chips)),
        pltpu.SemaphoreType.DMA((2, 2, chips - 1, shard // UNIT)),
    ]


def ring_scatter(lanes, collective_id):
    chips = lax.axis_size("wide") // 2
    rows, width = lanes[0].shape
    shard = rows // (2 * chips)
    return pl.pallas_call(
        lambda *refs: ring_kernel(chips, shard // UNIT, False, *refs),
        out_shape=jax.ShapeDtypeStruct((2, shard, width), BF16),
        in_specs=[pl.BlockSpec(memory_space=pl.ANY)] * 2,
        out_specs=pl.BlockSpec(memory_space=pltpu.VMEM),
        scratch_shapes=ring_scratch(chips, shard, width),
        compiler_params=pltpu.CompilerParams(
            collective_id=collective_id, has_side_effects=True, vmem_limit_bytes=40 << 20
        ),
        name="ring_scatter",
    )(*[lane.reshape(chips, 2, shard, width) for lane in lanes])


def ring_sum(lanes, part, loose, collective_id):
    chips = lax.axis_size("wide") // 2
    rows, width = lanes[0].shape
    shard = rows // (2 * chips)
    subs = shard // UNIT
    anywhere = pl.BlockSpec(memory_space=pl.ANY)
    inside = pl.BlockSpec(memory_space=pltpu.VMEM)
    sums, landed, loose_sum = pl.pallas_call(
        lambda *refs: ring_kernel(chips, subs, True, *refs),
        out_shape=[
            jax.ShapeDtypeStruct((2, chips, 2, shard, width), BF16),
            jax.ShapeDtypeStruct((part.shape[0] // 2, part.shape[1]), BF16),
            jax.ShapeDtypeStruct(loose.shape, F32),
        ],
        in_specs=[anywhere] * 3 + [inside],
        out_specs=[anywhere] * 2 + [inside],
        scratch_shapes=ring_scratch(chips, shard, width)
        + [
            pltpu.VMEM((2, shard, width), BF16),
            pltpu.VMEM(loose.shape, F32),
            pltpu.VMEM((chips,) + loose.shape, F32),
            pltpu.SemaphoreType.DMA((2,)),
            pltpu.SemaphoreType.DMA((2, 2, chips - 1, subs)),
            pltpu.SemaphoreType.DMA((2, 2, chips, subs)),
            pltpu.SemaphoreType.DMA((2, subs)),
            pltpu.SemaphoreType.DMA((2,)),
            pltpu.SemaphoreType.DMA((2, chips - 1)),
        ],
        compiler_params=pltpu.CompilerParams(
            collective_id=collective_id, has_side_effects=True, vmem_limit_bytes=40 << 20
        ),
        name="ring_sum",
    )(*[lane.reshape(chips, 2, shard, width) for lane in lanes], part, loose)
    return sums.reshape(2 * rows, width), landed, loose_sum


def ring_fits(lanes):
    count = lax.axis_size("wide")
    return lax.axis_size("narrow") == 2 and lanes[0].shape[0] % (count * UNIT) == 0


TILE = 256
LOG2E = 1.4426950408889634


def head_lanes(part_width):
    for head in range(part_width // HD):
        lo = head * HD // 128 * 128
        hi = min(-(-(head + 1) * HD // 128) * 128, part_width)
        lanes = lax.broadcasted_iota(jnp.int32, (1, hi - lo), 1) + lo
        yield head, lo, hi, (lanes >= head * HD) & (lanes < (head + 1) * HD)


def extend(first, left, own, right, ext):
    span = left.shape[1]
    ends = ext.shape[1] - span

    @pl.when(first)
    def _():
        for which in range(2):
            ext[which, :span] = left[which]
            ext[which, span:ends] = own[which][...]
            ext[which, ends:] = right[which]


def forward_kernel(tiles, q, k, v, left, right, q_ids, k_ids, out, lse, ext, total):
    tile = pl.program_id(0)
    part_width = q.shape[1]
    span = left.shape[1]
    ends = ext.shape[1] - span
    extend(tile == 0, left, (k, v), right, ext)
    scale = LOG2E * HD ** (-0.5)

    def run(extra):
        rows = pl.ds(pl.multiple_of(tile * TILE, TILE), TILE + 2 * span)
        keys, values = ext[0, rows], ext[1, rows]
        ids = k_ids[:, rows]
        if extra:
            keys = jnp.concatenate([keys, ext[0, ends:]], axis=0)
            values = jnp.concatenate([values, ext[1, ends:]], axis=0)
            ids = jnp.concatenate([ids, k_ids[:, ends:]], axis=1)
        same = q_ids[...] == ids
        queries = q[...]
        total[...] = jnp.zeros_like(total)
        packed = jnp.zeros((TILE, 128), F32)
        column = lax.broadcasted_iota(jnp.int32, (TILE, 128), 1)
        for head, lo, hi, mask in head_lanes(part_width):
            chosen = jnp.where(mask, queries[:, lo:hi], 0)
            scores = lax.dot_general(
                chosen, keys[:, lo:hi], (((1,), (1,)), ((), ())), preferred_element_type=F32
            )
            scores = jnp.where(same, scores * scale, NEG_FILL)
            top = jnp.max(scores, axis=1, keepdims=True)
            expo = jnp.exp2(scores - top)
            count = jnp.sum(expo, axis=1, keepdims=True)
            part = jnp.dot(expo.astype(BF16), values[:, lo:hi], preferred_element_type=F32)
            total[:, lo:hi] += jnp.where(mask, part / count, 0.0)
            packed = jnp.where(column == head, top + jnp.log2(count), packed)
        out[...] = total[...].astype(BF16)
        lse[...] = packed.T[: lse.shape[0]]

    split_tiles(tile, tiles, run)


def split_tiles(tile, tiles, run):
    first_extra = tiles - 512 // TILE
    extra = (tile >= first_extra) & (tile < tiles - 1)
    pl.when(extra)(lambda: run(True))
    pl.when(jnp.logical_not(extra))(lambda: run(False))


def rim_specs(part_width, span, tok_dev):
    whole = lambda shape: pl.BlockSpec(shape, lambda i: (0,) * len(shape))
    return whole((tok_dev, part_width)), whole((2, span, part_width))


def attention_forward(q, k, v, left, right, q_ids, k_ids):
    tok_dev, part_width = q.shape
    span = left.shape[1]
    tiles = tok_dev // TILE
    head_rows = -(-(part_width // HD) // 8) * 8
    own_spec, rim_spec = rim_specs(part_width, span, tok_dev)
    return pl.pallas_call(
        lambda *refs: forward_kernel(tiles, *refs),
        grid=(tiles,),
        out_shape=[
            jax.ShapeDtypeStruct((tok_dev, part_width), BF16),
            jax.ShapeDtypeStruct((head_rows, tok_dev), F32),
        ],
        in_specs=[
            pl.BlockSpec((TILE, part_width), lambda i: (i, 0)),
            own_spec,
            own_spec,
            rim_spec,
            rim_spec,
            pl.BlockSpec((TILE, 1), lambda i: (i, 0)),
            pl.BlockSpec((1, tok_dev + 2 * span), lambda i: (0, 0)),
        ],
        out_specs=[
            pl.BlockSpec((TILE, part_width), lambda i: (i, 0)),
            pl.BlockSpec((head_rows, TILE), lambda i: (0, i)),
        ],
        scratch_shapes=[
            pltpu.VMEM((2, tok_dev + 2 * span, part_width), BF16),
            pltpu.VMEM((TILE, part_width), F32),
        ],
        compiler_params=pltpu.CompilerParams(vmem_limit_bytes=40 << 20),
        cost_estimate=pl.CostEstimate(
            flops=4 * tok_dev * 512 * part_width,
            transcendentals=tok_dev * 512 * 8,
            bytes_accessed=8 * tok_dev * part_width,
        ),
        name="attention_forward",
    )(q, k, v, left, right, q_ids, k_ids)


def backward_kernel(tiles, q, k, v, left, right, grad, lse, q_ids, k_ids, *refs):
    d_q, d_own, d_rim, ext, d_ext, total = refs
    tile = pl.program_id(0)
    part_width = q.shape[1]
    span = left.shape[1]
    ends = ext.shape[1] - span
    extend(tile == 0, left, (k, v), right, ext)
    scale = HD ** (-0.5)

    @pl.when(tile == 0)
    def _():
        d_ext[...] = jnp.zeros_like(d_ext)

    def run(extra):
        rows = pl.ds(pl.multiple_of(tile * TILE, TILE), TILE + 2 * span)
        keys, values = ext[0, rows], ext[1, rows]
        ids = k_ids[rows]
        if extra:
            keys = jnp.concatenate([keys, ext[0, ends:]], axis=0)
            values = jnp.concatenate([values, ext[1, ends:]], axis=0)
            ids = jnp.concatenate([ids, k_ids[ends:]], axis=0)
        same = ids == q_ids[...]
        queries, grads = q[...], grad[...]
        total[...] = jnp.zeros_like(total)

        def across(left_side, right_side, dims):
            return lax.dot_general(
                left_side, right_side, (dims, ((), ())), preferred_element_type=F32
            )

        for head, lo, hi, mask in head_lanes(part_width):
            chosen = jnp.where(mask, queries[:, lo:hi], 0)
            pulled = jnp.where(mask, grads[:, lo:hi], 0)
            scores = across(keys[:, lo:hi], chosen, ((1,), (1,)))
            scores = jnp.where(same, scores * (scale * LOG2E), NEG_FILL)
            attend = jnp.exp2(scores - lse[head : head + 1])
            d_attend = across(values[:, lo:hi], pulled, ((1,), (1,)))
            centre = jnp.sum(attend * d_attend, axis=0, keepdims=True)
            d_scores = (attend * (d_attend - centre)).astype(BF16)
            d_key = across(d_scores, chosen, ((1,), (0,)))
            d_value = across(attend.astype(BF16), pulled, ((1,), (0,)))
            length = TILE + 2 * span
            d_ext[0, rows, lo:hi] += d_key[:length]
            d_ext[1, rows, lo:hi] += d_value[:length]
            if extra:
                d_ext[0, ends:, lo:hi] += d_key[length:]
                d_ext[1, ends:, lo:hi] += d_value[length:]
            d_query = across(d_scores, keys[:, lo:hi], ((0,), (0,)))
            total[:, lo:hi] += jnp.where(mask, d_query, 0.0)
        d_q[...] = (total[...] * scale).astype(BF16)

    split_tiles(tile, tiles, run)

    @pl.when(tile == tiles - 1)
    def _():
        for which, factor in ((0, scale), (1, 1.0)):
            d_rim[0, which] = (d_ext[which, :span] * factor).astype(BF16)
            d_own[which] = (d_ext[which, span:ends] * factor).astype(BF16)
            d_rim[1, which] = (d_ext[which, ends:] * factor).astype(BF16)


def attention_backward(q, k, v, left, right, grad, lse, q_ids, k_ids):
    tok_dev, part_width = q.shape
    span = left.shape[1]
    tiles = tok_dev // TILE
    own_spec, rim_spec = rim_specs(part_width, span, tok_dev)
    tile_spec = pl.BlockSpec((TILE, part_width), lambda i: (i, 0))
    return pl.pallas_call(
        lambda *refs: backward_kernel(tiles, *refs),
        grid=(tiles,),
        out_shape=[
            jax.ShapeDtypeStruct((tok_dev, part_width), BF16),
            jax.ShapeDtypeStruct((2, tok_dev, part_width), BF16),
            jax.ShapeDtypeStruct((2, 2, span, part_width), BF16),
        ],
        in_specs=[
            tile_spec,
            own_spec,
            own_spec,
            rim_spec,
            rim_spec,
            tile_spec,
            pl.BlockSpec((lse.shape[0], TILE), lambda i: (0, i)),
            pl.BlockSpec((1, TILE), lambda i: (0, i)),
            pl.BlockSpec((tok_dev + 2 * span, 1), lambda i: (0, 0)),
        ],
        out_specs=[
            tile_spec,
            pl.BlockSpec((2, tok_dev, part_width), lambda i: (0, 0, 0)),
            pl.BlockSpec((2, 2, span, part_width), lambda i: (0, 0, 0, 0)),
        ],
        scratch_shapes=[
            pltpu.VMEM((2, tok_dev + 2 * span, part_width), BF16),
            pltpu.VMEM((2, tok_dev + 2 * span, part_width), F32),
            pltpu.VMEM((TILE, part_width), F32),
        ],
        compiler_params=pltpu.CompilerParams(vmem_limit_bytes=48 << 20),
        cost_estimate=pl.CostEstimate(
            flops=10 * tok_dev * 512 * part_width,
            transcendentals=tok_dev * 512 * 8,
            bytes_accessed=16 * tok_dev * part_width,
        ),
        name="attention_backward",
    )(q, k, v, left, right, grad, lse, q_ids, k_ids)


def norm(field):
    centred = field - jnp.mean(field, axis=-1, keepdims=True)
    rstd = lax.rsqrt(jnp.mean(centred * centred, axis=-1, keepdims=True) + EPSILON)
    return centred * rstd, rstd


def norm_back(grad, xhat, rstd):
    return rstd * (
        grad
        - jnp.mean(grad, axis=-1, keepdims=True)
        - xhat * jnp.mean(grad * xhat, axis=-1, keepdims=True)
    )


def gelu_pair(v):
    c = 0.7978845608028654
    sq = v * v
    t = jnp.tanh(c * v * (1.0 + 0.044715 * sq))
    half = 0.5 * (1.0 + t)
    slope = half + 0.5 * v * (1.0 - t * t) * c * (1.0 + 3 * 0.044715 * sq)
    return v * half, slope


def matmul(left, right, dims=((1,), (0,))):
    return lax.dot_general(left, right, (dims, ((), ())), preferred_element_type=F32)


def pick(ids, table):
    slots = lax.broadcasted_iota(jnp.int32, (ids.shape[0], table.shape[0]), 1)
    return matmul((ids == slots).astype(BF16), table)


def gather_images(ids, terms, sums, fresh):
    slots = lax.broadcasted_iota(jnp.int32, (sums.shape[1], ids.shape[1]), 0)
    hot = (ids == slots).astype(BF16)
    for i, term in enumerate(terms):
        part = matmul(hot, term.astype(BF16))
        sums[i] = jnp.where(fresh, 0.0, sums[i]) + part


def halves_out(sums, out, halves):
    size = sums.shape[2] // halves
    for half in range(halves):
        for i in range(sums.shape[0]):
            out[half, i] = sums[i, :, half * size : (half + 1) * size].astype(BF16)


def whole(shape):
    return pl.BlockSpec(shape, lambda i: (0,) * len(shape))


def tiled(rows, width):
    return pl.BlockSpec((rows, width), lambda i: (i, 0))


def token_call(kernel, tokens, name, out_shape, in_specs, out_specs, scratch, flops, operands):
    size = sum(x.size * x.dtype.itemsize for x in operands)
    return pl.pallas_call(
        kernel,
        grid=(tokens // TILE,),
        out_shape=out_shape,
        in_specs=in_specs,
        out_specs=out_specs,
        scratch_shapes=scratch,
        compiler_params=pltpu.CompilerParams(vmem_limit_bytes=60 << 20),
        cost_estimate=pl.CostEstimate(
            flops=flops, transcendentals=0, bytes_accessed=size + size // 2
        ),
        name=name,
    )(*operands)


def shaped(shape, dtype=BF16):
    return jax.ShapeDtypeStruct(shape, dtype)


def project_kernel(split, *refs):
    if split:
        index, mine, theirs, *refs = refs
        held = pl.program_id(0) // (pl.num_programs(0) // 2) == index[0]
        rows = jnp.where(held, mine[...], theirs[...])
    else:
        tokens, *refs = refs
        rows = tokens[...]
    ids, table, weight, bias, q, k, v, norm_one = refs
    xhat, _ = norm(rows.astype(F32))
    normed = (xhat * (1.0 + pick(ids[...], table[1])) + pick(ids[...], table[0])).astype(BF16)
    norm_one[...] = normed
    size = q.shape[1]
    for i, out in enumerate((q, k, v)):
        rows = matmul(normed, weight[i * size : (i + 1) * size], ((1,), (1,)))
        if i != 1:
            rows = rows + bias[i // 2 : i // 2 + 1].astype(F32)
        out[...] = rows.astype(BF16)


def project(sources, ids, table, weight, bias):
    split = len(sources) == 3
    count, width = ids.shape[0], weight.shape[1]
    size = weight.shape[0] // 3
    specs = [tiled(TILE, width)]
    if split:
        half = pl.BlockSpec((TILE, width), lambda i: (i % (count // TILE // 2), 0))
        specs = [pl.BlockSpec(memory_space=pltpu.SMEM), half, half]
    return token_call(
        lambda *refs: project_kernel(split, *refs),
        count,
        "project",
        [shaped((count, size))] * 3 + [shaped((count, width))],
        specs + [tiled(TILE, 1), whole(table.shape), whole(weight.shape), whole(bias.shape)],
        [tiled(TILE, size)] * 3 + [tiled(TILE, width)],
        [],
        6 * count * width * size,
        tuple(sources) + (ids, table, weight, bias),
    )


def mlp_kernel(
    tokens, mine, theirs, cotangent, ids, live, table, out_bias, up, up_bias, down, *outs
):
    norm_two, hidden, d_upper, d_branch, d_norm, branch, up_sum, down_sum = outs
    first = pl.program_id(0) == 0
    ids, live = ids[...], live[...]
    attn = mine[...].astype(F32) + theirs[...].astype(F32) + out_bias[...].astype(F32)
    middle = tokens[...].astype(F32) + live * pick(ids, table[0]) * attn
    xhat, _ = norm(middle)
    normed = (xhat * (1.0 + pick(ids, table[2])) + pick(ids, table[1])).astype(BF16)
    norm_two[...] = normed
    pulled = (live * pick(ids, table[3]) * cotangent[...].astype(F32)).astype(BF16)
    d_branch[...] = pulled
    column = jnp.sum(pulled.astype(F32), axis=0, keepdims=True)
    down_sum[...] = jnp.where(first, 0.0, down_sum[...]) + column
    width = up.shape[1]
    step = 768 if width % 768 == 0 else width
    back = ahead = 0.0
    for lo in range(0, width, step):
        cols = slice(lo, lo + step)
        upper = matmul(normed, up[:, cols]) + up_bias[:, cols].astype(F32)
        d_hidden = matmul(pulled, down[cols], ((1,), (1,)))
        value, slope = gelu_pair(upper)
        value = value.astype(BF16)
        d_up = (d_hidden * slope).astype(BF16)
        hidden[:, cols] = value
        d_upper[:, cols] = d_up
        column = jnp.sum(d_up.astype(F32), axis=0, keepdims=True)
        up_sum[:, cols] = jnp.where(first, 0.0, up_sum[:, cols]) + column
        back += matmul(d_up, up[:, cols], ((1,), (1,)))
        ahead += matmul(value, down[cols])
    d_norm[...] = back.astype(BF16)
    branch[...] = ahead.astype(BF16)


def mlp(start, tokens, mine, theirs, cotangent, ids, live, table, out_bias, up, up_bias, down):
    count, width = mine.shape
    size = up.shape[1]
    first = start // TILE
    here = tiled(TILE, width)
    row = pl.BlockSpec((TILE, width), lambda i: (i + first, 0))
    col = pl.BlockSpec((TILE, 1), lambda i: (i + first, 0))
    consts = (table, out_bias, up, up_bias, down)
    return token_call(
        mlp_kernel,
        count,
        "mlp",
        [shaped((count, n)) for n in (width, size, size, width, width, width)]
        + [shaped((1, n), F32) for n in (size, width)],
        [row, here, here, row, col, col] + [whole(x.shape) for x in consts],
        [tiled(TILE, n) for n in (width, size, size, width, width, width)]
        + [whole((1, n)) for n in (size, width)],
        [],
        8 * count * width * size,
        (tokens, mine, theirs, cotangent, ids, live) + consts,
    )


def middle_kernel(halves, blocks, *refs):
    tokens, cotangent, context, ids, live, ids_row, *refs = refs
    parts = [refs[i * blocks : (i + 1) * blocks] for i in range(4)]
    table, out_bias, weight, d_middle, d_context, d_weight, d_images, d_bias, sums, total = refs[
        4 * blocks :
    ]
    tile = pl.program_id(0)
    first = tile == 0
    last = tile == pl.num_programs(0) - 1

    def rows_at(refs):
        rows = refs[0][...]
        for i in range(1, blocks):
            rows = jnp.where(tile >= i * (pl.num_programs(0) // blocks), refs[i][...], rows)
        return rows.astype(F32)

    mine, theirs, d_own, d_other = [rows_at(part) for part in parts]
    ids, live = ids[...], live[...]
    gate = live * pick(ids, table[0])
    attn = mine + theirs + out_bias[...].astype(F32)
    xhat, rstd = norm(tokens[...].astype(F32) + gate * attn)
    d_norm = d_own + d_other
    grad = cotangent[...].astype(F32) + norm_back(d_norm * (1.0 + pick(ids, table[2])), xhat, rstd)
    d_middle[...] = grad
    d_attn = (gate * grad).astype(BF16)
    d_context[...] = matmul(d_attn, weight[...], ((1,), (1,))).astype(BF16)
    part = matmul(context[...], d_attn, ((0,), (0,)))
    total[...] = jnp.where(first, 0.0, total[...]) + part
    column = jnp.sum(d_attn.astype(F32), axis=0, keepdims=True)
    d_bias[...] = jnp.where(first, 0.0, d_bias[...]) + column
    gather_images(ids_row[...], (live * grad * attn, d_norm, d_norm * xhat), sums, first)

    @pl.when(last)
    def _():
        d_weight[...] = total[...].astype(BF16)
        halves_out(sums, d_images, halves)


def middle_back(halves, parts, tokens, cotangent, context, ids, live, ids_row, table, out_bias, weight):
    count, width = tokens.shape
    size = context.shape[1]
    images = table.shape[1]
    blocks = len(parts[0])
    tiles = count // TILE // blocks
    row, col = tiled(TILE, width), tiled(TILE, 1)
    consts = (table, out_bias, weight)

    def block_spec(i):
        return pl.BlockSpec((TILE, width), lambda t: (jnp.clip(t - i * tiles, 0, tiles - 1), 0))

    return token_call(
        lambda *refs: middle_kernel(halves, blocks, *refs),
        count,
        "middle_back",
        [
            shaped((count, width), F32),
            shaped((count, size)),
            shaped((size, width)),
            shaped((halves, 3, images, width // halves)),
            shaped((1, width), F32),
        ],
        [row, row, tiled(TILE, size), col, col, pl.BlockSpec((1, TILE), lambda i: (0, i))]
        + [block_spec(i) for _ in parts for i in range(blocks)]
        + [whole(x.shape) for x in consts],
        [
            row,
            tiled(TILE, size),
            whole((size, width)),
            whole((halves, 3, images, width // halves)),
            whole((1, width)),
        ],
        [pltpu.VMEM((3, images, width), F32), pltpu.VMEM((size, width), F32)],
        4 * count * width * size,
        (tokens, cotangent, context, ids, live, ids_row) + tuple(sum(parts, [])) + consts,
    )


def project_back_kernel(halves, tokens, d_q, d_own, rims, tail_start, ids_row, weight, *refs):
    d_norm, d_kv, d_images, sums = refs
    tile = pl.program_id(0)
    span, size = rims.shape[2], d_q.shape[1]
    rows = lax.broadcasted_iota(jnp.int32, (TILE, span), 0) + tile * TILE
    cols = lax.broadcasted_iota(jnp.int32, (TILE, span), 1)
    head_rim = (rows == cols).astype(BF16)
    tail_rim = (rows == cols + tail_start[0]).astype(BF16)
    back = matmul(d_q[...], weight[:size])
    for which in range(2):
        rim = matmul(head_rim, rims[0, which]) + matmul(tail_rim, rims[1, which])
        part = (d_own[which].astype(F32) + rim).astype(BF16)
        d_kv[which] = part
        back += matmul(part, weight[(which + 1) * size : (which + 2) * size])
    back = back.astype(BF16)
    d_norm[...] = back
    xhat, _ = norm(tokens[...].astype(F32))
    back = back.astype(F32)
    gather_images(ids_row[...], (back, back * xhat), sums, tile == 0)

    @pl.when(tile == pl.num_programs(0) - 1)
    def _():
        part = sums.shape[2] // halves
        for half in range(halves):
            cut = slice(half * part, (half + 1) * part)
            both = jnp.concatenate([sums[0, :, cut], sums[1, :, cut]], axis=1)
            d_images[half] = both.astype(BF16)


def project_back(halves, images, tokens, d_q, d_own, rims, tail_start, ids_row, weight):
    count, width = tokens.shape
    size = d_q.shape[1]
    row = tiled(TILE, width)
    pair = pl.BlockSpec((2, TILE, size), lambda i: (0, i, 0))
    sums = (halves, images, 2 * width // halves)
    return token_call(
        lambda *refs: project_back_kernel(halves, *refs),
        count,
        "project_back",
        [shaped((count, width)), shaped((2, count, size)), shaped(sums)],
        [
            row,
            tiled(TILE, size),
            pair,
            whole(rims.shape),
            pl.BlockSpec(memory_space=pltpu.SMEM),
            pl.BlockSpec((1, TILE), lambda i: (0, i)),
            whole(weight.shape),
        ],
        [row, pair, whole(sums)],
        [pltpu.VMEM((2, images, width), F32)],
        6 * count * width * size,
        (tokens, d_q, d_own, rims, tail_start, ids_row, weight),
    )


def qkv_grads_kernel(split, norm_one, d_q, d_kv, top, bottom, d_bias, total):
    tile = pl.program_id(0)
    first = tile == 0
    size = d_q.shape[1]
    parts = [d_q[...], d_kv[0], d_kv[1]]
    normed = norm_one[...]
    for i, part in enumerate(parts):
        rows = slice(i * size, (i + 1) * size)
        total[rows] = jnp.where(first, 0.0, total[rows]) + matmul(part, normed, ((0,), (0,)))
    for i, part in ((0, parts[0]), (1, parts[2])):
        column = jnp.sum(part.astype(F32), axis=0, keepdims=True)
        d_bias[i : i + 1] = jnp.where(first, 0.0, d_bias[i : i + 1]) + column

    @pl.when(tile == pl.num_programs(0) - 1)
    def _():
        top[...] = total[:split].astype(BF16)
        bottom[...] = total[split:].astype(BF16)


def qkv_grads(split, norm_one, d_q, d_kv):
    count, width = norm_one.shape
    size = d_q.shape[1]
    shapes = [(split, width), (3 * size - split, width), (2, size)]
    return token_call(
        lambda *refs: qkv_grads_kernel(split, *refs),
        count,
        "qkv_grads",
        [shaped(shapes[0]), shaped(shapes[1]), shaped(shapes[2], F32)],
        [tiled(TILE, width), tiled(TILE, size), pl.BlockSpec((2, TILE, size), lambda i: (0, i, 0))],
        [whole(shape) for shape in shapes],
        [pltpu.VMEM((3 * size, width), F32)],
        6 * count * width * size,
        (norm_one, d_q, d_kv),
    )


def turned(part):
    rows, width = part.shape
    step = 384 if rows % 384 == 0 else rows

    def kernel(source, out):
        out[...] = source[...].astype(F32).T

    return pl.pallas_call(
        kernel,
        grid=(rows // step,),
        out_shape=shaped((width, rows), F32),
        in_specs=[tiled(step, width)],
        out_specs=pl.BlockSpec((width, step), lambda i: (0, i)),
        name="turned",
    )(part)


def widened(flat, counts):
    width = flat.shape[1]
    step = next(n for n in (576, 192, 96, 48, 16) if all(count % n == 0 for count in counts))
    starts = [sum(counts[:i]) // step for i in range(len(counts))]
    tiles = [count // step for count in counts]

    def spec(start, size):
        return pl.BlockSpec((step, width), lambda i: (jnp.clip(i - start, 0, size - 1), 0))

    def kernel(source, *outs):
        tile = pl.program_id(0)
        for out, start, size in zip(outs, starts, tiles):

            @pl.when((tile >= start) & (tile < start + size))
            def _():
                out[...] = source[...].astype(F32)

    return pl.pallas_call(
        kernel,
        grid=(sum(tiles),),
        out_shape=[shaped((count, width), F32) for count in counts],
        in_specs=[tiled(step, width)],
        out_specs=[spec(*pair) for pair in zip(starts, tiles)],
        compiler_params=pltpu.CompilerParams(vmem_limit_bytes=40 << 20),
        name="widened",
    )(flat)


def body(
    tokens,
    condition,
    cotangent,
    modulator,
    modulator_bias,
    qkv_weight,
    qv_bias,
    out_weight,
    out_bias,
    up_weight,
    up_bias,
    down_weight,
    down_bias,
    segment_ids,
    valid_counts,
):
    wide_count = lax.axis_size("wide")
    narrow_count = lax.axis_size("narrow")
    wide_index = lax.axis_index("wide")
    narrow_index = lax.axis_index("narrow")
    tok_dev, width = cotangent.shape
    share = tokens.shape[0]
    part_width = qkv_weight.shape[2]
    mod_width = modulator.shape[2]
    img_row = condition.shape[0]
    span = IMG_MAX
    own_count = valid_counts[wide_index]
    positions = jnp.arange(tok_dev, dtype=jnp.int32)
    own_ids = lax.dynamic_slice_in_dim(segment_ids, wide_index * tok_dev, tok_dev)
    live = (positions < own_count).astype(F32)[:, None]
    share_start = narrow_index * share
    ids_col, ids_row = own_ids[:, None], own_ids[None]
    onehot_full = (ids_col == jnp.arange(img_row, dtype=jnp.int32)[None]).astype(BF16)

    def own(rows):
        return lax.dynamic_slice_in_dim(rows, share_start, share)

    cond_rows = condition.astype(F32)
    sigmoid_rows = jax.nn.sigmoid(cond_rows)
    activated = (cond_rows * sigmoid_rows).astype(BF16)
    halves_held = narrow_count == 2 and share % TILE == 0
    tok_other = swap(tokens) if halves_held else None
    tok_full = narrow_gather(tokens, tok_other)
    mod_rows = jnp.transpose(modulator, (1, 2, 0)).reshape(6 * mod_width, width)

    def vectors(lo, hi):
        part = dot(activated, mod_rows[lo * mod_width : hi * mod_width], ((1,), (1,)))
        part = part + modulator_bias[lo:hi].astype(F32).reshape(1, -1)
        rows = jnp.moveaxis(part.astype(BF16).reshape(img_row, hi - lo, -1), 2, 0)
        return rows

    def table_of(rows, other=None):
        return jnp.transpose(narrow_gather(rows, other), (2, 1, 0))

    table_one = table_of(vectors(0, 2))
    rows_two = vectors(2, 6)
    sources = [narrow_index[None], tokens, tok_other] if halves_held else [tok_full]
    rows_two, sources[-1] = lax.optimization_barrier((rows_two, sources[-1]))
    other_two = swap(rows_two) if narrow_count == 2 else None
    flat_qkv = jnp.transpose(qkv_weight, (1, 2, 0)).reshape(3 * part_width, width)
    queries, key_rows, value_rows, norm_one = project(
        sources, ids_col, table_one, flat_qkv, qv_bias
    )
    other_two, queries = lax.optimization_barrier((other_two, queries))
    table_two = table_of(rows_two, other_two)
    tail_start = own_count - span

    def tail_of(rows):
        return lax.dynamic_slice_in_dim(rows, tail_start, span)

    def to_right(rows):
        return lax.ppermute(rows, "wide", [(i, i + 1) for i in range(wide_count - 1)])

    def to_left(rows):
        return lax.ppermute(rows, "wide", [(i + 1, i) for i in range(wide_count - 1)])

    from_left = to_right(jnp.stack([tail_of(key_rows), tail_of(value_rows)]))
    from_right = to_left(jnp.stack([key_rows[:span], value_rows[:span]]))
    left_index = jnp.maximum(wide_index - 1, 0)
    right_index = jnp.minimum(wide_index + 1, wide_count - 1)
    left_count = valid_counts[left_index]
    left_ids = lax.dynamic_slice_in_dim(segment_ids, left_index * tok_dev + left_count - span, span)
    left_ids = jnp.where(wide_index > 0, left_ids, -2)
    right_ids = lax.dynamic_slice_in_dim(segment_ids, right_index * tok_dev, span)
    right_ids = jnp.where(wide_index < wide_count - 1, right_ids, -2)
    own_keys = jnp.where(positions < own_count, own_ids, -1)
    extended_ids = jnp.concatenate([left_ids, own_keys, right_ids])
    context, log_sums = attention_forward(
        queries, key_rows, value_rows, from_left, from_right, own_keys[:, None], extended_ids[None]
    )
    block = min(512, tok_dev)
    blocks = tok_dev // block

    def rows_of(rows, block_idx):
        return rows[block_idx * block : (block_idx + 1) * block]

    out_row = out_bias[None]
    attn_parts, attn_others, mlp_outs, d_others = [], [], [], []
    for i in range(blocks):
        attn_parts.append(dot(rows_of(context, i), out_weight, ((1,), (0,)), BF16))
        attn_others.append(narrow_other(attn_parts[i]))
    for i in range(blocks):
        mlp_outs.append(
            mlp(
                i * block,
                tok_full,
                attn_parts[i],
                attn_others[i],
                cotangent,
                ids_col,
                live,
                table_two,
                out_row,
                up_weight,
                up_bias[None],
                down_weight,
            )
        )
        d_others.append(narrow_other(mlp_outs[i][4]))
    norm_two, hidden, d_upper, d_branch = [
        jnp.concatenate(parts, axis=0) for parts in list(zip(*mlp_outs))[:4]
    ]
    d_norms = [outs[4] for outs in mlp_outs]
    branch_parts = [outs[5] for outs in mlp_outs]
    up_sum, down_sum = [sum(outs[i] for outs in mlp_outs)[0] for i in (6, 7)]
    up_grad = dot(d_upper, norm_two, ((0,), (0,)), BF16)
    down_grad = dot(hidden, d_branch, ((0,), (0,)), BF16)
    halved = narrow_count == 2 and blocks == 2 and share == block

    def own_of(parts, index):
        if halved:
            return jnp.where(index == 0, parts[0], parts[1])
        return lax.dynamic_slice_in_dim(jnp.concatenate(parts, axis=0), index * share, share)

    if halved:
        branch_other = swap(own_of(branch_parts, 1 - narrow_index))
    if ring_fits([up_grad]):
        mine = ring_scatter([up_grad, down_grad], 1)
        mine, d_others = lax.optimization_barrier((mine, d_others))
        up_grad, down_grad = [
            lax.all_gather(mine[lane], "wide", axis=0, tiled=True) for lane in range(2)
        ]
    else:
        up_grad, down_grad = lax.psum((up_grad, down_grad), "wide")
    if halved:
        branch = own_of(branch_parts, narrow_index).astype(F32) + branch_other.astype(F32)
    else:
        branch = narrow_scatter(jnp.concatenate(branch_parts, axis=0))
    branch = branch + down_bias.astype(F32)
    d_middle, d_context, out_weight_grad, images_two, out_bias_sum = middle_back(
        narrow_count,
        [attn_parts, attn_others, d_norms, d_others],
        tok_full,
        cotangent,
        context,
        ids_col,
        live,
        ids_row,
        table_two,
        out_row,
        out_weight,
    )
    d_context, branch_parts = lax.optimization_barrier((d_context, branch_parts))
    first_bias = jnp.where(narrow_index == 0, down_bias.astype(F32), 0.0)
    d_gate_two = 0.0
    for i in range(blocks):
        term = rows_of(live, i) * rows_of(cotangent, i).astype(F32)
        term = term * (branch_parts[i].astype(F32) + first_bias)
        d_gate_two += dot(rows_of(onehot_full, i), term.astype(BF16), ((0,), (0,)))
    d_gate_two = narrow_scatter(d_gate_two.astype(BF16), 1)
    d_queries, d_own, d_rim = attention_backward(
        queries,
        key_rows,
        value_rows,
        from_left,
        from_right,
        d_context,
        log_sums,
        own_keys[None],
        extended_ids[:, None],
    )
    rims = jnp.stack([to_right(d_rim[1]), to_left(d_rim[0])])
    lane_rows = (4 * part_width * width + 6 * img_row * mod_width) // (2 * width)
    split = min(lane_rows, 3 * part_width - 16)
    d_norm_part, d_kv, images_one = project_back(
        narrow_count, img_row, tok_full, d_queries, d_own, rims, tail_start[None], ids_row, flat_qkv
    )
    top, bottom, qv_sums = qkv_grads(split, norm_one, d_queries, d_kv)

    def mine_of(images):
        return lax.dynamic_index_in_dim(images, narrow_index, 0, keepdims=False)

    if narrow_count == 2:
        theirs = lax.dynamic_index_in_dim(images_one, 1 - narrow_index, 0, keepdims=False)
        early = mine_of(images_one).astype(F32) + swap(theirs).astype(F32)
    else:
        early = mine_of(lax.psum(images_one, "narrow"))
    images_two = mine_of(images_two)
    loose_parts = [up_sum, down_sum, qv_sums[0], qv_sums[1], out_bias_sum[0]]
    longest = max(part.shape[0] for part in loose_parts)
    loose = [jnp.pad(part[None], ((0, 0), (0, longest - part.shape[0]))) for part in loose_parts]
    loose = jnp.concatenate(loose + [jnp.zeros((3, longest), F32)], axis=0)
    terms = [images_two[0], images_two[1], images_two[2], d_gate_two.astype(BF16)]
    d_mod = [early.astype(BF16)]
    d_mod += [jnp.concatenate(terms[2 * i : 2 * i + 2], axis=1) for i in range(2)]
    if 2 * mod_width == width:
        d_mod_flat = jnp.concatenate(d_mod, axis=0)
    else:
        d_mod_flat = jnp.concatenate(d_mod, axis=1).reshape(-1, width)
    rest = jnp.concatenate([bottom, out_weight_grad, d_mod_flat], axis=0)
    if ring_fits([top]) and top.shape == rest.shape:
        flat, d_norm_other, loose = ring_sum([top, rest], d_norm_part, loose, 0)
        d_norm_one = own(d_norm_part).astype(F32) + d_norm_other.astype(F32)
    else:
        d_norm_one = narrow_scatter(d_norm_part)
        flat = jnp.concatenate(lax.psum((top, rest), "wide"), axis=0)
        loose = lax.psum(loose, "wide")
    tok_own = tokens.astype(F32)
    xhat_one, rstd_one = norm(tok_own)
    hot_own = own(onehot_full)
    scale_one = dot(hot_own, table_one[1], ((1,), (0,)))
    tokens_grad = own(d_middle) + norm_back(d_norm_one * (1.0 + scale_one), xhat_one, rstd_one)
    attn_own = sum(own_of(parts, narrow_index).astype(F32) for parts in (attn_parts, attn_others))
    attn_own = attn_own + out_bias.astype(F32)
    live_own = own(live)
    gates = [dot(hot_own, table_two[j], ((1,), (0,))) for j in (0, 3)]
    layer_out = (tok_own + live_own * (gates[0] * attn_own + gates[1] * branch)).astype(BF16)
    up_weight_grad = turned(up_grad)
    down_weight_grad = down_grad.astype(F32)
    keep = 3 * part_width
    qkv_flat, out_weight_grad = widened(flat, (keep, part_width))
    qkv_weight_grad = jnp.transpose(qkv_flat.reshape(3, part_width, width), (2, 0, 1))
    up_bias_grad, down_bias_grad, query_bias, value_bias, out_bias_grad = [
        loose[i, : part.shape[0]] for i, part in enumerate(loose_parts)
    ]
    qv_bias_grad = jnp.stack([query_bias, value_bias])
    d_mod_flat = flat[keep + part_width :]
    if 2 * mod_width == width:
        d_mod = d_mod_flat.reshape(3, img_row, width)
    else:
        d_mod = jnp.moveaxis(d_mod_flat.reshape(img_row, 3, -1), 1, 0)
    modulator_grad = lax.dot_general(
        d_mod, activated, (((1,), (0,)), ((), ())), preferred_element_type=F32
    )
    modulator_grad = jnp.transpose(modulator_grad.reshape(6, mod_width, width), (2, 0, 1))
    modulator_bias_grad = jnp.sum(d_mod.astype(F32), axis=1).reshape(6, mod_width)
    mod_blocks = mod_rows.reshape(3, 2 * mod_width, width)
    d_activated = sum(dot(d_mod[i], mod_blocks[i], ((1,), (0,))) for i in range(3))
    cond_part = d_activated * sigmoid_rows * (1.0 + cond_rows * (1.0 - sigmoid_rows))
    cond_part = cond_part.astype(BF16)
    condition_grad = cond_part.astype(F32) + narrow_other(cond_part).astype(F32)
    return (
        layer_out,
        tokens_grad,
        condition_grad,
        modulator_grad,
        modulator_bias_grad,
        qkv_weight_grad,
        qv_bias_grad,
        out_weight_grad,
        out_bias_grad,
        up_weight_grad,
        up_bias_grad,
        down_weight_grad,
        down_bias_grad,
    )


def solution(mesh):
    in_specs = (
        P(("wide", "narrow"), None),
        P(),
        P("wide", None),
        P(None, None, "narrow"),
        P(None, "narrow"),
        P(None, None, "narrow"),
        P(None, "narrow"),
        P("narrow", None),
        P(),
        P(None, "narrow"),
        P("narrow"),
        P("narrow", None),
        P(),
        P(),
        P(),
    )
    out_specs = (
        P(("wide", "narrow"), None),
        P(("wide", "narrow"), None),
        P(),
        P(None, None, "narrow"),
        P(None, "narrow"),
        P(None, None, "narrow"),
        P(None, "narrow"),
        P("narrow", None),
        P(),
        P(None, "narrow"),
        P("narrow"),
        P("narrow", None),
        P(),
    )
    return jax.shard_map(body, mesh=mesh, in_specs=in_specs, out_specs=out_specs, check_vma=False)
```
